32 devices in a mesh: seg: 8 (over y, x, core), head: 4 (over z).
Axes of the slice: x: 2, y: 2, z: 4, core: 2. Of those that a mesh axis runs over, the one named last changes fastest.
Arguments:
- tokens: bfloat16 [8192, 2048], P(('seg', 'head')), may hold values from -6 to 6
- cotangent: bfloat16 [8192, 2048], P(('seg', 'head')), may hold values from -6 to 6
- gain_attn: float32 [2048], replicated, may hold values from 0.5 to 1.5
- gain_mlp: float32 [2048], replicated, may hold values from 0.5 to 1.5
- w_query: bfloat16 [2048, 2048], P(None, 'head'), may hold values from -0.1875 to 0.1875
- w_key: bfloat16 [2048, 2048], P(None, 'head'), may hold values from -0.125 to 0.125
- w_value: bfloat16 [2048, 2048], P(None, 'head'), may hold values from -0.125 to 0.125
- w_out: bfloat16 [2048, 2048], P('head'), may hold values from -0.5 to 0.5
- w_gate: bfloat16 [2048, 8192], P(None, 'head'), may hold values from -0.125 to 0.125
- w_up: bfloat16 [2048, 8192], P(None, 'head'), may hold values from -0.125 to 0.125
- w_down: bfloat16 [8192, 2048], P('head'), may hold values from -0.0625 to 0.0625
- mem_gate: float32 [16], P('head'), may hold values from -2 to 2
- lengths: int32 [2], replicated, may hold values from 256 to 768, as said below
Outputs:
- output: bfloat16 [8192, 2048], P(('seg', 'head'))
- grad_tokens: bfloat16 [8192, 2048], P(('seg', 'head'))
- memory_after: float32 [8, 16, 128, 128], P('seg', 'head')
- normal_after: float32 [8, 16, 128], P('seg', 'head')
- grad_gain_attn: float32 [2048], replicated
- grad_gain_mlp: float32 [2048], replicated
- grad_query: float32 [2048, 2048], P(None, 'head')
- grad_key: float32 [2048, 2048], P(None, 'head')
- grad_value: float32 [2048, 2048], P(None, 'head')
- grad_out: float32 [2048, 2048], P('head')
- grad_gate: float32 [2048, 8192], P(None, 'head')
- grad_up: float32 [2048, 8192], P(None, 'head')
- grad_down: float32 [8192, 2048], P('head')
- grad_mem_gate: float32 [16], P('head')
The draws below stay inside these ranges and needn't reach their ends.
Inputs may be any that keep to these rules, and one draw needn't show every extreme that they name: The last segment of sequence b holds valid tokens in its first lengths[b] places; the other places are padding. Some sequence has exactly 768.
All inputs are finite; a program needn't handle non-finite values.
Results may differ from the reference program's by a relative error of at most 0.014.
Values may be sent and summed in bfloat16 or wider, within the bound.
A program may use at most 320 MiB of HBM per device.

```python
import math
import jax
import jax.numpy as jnp
from jax import lax

D = 2048
H = 16
DH = 128
FF = 8192
SEG_LEN = 1024
SEGS = 4
SEQS = 2
SEGMENTS = 8
TOKENS = 8192


def draw_lengths(key, part):
    count_key = jax.random.fold_in(key, 7101)
    pick_key = jax.random.fold_in(key, 7202)
    lowest = SEG_LEN // 4
    highest_len = 3 * SEG_LEN // 4
    counts = jax.random.randint(count_key, (SEQS,), lowest, highest_len + 1)
    chosen = jax.random.randint(pick_key, (), 0, SEQS)
    counts = jnp.where(lax.iota(jnp.int32, SEQS) == chosen, highest_len, counts)
    return counts.astype(jnp.int32)


def block_levels(key, shape, pieces, low, largest):
    factor_of, own = 1.0, jax.random.fold_in(key, 6)
    for axis_at, parts in pieces:
        heights = jnp.exp(jax.random.uniform(jax.random.fold_in(own, axis_at), (parts,), jnp.float32, low / len(pieces), largest / len(pieces)))
        factor_of = factor_of * jnp.repeat(heights, shape[axis_at] // parts).reshape([-1 if axis == axis_at else 1 for axis in range(len(shape))])
    return factor_of


def noise(rng, dims, deviation, most, split=(), dtype=jnp.bfloat16):
    values = deviation * jax.random.normal(rng, dims, jnp.float32)
    if split:
        values = values * block_levels(rng, dims, split, -0.22, 0.18)
    return jnp.clip(values, -most, most).astype(dtype)


def setup_inputs(seed: int = 0) -> dict:
    arg_keys = jax.random.split(jax.random.key(seed), 14)
    return {
        "tokens": noise(arg_keys[0], (TOKENS, D), 1.0, 6.0, ((0, 32),)),
        "cotangent": noise(arg_keys[1], (TOKENS, D), 1.0, 6.0, ((0, 32),)),
        "gain_attn": jnp.clip(1.0 + 0.1 * jax.random.normal(arg_keys[2], (D,), jnp.float32), 0.5, 1.5),
        "gain_mlp": jnp.clip(1.0 + 0.1 * jax.random.normal(arg_keys[3], (D,), jnp.float32), 0.5, 1.5),
        "w_query": noise(arg_keys[4], (D, H * DH), (D // 2) ** -0.5, 0.1875, ((1, 4),)),
        "w_key": noise(arg_keys[5], (D, H * DH), D ** -0.5, 0.125, ((1, 4),)),
        "w_value": noise(arg_keys[6], (D, H * DH), D ** -0.5, 0.125, ((1, 4),)),
        "w_out": noise(arg_keys[7], (H * DH, D), (H * DH // 16) ** -0.5, 0.5, ((0, 4),)),
        "w_gate": noise(arg_keys[8], (D, FF), D ** -0.5, 0.125, ((1, 4),)),
        "w_up": noise(arg_keys[9], (D, FF), D ** -0.5, 0.125, ((1, 4),)),
        "w_down": noise(arg_keys[10], (FF, D), FF ** -0.5, 0.0625, ((0, 4),)),
        "mem_gate": jnp.clip(jax.random.uniform(arg_keys[11], (H,), jnp.float32, -2.0, 2.0) * block_levels(arg_keys[11], (H,), ((0, 4),), -0.4, 0.0), -2.0, 2.0),
        "lengths": draw_lengths(jax.random.fold_in(arg_keys[13], 71), 0),
    }


highest = lax.Precision.HIGHEST
epsilon = 1e-05
masked_score = -1e+30

@jax.custom_vjp
def low(v):
    return lax.optimization_barrier(v.astype(jnp.bfloat16)).astype(jnp.float32)

@jax.custom_vjp
def low_back(v):
    return v

def low_keep(v):
    return (low(v), None)

def low_pass(kept, grad):
    return (grad,)

def back_keep(v):
    return (v, None)

def back_low(kept, grad):
    return (low(grad),)
low.defvjp(low_keep, low_pass)
low_back.defvjp(back_keep, back_low)

def rms_scaled(values, gain_vec):
    return values * lax.rsqrt(lax.optimization_barrier(jnp.mean(values * values, axis=-1, keepdims=True)) + epsilon) * gain_vec

def matmul(left, right):
    return jnp.dot(left, right, precision=highest)

def elu_plus(values):
    return jnp.where(values > 0, values + 1.0, jnp.exp(jnp.minimum(values, 0.0)))

def split_heads(values):
    return values.reshape(SEQS, SEGS, SEG_LEN, H, DH).transpose(1, 0, 3, 2, 4)

def block_layer(tokens, gain_attn, gain_mlp, w_query, w_key, w_value, w_out, w_gate, w_up, w_down, mem_gate, valid_mask):
    normed_attn = low(rms_scaled(tokens, gain_attn))
    queries = low_back(low(matmul(normed_attn, w_query)))
    key_rows = low_back(low(matmul(normed_attn, w_key)))
    value_rows = low_back(low(matmul(normed_attn, w_value)))
    place_index = lax.iota(jnp.int32, SEG_LEN)
    causal = place_index[:, None] >= place_index[None, :]
    mix_weight = jax.nn.sigmoid(mem_gate)[None, :, None, None]
    score_scale = 1.0 / math.sqrt(DH)

    def segment_step(carried, inputs):
        memory, normal = carried
        query_seg, key_seg, value_seg, valid_seg = inputs
        query_feat = elu_plus(query_seg)
        key_feat = elu_plus(key_seg) * valid_seg[:, None, :, None]
        numerator = jnp.einsum('bhld,bhde->bhle', query_feat, memory, precision=highest)
        denominator = jnp.einsum('bhld,bhd->bhl', query_feat, normal, precision=highest) + 1.0
        retrieved = numerator / denominator[..., None]
        raw_scores = low_back(jnp.einsum('bhqd,bhkd->bhqk', query_seg, key_seg, precision=highest)) * score_scale
        allowed = causal[None, None] & (valid_seg[:, None, None, :] > 0.5)
        soft_weights = low(jax.nn.softmax(jnp.where(allowed, raw_scores, masked_score), axis=-1))
        local_attn = low_back(jnp.einsum('bhqk,bhkd->bhqd', soft_weights, value_seg, precision=highest))
        mixed_out = mix_weight * retrieved + (1.0 - mix_weight) * local_attn
        memory_new = memory + jnp.einsum('bhld,bhle->bhde', key_feat, value_seg, precision=highest)
        normal_new = normal + lax.optimization_barrier(jnp.sum(key_feat, axis=2))
        return ((memory_new, normal_new), (mixed_out, memory_new, normal_new))
    initial = (jnp.zeros((SEQS, H, DH, DH), jnp.float32), jnp.zeros((SEQS, H, DH), jnp.float32))
    inputs = (split_heads(queries), split_heads(key_rows), split_heads(value_rows), valid_mask.transpose(1, 0, 2))
    final_state, (mixed_out, memories, normals) = lax.scan(jax.checkpoint(segment_step), initial, inputs)
    mixed_attn = low(mixed_out.transpose(1, 0, 3, 2, 4).reshape(TOKENS, H * DH))
    attn_out = low_back(matmul(mixed_attn, w_out))
    hidden_res = tokens + attn_out
    normed_mlp = low(rms_scaled(hidden_res, gain_mlp))
    gate_pre = low_back(matmul(normed_mlp, w_gate))
    up_proj = low_back(matmul(normed_mlp, w_up))
    activation = low(jax.nn.silu(gate_pre) * up_proj)
    output = hidden_res + matmul(activation, w_down)
    memory_after = memories.transpose(1, 0, 2, 3, 4).reshape(SEGMENTS, H, DH, DH) * (1.0 / math.sqrt(SEG_LEN))
    normal_after = normals.transpose(1, 0, 2, 3).reshape(SEGMENTS, H, DH) / SEG_LEN
    return (output, (memory_after, normal_after))

def reference(tokens, cotangent, gain_attn, gain_mlp, w_query, w_key, w_value, w_out, w_gate, w_up, w_down, mem_gate, lengths):
    place_index = lax.iota(jnp.int32, SEG_LEN)
    last_segment = lax.iota(jnp.int32, SEGS) == SEGS - 1
    valid_mask = jnp.where(last_segment[None, :, None], place_index[None, None, :] < lengths[:, None, None], True).astype(jnp.float32)
    primals = (tokens.astype(jnp.float32), gain_attn, gain_mlp, w_query.astype(jnp.float32), w_key.astype(jnp.float32), w_value.astype(jnp.float32), w_out.astype(jnp.float32), w_gate.astype(jnp.float32), w_up.astype(jnp.float32), w_down.astype(jnp.float32), mem_gate)

    def forward(*values):
        return block_layer(*values, valid_mask)
    output, pullback, (memory_after, normal_after) = jax.vjp(forward, *primals, has_aux=True)
    gradients = pullback(cotangent.astype(jnp.float32))
    return (output.astype(jnp.bfloat16), gradients[0].astype(jnp.bfloat16), memory_after, normal_after, gradients[1], gradients[2], gradients[3], gradients[4], gradients[5], gradients[6], gradients[7], gradients[8], gradients[9], gradients[10])
```

```python
import functools

import jax
import jax.numpy as jnp
from jax import lax
from jax.experimental import pallas as pl
from jax.experimental.pallas import tpu as pltpu
from jax.sharding import PartitionSpec as P

DH = 128
SEG_LEN = 1024
SEGS = 4
MEM_ROWS = DH + 8
BLOCK = 256

epsilon = 1e-05
masked_score = -1e30
highest = lax.Precision.HIGHEST
F32 = jnp.float32
BF16 = jnp.bfloat16


MESH = pl.DeviceIdType.MESH
LAND_SLOTS = 8
RESULT_SLOTS = 12
SUM_SEMS = 8
SUM_HOP = 2


def bits_of(size):
    return size.bit_length() - 1


def flip(index, power):
    return index + power - 2 * power * lax.rem(index // power, 2)


def sum_engine(arrays, outs, tile, seg_bits, scratch):
    mine, result, send_sem, recv_sem, load_sem, store_sem, *lands = scratch
    seg = lax.axis_index("seg")
    planes = seg_bits - 1
    high, wide = tile
    shapes = [array.shape for array in arrays]
    counts = [(rows // high) * (cols // wide) for rows, cols in shapes]
    starts = [sum(counts[:i]) for i in range(len(counts))]
    total = sum(counts)

    def power(k, level):
        if level == 0:
            return 1
        which = lax.rem(k + level - 1, planes)
        value = 2
        for bit in range(1, planes):
            value = jnp.where(which == bit, 2 << bit, value)
        return value

    def my_bit(k, level):
        return lax.rem(seg // power(k, level), 2)

    def part(k, level, own):
        half = high >> (level + 1)
        bit = my_bit(k, level) if own else 1 - my_bit(k, level)
        return pl.ds(pl.multiple_of(bit * half, half), half)

    def kept(k, levels):
        first = 0
        for level in range(levels):
            first = first + my_bit(k, level) * (high >> (level + 1))
        return pl.ds(pl.multiple_of(first, high >> levels), high >> levels)

    def pick(k, act):
        for i in range(len(arrays)):

            @pl.when((k >= starts[i]) & (k < starts[i] + counts[i]))
            def _(i=i):
                across = shapes[i][1] // wide
                place = k - starts[i]
                row = pl.multiple_of((place // across) * high, high)
                col = pl.multiple_of(lax.rem(place, across) * wide, wide)
                act(i, row, col)

    def halving(k, level, source):
        return pltpu.make_async_remote_copy(
            src_ref=source,
            dst_ref=lands[level].at[lax.rem(k, LAND_SLOTS)],
            send_sem=send_sem.at[level, lax.rem(k, SUM_SEMS)],
            recv_sem=recv_sem.at[level, lax.rem(k, SUM_SEMS)],
            device_id={"seg": flip(seg, power(k, level))},
            device_id_type=MESH,
        )

    def first_source(k, i, row, col, own):
        half = high // 2
        bit = my_bit(k, 0) if own else 1 - my_bit(k, 0)
        return arrays[i].at[pl.ds(pl.multiple_of(row + bit * half, half), half), pl.ds(col, wide)]

    def keep(k, i, row, col):
        slot = lax.rem(k, 4)
        return pltpu.make_async_copy(
            first_source(k, i, row, col, True), mine.at[slot], load_sem.at[slot]
        )

    def level_source(k, level):
        return lands[level - 1].at[lax.rem(k, LAND_SLOTS), part(k, level, False)]

    def doubling(k, level):
        ref = result.at[lax.rem(k, RESULT_SLOTS), kept(k, level + 1)]
        return pltpu.make_async_remote_copy(
            src_ref=ref,
            dst_ref=ref,
            send_sem=send_sem.at[seg_bits + level, lax.rem(k, SUM_SEMS)],
            recv_sem=recv_sem.at[seg_bits + level, lax.rem(k, SUM_SEMS)],
            device_id={"seg": flip(seg, power(k, level))},
            device_id_type=MESH,
        )

    def store(k, i, row, col):
        slot = lax.rem(k, 4)
        return pltpu.make_async_copy(
            result.at[lax.rem(k, RESULT_SLOTS)],
            outs[i].at[pl.ds(row, high), pl.ds(col, wide)],
            store_sem.at[slot],
        )

    def do_first(k):
        def go(i, row, col):
            halving(k, 0, first_source(k, i, row, col, False)).start()
            keep(k, i, row, col).start()

        pick(k, go)

    def arrived(k, level):
        slot = lax.rem(k, LAND_SLOTS)
        if level == 0:
            halving(k, 0, first_source(k, 0, 0, 0, False)).wait()
            keep(k, 0, 0, 0).wait()
            other = mine[lax.rem(k, 4)]
        else:
            halving(k, level, level_source(k, level)).wait()
            other = lands[level - 1][slot, part(k, level, True)]
        return (lands[level][slot].astype(F32) + other.astype(F32)).astype(BF16)

    def do_level(k, level):
        lands[level - 1][lax.rem(k, LAND_SLOTS)] = arrived(k, level - 1)
        halving(k, level, level_source(k, level)).start()

    def do_total(k):
        result[lax.rem(k, RESULT_SLOTS), kept(k, seg_bits)] = arrived(k, seg_bits - 1)
        doubling(k, seg_bits - 1).start()

    def do_spread(k, level):
        doubling(k, level + 1).wait()
        doubling(k, level).start()

    def do_finish(k):
        doubling(k, 0).wait()
        pick(k, lambda i, row, col: store(k, i, row, col).start())

    def do_store(k):
        store(k, 0, 0, 0).wait()

    stages = [(0, do_first), (1, functools.partial(do_level, level=1))]
    when = 1
    for level in range(2, seg_bits):
        when += SUM_HOP
        stages.append((when, functools.partial(do_level, level=level)))
    when += SUM_HOP
    stages.append((when, do_total))
    for level in range(seg_bits - 2, -1, -1):
        when += SUM_HOP
        stages.append((when, functools.partial(do_spread, level=level)))
    stages.append((when + 1, do_finish))
    stages.append((when + 3, do_store))

    def step(t):
        for delay, act in reversed(stages):
            k = t - delay

            @pl.when((k >= 0) & (k < total))
            def _(act=act, k=k):
                act(k)

    return step, total + when + 3


def engine_scratch(tile, seg_bits):
    high, wide = tile
    return [
        pltpu.VMEM((4, high // 2, wide), BF16),
        pltpu.VMEM((RESULT_SLOTS, high, wide), BF16),
        pltpu.SemaphoreType.DMA((2 * seg_bits, SUM_SEMS)),
        pltpu.SemaphoreType.DMA((2 * seg_bits, SUM_SEMS)),
        pltpu.SemaphoreType.DMA((4,)),
        pltpu.SemaphoreType.DMA((4,)),
    ] + [pltpu.VMEM((LAND_SLOTS, high >> (l + 1), wide), BF16) for l in range(seg_bits)]


def greet_seg(seg_bits):
    barrier = pltpu.get_barrier_semaphore()
    seg = lax.axis_index("seg")
    for bit in range(seg_bits):
        pl.semaphore_signal(
            barrier, inc=1, device_id={"seg": flip(seg, 1 << bit)}, device_id_type=MESH
        )


def grad_sum_kernel(count, tile, seg_bits, head_bits, *refs):
    small_in, arrays = refs[0], refs[1 : 1 + count]
    small_out, outs = refs[1 + count], refs[2 + count : 2 + 2 * count]
    small_buf, small_land, small_send, small_recv, *scratch = refs[2 + 2 * count :]
    seg, head = lax.axis_index("seg"), lax.axis_index("head")
    greet_seg(seg_bits)
    barrier = pltpu.get_barrier_semaphore()
    for bit in range(head_bits):
        pl.semaphore_signal(
            barrier, inc=1, device_id={"head": flip(head, 1 << bit)}, device_id_type=MESH
        )
    pl.semaphore_wait(barrier, seg_bits + head_bits)
    rounds = seg_bits + head_bits

    def small_copy(j):
        if j < seg_bits:
            where = {"seg": flip(seg, 1 << j)}
        else:
            where = {"head": flip(head, 1 << (j - seg_bits))}
        return pltpu.make_async_remote_copy(
            src_ref=small_buf.at[j],
            dst_ref=small_land.at[j],
            send_sem=small_send.at[j],
            recv_sem=small_recv.at[j],
            device_id=where,
            device_id_type=MESH,
        )

    engine_step, steps = sum_engine(arrays, outs, tile, seg_bits, scratch)

    def step(t, carry):
        engine_step(t)
        for j in range(rounds + 1):

            @pl.when(t == 3 * j)
            def _(j=j):
                if j == 0:
                    small_buf[0] = small_in[...]
                else:
                    small_copy(j - 1).wait()
                    value = small_buf[j - 1] + small_land[j - 1]
                    if j < rounds:
                        small_buf[j] = value
                    else:
                        small_out[...] = value
                if j < rounds:
                    small_copy(j).start()

        return carry

    lax.fori_loop(0, max(steps, 3 * rounds + 1), step, 0)


def grad_sum(small, arrays, tile, seg_size, head_size, cid):
    seg_bits, head_bits = bits_of(seg_size), bits_of(head_size)
    rounds = seg_bits + head_bits
    count = len(arrays)
    moved = sum(rows * cols for rows, cols in (array.shape for array in arrays))
    any_, vmem = pl.BlockSpec(memory_space=pltpu.HBM), pl.BlockSpec(memory_space=pltpu.VMEM)
    return pl.pallas_call(
        functools.partial(grad_sum_kernel, count, tile, seg_bits, head_bits),
        in_specs=[vmem] + [any_] * count,
        out_specs=[vmem] + [any_] * count,
        out_shape=[jax.ShapeDtypeStruct(small.shape, F32)]
        + [jax.ShapeDtypeStruct(array.shape, BF16) for array in arrays],
        scratch_shapes=[
            pltpu.VMEM((rounds, *small.shape), F32),
            pltpu.VMEM((rounds, *small.shape), F32),
            pltpu.SemaphoreType.DMA((rounds,)),
            pltpu.SemaphoreType.DMA((rounds,)),
        ]
        + engine_scratch(tile, seg_bits),
        cost_estimate=pl.CostEstimate(flops=0, bytes_accessed=moved * 60, transcendentals=0),
        compiler_params=pltpu.CompilerParams(
            collective_id=cid, has_side_effects=True, vmem_limit_bytes=48 * 2**20
        ),
    )(small, *arrays)


ROWS = 32
HOP = 2
SEND_SLOTS = 4
BLOCK_ROWS = 256
LINE_REFS = 8


def line_exchange(own, finish, before, scratch, extra=None, extra_steps=0):
    up_land, down_land, up_send, down_send, up_recv_sem, down_recv_sem, up_send_sem, down_send_sem = scratch
    size = lax.axis_size("head")
    place = lax.axis_index("head")
    slots = up_land.shape[0]
    chunks = own.shape[0] // ROWS
    last = size - 1

    def up_copy(k):
        return pltpu.make_async_remote_copy(
            src_ref=up_send.at[lax.rem(k, SEND_SLOTS)],
            dst_ref=up_land.at[lax.rem(k, slots)],
            send_sem=up_send_sem.at[lax.rem(k, SEND_SLOTS)],
            recv_sem=up_recv_sem.at[lax.rem(k, slots)],
            device_id={"head": lax.rem(place + 1, size)},
            device_id_type=MESH,
        )

    def down_copy(k):
        return pltpu.make_async_remote_copy(
            src_ref=down_send.at[lax.rem(k, SEND_SLOTS)],
            dst_ref=down_land.at[lax.rem(k, slots)],
            send_sem=down_send_sem.at[lax.rem(k, SEND_SLOTS)],
            recv_sem=down_recv_sem.at[lax.rem(k, slots)],
            device_id={"head": lax.rem(place + last, size)},
            device_id_type=MESH,
        )

    def rows_of(k):
        return pl.ds(pl.multiple_of(k * ROWS, ROWS), ROWS)

    def pass_on(k, copy, land, send, has_source, has_target):
        @pl.when(has_source)
        def _():
            copy(k).wait_recv()

        @pl.when(has_target)
        def _():
            slot = lax.rem(k, SEND_SLOTS)

            @pl.when(k >= SEND_SLOTS)
            def _():
                copy(k - SEND_SLOTS).wait_send()

            @pl.when(has_source)
            def _():
                send[slot] = (own[rows_of(k)] + land[lax.rem(k, slots)].astype(F32)).astype(BF16)

            @pl.when(jnp.logical_not(has_source))
            def _():
                send[slot] = own[rows_of(k)].astype(BF16)

            copy(k).start()

    far = jnp.maximum(place, last - place)

    def step(t, carry):
        before(t)
        down = t - (last - place) * HOP

        @pl.when((down >= 0) & (down < chunks))
        def _():
            pass_on(down, down_copy, down_land, down_send, place < last, place > 0)

        up = t - place * HOP

        @pl.when((up >= 0) & (up < chunks))
        def _():
            pass_on(up, up_copy, up_land, up_send, place > 0, place < last)

        k = t - far * HOP

        @pl.when((k >= 0) & (k < chunks))
        def _():
            slot = lax.rem(k, slots)

            @pl.when(place == 0)
            def _():
                finish(k, own[rows_of(k)] + down_land[slot].astype(F32))

            @pl.when(place == last)
            def _():
                finish(k, own[rows_of(k)] + up_land[slot].astype(F32))

            @pl.when((place > 0) & (place < last))
            def _():
                finish(
                    k,
                    own[rows_of(k)] + up_land[slot].astype(F32) + down_land[slot].astype(F32),
                )

        if extra is not None:
            extra(t)
        return carry

    lax.fori_loop(0, max(chunks + last * HOP, extra_steps), step, 0)
    for k in range(chunks - SEND_SLOTS, chunks):

        @pl.when(place < last)
        def _(k=k):
            up_copy(k).wait_send()

        @pl.when(place > 0)
        def _(k=k):
            down_copy(k).wait_send()


def line_barrier(others=0):
    size = lax.axis_size("head")
    place = lax.axis_index("head")
    barrier = pltpu.get_barrier_semaphore()
    inner = (place > 0) & (place < size - 1)

    def greet(near):
        pl.semaphore_signal(
            barrier, inc=1, device_id={"head": lax.rem(near, size)}, device_id_type=MESH
        )

    @pl.when(place > 0)
    def _():
        greet(place + size - 1)

    @pl.when(place < size - 1)
    def _():
        greet(place + 1)

    @pl.when(inner)
    def _():
        pl.semaphore_wait(barrier, 2 + others)

    @pl.when(jnp.logical_not(inner))
    def _():
        pl.semaphore_wait(barrier, 1 + others)


def line_scratch(size, width):
    slots = (size - 1) * HOP + 2
    return [
        pltpu.VMEM((slots, ROWS, width), BF16),
        pltpu.VMEM((slots, ROWS, width), BF16),
        pltpu.VMEM((SEND_SLOTS, ROWS, width), BF16),
        pltpu.VMEM((SEND_SLOTS, ROWS, width), BF16),
        pltpu.SemaphoreType.DMA((slots,)),
        pltpu.SemaphoreType.DMA((slots,)),
        pltpu.SemaphoreType.DMA((SEND_SLOTS,)),
        pltpu.SemaphoreType.DMA((SEND_SLOTS,)),
    ]


def attn_out_kernel(
    mixed_ref, weight_ref, token_ref, gain_ref, hidden_ref, normed_ref,
    hidden, normed, hidden_sem, normed_sem, *scratch
):
    line_barrier()
    per_block = BLOCK_ROWS // ROWS
    blocks = hidden.shape[0] // BLOCK_ROWS

    def block_rows(b):
        return pl.ds(pl.multiple_of(b * BLOCK_ROWS, BLOCK_ROWS), BLOCK_ROWS)

    def before(t):
        @pl.when((lax.rem(t, per_block) == 0) & (t < blocks * per_block))
        def _():
            rows = block_rows(t // per_block)
            hidden[rows] = dot(mixed_ref[rows], weight_ref[...], NN)

    def stores(b):
        rows = block_rows(b)
        return (
            pltpu.make_async_copy(hidden.at[rows], hidden_ref.at[rows], hidden_sem.at[b]),
            pltpu.make_async_copy(normed.at[rows], normed_ref.at[rows], normed_sem.at[b]),
        )

    def finish(k, total):
        rows = pl.ds(pl.multiple_of(k * ROWS, ROWS), ROWS)
        value = token_ref[rows].astype(F32) + total
        hidden[rows] = value
        normed[rows] = (value * inverse_rms(value) * gain_ref[...]).astype(BF16)

        @pl.when(lax.rem(k, per_block) == per_block - 1)
        def _():
            for copy in stores(k // per_block):
                copy.start()

    line_exchange(hidden, finish, before, scratch)
    for b in range(blocks):
        for copy in stores(b):
            copy.wait()


def attn_out_sum(mixed, weight, tokens, gain, size, cid):
    rows, width = tokens.shape
    vmem, any_ = pl.BlockSpec(memory_space=pltpu.VMEM), pl.BlockSpec(memory_space=pl.ANY)
    blocks = rows // BLOCK_ROWS
    return pl.pallas_call(
        attn_out_kernel,
        in_specs=[vmem] * 4,
        out_specs=[any_] * 2,
        out_shape=[jax.ShapeDtypeStruct((rows, width), F32), jax.ShapeDtypeStruct((rows, width), BF16)],
        scratch_shapes=[
            pltpu.VMEM((rows, width), F32),
            pltpu.VMEM((rows, width), BF16),
            pltpu.SemaphoreType.DMA((blocks,)),
            pltpu.SemaphoreType.DMA((blocks,)),
        ]
        + line_scratch(size, width),
        cost_estimate=pl.CostEstimate(
            flops=2 * rows * width * mixed.shape[1], bytes_accessed=150 * 2**20, transcendentals=0
        ),
        compiler_params=pltpu.CompilerParams(
            collective_id=cid, has_side_effects=True, vmem_limit_bytes=48 * 2**20
        ),
    )(mixed, weight, tokens, gain.reshape(1, width))


def mlp_back_kernel(
    tile, seg_bits,
    d_gate_hbm, d_up_hbm, w_gate_hbm, w_up_hbm, hidden_hbm, grad_hbm, gain_ref, sum_in,
    d_out_ref, d_own_ref, gain_part_ref, sum_out,
    d_gate, d_up, w_gate, w_up, hidden, grad, own, load_sem, store_sem, *scratch
):
    per_block = BLOCK_ROWS // ROWS
    blocks = own.shape[0] // BLOCK_ROWS
    size = lax.axis_size("head")
    place = lax.axis_index("head")
    per_device = own.shape[0] // ROWS // size
    loads = [
        pltpu.make_async_copy(source, target, load_sem.at[i])
        for i, (source, target) in enumerate(
            ((d_gate_hbm, d_gate), (w_gate_hbm, w_gate), (d_up_hbm, d_up), (w_up_hbm, w_up),
             (hidden_hbm, hidden), (grad_hbm, grad))
        )
    ]
    for load in loads:
        load.start()
    gain_part_ref[...] = jnp.zeros_like(gain_part_ref)
    greet_seg(seg_bits)
    line_barrier(seg_bits)
    engine_step, steps = sum_engine(
        [sum_in], [sum_out], tile, seg_bits, scratch[LINE_REFS:]
    )

    def block_rows(b):
        return pl.ds(pl.multiple_of(b * BLOCK_ROWS, BLOCK_ROWS), BLOCK_ROWS)

    for load in loads[:4]:
        load.wait()

    def before(t):
        @pl.when((lax.rem(t, per_block) == 0) & (t < blocks * per_block))
        def _():
            rows = block_rows(t // per_block)
            own[rows] = dot(d_gate[rows], w_gate[...], NT) + dot(d_up[rows], w_up[...], NT)

        @pl.when(t == 0)
        def _():
            for load in loads[4:]:
                load.wait()

    def store(b):
        rows = block_rows(b)
        return pltpu.make_async_copy(grad.at[rows], d_out_ref.at[rows], store_sem.at[b])

    def finish(k, total):
        rows = pl.ds(pl.multiple_of(k * ROWS, ROWS), ROWS)
        value = hidden[rows]
        inverse = inverse_rms(value)
        normal = value * inverse
        scaled = gain_ref[...] * total
        mean = jnp.mean(scaled * normal, axis=-1, keepdims=True)
        d_hidden = grad[rows].astype(F32) + inverse * (scaled - normal * mean)
        grad[rows] = d_hidden.astype(BF16)

        @pl.when(k // per_device == place)
        def _():
            mine = pl.ds(pl.multiple_of(lax.rem(k, per_device) * ROWS, ROWS), ROWS)
            d_own_ref[mine] = d_hidden
            gain_part_ref[...] += jnp.sum((total * normal).reshape(ROWS // 8, 8, -1), axis=0)

        @pl.when(lax.rem(k, per_block) == per_block - 1)
        def _():
            store(k // per_block).start()

    line_exchange(own, finish, before, scratch[:LINE_REFS], engine_step, steps)
    for b in range(blocks):
        store(b).wait()


def mlp_back_sum(d_gate, d_up, w_gate, w_up, hidden, grad, gain, summed, tile, seg_size, size, cid):
    rows, width = hidden.shape
    units = d_gate.shape[1]
    seg_bits = bits_of(seg_size)
    vmem, any_ = pl.BlockSpec(memory_space=pltpu.VMEM), pl.BlockSpec(memory_space=pltpu.HBM)
    blocks = rows // BLOCK_ROWS
    return pl.pallas_call(
        functools.partial(mlp_back_kernel, tile, seg_bits),
        in_specs=[any_] * 6 + [vmem, any_],
        out_specs=[any_, vmem, vmem, any_],
        out_shape=[
            jax.ShapeDtypeStruct((rows, width), BF16),
            jax.ShapeDtypeStruct((rows // size, width), F32),
            jax.ShapeDtypeStruct((8, width), F32),
            jax.ShapeDtypeStruct(summed.shape, BF16),
        ],
        scratch_shapes=[
            pltpu.VMEM((rows, units), BF16),
            pltpu.VMEM((rows, units), BF16),
            pltpu.VMEM((width, units), BF16),
            pltpu.VMEM((width, units), BF16),
            pltpu.VMEM((rows, width), F32),
            pltpu.VMEM((rows, width), BF16),
            pltpu.VMEM((rows, width), F32),
            pltpu.SemaphoreType.DMA((6,)),
            pltpu.SemaphoreType.DMA((blocks,)),
        ]
        + line_scratch(size, width)
        + engine_scratch(tile, seg_bits),
        cost_estimate=pl.CostEstimate(
            flops=4 * rows * width * units, bytes_accessed=250 * 2**20, transcendentals=0
        ),
        compiler_params=pltpu.CompilerParams(
            collective_id=cid, has_side_effects=True, vmem_limit_bytes=62 * 2**20
        ),
    )(d_gate, d_up, w_gate, w_up, hidden, grad, gain.reshape(1, width), summed)


MLP_BLOCK = 256
MLP_ROWS = 1024


def mlp_kernel(
    rows_ref, grad_ref, w_gate_ref, w_up_ref, w_down_ref,
    d_gate_ref, d_up_ref, grad_gate_ref, grad_up_top, grad_up_low, grad_down_ref, out_ref,
    flipped, act, total,
):
    count, width = rows_ref.shape
    first = pl.program_id(0) == 0
    last = pl.program_id(0) == pl.num_programs(0) - 1

    @pl.when(first)
    def _():
        total[...] = jnp.zeros_like(total)

        @pl.loop(0, width // MLP_ROWS)
        def _(i):
            part = pl.ds(pl.multiple_of(i * MLP_ROWS, MLP_ROWS), MLP_ROWS)
            flipped[part] = rows_ref[:, part].T

    @pl.loop(0, count // MLP_ROWS)
    def _(i):
        part = pl.ds(pl.multiple_of(i * MLP_ROWS, MLP_ROWS), MLP_ROWS)
        rows = rows_ref[part]
        gate_pre = dot(rows, w_gate_ref[...], NN)
        up_proj = dot(rows, w_up_ref[...], NN)
        d_act = dot(grad_ref[part], w_down_ref[...], NT)
        gate_sig = jax.nn.sigmoid(gate_pre)
        silu_gate = gate_pre * gate_sig
        activation = (silu_gate * up_proj).astype(BF16)
        act[part] = activation
        d_gate_ref[part] = (
            d_act * up_proj * gate_sig * (1.0 + gate_pre * (1.0 - gate_sig))
        ).astype(BF16)
        d_up_ref[part] = (d_act * silu_gate).astype(BF16)
        total[part] += dot(activation, w_down_ref[...], NN)

    @pl.loop(0, width // MLP_ROWS)
    def _(i):
        part = pl.ds(pl.multiple_of(i * MLP_ROWS, MLP_ROWS), MLP_ROWS)
        grad_gate_ref[part] = dot(flipped[part], d_gate_ref[...], NN).astype(BF16)
        grad_down_ref[:, part] = dot(act[...], grad_ref[:, part], TN).astype(BF16)

    top = grad_up_top.shape[0]
    grad_up_top[...] = dot(flipped[:top], d_up_ref[...], NN).astype(BF16)
    grad_up_low[...] = dot(flipped[top:], d_up_ref[...], NN).astype(BF16)

    @pl.when(last)
    def _():
        out_ref[...] = total[...].astype(BF16)


def mlp_both(rows, grad, w_gate, w_up, w_down):
    count, width = rows.shape
    units = w_gate.shape[1]
    block = min(MLP_BLOCK, units)
    once = pl.Buffered(1)
    whole = pl.BlockSpec((count, width), lambda j: (0, 0), pipeline_mode=once)
    side = pl.BlockSpec((count, block), lambda j: (0, j))
    tall = pl.BlockSpec((width, block), lambda j: (0, j))
    wide = pl.BlockSpec((block, width), lambda j: (j, 0))
    top = width // 4
    parts = [pl.BlockSpec((rows, block), lambda j: (0, j)) for rows in (top, width - top)]
    return pl.pallas_call(
        mlp_kernel,
        grid=(units // block,),
        in_specs=[whole, whole, tall, tall, wide],
        out_specs=[side, side, tall, *parts, wide, whole],
        out_shape=[
            jax.ShapeDtypeStruct((count, units), BF16),
            jax.ShapeDtypeStruct((count, units), BF16),
            jax.ShapeDtypeStruct((width, units), BF16),
            jax.ShapeDtypeStruct((top, units), BF16),
            jax.ShapeDtypeStruct((width - top, units), BF16),
            jax.ShapeDtypeStruct((units, width), BF16),
            jax.ShapeDtypeStruct((count, width), BF16),
        ],
        scratch_shapes=[
            pltpu.VMEM((width, count), BF16),
            pltpu.VMEM((count, block), BF16),
            pltpu.VMEM((count, width), F32),
        ],
        cost_estimate=pl.CostEstimate(
            flops=14 * count * width * units,
            bytes_accessed=2 * (3 * count * width + 6 * width * units + 2 * count * units),
            transcendentals=count * units,
        ),
        compiler_params=pltpu.CompilerParams(vmem_limit_bytes=56 * 2**20),
    )(rows, grad, w_gate, w_up, w_down)


WIDEN_SLOTS = 4


def widen_kernel(shapes, places, wide_count, tile, *refs):
    count = len(shapes)
    sources, targets = refs[:count], refs[count : count + wide_count]
    narrow, wide, load_sem, store_sem = refs[count + wide_count :]
    high, broad = tile
    counts = [(rows // high) * (width // broad) for rows, width in shapes]
    total = sum(counts)

    def pick(k, act):
        first = 0
        for i in range(count):
            @pl.when((k >= first) & (k < first + counts[i]))
            def _(i=i, first=first):
                across = shapes[i][1] // broad
                place = k - first
                row = pl.multiple_of((place // across) * high, high)
                col = pl.multiple_of(lax.rem(place, across) * broad, broad)
                act(i, (pl.ds(row, high), pl.ds(col, broad)))
            first += counts[i]

    def load(k, i, where):
        slot = lax.rem(k, WIDEN_SLOTS)
        return pltpu.make_async_copy(sources[i].at[where], narrow.at[slot], load_sem.at[slot])

    def store(k, i, where):
        slot = lax.rem(k, WIDEN_SLOTS)
        target, first = places[i]
        rows = pl.ds(pl.multiple_of(first + where[0].start, high), high)
        return pltpu.make_async_copy(
            wide.at[slot], targets[target].at[rows, where[1]], store_sem.at[slot]
        )

    zero = (pl.ds(0, high), pl.ds(0, broad))
    ahead = WIDEN_SLOTS - 1
    for k in range(ahead):
        pick(k, lambda i, where, k=k: load(k, i, where).start())

    def step(k, carry):
        @pl.when(k + ahead < total)
        def _():
            pick(k + ahead, lambda i, where: load(k + ahead, i, where).start())

        @pl.when(k >= WIDEN_SLOTS)
        def _():
            store(k - WIDEN_SLOTS, 0, zero).wait()

        load(k, 0, zero).wait()
        slot = lax.rem(k, WIDEN_SLOTS)
        wide[slot] = narrow[slot].astype(F32)
        pick(k, lambda i, where: store(k, i, where).start())
        return carry

    lax.fori_loop(0, total, step, 0)
    for k in range(total - WIDEN_SLOTS, total):
        store(k, 0, zero).wait()


def widen(groups, tile):
    arrays, places, targets = [], [], []
    for group in groups:
        rows = 0
        for value in group:
            arrays.append(value)
            places.append((len(targets), rows))
            rows += value.shape[0]
        targets.append((rows, group[0].shape[1]))
    shapes = [value.shape for value in arrays]
    any_ = pl.BlockSpec(memory_space=pltpu.HBM)
    return pl.pallas_call(
        functools.partial(widen_kernel, shapes, places, len(targets), tile),
        in_specs=[any_] * len(arrays),
        out_specs=[any_] * len(targets),
        out_shape=[jax.ShapeDtypeStruct(shape, F32) for shape in targets],
        scratch_shapes=[
            pltpu.VMEM((WIDEN_SLOTS, *tile), BF16),
            pltpu.VMEM((WIDEN_SLOTS, *tile), F32),
            pltpu.SemaphoreType.DMA((WIDEN_SLOTS,)),
            pltpu.SemaphoreType.DMA((WIDEN_SLOTS,)),
        ],
        cost_estimate=pl.CostEstimate(
            flops=0, bytes_accessed=6 * sum(r * c for r, c in shapes), transcendentals=0
        ),
        compiler_params=pltpu.CompilerParams(vmem_limit_bytes=40 * 2**20),
    )(*arrays)


def attn_weights_kernel(
    rows_ref, d_out_ref, mixed_ref, d_query_ref, d_key_ref, d_value_ref,
    w_query_ref, w_key_ref, w_value_ref,
    d_rows_ref, grad_query_ref, grad_key_ref, grad_value_ref, grad_out_ref, gain_part_ref,
    flipped_mixed, flipped_rows,
):
    @pl.when(pl.program_id(0) == 0)
    def _():
        flipped_mixed[...] = mixed_ref[...].T

    flipped_rows[...] = rows_ref[...].T
    d_rows = (
        dot(d_query_ref[...], w_query_ref[...], NT)
        + dot(d_key_ref[...], w_key_ref[...], NT)
        + dot(d_value_ref[...], w_value_ref[...], NT)
    )
    d_rows_ref[...] = d_rows.astype(BF16)
    product = d_rows * rows_ref[...].astype(F32)
    gain_part_ref[...] = jnp.sum(product.reshape(-1, 8, product.shape[1]), axis=0)
    grad_query_ref[...] = dot(flipped_rows[...], d_query_ref[...], NN).astype(BF16)
    grad_key_ref[...] = dot(flipped_rows[...], d_key_ref[...], NN).astype(BF16)
    grad_value_ref[...] = dot(flipped_rows[...], d_value_ref[...], NN).astype(BF16)
    grad_out_ref[...] = dot(flipped_mixed[...], d_out_ref[...], NN).astype(BF16)


def attn_weights(rows, d_out, mixed, d_query, d_key, d_value, w_query, w_key, w_value):
    count, width = rows.shape
    cols = mixed.shape[1]
    block = 512
    once = pl.Buffered(1)
    slim = pl.BlockSpec((count, cols), lambda j: (0, 0), pipeline_mode=once)
    side = pl.BlockSpec((count, block), lambda j: (0, j))
    tall = pl.BlockSpec((block, cols), lambda j: (j, 0))
    wide = pl.BlockSpec((cols, block), lambda j: (0, j))
    tall_type = jax.ShapeDtypeStruct((width, cols), BF16)
    return pl.pallas_call(
        attn_weights_kernel,
        grid=(width // block,),
        in_specs=[side, side, slim, slim, slim, slim, tall, tall, tall],
        out_specs=[side, tall, tall, tall, wide, pl.BlockSpec((8, block), lambda j: (0, j))],
        out_shape=[
            jax.ShapeDtypeStruct((count, width), BF16),
            tall_type,
            tall_type,
            tall_type,
            jax.ShapeDtypeStruct((cols, width), BF16),
            jax.ShapeDtypeStruct((8, width), F32),
        ],
        scratch_shapes=[pltpu.VMEM((cols, count), BF16), pltpu.VMEM((block, count), BF16)],
        cost_estimate=pl.CostEstimate(
            flops=14 * count * width * cols,
            bytes_accessed=2 * (3 * count * width + 4 * count * cols + 7 * width * cols),
            transcendentals=0,
        ),
        compiler_params=pltpu.CompilerParams(vmem_limit_bytes=48 * 2**20),
    )(rows, d_out, mixed, d_query, d_key, d_value, w_query, w_key, w_value)


def from_behind(value, axis, steps):
    count = lax.axis_size(axis)
    initial, last = (max(0, -steps), min(count, count - steps))
    return lax.ppermute(value, axis, [(source, source + steps) for source in range(initial, last)])


def elu_plus(values):
    return jnp.where(values > 0, values + 1.0, jnp.exp(jnp.minimum(values, 0.0)))


def elu_slope(values):
    return jnp.where(values > 0, 1.0, jnp.exp(jnp.minimum(values, 0.0)))


def inverse_rms(values):
    return lax.rsqrt(jnp.mean(values * values, axis=-1, keepdims=True) + epsilon)


def norm_backward(values, inverse, gain_vec, grad_out):
    normal = values * inverse
    scaled = gain_vec * grad_out
    grad_in = inverse * (scaled - normal * jnp.mean(scaled * normal, axis=-1, keepdims=True))
    return grad_in


def dot(left, right, dims, precision=None):
    return lax.dot_general(
        left, right, (dims, ((), ())), precision=precision, preferred_element_type=F32
    )


NN = ((1,), (0,))
NT = ((1,), (1,))
TN = ((0,), (0,))


def valid_column(valid_len):
    return (lax.broadcasted_iota(jnp.int32, (SEG_LEN, 1), 0) < valid_len).astype(F32)


def update_kernel(valid_ref, key_ref, value_ref, out_ref):
    key_feat = elu_plus(key_ref[...].astype(F32)) * valid_column(valid_ref[0])
    out_ref[0, :DH] = dot(key_feat, value_ref[...].astype(F32), TN, highest)
    out_ref[0, DH:] = jnp.broadcast_to(jnp.sum(key_feat, axis=0, keepdims=True), (8, DH))


def block_probs(query_block, key_ref, start, valid_len):
    cols = start + query_block.shape[0]
    scores = dot(query_block, key_ref[:cols], NT) * (DH**-0.5)
    row_pos = start + lax.broadcasted_iota(jnp.int32, scores.shape, 0)
    col_pos = lax.broadcasted_iota(jnp.int32, scores.shape, 1)
    allowed = (row_pos >= col_pos) & (col_pos < valid_len)
    scores = jnp.where(allowed, scores, masked_score)
    weights = jnp.exp(scores - jnp.max(scores, axis=-1, keepdims=True))
    return weights / jnp.sum(weights, axis=-1, keepdims=True)


def local_kernel(valid_ref, query_ref, key_ref, value_ref, out_ref):
    for start in range(0, SEG_LEN, BLOCK):
        rows = slice(start, start + BLOCK)
        probs = block_probs(query_ref[rows], key_ref, start, valid_ref[0])
        out_ref[rows] = dot(probs.astype(BF16), value_ref[: start + BLOCK], NN)


def retrieve(query_feat, memory, normal):
    numerator = dot(query_feat, memory, NN, highest)
    denominator = jnp.sum(query_feat * normal, axis=-1, keepdims=True) + 1.0
    return numerator / denominator, denominator


def mix_kernel(gate_ref, query_ref, local_ref, memory_ref, out_ref):
    gate = gate_ref[pl.program_id(0)]
    query_feat = elu_plus(query_ref[...].astype(F32))
    retrieved, _ = retrieve(query_feat, memory_ref[0, :DH], memory_ref[0, DH : DH + 1])
    out_ref[...] = (gate * retrieved + (1.0 - gate) * local_ref[...]).astype(BF16)


def memory_back_kernel(
    gate_ref, query_ref, local_ref, memory_ref, d_mixed_ref, feat_ref, back_ref, gate_grad_ref
):
    gate = gate_ref[pl.program_id(0)]
    query_vals = query_ref[...].astype(F32)
    query_feat = elu_plus(query_vals)
    memory, normal = memory_ref[0, :DH], memory_ref[0, DH : DH + 1]
    retrieved, denominator = retrieve(query_feat, memory, normal)
    d_mixed = d_mixed_ref[...]
    gate_grad_ref[0] = jnp.broadcast_to(
        jnp.sum(d_mixed * (retrieved - local_ref[...]), axis=0, keepdims=True), (8, DH)
    )
    d_retrieved = gate * d_mixed
    d_numerator = d_retrieved / denominator
    d_denominator = -jnp.sum(d_retrieved * retrieved, axis=-1, keepdims=True) / denominator
    d_feat = dot(d_numerator, memory, NT, highest) + d_denominator * normal
    feat_ref[...] = d_feat * elu_slope(query_vals)
    back_ref[0, :DH] = dot(query_feat, d_numerator, TN, highest)
    back_ref[0, DH:] = jnp.broadcast_to(
        jnp.sum(d_denominator * query_feat, axis=0, keepdims=True), (8, DH)
    )


def local_back_kernel(
    gate_ref,
    valid_ref,
    query_ref,
    key_ref,
    value_ref,
    d_mixed_ref,
    feat_ref,
    d_query_ref,
    d_key_ref,
    d_value_ref,
):
    keep = 1.0 - gate_ref[pl.program_id(0)]
    d_key_ref[...] = jnp.zeros_like(d_key_ref)
    d_value_ref[...] = jnp.zeros_like(d_value_ref)
    for start in range(0, SEG_LEN, BLOCK):
        rows = slice(start, start + BLOCK)
        cols = slice(0, start + BLOCK)
        query_block = query_ref[rows]
        probs = block_probs(query_block, key_ref, start, valid_ref[0])
        d_local = (keep * d_mixed_ref[rows]).astype(BF16)
        d_probs = dot(d_local, value_ref[cols], NT)
        row_dot = jnp.sum(probs * d_probs, axis=-1, keepdims=True)
        d_scores = (probs * (d_probs - row_dot) * (DH**-0.5)).astype(BF16)
        d_query_ref[rows] = (dot(d_scores, key_ref[cols], NN) + feat_ref[rows]).astype(BF16)
        d_key_ref[cols] += dot(d_scores, query_block, TN)
        d_value_ref[cols] += dot(probs.astype(BF16), d_local, TN)


def finish_back_kernel(
    valid_ref, key_ref, value_ref, d_key_in, d_value_in, memory_ref, d_key_ref, d_value_ref
):
    valid = valid_column(valid_ref[0])
    key_vals = key_ref[...].astype(F32)
    memory, normal = memory_ref[0, :DH], memory_ref[0, DH : DH + 1]
    d_feat = (dot(value_ref[...].astype(F32), memory, NT, highest) + normal) * valid
    d_key_ref[...] = (d_key_in[...] + d_feat * elu_slope(key_vals)).astype(BF16)
    key_feat = elu_plus(key_vals) * valid
    d_value_ref[...] = (d_value_in[...] + dot(key_feat, memory, NN, highest)).astype(BF16)


SCALAR = pl.BlockSpec(memory_space=pltpu.SMEM)
COLUMN = pl.BlockSpec((SEG_LEN, DH), lambda head: (0, head))
MEMORY = pl.BlockSpec((1, MEM_ROWS, DH), lambda head: (head, 0, 0))
SMALL = pl.BlockSpec((1, 8, DH), lambda head: (head, 0, 0))


def per_head(kernel, heads, in_specs, out_specs, out_types, flops, transcendentals=0):
    moved = heads * SEG_LEN * DH * 4 * len(in_specs)
    return pl.pallas_call(
        kernel,
        grid=(heads,),
        in_specs=in_specs,
        out_specs=out_specs,
        out_shape=out_types,
        cost_estimate=pl.CostEstimate(
            flops=flops, bytes_accessed=moved, transcendentals=transcendentals
        ),
        compiler_params=pltpu.CompilerParams(vmem_limit_bytes=40 * 1024 * 1024),
    )


def per_device(
    tokens,
    cotangent,
    gain_attn,
    gain_mlp,
    w_query,
    w_key,
    w_value,
    w_out,
    w_gate,
    w_up,
    w_down,
    mem_gate,
    lengths,
):
    seg_index = lax.axis_index("seg")
    head_index = lax.axis_index("head")
    head_groups = lax.axis_size("head")
    seg_size = lax.axis_size("seg")
    position = seg_index % SEGS
    sequence = seg_index // SEGS
    seq_length = jnp.sum(jnp.where(lax.iota(jnp.int32, lengths.shape[0]) == sequence, lengths, 0))
    valid_len = jnp.where(position == SEGS - 1, seq_length, SEG_LEN).reshape(1)
    heads = mem_gate.shape[0]
    cols = heads * DH
    col_f32 = jax.ShapeDtypeStruct((SEG_LEN, cols), F32)
    col_bf16 = jax.ShapeDtypeStruct((SEG_LEN, cols), BF16)
    mem_f32 = jax.ShapeDtypeStruct((heads, MEM_ROWS, DH), F32)
    small_f32 = jax.ShapeDtypeStruct((heads, 8, DH), F32)
    unit = 2 * heads * SEG_LEN * DH * DH
    pairs = heads * SEG_LEN * SEG_LEN

    token_vals = tokens.astype(F32)
    gathered_tokens = lax.all_gather(tokens, "head", axis=0, tiled=True)
    gathered_grad = lax.all_gather(cotangent, "head", axis=0, tiled=True)
    all_tokens = gathered_tokens.astype(F32)
    gathered_attn = (all_tokens * inverse_rms(all_tokens) * gain_attn).astype(BF16)

    def project(weight):
        return jnp.dot(gathered_attn, weight, preferred_element_type=F32).astype(BF16)

    key_rows = project(w_key)
    value_rows = project(w_value)
    update = per_head(update_kernel, heads, [SCALAR, COLUMN, COLUMN], MEMORY, mem_f32, 6 * unit)(
        valid_len, key_rows, value_rows
    )
    query_rows = project(w_query)
    memory_prev = jnp.zeros_like(update)
    for distance in range(1, SEGS):
        moved = from_behind(update, "seg", distance)
        memory_prev = memory_prev + jnp.where(position >= distance, moved, 0.0)
    local_attn = per_head(
        local_kernel, heads, [SCALAR, COLUMN, COLUMN, COLUMN], COLUMN, col_f32, 4 * pairs * DH, pairs
    )(valid_len, query_rows, key_rows, value_rows)
    after = memory_prev + update
    memory_after = (after[:, :DH] * SEG_LEN ** (-0.5))[None]
    normal_after = (after[:, DH] / SEG_LEN)[None]
    mix_sig = jax.nn.sigmoid(mem_gate)
    mixed_attn = per_head(
        mix_kernel, heads, [SCALAR, COLUMN, COLUMN, MEMORY], COLUMN, col_bf16, 6 * unit
    )(mix_sig, query_rows, local_attn, memory_prev)
    all_hidden, gathered_mlp = attn_out_sum(
        mixed_attn, w_out, gathered_tokens, gain_mlp, head_groups, 1
    )
    own_rows = tokens.shape[0]
    hidden_res = lax.dynamic_slice_in_dim(all_hidden, head_index * own_rows, own_rows, 0)
    d_gate, d_up, grad_gate, up_top, up_low, grad_down, mlp_part = mlp_both(
        gathered_mlp, gathered_grad, w_gate, w_up, w_down
    )
    sum_gate, sum_up_top = lax.psum((grad_gate, up_top), "seg")
    gathered_hidden, d_hidden, gain_mlp_rows, summed_down = mlp_back_sum(
        d_gate,
        d_up,
        w_gate,
        w_up,
        all_hidden,
        gathered_grad,
        gain_mlp,
        grad_down,
        (BLOCK, cols),
        seg_size,
        head_groups,
        2,
    )
    mlp_out = lax.psum_scatter(mlp_part, "head", scatter_dimension=0, tiled=True)
    output = (hidden_res + mlp_out.astype(F32)).astype(BF16)
    d_mixed = dot(gathered_hidden, w_out, NT)
    feat_grad, back, gate_cols = per_head(
        memory_back_kernel,
        heads,
        [SCALAR, COLUMN, COLUMN, MEMORY, COLUMN],
        [COLUMN, MEMORY, SMALL],
        [col_f32, mem_f32, small_f32],
        18 * unit,
    )(mix_sig, query_rows, local_attn, memory_prev, d_mixed)
    back_update = jnp.zeros_like(back)
    for distance in range(1, SEGS):
        moved = from_behind(back, "seg", -distance)
        back_update = back_update + jnp.where(position + distance <= SEGS - 1, moved, 0.0)
    d_queries, key_local, value_local = per_head(
        local_back_kernel,
        heads,
        [SCALAR, SCALAR] + [COLUMN] * 5,
        [COLUMN] * 3,
        [col_bf16, col_f32, col_f32],
        10 * pairs * DH,
        pairs,
    )(mix_sig, valid_len, query_rows, key_rows, value_rows, d_mixed, feat_grad)
    d_keys, d_values = per_head(
        finish_back_kernel,
        heads,
        [SCALAR] + [COLUMN] * 4 + [MEMORY],
        [COLUMN] * 2,
        [col_bf16, col_bf16],
        12 * unit,
    )(valid_len, key_rows, value_rows, key_local, value_local, back_update)
    d_part, grad_query, grad_key, grad_value, grad_out, gain_attn_rows = attn_weights(
        gathered_attn,
        gathered_hidden,
        mixed_attn,
        d_queries,
        d_keys,
        d_values,
        w_query,
        w_key,
        w_value,
    )
    d_normed_attn = lax.psum_scatter(d_part, "head", scatter_dimension=0, tiled=True).astype(F32)
    grad_in_attn = norm_backward(token_vals, inverse_rms(token_vals), gain_attn, d_normed_attn)
    grad_tokens = (d_hidden + grad_in_attn).astype(BF16)
    gate_part = mix_sig * (1.0 - mix_sig) * jnp.sum(gate_cols[:, 0], axis=-1)
    slots = jnp.where(
        (lax.iota(jnp.int32, head_groups) == head_index)[:, None], gate_part[None], 0.0
    )
    width = gain_attn.shape[0]
    gain_attn_part = jnp.sum(gain_attn_rows, axis=0) / gain_attn
    gain_mlp_part = jnp.sum(gain_mlp_rows, axis=0)
    parts = jnp.concatenate([gain_attn_part, gain_mlp_part, slots.reshape(-1)])
    lines = -(-parts.shape[0] // (8 * DH)) * 8
    parts = jnp.pad(parts, (0, lines * DH - parts.shape[0])).reshape(lines, DH)
    small, *late = grad_sum(
        parts,
        [up_low, grad_out, grad_query, grad_key, grad_value],
        (cols, cols),
        seg_size,
        head_groups,
        0,
    )
    small = small.reshape(-1)
    grad_mem_gate = lax.dynamic_slice(small, (2 * width + head_index * heads,), (heads,))
    grads = widen(
        [(sum_gate,), (sum_up_top, late[0]), (summed_down,)] + [(grad,) for grad in late[1:]],
        (cols, cols),
    )
    return (
        output,
        grad_tokens,
        memory_after,
        normal_after,
        small[:width],
        small[width : 2 * width],
        grads[4],
        grads[5],
        grads[6],
        grads[3],
        grads[0],
        grads[1],
        grads[2],
        grad_mem_gate,
    )


def solution(mesh):
    return jax.shard_map(
        per_device,
        mesh=mesh,
        in_specs=(
            P(("seg", "head"), None),
            P(("seg", "head"), None),
            P(),
            P(),
            P(None, "head"),
            P(None, "head"),
            P(None, "head"),
            P("head", None),
            P(None, "head"),
            P(None, "head"),
            P("head", None),
            P("head"),
            P(),
        ),
        out_specs=(
            P(("seg", "head"), None),
            P(("seg", "head"), None),
            P("seg", "head", None, None),
            P("seg", "head", None),
            P(),
            P(),
            P(None, "head"),
            P(None, "head"),
            P(None, "head"),
            P("head", None),
            P(None, "head"),
            P(None, "head"),
            P("head", None),
            P("head"),
        ),
        check_vma=False,
    )
```

```python
import functools

import jax
import jax.numpy as jnp
from jax import lax
from jax.experimental import pallas as pl
from jax.experimental.pallas import tpu as pltpu
from jax.sharding import PartitionSpec as P

DH = 128
SEG_LEN = 1024
SEGS = 4
MEM_ROWS = DH + 16
BLOCK = 256

epsilon = 1e-05
masked_score = -1e30
highest = lax.Precision.HIGHEST
F32 = jnp.float32
BF16 = jnp.bfloat16


MESH = pl.DeviceIdType.MESH
LAND_SLOTS = 8
RESULT_SLOTS = 12
SUM_SEMS = 8
SUM_HOP = 2


def bits_of(size):
    return size.bit_length() - 1


def flip(index, power):
    return index + power - 2 * power * lax.rem(index // power, 2)


def sum_engine(arrays, outs, tile, seg_bits, scratch):
    mine, result, send_sem, recv_sem, load_sem, store_sem, *lands = scratch
    seg = lax.axis_index("seg")
    planes = seg_bits - 1
    high, wide = tile
    shapes = [array.shape for array in arrays]
    counts = [(rows // high) * (cols // wide) for rows, cols in shapes]
    starts = [sum(counts[:i]) for i in range(len(counts))]
    total = sum(counts)

    def power(k, level):
        if level == 0:
            return 1
        which = lax.rem(k + level - 1, planes)
        value = 2
        for bit in range(1, planes):
            value = jnp.where(which == bit, 2 << bit, value)
        return value

    def my_bit(k, level):
        return lax.rem(seg // power(k, level), 2)

    def part(k, level, own):
        half = high >> (level + 1)
        bit = my_bit(k, level) if own else 1 - my_bit(k, level)
        return pl.ds(pl.multiple_of(bit * half, half), half)

    def kept(k, levels):
        first = 0
        for level in range(levels):
            first = first + my_bit(k, level) * (high >> (level + 1))
        return pl.ds(pl.multiple_of(first, high >> levels), high >> levels)

    def pick(k, act):
        for i in range(len(arrays)):

            @pl.when((k >= starts[i]) & (k < starts[i] + counts[i]))
            def _(i=i):
                across = shapes[i][1] // wide
                place = k - starts[i]
                row = pl.multiple_of((place // across) * high, high)
                col = pl.multiple_of(lax.rem(place, across) * wide, wide)
                act(i, row, col)

    def halving(k, level, source):
        return pltpu.make_async_remote_copy(
            src_ref=source,
            dst_ref=lands[level].at[lax.rem(k, LAND_SLOTS)],
            send_sem=send_sem.at[level, lax.rem(k, SUM_SEMS)],
            recv_sem=recv_sem.at[level, lax.rem(k, SUM_SEMS)],
            device_id={"seg": flip(seg, power(k, level))},
            device_id_type=MESH,
        )

    def first_source(k, i, row, col, own):
        half = high // 2
        bit = my_bit(k, 0) if own else 1 - my_bit(k, 0)
        return arrays[i].at[pl.ds(pl.multiple_of(row + bit * half, half), half), pl.ds(col, wide)]

    def keep(k, i, row, col):
        slot = lax.rem(k, 4)
        return pltpu.make_async_copy(
            first_source(k, i, row, col, True), mine.at[slot], load_sem.at[slot]
        )

    def level_source(k, level):
        return lands[level - 1].at[lax.rem(k, LAND_SLOTS), part(k, level, False)]

    def doubling(k, level):
        ref = result.at[lax.rem(k, RESULT_SLOTS), kept(k, level + 1)]
        return pltpu.make_async_remote_copy(
            src_ref=ref,
            dst_ref=ref,
            send_sem=send_sem.at[seg_bits + level, lax.rem(k, SUM_SEMS)],
            recv_sem=recv_sem.at[seg_bits + level, lax.rem(k, SUM_SEMS)],
            device_id={"seg": flip(seg, power(k, level))},
            device_id_type=MESH,
        )

    def store(k, i, row, col):
        slot = lax.rem(k, 4)
        return pltpu.make_async_copy(
            result.at[lax.rem(k, RESULT_SLOTS)],
            outs[i].at[pl.ds(row, high), pl.ds(col, wide)],
            store_sem.at[slot],
        )

    def do_first(k):
        def go(i, row, col):
            halving(k, 0, first_source(k, i, row, col, False)).start()
            keep(k, i, row, col).start()

        pick(k, go)

    def arrived(k, level):
        slot = lax.rem(k, LAND_SLOTS)
        if level == 0:
            halving(k, 0, first_source(k, 0, 0, 0, False)).wait()
            keep(k, 0, 0, 0).wait()
            other = mine[lax.rem(k, 4)]
        else:
            halving(k, level, level_source(k, level)).wait()
            other = lands[level - 1][slot, part(k, level, True)]
        return (lands[level][slot].astype(F32) + other.astype(F32)).astype(BF16)

    def do_level(k, level):
        lands[level - 1][lax.rem(k, LAND_SLOTS)] = arrived(k, level - 1)
        halving(k, level, level_source(k, level)).start()

    def do_total(k):
        result[lax.rem(k, RESULT_SLOTS), kept(k, seg_bits)] = arrived(k, seg_bits - 1)
        doubling(k, seg_bits - 1).start()

    def do_spread(k, level):
        doubling(k, level + 1).wait()
        doubling(k, level).start()

    def do_finish(k):
        doubling(k, 0).wait()
        pick(k, lambda i, row, col: store(k, i, row, col).start())

    def do_store(k):
        store(k, 0, 0, 0).wait()

    stages = [(0, do_first), (1, functools.partial(do_level, level=1))]
    when = 1
    for level in range(2, seg_bits):
        when += SUM_HOP
        stages.append((when, functools.partial(do_level, level=level)))
    when += SUM_HOP
    stages.append((when, do_total))
    for level in range(seg_bits - 2, -1, -1):
        when += SUM_HOP
        stages.append((when, functools.partial(do_spread, level=level)))
    stages.append((when + 1, do_finish))
    stages.append((when + 3, do_store))

    def step(t):
        for delay, act in reversed(stages):
            k = t - delay

            @pl.when((k >= 0) & (k < total))
            def _(act=act, k=k):
                act(k)

    return step, total + when + 3


def engine_scratch(tile, seg_bits):
    high, wide = tile
    return [
        pltpu.VMEM((4, high // 2, wide), BF16),
        pltpu.VMEM((RESULT_SLOTS, high, wide), BF16),
        pltpu.SemaphoreType.DMA((2 * seg_bits, SUM_SEMS)),
        pltpu.SemaphoreType.DMA((2 * seg_bits, SUM_SEMS)),
        pltpu.SemaphoreType.DMA((4,)),
        pltpu.SemaphoreType.DMA((4,)),
    ] + [pltpu.VMEM((LAND_SLOTS, high >> (l + 1), wide), BF16) for l in range(seg_bits)]


def greet_seg(seg_bits):
    barrier = pltpu.get_barrier_semaphore()
    seg = lax.axis_index("seg")
    for bit in range(seg_bits):
        pl.semaphore_signal(
            barrier, inc=1, device_id={"seg": flip(seg, 1 << bit)}, device_id_type=MESH
        )


def grad_sum_kernel(count, tile, seg_bits, head_bits, *refs):
    small_in, arrays = refs[0], refs[1 : 1 + count]
    small_out, outs = refs[1 + count], refs[2 + count : 2 + 2 * count]
    small_buf, small_land, small_send, small_recv, *scratch = refs[2 + 2 * count :]
    seg, head = lax.axis_index("seg"), lax.axis_index("head")
    greet_seg(seg_bits)
    barrier = pltpu.get_barrier_semaphore()
    for bit in range(head_bits):
        pl.semaphore_signal(
            barrier, inc=1, device_id={"head": flip(head, 1 << bit)}, device_id_type=MESH
        )
    pl.semaphore_wait(barrier, seg_bits + head_bits)
    rounds = seg_bits + head_bits

    def small_copy(j):
        if j < seg_bits:
            where = {"seg": flip(seg, 1 << j)}
        else:
            where = {"head": flip(head, 1 << (j - seg_bits))}
        return pltpu.make_async_remote_copy(
            src_ref=small_buf.at[j],
            dst_ref=small_land.at[j],
            send_sem=small_send.at[j],
            recv_sem=small_recv.at[j],
            device_id=where,
            device_id_type=MESH,
        )

    engine_step, steps = sum_engine(arrays, outs, tile, seg_bits, scratch)

    def step(t, carry):
        engine_step(t)
        for j in range(rounds + 1):

            @pl.when(t == 3 * j)
            def _(j=j):
                if j == 0:
                    small_buf[0] = small_in[...]
                else:
                    small_copy(j - 1).wait()
                    value = small_buf[j - 1] + small_land[j - 1]
                    if j < rounds:
                        small_buf[j] = value
                    else:
                        small_out[...] = value
                if j < rounds:
                    small_copy(j).start()

        return carry

    lax.fori_loop(0, max(steps, 3 * rounds + 1), step, 0)


def grad_sum(small, arrays, tile, seg_size, head_size, cid):
    seg_bits, head_bits = bits_of(seg_size), bits_of(head_size)
    rounds = seg_bits + head_bits
    count = len(arrays)
    moved = sum(rows * cols for rows, cols in (array.shape for array in arrays))
    any_, vmem = pl.BlockSpec(memory_space=pltpu.HBM), pl.BlockSpec(memory_space=pltpu.VMEM)
    return pl.pallas_call(
        functools.partial(grad_sum_kernel, count, tile, seg_bits, head_bits),
        in_specs=[vmem] + [any_] * count,
        out_specs=[vmem] + [any_] * count,
        out_shape=[jax.ShapeDtypeStruct(small.shape, F32)]
        + [jax.ShapeDtypeStruct(array.shape, BF16) for array in arrays],
        scratch_shapes=[
            pltpu.VMEM((rounds, *small.shape), F32),
            pltpu.VMEM((rounds, *small.shape), F32),
            pltpu.SemaphoreType.DMA((rounds,)),
            pltpu.SemaphoreType.DMA((rounds,)),
        ]
        + engine_scratch(tile, seg_bits),
        cost_estimate=pl.CostEstimate(flops=0, bytes_accessed=moved * 60, transcendentals=0),
        compiler_params=pltpu.CompilerParams(
            collective_id=cid, has_side_effects=True, vmem_limit_bytes=48 * 2**20
        ),
    )(small, *arrays)


ROWS = 32
HOP = 2
SEND_SLOTS = 4
BLOCK_ROWS = 256
UNIT_GROUP = 512
LINE_REFS = 8


def line_exchange(own, finish, before, scratch, extra=None, extra_steps=0):
    up_land, down_land, up_send, down_send, up_recv_sem, down_recv_sem, up_send_sem, down_send_sem = scratch
    size = lax.axis_size("head")
    place = lax.axis_index("head")
    slots = up_land.shape[0]
    chunks = own.shape[0] // ROWS
    last = size - 1

    def up_copy(k):
        return pltpu.make_async_remote_copy(
            src_ref=up_send.at[lax.rem(k, SEND_SLOTS)],
            dst_ref=up_land.at[lax.rem(k, slots)],
            send_sem=up_send_sem.at[lax.rem(k, SEND_SLOTS)],
            recv_sem=up_recv_sem.at[lax.rem(k, slots)],
            device_id={"head": lax.rem(place + 1, size)},
            device_id_type=MESH,
        )

    def down_copy(k):
        return pltpu.make_async_remote_copy(
            src_ref=down_send.at[lax.rem(k, SEND_SLOTS)],
            dst_ref=down_land.at[lax.rem(k, slots)],
            send_sem=down_send_sem.at[lax.rem(k, SEND_SLOTS)],
            recv_sem=down_recv_sem.at[lax.rem(k, slots)],
            device_id={"head": lax.rem(place + last, size)},
            device_id_type=MESH,
        )

    def rows_of(k):
        return pl.ds(pl.multiple_of(k * ROWS, ROWS), ROWS)

    def pass_on(k, copy, land, send, has_source, has_target):
        @pl.when(has_source)
        def _():
            copy(k).wait_recv()

        @pl.when(has_target)
        def _():
            slot = lax.rem(k, SEND_SLOTS)

            @pl.when(k >= SEND_SLOTS)
            def _():
                copy(k - SEND_SLOTS).wait_send()

            @pl.when(has_source)
            def _():
                send[slot] = (own[rows_of(k)] + land[lax.rem(k, slots)].astype(F32)).astype(BF16)

            @pl.when(jnp.logical_not(has_source))
            def _():
                send[slot] = own[rows_of(k)].astype(BF16)

            copy(k).start()

    far = jnp.maximum(place, last - place)

    def step(t, carry):
        before(t)
        down = t - (last - place) * HOP

        @pl.when((down >= 0) & (down < chunks))
        def _():
            pass_on(down, down_copy, down_land, down_send, place < last, place > 0)

        up = t - place * HOP

        @pl.when((up >= 0) & (up < chunks))
        def _():
            pass_on(up, up_copy, up_land, up_send, place > 0, place < last)

        k = t - far * HOP

        @pl.when((k >= 0) & (k < chunks))
        def _():
            slot = lax.rem(k, slots)

            @pl.when(place == 0)
            def _():
                finish(k, own[rows_of(k)] + down_land[slot].astype(F32))

            @pl.when(place == last)
            def _():
                finish(k, own[rows_of(k)] + up_land[slot].astype(F32))

            @pl.when((place > 0) & (place < last))
            def _():
                finish(
                    k,
                    own[rows_of(k)] + up_land[slot].astype(F32) + down_land[slot].astype(F32),
                )

        if extra is not None:
            extra(t)
        return carry

    lax.fori_loop(0, max(chunks + last * HOP, extra_steps), step, 0)
    for k in range(chunks - SEND_SLOTS, chunks):

        @pl.when(place < last)
        def _(k=k):
            up_copy(k).wait_send()

        @pl.when(place > 0)
        def _(k=k):
            down_copy(k).wait_send()


def line_barrier(others=0):
    size = lax.axis_size("head")
    place = lax.axis_index("head")
    barrier = pltpu.get_barrier_semaphore()
    inner = (place > 0) & (place < size - 1)

    def greet(near):
        pl.semaphore_signal(
            barrier, inc=1, device_id={"head": lax.rem(near, size)}, device_id_type=MESH
        )

    @pl.when(place > 0)
    def _():
        greet(place + size - 1)

    @pl.when(place < size - 1)
    def _():
        greet(place + 1)

    @pl.when(inner)
    def _():
        pl.semaphore_wait(barrier, 2 + others)

    @pl.when(jnp.logical_not(inner))
    def _():
        pl.semaphore_wait(barrier, 1 + others)


def line_scratch(size, width):
    slots = (size - 1) * HOP + 2
    return [
        pltpu.VMEM((slots, ROWS, width), BF16),
        pltpu.VMEM((slots, ROWS, width), BF16),
        pltpu.VMEM((SEND_SLOTS, ROWS, width), BF16),
        pltpu.VMEM((SEND_SLOTS, ROWS, width), BF16),
        pltpu.SemaphoreType.DMA((slots,)),
        pltpu.SemaphoreType.DMA((slots,)),
        pltpu.SemaphoreType.DMA((SEND_SLOTS,)),
        pltpu.SemaphoreType.DMA((SEND_SLOTS,)),
    ]


def attn_out_kernel(
    mixed_ref, weight_ref, token_ref, gain_ref, w_gate_hbm, w_up_hbm,
    hidden_ref, normed_ref, silu_ref, slope_ref, act_ref,
    hidden, normed, w_gate, w_up, silu, slope, act,
    hidden_sem, normed_sem, load_sem, out_sem, *scratch
):
    loads = [
        pltpu.make_async_copy(source, target, load_sem.at[i])
        for i, (source, target) in enumerate(((w_gate_hbm, w_gate), (w_up_hbm, w_up)))
    ]
    for load in loads:
        load.start()
    line_barrier()
    per_block = BLOCK_ROWS // ROWS
    blocks = hidden.shape[0] // BLOCK_ROWS
    groups = w_gate.shape[1] // UNIT_GROUP
    slots = act.shape[0]
    lag = per_block + (lax.axis_size("head") - 1) * HOP
    pace = per_block // groups

    def block_rows(b):
        return pl.ds(pl.multiple_of(b * BLOCK_ROWS, BLOCK_ROWS), BLOCK_ROWS)

    def unit_copies(u):
        slot = lax.rem(u, slots)
        where = (block_rows(u // groups), unit_cols(u))
        return [
            pltpu.make_async_copy(source.at[slot], target.at[where], out_sem.at[i, slot])
            for i, (source, target) in enumerate(
                ((silu, silu_ref), (slope, slope_ref), (act, act_ref))
            )
        ]

    def unit_cols(u):
        return pl.ds(pl.multiple_of(lax.rem(u, groups) * UNIT_GROUP, UNIT_GROUP), UNIT_GROUP)

    def forward(u):
        slot = lax.rem(u, slots)

        @pl.when(u >= slots)
        def _():
            for copy in unit_copies(u - slots):
                copy.wait()

        rows, cols = normed[block_rows(u // groups)], unit_cols(u)
        gate_pre = dot(rows, w_gate[:, cols], NN)
        up_proj = dot(rows, w_up[:, cols], NN)
        gate_sig = jax.nn.sigmoid(gate_pre)
        silu_gate = gate_pre * gate_sig
        silu[slot] = silu_gate
        slope[slot] = up_proj * gate_sig * (1.0 + gate_pre * (1.0 - gate_sig))
        act[slot] = (silu_gate * up_proj).astype(BF16)
        for copy in unit_copies(u):
            copy.start()

    def before(t):
        @pl.when((lax.rem(t, per_block) == 0) & (t < blocks * per_block))
        def _():
            rows = block_rows(t // per_block)
            hidden[rows] = dot(mixed_ref[rows], weight_ref[...], NN)

    def after(t):
        @pl.when(t == lag)
        def _():
            for load in loads:
                load.wait()

        late = t - lag

        @pl.when((late >= 0) & (lax.rem(late, pace) == 0) & (late // pace < blocks * groups))
        def _():
            forward(late // pace)

    def stores(b):
        rows = block_rows(b)
        return (
            pltpu.make_async_copy(hidden.at[rows], hidden_ref.at[rows], hidden_sem.at[b]),
            pltpu.make_async_copy(normed.at[rows], normed_ref.at[rows], normed_sem.at[b]),
        )

    def finish(k, total):
        rows = pl.ds(pl.multiple_of(k * ROWS, ROWS), ROWS)
        value = token_ref[rows].astype(F32) + total
        hidden[rows] = value
        normed[rows] = (value * inverse_rms(value) * gain_ref[...]).astype(BF16)

        @pl.when(lax.rem(k, per_block) == per_block - 1)
        def _():
            for copy in stores(k // per_block):
                copy.start()

    line_exchange(hidden, finish, before, scratch, after, lag + blocks * per_block)
    for b in range(blocks):
        for copy in stores(b):
            copy.wait()
    for u in range(blocks * groups - slots, blocks * groups):
        for copy in unit_copies(u):
            copy.wait()


def attn_out_sum(mixed, weight, tokens, gain, w_gate, w_up, size, cid):
    rows, width = tokens.shape
    units = w_gate.shape[1]
    vmem, any_ = pl.BlockSpec(memory_space=pltpu.VMEM), pl.BlockSpec(memory_space=pltpu.HBM)
    blocks, slots = rows // BLOCK_ROWS, 2
    return pl.pallas_call(
        attn_out_kernel,
        in_specs=[vmem] * 4 + [any_] * 2,
        out_specs=[any_] * 5,
        out_shape=[
            jax.ShapeDtypeStruct((rows, width), F32),
            jax.ShapeDtypeStruct((rows, width), BF16),
            jax.ShapeDtypeStruct((rows, units), F32),
            jax.ShapeDtypeStruct((rows, units), F32),
            jax.ShapeDtypeStruct((rows, units), BF16),
        ],
        scratch_shapes=[
            pltpu.VMEM((rows, width), F32),
            pltpu.VMEM((rows, width), BF16),
            pltpu.VMEM((width, units), BF16),
            pltpu.VMEM((width, units), BF16),
            pltpu.VMEM((slots, BLOCK_ROWS, UNIT_GROUP), F32),
            pltpu.VMEM((slots, BLOCK_ROWS, UNIT_GROUP), F32),
            pltpu.VMEM((slots, BLOCK_ROWS, UNIT_GROUP), BF16),
            pltpu.SemaphoreType.DMA((blocks,)),
            pltpu.SemaphoreType.DMA((blocks,)),
            pltpu.SemaphoreType.DMA((2,)),
            pltpu.SemaphoreType.DMA((3, slots)),
        ]
        + line_scratch(size, width),
        cost_estimate=pl.CostEstimate(
            flops=2 * rows * width * (mixed.shape[1] + 2 * units),
            bytes_accessed=250 * 2**20,
            transcendentals=rows * units,
        ),
        compiler_params=pltpu.CompilerParams(
            collective_id=cid, has_side_effects=True, vmem_limit_bytes=60 * 2**20
        ),
    )(mixed, weight, tokens, gain.reshape(1, width), w_gate, w_up)


def mlp_back_kernel(
    tile, seg_bits,
    d_gate_hbm, d_up_hbm, w_gate_hbm, w_up_hbm, hidden_hbm, grad_hbm, gain_ref, sum_in,
    d_out_ref, d_own_ref, gain_part_ref, sum_out,
    d_gate, d_up, w_gate, w_up, hidden, grad, own, load_sem, store_sem, *scratch
):
    per_block = BLOCK_ROWS // ROWS
    blocks = own.shape[0] // BLOCK_ROWS
    size = lax.axis_size("head")
    place = lax.axis_index("head")
    per_device = own.shape[0] // ROWS // size
    loads = [
        pltpu.make_async_copy(source, target, load_sem.at[i])
        for i, (source, target) in enumerate(
            ((d_gate_hbm, d_gate), (w_gate_hbm, w_gate), (d_up_hbm, d_up), (w_up_hbm, w_up),
             (hidden_hbm, hidden), (grad_hbm, grad))
        )
    ]
    for load in loads:
        load.start()
    gain_part_ref[...] = jnp.zeros_like(gain_part_ref)
    greet_seg(seg_bits)
    line_barrier(seg_bits)
    engine_step, steps = sum_engine(
        [sum_in], [sum_out], tile, seg_bits, scratch[LINE_REFS:]
    )

    def block_rows(b):
        return pl.ds(pl.multiple_of(b * BLOCK_ROWS, BLOCK_ROWS), BLOCK_ROWS)

    for load in loads[:4]:
        load.wait()

    def before(t):
        @pl.when((lax.rem(t, per_block) == 0) & (t < blocks * per_block))
        def _():
            rows = block_rows(t // per_block)
            own[rows] = dot(d_gate[rows], w_gate[...], NT) + dot(d_up[rows], w_up[...], NT)

        @pl.when(t == 0)
        def _():
            for load in loads[4:]:
                load.wait()

    def store(b):
        rows = block_rows(b)
        return pltpu.make_async_copy(grad.at[rows], d_out_ref.at[rows], store_sem.at[b])

    def finish(k, total):
        rows = pl.ds(pl.multiple_of(k * ROWS, ROWS), ROWS)
        value = hidden[rows]
        inverse = inverse_rms(value)
        normal = value * inverse
        scaled = gain_ref[...] * total
        mean = jnp.mean(scaled * normal, axis=-1, keepdims=True)
        d_hidden = grad[rows].astype(F32) + inverse * (scaled - normal * mean)
        grad[rows] = d_hidden.astype(BF16)

        @pl.when(k // per_device == place)
        def _():
            mine = pl.ds(pl.multiple_of(lax.rem(k, per_device) * ROWS, ROWS), ROWS)
            d_own_ref[mine] = d_hidden
            gain_part_ref[...] += jnp.sum((total * normal).reshape(ROWS // 8, 8, -1), axis=0)

        @pl.when(lax.rem(k, per_block) == per_block - 1)
        def _():
            store(k // per_block).start()

    line_exchange(own, finish, before, scratch[:LINE_REFS], engine_step, steps)
    for b in range(blocks):
        store(b).wait()


def mlp_back_sum(d_gate, d_up, w_gate, w_up, hidden, grad, gain, summed, tile, seg_size, size, cid):
    rows, width = hidden.shape
    units = d_gate.shape[1]
    seg_bits = bits_of(seg_size)
    vmem, any_ = pl.BlockSpec(memory_space=pltpu.VMEM), pl.BlockSpec(memory_space=pltpu.HBM)
    blocks = rows // BLOCK_ROWS
    return pl.pallas_call(
        functools.partial(mlp_back_kernel, tile, seg_bits),
        in_specs=[any_] * 6 + [vmem, any_],
        out_specs=[any_, vmem, vmem, any_],
        out_shape=[
            jax.ShapeDtypeStruct((rows, width), BF16),
            jax.ShapeDtypeStruct((rows // size, width), F32),
            jax.ShapeDtypeStruct((8, width), F32),
            jax.ShapeDtypeStruct(summed.shape, BF16),
        ],
        scratch_shapes=[
            pltpu.VMEM((rows, units), BF16),
            pltpu.VMEM((rows, units), BF16),
            pltpu.VMEM((width, units), BF16),
            pltpu.VMEM((width, units), BF16),
            pltpu.VMEM((rows, width), F32),
            pltpu.VMEM((rows, width), BF16),
            pltpu.VMEM((rows, width), F32),
            pltpu.SemaphoreType.DMA((6,)),
            pltpu.SemaphoreType.DMA((blocks,)),
        ]
        + line_scratch(size, width)
        + engine_scratch(tile, seg_bits),
        cost_estimate=pl.CostEstimate(
            flops=4 * rows * width * units, bytes_accessed=250 * 2**20, transcendentals=0
        ),
        compiler_params=pltpu.CompilerParams(
            collective_id=cid, has_side_effects=True, vmem_limit_bytes=62 * 2**20
        ),
    )(d_gate, d_up, w_gate, w_up, hidden, grad, gain.reshape(1, width), summed)


MLP_BLOCK = 256


def mlp_kernel(
    rows_ref, grad_ref, silu_ref, slope_ref, act_ref, w_down_ref,
    d_gate_ref, d_up_ref, grad_gate_ref, grad_up_top, grad_up_low, grad_down_ref, out_ref,
    flipped, total,
):
    width = rows_ref.shape[1]
    first = pl.program_id(0) == 0
    last = pl.program_id(0) == pl.num_programs(0) - 1
    half = width // 2

    @pl.when(first)
    def _():
        total[...] = jnp.zeros_like(total)
        for i in range(2):
            part = slice(i * half, (i + 1) * half)
            flipped[part] = rows_ref[:, part].T

    d_act = dot(grad_ref[...], w_down_ref[...], NT)
    d_gate_ref[...] = (d_act * slope_ref[...]).astype(BF16)
    d_up_ref[...] = (d_act * silu_ref[...]).astype(BF16)
    total[...] += dot(act_ref[...], w_down_ref[...], NN)
    for i in range(2):
        part = slice(i * half, (i + 1) * half)
        grad_gate_ref[part] = dot(flipped[part], d_gate_ref[...], NN).astype(BF16)
        grad_down_ref[:, part] = dot(act_ref[...], grad_ref[:, part], TN).astype(BF16)
    top = grad_up_top.shape[0]
    grad_up_top[...] = dot(flipped[:top], d_up_ref[...], NN).astype(BF16)
    grad_up_low[...] = dot(flipped[top:], d_up_ref[...], NN).astype(BF16)

    @pl.when(last)
    def _():
        out_ref[...] = total[...].astype(BF16)


def mlp_both(rows, grad, silu, slope, act, w_down):
    count, width = rows.shape
    units = act.shape[1]
    block = min(MLP_BLOCK, units)
    once = pl.Buffered(1)
    whole = pl.BlockSpec((count, width), lambda j: (0, 0), pipeline_mode=once)
    side = pl.BlockSpec((count, block), lambda j: (0, j))
    tall = pl.BlockSpec((width, block), lambda j: (0, j))
    wide = pl.BlockSpec((block, width), lambda j: (j, 0))
    top = width // 4
    parts = [pl.BlockSpec((rows, block), lambda j: (0, j)) for rows in (top, width - top)]
    return pl.pallas_call(
        mlp_kernel,
        grid=(units // block,),
        in_specs=[whole, whole, side, side, side, wide],
        out_specs=[side, side, tall, *parts, wide, whole],
        out_shape=[
            jax.ShapeDtypeStruct((count, units), BF16),
            jax.ShapeDtypeStruct((count, units), BF16),
            jax.ShapeDtypeStruct((width, units), BF16),
            jax.ShapeDtypeStruct((top, units), BF16),
            jax.ShapeDtypeStruct((width - top, units), BF16),
            jax.ShapeDtypeStruct((units, width), BF16),
            jax.ShapeDtypeStruct((count, width), BF16),
        ],
        scratch_shapes=[pltpu.VMEM((width, count), BF16), pltpu.VMEM((count, width), F32)],
        cost_estimate=pl.CostEstimate(
            flops=10 * count * width * units,
            bytes_accessed=2 * (3 * count * width + 4 * width * units + 7 * count * units),
            transcendentals=0,
        ),
        compiler_params=pltpu.CompilerParams(vmem_limit_bytes=56 * 2**20),
    )(rows, grad, silu, slope, act, w_down)


WIDEN_SLOTS = 4


def widen_kernel(shapes, places, wide_count, tile, *refs):
    count = len(shapes)
    sources, targets = refs[:count], refs[count : count + wide_count]
    narrow, wide, load_sem, store_sem = refs[count + wide_count :]
    high, broad = tile
    counts = [(rows // high) * (width // broad) for rows, width in shapes]
    total = sum(counts)

    def pick(k, act):
        first = 0
        for i in range(count):
            @pl.when((k >= first) & (k < first + counts[i]))
            def _(i=i, first=first):
                across = shapes[i][1] // broad
                place = k - first
                row = pl.multiple_of((place // across) * high, high)
                col = pl.multiple_of(lax.rem(place, across) * broad, broad)
                act(i, (pl.ds(row, high), pl.ds(col, broad)))
            first += counts[i]

    def load(k, i, where):
        slot = lax.rem(k, WIDEN_SLOTS)
        return pltpu.make_async_copy(sources[i].at[where], narrow.at[slot], load_sem.at[slot])

    def store(k, i, where):
        slot = lax.rem(k, WIDEN_SLOTS)
        target, first = places[i]
        rows = pl.ds(pl.multiple_of(first + where[0].start, high), high)
        return pltpu.make_async_copy(
            wide.at[slot], targets[target].at[rows, where[1]], store_sem.at[slot]
        )

    zero = (pl.ds(0, high), pl.ds(0, broad))
    ahead = WIDEN_SLOTS - 1
    for k in range(ahead):
        pick(k, lambda i, where, k=k: load(k, i, where).start())

    def step(k, carry):
        @pl.when(k + ahead < total)
        def _():
            pick(k + ahead, lambda i, where: load(k + ahead, i, where).start())

        @pl.when(k >= WIDEN_SLOTS)
        def _():
            store(k - WIDEN_SLOTS, 0, zero).wait()

        load(k, 0, zero).wait()
        slot = lax.rem(k, WIDEN_SLOTS)
        wide[slot] = narrow[slot].astype(F32)
        pick(k, lambda i, where: store(k, i, where).start())
        return carry

    lax.fori_loop(0, total, step, 0)
    for k in range(total - WIDEN_SLOTS, total):
        store(k, 0, zero).wait()


def widen(groups, tile):
    arrays, places, targets = [], [], []
    for group in groups:
        rows = 0
        for value in group:
            arrays.append(value)
            places.append((len(targets), rows))
            rows += value.shape[0]
        targets.append((rows, group[0].shape[1]))
    shapes = [value.shape for value in arrays]
    any_ = pl.BlockSpec(memory_space=pltpu.HBM)
    return pl.pallas_call(
        functools.partial(widen_kernel, shapes, places, len(targets), tile),
        in_specs=[any_] * len(arrays),
        out_specs=[any_] * len(targets),
        out_shape=[jax.ShapeDtypeStruct(shape, F32) for shape in targets],
        scratch_shapes=[
            pltpu.VMEM((WIDEN_SLOTS, *tile), BF16),
            pltpu.VMEM((WIDEN_SLOTS, *tile), F32),
            pltpu.SemaphoreType.DMA((WIDEN_SLOTS,)),
            pltpu.SemaphoreType.DMA((WIDEN_SLOTS,)),
        ],
        cost_estimate=pl.CostEstimate(
            flops=0, bytes_accessed=6 * sum(r * c for r, c in shapes), transcendentals=0
        ),
        compiler_params=pltpu.CompilerParams(vmem_limit_bytes=40 * 2**20),
    )(*arrays)


def attn_weights_kernel(
    rows_ref, d_out_ref, mixed_ref, d_query_ref, d_key_ref, d_value_ref,
    w_query_ref, w_key_ref, w_value_ref,
    d_rows_ref, grad_query_ref, grad_key_ref, grad_value_ref, grad_out_ref, gain_part_ref,
    flipped_mixed, flipped_rows,
):
    @pl.when(pl.program_id(0) == 0)
    def _():
        flipped_mixed[...] = mixed_ref[...].T

    flipped_rows[...] = rows_ref[...].T
    d_rows = (
        dot(d_query_ref[...], w_query_ref[...], NT)
        + dot(d_key_ref[...], w_key_ref[...], NT)
        + dot(d_value_ref[...], w_value_ref[...], NT)
    )
    d_rows_ref[...] = d_rows.astype(BF16)
    product = d_rows * rows_ref[...].astype(F32)
    gain_part_ref[...] = jnp.sum(product.reshape(-1, 8, product.shape[1]), axis=0)
    grad_query_ref[...] = dot(flipped_rows[...], d_query_ref[...], NN).astype(BF16)
    grad_key_ref[...] = dot(flipped_rows[...], d_key_ref[...], NN).astype(BF16)
    grad_value_ref[...] = dot(flipped_rows[...], d_value_ref[...], NN).astype(BF16)
    grad_out_ref[...] = dot(flipped_mixed[...], d_out_ref[...], NN).astype(BF16)


def attn_weights(rows, d_out, mixed, d_query, d_key, d_value, w_query, w_key, w_value):
    count, width = rows.shape
    cols = mixed.shape[1]
    block = 512
    once = pl.Buffered(1)
    slim = pl.BlockSpec((count, cols), lambda j: (0, 0), pipeline_mode=once)
    side = pl.BlockSpec((count, block), lambda j: (0, j))
    tall = pl.BlockSpec((block, cols), lambda j: (j, 0))
    wide = pl.BlockSpec((cols, block), lambda j: (0, j))
    tall_type = jax.ShapeDtypeStruct((width, cols), BF16)
    return pl.pallas_call(
        attn_weights_kernel,
        grid=(width // block,),
        in_specs=[side, side, slim, slim, slim, slim, tall, tall, tall],
        out_specs=[side, tall, tall, tall, wide, pl.BlockSpec((8, block), lambda j: (0, j))],
        out_shape=[
            jax.ShapeDtypeStruct((count, width), BF16),
            tall_type,
            tall_type,
            tall_type,
            jax.ShapeDtypeStruct((cols, width), BF16),
            jax.ShapeDtypeStruct((8, width), F32),
        ],
        scratch_shapes=[pltpu.VMEM((cols, count), BF16), pltpu.VMEM((block, count), BF16)],
        cost_estimate=pl.CostEstimate(
            flops=14 * count * width * cols,
            bytes_accessed=2 * (3 * count * width + 4 * count * cols + 7 * width * cols),
            transcendentals=0,
        ),
        compiler_params=pltpu.CompilerParams(vmem_limit_bytes=48 * 2**20),
    )(rows, d_out, mixed, d_query, d_key, d_value, w_query, w_key, w_value)


def from_behind(value, axis, steps):
    count = lax.axis_size(axis)
    initial, last = (max(0, -steps), min(count, count - steps))
    return lax.ppermute(value, axis, [(source, source + steps) for source in range(initial, last)])


def elu_plus(values):
    return jnp.where(values > 0, values + 1.0, jnp.exp(jnp.minimum(values, 0.0)))


def elu_slope(values):
    return jnp.where(values > 0, 1.0, jnp.exp(jnp.minimum(values, 0.0)))


def inverse_rms(values):
    return lax.rsqrt(jnp.mean(values * values, axis=-1, keepdims=True) + epsilon)


def norm_backward(values, inverse, gain_vec, grad_out):
    normal = values * inverse
    scaled = gain_vec * grad_out
    grad_in = inverse * (scaled - normal * jnp.mean(scaled * normal, axis=-1, keepdims=True))
    return grad_in


def dot(left, right, dims, precision=None):
    return lax.dot_general(
        left, right, (dims, ((), ())), precision=precision, preferred_element_type=F32
    )


NN = ((1,), (0,))
NT = ((1,), (1,))
TN = ((0,), (0,))


def valid_column(valid_len):
    return (lax.broadcasted_iota(jnp.int32, (SEG_LEN, 1), 0) < valid_len).astype(F32)


def update_kernel(valid_ref, key_ref, value_ref, out_ref):
    key_feat = elu_plus(key_ref[...].astype(F32)) * valid_column(valid_ref[0])
    out_ref[0, :DH] = dot(key_feat, value_ref[...].astype(F32), TN, highest)
    out_ref[0, DH:] = jnp.broadcast_to(
        jnp.sum(key_feat, axis=0, keepdims=True), (MEM_ROWS - DH, DH)
    )


def block_probs(query_block, key_rows, start, valid_len):
    scores = dot(query_block, key_rows, NT) * (DH**-0.5)
    row_pos = start + lax.broadcasted_iota(jnp.int32, scores.shape, 0)
    col_pos = lax.broadcasted_iota(jnp.int32, scores.shape, 1)
    allowed = (row_pos >= col_pos) & (col_pos < valid_len)
    scores = jnp.where(allowed, scores, masked_score)
    weights = jnp.exp(scores - jnp.max(scores, axis=-1, keepdims=True))
    return weights / jnp.sum(weights, axis=-1, keepdims=True)


def local_kernel(valid_ref, query_ref, key_ref, value_ref, out_ref):
    for start in range(0, SEG_LEN, BLOCK):
        rows = slice(start, start + BLOCK)
        key_rows = key_ref[: start + BLOCK]
        probs = block_probs(query_ref[rows], key_rows, start, valid_ref[0])
        out_ref[rows] = dot(probs.astype(BF16), value_ref[: start + BLOCK], NN)


def retrieve(query_feat, memory, normal):
    numerator = dot(query_feat, memory, NN, highest)
    denominator = jnp.sum(query_feat * normal, axis=-1, keepdims=True) + 1.0
    return numerator / denominator, denominator


def mix_kernel(gate_ref, query_ref, local_ref, memory_ref, out_ref):
    gate = gate_ref[pl.program_id(0)]
    query_feat = elu_plus(query_ref[...].astype(F32))
    retrieved, _ = retrieve(query_feat, memory_ref[0, :DH], memory_ref[0, DH : DH + 1])
    out_ref[...] = (gate * retrieved + (1.0 - gate) * local_ref[...]).astype(BF16)


def greet_sequence():
    seg = lax.axis_index("seg")
    place = lax.rem(seg, SEGS)
    barrier = pltpu.get_barrier_semaphore()
    for distance in range(1, SEGS):
        other = seg - place + lax.rem(place + distance, SEGS)
        pl.semaphore_signal(barrier, inc=1, device_id={"seg": other}, device_id_type=MESH)
    pl.semaphore_wait(barrier, SEGS - 1)


def sequence_copies(source, land, send_sem, recv_sem, sign):
    seg = lax.axis_index("seg")
    count = lax.axis_size("seg")
    place = lax.rem(seg, SEGS)
    copies = []
    for distance in range(1, SEGS):
        copy = pltpu.make_async_remote_copy(
            src_ref=source,
            dst_ref=land.at[distance - 1],
            send_sem=send_sem.at[distance - 1],
            recv_sem=recv_sem.at[distance - 1],
            device_id={"seg": lax.rem(seg + count + sign * distance, count)},
            device_id_type=MESH,
        )
        after, before = place + distance < SEGS, place >= distance
        copies.append((copy, after, before) if sign > 0 else (copy, before, after))
    return copies


def head_cols(head):
    return pl.ds(pl.multiple_of(head * DH, DH), DH)


def attn_back_kernel(
    gate_ref, valid_ref, d_out_ref, weight_ref, query_ref, key_ref, value_ref, local_ref, memory_ref,
    d_query_ref, d_key_ref, d_value_ref, gate_grad_ref,
    d_mixed, feat, d_key_sum, d_value_sum, back, land, update, send_sem, recv_sem,
):
    heads = memory_ref.shape[0]
    valid_len = valid_ref[0]
    greet_sequence()
    copies = sequence_copies(back, land, send_sem, recv_sem, -1)
    d_mixed[...] = dot(d_out_ref[...], weight_ref[...], NT)

    def memory_back(head, carry):
        cols = head_cols(head)
        gate = gate_ref[head]
        query_vals = query_ref[:, cols].astype(F32)
        query_feat = elu_plus(query_vals)
        memory, normal = memory_ref[head, :DH], memory_ref[head, DH : DH + 1]
        retrieved, denominator = retrieve(query_feat, memory, normal)
        d_head = d_mixed[:, cols]
        gate_grad_ref[head] = jnp.broadcast_to(
            jnp.sum(d_head * (retrieved - local_ref[:, cols]), axis=0, keepdims=True), (8, DH)
        )
        d_retrieved = gate * d_head
        d_numerator = d_retrieved / denominator
        d_denominator = -jnp.sum(d_retrieved * retrieved, axis=-1, keepdims=True) / denominator
        d_feat = dot(d_numerator, memory, NT, highest) + d_denominator * normal
        feat[:, cols] = d_feat * elu_slope(query_vals)
        back[head, :DH] = dot(query_feat, d_numerator, TN, highest).astype(BF16)
        d_normal = jnp.sum(d_denominator * query_feat, axis=0, keepdims=True)
        back[head, DH:] = jnp.broadcast_to(d_normal, (MEM_ROWS - DH, DH)).astype(BF16)
        return carry

    lax.fori_loop(0, heads, memory_back, 0)
    for copy, sends, _ in copies:

        @pl.when(sends)
        def _(copy=copy):
            copy.start()

    d_key_sum[...] = jnp.zeros_like(d_key_sum)
    d_value_sum[...] = jnp.zeros_like(d_value_sum)

    def local_back(head, carry):
        cols = head_cols(head)
        keep = 1.0 - gate_ref[head]
        for start in range(0, SEG_LEN, BLOCK):
            rows, seen = slice(start, start + BLOCK), slice(0, start + BLOCK)
            query_block = query_ref[rows, cols]
            probs = block_probs(query_block, key_ref[seen, cols], start, valid_len)
            d_local = (keep * d_mixed[rows, cols]).astype(BF16)
            d_probs = dot(d_local, value_ref[seen, cols], NT)
            row_dot = jnp.sum(probs * d_probs, axis=-1, keepdims=True)
            d_scores = (probs * (d_probs - row_dot) * (DH**-0.5)).astype(BF16)
            d_query = dot(d_scores, key_ref[seen, cols], NN) + feat[rows, cols]
            d_query_ref[rows, cols] = d_query.astype(BF16)
            d_key_sum[seen, cols] += dot(d_scores, query_block, TN)
            d_value_sum[seen, cols] += dot(probs.astype(BF16), d_local, TN)
        return carry

    lax.fori_loop(0, heads, local_back, 0)
    update[...] = jnp.zeros_like(update)
    for distance, (copy, sends, gets) in enumerate(copies):

        @pl.when(sends)
        def _(copy=copy):
            copy.wait_send()

        @pl.when(gets)
        def _(copy=copy, distance=distance):
            copy.wait_recv()
            update[...] += land[distance].astype(F32)

    def finish_back(head, carry):
        cols = head_cols(head)
        valid = valid_column(valid_len)
        key_vals = key_ref[:, cols].astype(F32)
        memory, normal = update[head, :DH], update[head, DH : DH + 1]
        d_feat = (dot(value_ref[:, cols].astype(F32), memory, NT, highest) + normal) * valid
        d_key_ref[:, cols] = (d_key_sum[:, cols] + d_feat * elu_slope(key_vals)).astype(BF16)
        key_feat = elu_plus(key_vals) * valid
        d_value = d_value_sum[:, cols] + dot(key_feat, memory, NN, highest)
        d_value_ref[:, cols] = d_value.astype(BF16)
        return carry

    lax.fori_loop(0, heads, finish_back, 0)


def attn_back(gate, valid, d_out, weight, query, key, value, local, memory, cid):
    rows, cols = query.shape
    heads = cols // DH
    scalar, vmem = pl.BlockSpec(memory_space=pltpu.SMEM), pl.BlockSpec(memory_space=pltpu.VMEM)
    wide = pltpu.VMEM((rows, cols), F32)
    narrow = jax.ShapeDtypeStruct((rows, cols), BF16)
    return pl.pallas_call(
        attn_back_kernel,
        in_specs=[scalar] * 2 + [vmem] * 7,
        out_specs=[vmem] * 4,
        out_shape=[narrow, narrow, narrow, jax.ShapeDtypeStruct((heads, 8, DH), F32)],
        scratch_shapes=[
            wide,
            wide,
            wide,
            wide,
            pltpu.VMEM((heads, MEM_ROWS, DH), BF16),
            pltpu.VMEM((SEGS - 1, heads, MEM_ROWS, DH), BF16),
            pltpu.VMEM((heads, MEM_ROWS, DH), F32),
            pltpu.SemaphoreType.DMA((SEGS - 1,)),
            pltpu.SemaphoreType.DMA((SEGS - 1,)),
        ],
        cost_estimate=pl.CostEstimate(
            flops=10 * rows * rows * cols + 2 * rows * cols * d_out.shape[1],
            bytes_accessed=100 * 2**20,
            transcendentals=rows * rows * heads,
        ),
        compiler_params=pltpu.CompilerParams(
            collective_id=cid, has_side_effects=True, vmem_limit_bytes=48 * 2**20
        ),
    )(gate, valid, d_out, weight, query, key, value, local, memory)


SCALAR = pl.BlockSpec(memory_space=pltpu.SMEM)
COLUMN = pl.BlockSpec((SEG_LEN, DH), lambda head: (0, head))
MEMORY = pl.BlockSpec((1, MEM_ROWS, DH), lambda head: (head, 0, 0))


def per_head(kernel, heads, in_specs, out_specs, out_types, flops, transcendentals=0):
    moved = heads * SEG_LEN * DH * 4 * len(in_specs)
    return pl.pallas_call(
        kernel,
        grid=(heads,),
        in_specs=in_specs,
        out_specs=out_specs,
        out_shape=out_types,
        cost_estimate=pl.CostEstimate(
            flops=flops, bytes_accessed=moved, transcendentals=transcendentals
        ),
        compiler_params=pltpu.CompilerParams(vmem_limit_bytes=40 * 1024 * 1024),
    )


def per_device(
    tokens,
    cotangent,
    gain_attn,
    gain_mlp,
    w_query,
    w_key,
    w_value,
    w_out,
    w_gate,
    w_up,
    w_down,
    mem_gate,
    lengths,
):
    seg_index = lax.axis_index("seg")
    head_index = lax.axis_index("head")
    head_groups = lax.axis_size("head")
    seg_size = lax.axis_size("seg")
    position = seg_index % SEGS
    sequence = seg_index // SEGS
    seq_length = jnp.sum(jnp.where(lax.iota(jnp.int32, lengths.shape[0]) == sequence, lengths, 0))
    valid_len = jnp.where(position == SEGS - 1, seq_length, SEG_LEN).reshape(1)
    heads = mem_gate.shape[0]
    cols = heads * DH
    col_f32 = jax.ShapeDtypeStruct((SEG_LEN, cols), F32)
    col_bf16 = jax.ShapeDtypeStruct((SEG_LEN, cols), BF16)
    mem_f32 = jax.ShapeDtypeStruct((heads, MEM_ROWS, DH), F32)
    unit = 2 * heads * SEG_LEN * DH * DH
    pairs = heads * SEG_LEN * SEG_LEN

    token_vals = tokens.astype(F32)
    gathered_tokens = lax.all_gather(tokens, "head", axis=0, tiled=True)
    gathered_grad = lax.all_gather(cotangent, "head", axis=0, tiled=True)
    all_tokens = gathered_tokens.astype(F32)
    gathered_attn = (all_tokens * inverse_rms(all_tokens) * gain_attn).astype(BF16)

    def project(weight):
        return jnp.dot(gathered_attn, weight, preferred_element_type=F32).astype(BF16)

    key_rows = project(w_key)
    value_rows = project(w_value)
    update = per_head(update_kernel, heads, [SCALAR, COLUMN, COLUMN], MEMORY, mem_f32, 6 * unit)(
        valid_len, key_rows, value_rows
    )
    query_rows = project(w_query)
    memory_prev = jnp.zeros_like(update)
    for distance in range(1, SEGS):
        moved = from_behind(update, "seg", distance)
        memory_prev = memory_prev + jnp.where(position >= distance, moved, 0.0)
    local_attn = per_head(
        local_kernel, heads, [SCALAR, COLUMN, COLUMN, COLUMN], COLUMN, col_f32, 4 * pairs * DH, pairs
    )(valid_len, query_rows, key_rows, value_rows)
    after = memory_prev + update
    memory_after = (after[:, :DH] * SEG_LEN ** (-0.5))[None]
    normal_after = (after[:, DH] / SEG_LEN)[None]
    mix_sig = jax.nn.sigmoid(mem_gate)
    mixed_attn = per_head(
        mix_kernel, heads, [SCALAR, COLUMN, COLUMN, MEMORY], COLUMN, col_bf16, 6 * unit
    )(mix_sig, query_rows, local_attn, memory_prev)
    all_hidden, gathered_mlp, silu, slope, act = attn_out_sum(
        mixed_attn, w_out, gathered_tokens, gain_mlp, w_gate, w_up, head_groups, 1
    )
    own_rows = tokens.shape[0]
    hidden_res = lax.dynamic_slice_in_dim(all_hidden, head_index * own_rows, own_rows, 0)
    d_gate, d_up, grad_gate, up_top, up_low, grad_down, mlp_part = mlp_both(
        gathered_mlp, gathered_grad, silu, slope, act, w_down
    )
    sum_gate, sum_up_top = lax.psum((grad_gate, up_top), "seg")
    gathered_hidden, d_hidden, gain_mlp_rows, summed_down = mlp_back_sum(
        d_gate,
        d_up,
        w_gate,
        w_up,
        all_hidden,
        gathered_grad,
        gain_mlp,
        grad_down,
        (BLOCK, cols),
        seg_size,
        head_groups,
        2,
    )
    mlp_out = lax.psum_scatter(mlp_part, "head", scatter_dimension=0, tiled=True)
    output = (hidden_res + mlp_out.astype(F32)).astype(BF16)
    d_queries, d_keys, d_values, gate_cols = attn_back(
        mix_sig,
        valid_len,
        gathered_hidden,
        w_out,
        query_rows,
        key_rows,
        value_rows,
        local_attn,
        memory_prev,
        3,
    )
    d_part, grad_query, grad_key, grad_value, grad_out, gain_attn_rows = attn_weights(
        gathered_attn,
        gathered_hidden,
        mixed_attn,
        d_queries,
        d_keys,
        d_values,
        w_query,
        w_key,
        w_value,
    )
    d_normed_attn = lax.psum_scatter(d_part, "head", scatter_dimension=0, tiled=True).astype(F32)
    grad_in_attn = norm_backward(token_vals, inverse_rms(token_vals), gain_attn, d_normed_attn)
    grad_tokens = (d_hidden + grad_in_attn).astype(BF16)
    gate_part = mix_sig * (1.0 - mix_sig) * jnp.sum(gate_cols[:, 0], axis=-1)
    slots = jnp.where(
        (lax.iota(jnp.int32, head_groups) == head_index)[:, None], gate_part[None], 0.0
    )
    width = gain_attn.shape[0]
    gain_attn_part = jnp.sum(gain_attn_rows, axis=0) / gain_attn
    gain_mlp_part = jnp.sum(gain_mlp_rows, axis=0)
    parts = jnp.concatenate([gain_attn_part, gain_mlp_part, slots.reshape(-1)])
    lines = -(-parts.shape[0] // (8 * DH)) * 8
    parts = jnp.pad(parts, (0, lines * DH - parts.shape[0])).reshape(lines, DH)
    small, *late = grad_sum(
        parts,
        [up_low, grad_out, grad_query, grad_key, grad_value],
        (cols, cols),
        seg_size,
        head_groups,
        0,
    )
    small = small.reshape(-1)
    grad_mem_gate = lax.dynamic_slice(small, (2 * width + head_index * heads,), (heads,))
    grads = widen(
        [(sum_gate,), (sum_up_top, late[0]), (summed_down,)] + [(grad,) for grad in late[1:]],
        (cols, cols),
    )
    return (
        output,
        grad_tokens,
        memory_after,
        normal_after,
        small[:width],
        small[width : 2 * width],
        grads[4],
        grads[5],
        grads[6],
        grads[3],
        grads[0],
        grads[1],
        grads[2],
        grad_mem_gate,
    )


def solution(mesh):
    return jax.shard_map(
        per_device,
        mesh=mesh,
        in_specs=(
            P(("seg", "head"), None),
            P(("seg", "head"), None),
            P(),
            P(),
            P(None, "head"),
            P(None, "head"),
            P(None, "head"),
            P("head", None),
            P(None, "head"),
            P(None, "head"),
            P("head", None),
            P("head"),
            P(),
        ),
        out_specs=(
            P(("seg", "head"), None),
            P(("seg", "head"), None),
            P("seg", "head", None, None),
            P("seg", "head", None),
            P(),
            P(),
            P(None, "head"),
            P(None, "head"),
            P(None, "head"),
            P("head", None),
            P(None, "head"),
            P(None, "head"),
            P("head", None),
            P("head"),
        ),
        check_vma=False,
    )
```

```python
import functools

import jax
import jax.numpy as jnp
from jax import lax
from jax.experimental import pallas as pl
from jax.experimental.pallas import tpu as pltpu
from jax.sharding import PartitionSpec as P

DH = 128
SEG_LEN = 1024
SEGS = 4
MEM_ROWS = DH + 16
BLOCK = 256

epsilon = 1e-05
masked_score = -1e30
F32 = jnp.float32
BF16 = jnp.bfloat16


MESH = pl.DeviceIdType.MESH
LAND_SLOTS = 12
RESULT_SLOTS = 16
SUM_SEMS = 8
SUM_HOP = 3


def bits_of(size):
    return size.bit_length() - 1


def flip(index, power):
    return index + power - 2 * power * lax.rem(index // power, 2)


def sum_engine(arrays, outs, tile, seg_bits, scratch):
    mine, result, send_sem, recv_sem, load_sem, store_sem, *lands = scratch
    seg = lax.axis_index("seg")
    planes = seg_bits - 1
    high, wide = tile
    shapes = [array.shape for array in arrays]
    counts = [(rows // high) * (cols // wide) for rows, cols in shapes]
    starts = [sum(counts[:i]) for i in range(len(counts))]
    total = sum(counts)

    def power(k, level):
        if level == 0:
            return 1
        which = lax.rem(k + level - 1, planes)
        value = 2
        for bit in range(1, planes):
            value = jnp.where(which == bit, 2 << bit, value)
        return value

    def my_bit(k, level):
        return lax.rem(seg // power(k, level), 2)

    def part(k, level, own):
        half = high >> (level + 1)
        bit = my_bit(k, level) if own else 1 - my_bit(k, level)
        return pl.ds(pl.multiple_of(bit * half, half), half)

    def kept(k, levels):
        first = 0
        for level in range(levels):
            first = first + my_bit(k, level) * (high >> (level + 1))
        return pl.ds(pl.multiple_of(first, high >> levels), high >> levels)

    def pick(k, act):
        for i in range(len(arrays)):

            @pl.when((k >= starts[i]) & (k < starts[i] + counts[i]))
            def _(i=i):
                across = shapes[i][1] // wide
                place = k - starts[i]
                row = pl.multiple_of((place // across) * high, high)
                col = pl.multiple_of(lax.rem(place, across) * wide, wide)
                act(i, row, col)

    def halving(k, level, source):
        return pltpu.make_async_remote_copy(
            src_ref=source,
            dst_ref=lands[level].at[lax.rem(k, LAND_SLOTS)],
            send_sem=send_sem.at[level, lax.rem(k, SUM_SEMS)],
            recv_sem=recv_sem.at[level, lax.rem(k, SUM_SEMS)],
            device_id={"seg": flip(seg, power(k, level))},
            device_id_type=MESH,
        )

    def first_source(k, i, row, col, own):
        half = high // 2
        bit = my_bit(k, 0) if own else 1 - my_bit(k, 0)
        return arrays[i].at[pl.ds(pl.multiple_of(row + bit * half, half), half), pl.ds(col, wide)]

    def keep(k, i, row, col):
        slot = lax.rem(k, 4)
        return pltpu.make_async_copy(
            first_source(k, i, row, col, True), mine.at[slot], load_sem.at[slot]
        )

    def level_source(k, level):
        return lands[level - 1].at[lax.rem(k, LAND_SLOTS), part(k, level, False)]

    def doubling(k, level):
        ref = result.at[lax.rem(k, RESULT_SLOTS), kept(k, level + 1)]
        return pltpu.make_async_remote_copy(
            src_ref=ref,
            dst_ref=ref,
            send_sem=send_sem.at[seg_bits + level, lax.rem(k, SUM_SEMS)],
            recv_sem=recv_sem.at[seg_bits + level, lax.rem(k, SUM_SEMS)],
            device_id={"seg": flip(seg, power(k, level))},
            device_id_type=MESH,
        )

    def store(k, i, row, col):
        slot = lax.rem(k, 4)
        return pltpu.make_async_copy(
            result.at[lax.rem(k, RESULT_SLOTS)],
            outs[i].at[pl.ds(row, high), pl.ds(col, wide)],
            store_sem.at[slot],
        )

    def do_first(k):
        def go(i, row, col):
            halving(k, 0, first_source(k, i, row, col, False)).start()
            keep(k, i, row, col).start()

        pick(k, go)

    def arrived(k, level):
        slot = lax.rem(k, LAND_SLOTS)
        if level == 0:
            halving(k, 0, first_source(k, 0, 0, 0, False)).wait()
            keep(k, 0, 0, 0).wait()
            other = mine[lax.rem(k, 4)]
        else:
            halving(k, level, level_source(k, level)).wait()
            other = lands[level - 1][slot, part(k, level, True)]
        return (lands[level][slot].astype(F32) + other.astype(F32)).astype(BF16)

    def do_level(k, level):
        lands[level - 1][lax.rem(k, LAND_SLOTS)] = arrived(k, level - 1)
        halving(k, level, level_source(k, level)).start()

    def do_total(k):
        result[lax.rem(k, RESULT_SLOTS), kept(k, seg_bits)] = arrived(k, seg_bits - 1)
        doubling(k, seg_bits - 1).start()

    def do_spread(k, level):
        doubling(k, level + 1).wait()
        doubling(k, level).start()

    def do_finish(k):
        doubling(k, 0).wait()
        pick(k, lambda i, row, col: store(k, i, row, col).start())

    def do_store(k):
        store(k, 0, 0, 0).wait()

    stages = [(0, do_first), (1, functools.partial(do_level, level=1))]
    when = 1
    for level in range(2, seg_bits):
        when += SUM_HOP
        stages.append((when, functools.partial(do_level, level=level)))
    when += SUM_HOP
    stages.append((when, do_total))
    for level in range(seg_bits - 2, -1, -1):
        when += SUM_HOP
        stages.append((when, functools.partial(do_spread, level=level)))
    stages.append((when + 1, do_finish))
    stages.append((when + 3, do_store))

    def step(t):
        for delay, act in reversed(stages):
            k = t - delay

            @pl.when((k >= 0) & (k < total))
            def _(act=act, k=k):
                act(k)

    return step, total + when + 3


def engine_scratch(tile, seg_bits):
    high, wide = tile
    return [
        pltpu.VMEM((4, high // 2, wide), BF16),
        pltpu.VMEM((RESULT_SLOTS, high, wide), BF16),
        pltpu.SemaphoreType.DMA((2 * seg_bits, SUM_SEMS)),
        pltpu.SemaphoreType.DMA((2 * seg_bits, SUM_SEMS)),
        pltpu.SemaphoreType.DMA((4,)),
        pltpu.SemaphoreType.DMA((4,)),
    ] + [pltpu.VMEM((LAND_SLOTS, high >> (l + 1), wide), BF16) for l in range(seg_bits)]


def greet_seg(seg_bits):
    barrier = pltpu.get_barrier_semaphore()
    seg = lax.axis_index("seg")
    for bit in range(seg_bits):
        pl.semaphore_signal(
            barrier, inc=1, device_id={"seg": flip(seg, 1 << bit)}, device_id_type=MESH
        )


def grad_sum_kernel(count, tile, seg_bits, head_bits, *refs):
    small_in, arrays = refs[0], refs[1 : 1 + count]
    small_out, outs = refs[1 + count], refs[2 + count : 2 + 2 * count]
    small_buf, small_land, small_send, small_recv, *scratch = refs[2 + 2 * count :]
    seg, head = lax.axis_index("seg"), lax.axis_index("head")
    greet_seg(seg_bits)
    barrier = pltpu.get_barrier_semaphore()
    for bit in range(head_bits):
        pl.semaphore_signal(
            barrier, inc=1, device_id={"head": flip(head, 1 << bit)}, device_id_type=MESH
        )
    pl.semaphore_wait(barrier, seg_bits + head_bits)
    rounds = seg_bits + head_bits

    def small_copy(j):
        if j < seg_bits:
            where = {"seg": flip(seg, 1 << j)}
        else:
            where = {"head": flip(head, 1 << (j - seg_bits))}
        return pltpu.make_async_remote_copy(
            src_ref=small_buf.at[j],
            dst_ref=small_land.at[j],
            send_sem=small_send.at[j],
            recv_sem=small_recv.at[j],
            device_id=where,
            device_id_type=MESH,
        )

    engine_step, steps = sum_engine(arrays, outs, tile, seg_bits, scratch)

    def step(t, carry):
        engine_step(t)
        for j in range(rounds + 1):

            @pl.when(t == 3 * j)
            def _(j=j):
                if j == 0:
                    small_buf[0] = small_in[...]
                else:
                    small_copy(j - 1).wait()
                    value = small_buf[j - 1] + small_land[j - 1]
                    if j < rounds:
                        small_buf[j] = value
                    else:
                        small_out[...] = value
                if j < rounds:
                    small_copy(j).start()

        return carry

    lax.fori_loop(0, max(steps, 3 * rounds + 1), step, 0)


def grad_sum(small, arrays, tile, seg_size, head_size, cid):
    seg_bits, head_bits = bits_of(seg_size), bits_of(head_size)
    rounds = seg_bits + head_bits
    count = len(arrays)
    moved = sum(rows * cols for rows, cols in (array.shape for array in arrays))
    any_, vmem = pl.BlockSpec(memory_space=pltpu.HBM), pl.BlockSpec(memory_space=pltpu.VMEM)
    return pl.pallas_call(
        functools.partial(grad_sum_kernel, count, tile, seg_bits, head_bits),
        in_specs=[vmem] + [any_] * count,
        out_specs=[vmem] + [any_] * count,
        out_shape=[jax.ShapeDtypeStruct(small.shape, F32)]
        + [jax.ShapeDtypeStruct(array.shape, BF16) for array in arrays],
        scratch_shapes=[
            pltpu.VMEM((rounds, *small.shape), F32),
            pltpu.VMEM((rounds, *small.shape), F32),
            pltpu.SemaphoreType.DMA((rounds,)),
            pltpu.SemaphoreType.DMA((rounds,)),
        ]
        + engine_scratch(tile, seg_bits),
        cost_estimate=pl.CostEstimate(flops=0, bytes_accessed=moved * 60, transcendentals=0),
        compiler_params=pltpu.CompilerParams(
            collective_id=cid, has_side_effects=True, vmem_limit_bytes=60 * 2**20
        ),
    )(small, *arrays)


ROWS = 32
HOP = 2
SEND_SLOTS = 4
BLOCK_ROWS = 256
UNIT_GROUP = 512
LINE_REFS = 8


def line_exchange(own, finish, before, scratch, extra=None, extra_steps=0):
    up_land, down_land, up_send, down_send, up_recv_sem, down_recv_sem, up_send_sem, down_send_sem = scratch
    size = lax.axis_size("head")
    place = lax.axis_index("head")
    slots = up_land.shape[0]
    chunks = own.shape[0] // ROWS
    last = size - 1

    def up_copy(k):
        return pltpu.make_async_remote_copy(
            src_ref=up_send.at[lax.rem(k, SEND_SLOTS)],
            dst_ref=up_land.at[lax.rem(k, slots)],
            send_sem=up_send_sem.at[lax.rem(k, SEND_SLOTS)],
            recv_sem=up_recv_sem.at[lax.rem(k, slots)],
            device_id={"head": lax.rem(place + 1, size)},
            device_id_type=MESH,
        )

    def down_copy(k):
        return pltpu.make_async_remote_copy(
            src_ref=down_send.at[lax.rem(k, SEND_SLOTS)],
            dst_ref=down_land.at[lax.rem(k, slots)],
            send_sem=down_send_sem.at[lax.rem(k, SEND_SLOTS)],
            recv_sem=down_recv_sem.at[lax.rem(k, slots)],
            device_id={"head": lax.rem(place + last, size)},
            device_id_type=MESH,
        )

    def rows_of(k):
        return pl.ds(pl.multiple_of(k * ROWS, ROWS), ROWS)

    def pass_on(k, copy, land, send, has_source, has_target):
        @pl.when(has_source)
        def _():
            copy(k).wait_recv()

        @pl.when(has_target)
        def _():
            slot = lax.rem(k, SEND_SLOTS)

            @pl.when(k >= SEND_SLOTS)
            def _():
                copy(k - SEND_SLOTS).wait_send()

            @pl.when(has_source)
            def _():
                send[slot] = (own[rows_of(k)] + land[lax.rem(k, slots)].astype(F32)).astype(BF16)

            @pl.when(jnp.logical_not(has_source))
            def _():
                send[slot] = own[rows_of(k)].astype(BF16)

            copy(k).start()

    far = jnp.maximum(place, last - place)

    def step(t, carry):
        before(t)
        down = t - (last - place) * HOP

        @pl.when((down >= 0) & (down < chunks))
        def _():
            pass_on(down, down_copy, down_land, down_send, place < last, place > 0)

        up = t - place * HOP

        @pl.when((up >= 0) & (up < chunks))
        def _():
            pass_on(up, up_copy, up_land, up_send, place > 0, place < last)

        k = t - far * HOP

        @pl.when((k >= 0) & (k < chunks))
        def _():
            slot = lax.rem(k, slots)

            @pl.when(place == 0)
            def _():
                finish(k, own[rows_of(k)] + down_land[slot].astype(F32))

            @pl.when(place == last)
            def _():
                finish(k, own[rows_of(k)] + up_land[slot].astype(F32))

            @pl.when((place > 0) & (place < last))
            def _():
                finish(
                    k,
                    own[rows_of(k)] + up_land[slot].astype(F32) + down_land[slot].astype(F32),
                )

        if extra is not None:
            extra(t)
        return carry

    lax.fori_loop(0, max(chunks + last * HOP, extra_steps), step, 0)
    for k in range(chunks - SEND_SLOTS, chunks):

        @pl.when(place < last)
        def _(k=k):
            up_copy(k).wait_send()

        @pl.when(place > 0)
        def _(k=k):
            down_copy(k).wait_send()


def line_barrier(others=0):
    size = lax.axis_size("head")
    place = lax.axis_index("head")
    barrier = pltpu.get_barrier_semaphore()
    inner = (place > 0) & (place < size - 1)

    def greet(near):
        pl.semaphore_signal(
            barrier, inc=1, device_id={"head": lax.rem(near, size)}, device_id_type=MESH
        )

    @pl.when(place > 0)
    def _():
        greet(place + size - 1)

    @pl.when(place < size - 1)
    def _():
        greet(place + 1)

    @pl.when(inner)
    def _():
        pl.semaphore_wait(barrier, 2 + others)

    @pl.when(jnp.logical_not(inner))
    def _():
        pl.semaphore_wait(barrier, 1 + others)


def line_scratch(size, width):
    slots = (size - 1) * HOP + 2
    return [
        pltpu.VMEM((slots, ROWS, width), BF16),
        pltpu.VMEM((slots, ROWS, width), BF16),
        pltpu.VMEM((SEND_SLOTS, ROWS, width), BF16),
        pltpu.VMEM((SEND_SLOTS, ROWS, width), BF16),
        pltpu.SemaphoreType.DMA((slots,)),
        pltpu.SemaphoreType.DMA((slots,)),
        pltpu.SemaphoreType.DMA((SEND_SLOTS,)),
        pltpu.SemaphoreType.DMA((SEND_SLOTS,)),
    ]


GATHER_PARTS = 4


def gather_kernel(
    token_hbm, gain_ref, w_query_hbm, w_key_hbm, w_value_hbm,
    all_ref, normed_ref, query_ref, key_ref, value_ref,
    land, normed, w_query, w_key, w_value,
    own_sem, load_sem, all_sem, normed_sem, up_send, up_recv, down_send, down_recv,
):
    size = lax.axis_size("head")
    place = lax.axis_index("head")
    last = size - 1
    own_rows = token_hbm.shape[0]
    chunk = own_rows // GATHER_PARTS
    loads = [
        pltpu.make_async_copy(source, target, load_sem.at[i])
        for i, (source, target) in enumerate(
            ((w_key_hbm, w_key), (w_value_hbm, w_value), (w_query_hbm, w_query))
        )
    ]

    def shard_rows(shard):
        return pl.ds(pl.multiple_of(shard * own_rows, own_rows), own_rows)

    own = pltpu.make_async_copy(token_hbm, land.at[shard_rows(place)], own_sem)
    own.start()
    for load in loads:
        load.start()
    line_barrier()

    def chunk_copy(shard, i, send_sem, recv_sem, target):
        first = pl.multiple_of(shard * own_rows + lax.rem(i, GATHER_PARTS) * chunk, chunk)
        ref = land.at[pl.ds(first, chunk)]
        return pltpu.make_async_remote_copy(
            src_ref=ref,
            dst_ref=ref,
            send_sem=send_sem.at[i],
            recv_sem=recv_sem.at[i],
            device_id={"head": target},
            device_id_type=MESH,
        )

    above, below = lax.rem(place + 1, size), lax.rem(place + last, size)

    def up_copy(i, first_shard):
        return chunk_copy(first_shard - i // GATHER_PARTS, i, up_send, up_recv, above)

    def down_copy(i, first_shard):
        return chunk_copy(first_shard + i // GATHER_PARTS, i, down_send, down_recv, below)

    own.wait()
    for i in range(GATHER_PARTS):

        @pl.when(place < last)
        def _(i=i):
            up_copy(i, place).start()

        @pl.when(place > 0)
        def _(i=i):
            down_copy(i, place).start()

    def stores(shard):
        rows = shard_rows(shard)
        return (
            pltpu.make_async_copy(land.at[rows], all_ref.at[rows], all_sem.at[shard]),
            pltpu.make_async_copy(normed.at[rows], normed_ref.at[rows], normed_sem.at[shard]),
        )

    def project(shard):
        rows = shard_rows(shard)
        value = land[rows].astype(F32)
        normed[rows] = (value * inverse_rms(value) * gain_ref[...]).astype(BF16)
        for copy in stores(shard):
            copy.start()
        for weight, target in ((w_key, key_ref), (w_value, value_ref), (w_query, query_ref)):
            target[rows] = dot(normed[rows], weight[...], NN).astype(BF16)

    for load in loads:
        load.wait()
    project(place)

    def step(i, carry):
        @pl.when(i < place * GATHER_PARTS)
        def _():
            up_copy(i, place - 1).wait_recv()

            @pl.when(place < last)
            def _():
                up_copy(i + GATHER_PARTS, place).start()

        @pl.when(i < (last - place) * GATHER_PARTS)
        def _():
            down_copy(i, place + 1).wait_recv()

            @pl.when(place > 0)
            def _():
                down_copy(i + GATHER_PARTS, place).start()

        distance = (i + 1) // GATHER_PARTS
        whole = lax.rem(i + 1, GATHER_PARTS) == 0

        @pl.when(whole & (place >= distance))
        def _():
            project(place - distance)

        @pl.when(whole & (place + distance <= last))
        def _():
            project(place + distance)

        return carry

    lax.fori_loop(0, last * GATHER_PARTS, step, 0)

    def drain(i, carry):
        @pl.when((place < last) & (i < (place + 1) * GATHER_PARTS))
        def _():
            up_copy(i, place).wait_send()

        @pl.when((place > 0) & (i < (size - place) * GATHER_PARTS))
        def _():
            down_copy(i, place).wait_send()

        return carry

    lax.fori_loop(0, size * GATHER_PARTS, drain, 0)
    for shard in range(size):
        for copy in stores(shard):
            copy.wait()


def gather_project(tokens, gain, w_query, w_key, w_value, size, cid):
    own_rows, width = tokens.shape
    rows, cols = own_rows * size, w_query.shape[1]
    vmem, any_ = pl.BlockSpec(memory_space=pltpu.VMEM), pl.BlockSpec(memory_space=pltpu.HBM)
    weight = pltpu.VMEM((width, cols), BF16)
    hops = pltpu.SemaphoreType.DMA((size * GATHER_PARTS,))
    return pl.pallas_call(
        gather_kernel,
        in_specs=[any_, vmem] + [any_] * 3,
        out_specs=[any_, any_, vmem, vmem, vmem],
        out_shape=[jax.ShapeDtypeStruct((rows, width), BF16)] * 2
        + [jax.ShapeDtypeStruct((rows, cols), BF16)] * 3,
        scratch_shapes=[
            pltpu.VMEM((rows, width), BF16),
            pltpu.VMEM((rows, width), BF16),
            weight,
            weight,
            weight,
            pltpu.SemaphoreType.DMA(()),
            pltpu.SemaphoreType.DMA((3,)),
            pltpu.SemaphoreType.DMA((size,)),
            pltpu.SemaphoreType.DMA((size,)),
            hops,
            hops,
            hops,
            hops,
        ],
        cost_estimate=pl.CostEstimate(
            flops=6 * rows * width * cols, bytes_accessed=150 * 2**20, transcendentals=0
        ),
        compiler_params=pltpu.CompilerParams(
            collective_id=cid, has_side_effects=True, vmem_limit_bytes=48 * 2**20
        ),
    )(tokens, gain.reshape(1, width), w_query, w_key, w_value)


def attn_out_kernel(
    mixed_ref, weight_ref, token_ref, gain_ref, w_gate_hbm, w_up_hbm, w_down_hbm,
    hidden_ref, flip_ref, silu_ref, slope_ref, act_ref, part_ref,
    hidden, normed, w_gate, w_up, w_down, silu, slope, act, flip, part, part_out,
    hidden_sem, load_sem, out_sem, block_sem, *scratch
):
    loads = [
        pltpu.make_async_copy(source, target, load_sem.at[i])
        for i, (source, target) in enumerate(
            ((w_gate_hbm, w_gate), (w_up_hbm, w_up), (w_down_hbm, w_down))
        )
    ]
    for load in loads:
        load.start()
    line_barrier()
    per_block = BLOCK_ROWS // ROWS
    blocks = hidden.shape[0] // BLOCK_ROWS
    groups = w_gate.shape[1] // UNIT_GROUP
    slots = act.shape[0]
    lag = per_block + (lax.axis_size("head") - 1) * HOP
    pace = per_block // groups

    def block_rows(b):
        return pl.ds(pl.multiple_of(b * BLOCK_ROWS, BLOCK_ROWS), BLOCK_ROWS)

    def unit_copies(u):
        slot = lax.rem(u, slots)
        where = (block_rows(u // groups), unit_cols(u))
        return [
            pltpu.make_async_copy(source.at[slot], target.at[where], out_sem.at[i, slot])
            for i, (source, target) in enumerate(
                ((silu, silu_ref), (slope, slope_ref), (act, act_ref))
            )
        ]

    def unit_cols(u):
        return pl.ds(pl.multiple_of(lax.rem(u, groups) * UNIT_GROUP, UNIT_GROUP), UNIT_GROUP)

    def flip_copy(b):
        return pltpu.make_async_copy(flip, flip_ref.at[:, block_rows(b)], block_sem.at[0])

    def part_copy(b):
        return pltpu.make_async_copy(part_out, part_ref.at[block_rows(b)], block_sem.at[1])

    def forward(u):
        slot = lax.rem(u, slots)
        b, group = u // groups, lax.rem(u, groups)

        @pl.when(group == 0)
        def _():
            @pl.when(b > 0)
            def _():
                flip_copy(b - 1).wait()

            flip[...] = normed[block_rows(b)].T
            flip_copy(b).start()

        @pl.when(u >= slots)
        def _():
            for copy in unit_copies(u - slots):
                copy.wait()

        rows, cols = normed[block_rows(u // groups)], unit_cols(u)
        gate_pre = dot(rows, w_gate[:, cols], NN)
        up_proj = dot(rows, w_up[:, cols], NN)
        gate_sig = jax.nn.sigmoid(gate_pre)
        silu_gate = gate_pre * gate_sig
        silu[slot] = silu_gate
        slope[slot] = up_proj * gate_sig * (1.0 + gate_pre * (1.0 - gate_sig))
        act[slot] = (silu_gate * up_proj).astype(BF16)
        for copy in unit_copies(u):
            copy.start()
        share = dot(act[slot], w_down[cols], NN)

        @pl.when(group == 0)
        def _():
            part[...] = share

        @pl.when(group > 0)
        def _():
            part[...] += share

        @pl.when(group == groups - 1)
        def _():
            @pl.when(b > 0)
            def _():
                part_copy(b - 1).wait()

            part_out[...] = part[...].astype(BF16)
            part_copy(b).start()

    def before(t):
        @pl.when((lax.rem(t, per_block) == 0) & (t < blocks * per_block))
        def _():
            rows = block_rows(t // per_block)
            hidden[rows] = dot(mixed_ref[rows], weight_ref[...], NN)

    def after(t):
        @pl.when(t == lag)
        def _():
            for load in loads:
                load.wait()

        late = t - lag

        @pl.when((late >= 0) & (lax.rem(late, pace) == 0) & (late // pace < blocks * groups))
        def _():
            forward(late // pace)

    def store(b):
        rows = block_rows(b)
        return pltpu.make_async_copy(hidden.at[rows], hidden_ref.at[rows], hidden_sem.at[b])

    def finish(k, total):
        rows = pl.ds(pl.multiple_of(k * ROWS, ROWS), ROWS)
        value = token_ref[rows].astype(F32) + total
        hidden[rows] = value
        normed[rows] = (value * inverse_rms(value) * gain_ref[...]).astype(BF16)

        @pl.when(lax.rem(k, per_block) == per_block - 1)
        def _():
            store(k // per_block).start()

    line_exchange(hidden, finish, before, scratch, after, lag + blocks * per_block)
    for b in range(blocks):
        store(b).wait()
    flip_copy(blocks - 1).wait()
    part_copy(blocks - 1).wait()
    for u in range(blocks * groups - slots, blocks * groups):
        for copy in unit_copies(u):
            copy.wait()


def attn_out_sum(mixed, weight, tokens, gain, w_gate, w_up, w_down, size, cid):
    rows, width = tokens.shape
    units = w_gate.shape[1]
    vmem, any_ = pl.BlockSpec(memory_space=pltpu.VMEM), pl.BlockSpec(memory_space=pltpu.HBM)
    blocks, slots = rows // BLOCK_ROWS, 2
    return pl.pallas_call(
        attn_out_kernel,
        in_specs=[vmem] * 4 + [any_] * 3,
        out_specs=[any_] * 6,
        out_shape=[
            jax.ShapeDtypeStruct((rows, width), F32),
            jax.ShapeDtypeStruct((width, rows), BF16),
            jax.ShapeDtypeStruct((rows, units), F32),
            jax.ShapeDtypeStruct((rows, units), F32),
            jax.ShapeDtypeStruct((rows, units), BF16),
            jax.ShapeDtypeStruct((rows, width), BF16),
        ],
        scratch_shapes=[
            pltpu.VMEM((rows, width), F32),
            pltpu.VMEM((rows, width), BF16),
            pltpu.VMEM((width, units), BF16),
            pltpu.VMEM((width, units), BF16),
            pltpu.VMEM((units, width), BF16),
            pltpu.VMEM((slots, BLOCK_ROWS, UNIT_GROUP), F32),
            pltpu.VMEM((slots, BLOCK_ROWS, UNIT_GROUP), F32),
            pltpu.VMEM((slots, BLOCK_ROWS, UNIT_GROUP), BF16),
            pltpu.VMEM((width, BLOCK_ROWS), BF16),
            pltpu.VMEM((BLOCK_ROWS, width), F32),
            pltpu.VMEM((BLOCK_ROWS, width), BF16),
            pltpu.SemaphoreType.DMA((blocks,)),
            pltpu.SemaphoreType.DMA((3,)),
            pltpu.SemaphoreType.DMA((3, slots)),
            pltpu.SemaphoreType.DMA((2,)),
        ]
        + line_scratch(size, width),
        cost_estimate=pl.CostEstimate(
            flops=2 * rows * width * (mixed.shape[1] + 3 * units),
            bytes_accessed=250 * 2**20,
            transcendentals=rows * units,
        ),
        compiler_params=pltpu.CompilerParams(
            collective_id=cid, has_side_effects=True, vmem_limit_bytes=60 * 2**20
        ),
    )(mixed, weight, tokens, gain.reshape(1, width), w_gate, w_up, w_down)


def mlp_back_kernel(
    tile, seg_bits,
    d_gate_a, d_gate_b, d_up_a, d_up_b, w_gate_hbm, w_up_hbm, hidden_hbm, grad_hbm, gain_ref,
    down_in, gate_in,
    d_out_ref, d_own_ref, gain_part_ref, down_out, gate_out,
    d_gate, d_up, w_gate, w_up, hidden, grad, own, load_sem, store_sem, *scratch
):
    per_block = BLOCK_ROWS // ROWS
    blocks = own.shape[0] // BLOCK_ROWS
    size = lax.axis_size("head")
    place = lax.axis_index("head")
    per_device = own.shape[0] // ROWS // size
    half = d_gate.shape[1] // 2
    low, high = pl.ds(0, half), pl.ds(half, half)
    loads = [
        pltpu.make_async_copy(source, target, load_sem.at[i])
        for i, (source, target) in enumerate(
            ((d_gate_a, d_gate.at[:, low]), (d_gate_b, d_gate.at[:, high]), (w_gate_hbm, w_gate),
             (d_up_a, d_up.at[:, low]), (d_up_b, d_up.at[:, high]), (w_up_hbm, w_up),
             (hidden_hbm, hidden), (grad_hbm, grad))
        )
    ]
    for load in loads:
        load.start()
    gain_part_ref[...] = jnp.zeros_like(gain_part_ref)
    greet_seg(seg_bits)
    line_barrier(seg_bits)
    engine_step, steps = sum_engine(
        [down_in, gate_in], [down_out, gate_out], tile, seg_bits, scratch[LINE_REFS:]
    )

    def block_rows(b):
        return pl.ds(pl.multiple_of(b * BLOCK_ROWS, BLOCK_ROWS), BLOCK_ROWS)

    for load in loads[:6]:
        load.wait()

    def before(t):
        @pl.when((lax.rem(t, per_block) == 0) & (t < blocks * per_block))
        def _():
            rows = block_rows(t // per_block)
            own[rows] = dot(d_gate[rows], w_gate[...], NT) + dot(d_up[rows], w_up[...], NT)

        @pl.when(t == 0)
        def _():
            for load in loads[6:]:
                load.wait()

    def store(b):
        rows = block_rows(b)
        return pltpu.make_async_copy(grad.at[rows], d_out_ref.at[rows], store_sem.at[b])

    def finish(k, total):
        rows = pl.ds(pl.multiple_of(k * ROWS, ROWS), ROWS)
        value = hidden[rows]
        inverse = inverse_rms(value)
        normal = value * inverse
        scaled = gain_ref[...] * total
        mean = jnp.mean(scaled * normal, axis=-1, keepdims=True)
        d_hidden = grad[rows].astype(F32) + inverse * (scaled - normal * mean)
        grad[rows] = d_hidden.astype(BF16)

        @pl.when(k // per_device == place)
        def _():
            mine = pl.ds(pl.multiple_of(lax.rem(k, per_device) * ROWS, ROWS), ROWS)
            d_own_ref[mine] = d_hidden
            gain_part_ref[...] += jnp.sum((total * normal).reshape(ROWS // 8, 8, -1), axis=0)

        @pl.when(lax.rem(k, per_block) == per_block - 1)
        def _():
            store(k // per_block).start()

    line_exchange(own, finish, before, scratch[:LINE_REFS], engine_step, steps)
    for b in range(blocks):
        store(b).wait()


def mlp_back_sum(
    d_gate, d_up, w_gate, w_up, hidden, grad, gain, summed, tile, seg_size, size, cid
):
    rows, width = hidden.shape
    units = w_gate.shape[1]
    seg_bits = bits_of(seg_size)
    vmem, any_ = pl.BlockSpec(memory_space=pltpu.VMEM), pl.BlockSpec(memory_space=pltpu.HBM)
    blocks = rows // BLOCK_ROWS
    return pl.pallas_call(
        functools.partial(mlp_back_kernel, tile, seg_bits),
        in_specs=[any_] * 8 + [vmem, any_, any_],
        out_specs=[any_, vmem, vmem, any_, any_],
        out_shape=[
            jax.ShapeDtypeStruct((rows, width), BF16),
            jax.ShapeDtypeStruct((rows // size, width), F32),
            jax.ShapeDtypeStruct((8, width), F32),
        ]
        + [jax.ShapeDtypeStruct(array.shape, BF16) for array in summed],
        scratch_shapes=[
            pltpu.VMEM((rows, units), BF16),
            pltpu.VMEM((rows, units), BF16),
            pltpu.VMEM((width, units), BF16),
            pltpu.VMEM((width, units), BF16),
            pltpu.VMEM((rows, width), F32),
            pltpu.VMEM((rows, width), BF16),
            pltpu.VMEM((rows, width), F32),
            pltpu.SemaphoreType.DMA((8,)),
            pltpu.SemaphoreType.DMA((blocks,)),
        ]
        + line_scratch(size, width)
        + engine_scratch(tile, seg_bits),
        cost_estimate=pl.CostEstimate(
            flops=4 * rows * width * units, bytes_accessed=250 * 2**20, transcendentals=0
        ),
        compiler_params=pltpu.CompilerParams(
            collective_id=cid, has_side_effects=True, vmem_limit_bytes=62 * 2**20
        ),
    )(*d_gate, *d_up, w_gate, w_up, hidden, grad, gain.reshape(1, width), *summed)


MLP_BLOCK = 512


def mlp_kernel(
    flip_ref, grad_ref, silu_ref, slope_ref, act_ref, w_down_ref,
    d_gate_ref, d_up_ref, grad_gate_ref, grad_up_ref, grad_down_ref,
):
    width = flip_ref.shape[0]
    d_act = dot(grad_ref[...], w_down_ref[...], NT)
    d_gate_ref[...] = (d_act * slope_ref[...]).astype(BF16)
    d_up_ref[...] = (d_act * silu_ref[...]).astype(BF16)
    half = width // 2
    for i in range(2):
        part = slice(i * half, (i + 1) * half)
        grad_gate_ref[part] = dot(flip_ref[part], d_gate_ref[...], NN).astype(BF16)
        grad_up_ref[part] = dot(flip_ref[part], d_up_ref[...], NN).astype(BF16)
        grad_down_ref[:, part] = dot(act_ref[...], grad_ref[:, part], TN).astype(BF16)


def mlp_half(flip, grad, silu, slope, act, w_down, which):
    width, count = flip.shape
    units = act.shape[1] // 2
    block = min(MLP_BLOCK, units)
    first = which * (units // block)
    once = pl.Buffered(1)
    side = pl.BlockSpec((count, block), lambda j: (0, first + j))
    side_out = pl.BlockSpec((count, block), lambda j: (0, j))
    tall = pl.BlockSpec((width, block), lambda j: (0, j))
    return pl.pallas_call(
        mlp_kernel,
        grid=(units // block,),
        in_specs=[
            pl.BlockSpec((width, count), lambda j: (0, 0), pipeline_mode=once),
            pl.BlockSpec((count, width), lambda j: (0, 0), pipeline_mode=once),
            side,
            side,
            side,
            pl.BlockSpec((block, width), lambda j: (first + j, 0)),
        ],
        out_specs=[side_out, side_out, tall, tall, pl.BlockSpec((block, width), lambda j: (j, 0))],
        out_shape=[
            jax.ShapeDtypeStruct((count, units), BF16),
            jax.ShapeDtypeStruct((count, units), BF16),
            jax.ShapeDtypeStruct((width, units), BF16),
            jax.ShapeDtypeStruct((width, units), BF16),
            jax.ShapeDtypeStruct((units, width), BF16),
        ],
        cost_estimate=pl.CostEstimate(
            flops=8 * count * width * units,
            bytes_accessed=2 * (2 * count * width + 4 * width * units + 7 * count * units),
            transcendentals=0,
        ),
        compiler_params=pltpu.CompilerParams(vmem_limit_bytes=56 * 2**20),
    )(flip, grad, silu, slope, act, w_down)


WIDEN_SLOTS = 4


def widen_kernel(shapes, places, wide_count, tile, *refs):
    count = len(shapes)
    sources, targets = refs[:count], refs[count : count + wide_count]
    narrow, wide, load_sem, store_sem = refs[count + wide_count :]
    high, broad = tile
    counts = [(rows // high) * (width // broad) for rows, width in shapes]
    total = sum(counts)

    def pick(k, act):
        first = 0
        for i in range(count):
            @pl.when((k >= first) & (k < first + counts[i]))
            def _(i=i, first=first):
                across = shapes[i][1] // broad
                place = k - first
                row = pl.multiple_of((place // across) * high, high)
                col = pl.multiple_of(lax.rem(place, across) * broad, broad)
                act(i, (pl.ds(row, high), pl.ds(col, broad)))
            first += counts[i]

    def load(k, i, where):
        slot = lax.rem(k, WIDEN_SLOTS)
        return pltpu.make_async_copy(sources[i].at[where], narrow.at[slot], load_sem.at[slot])

    def store(k, i, where):
        slot = lax.rem(k, WIDEN_SLOTS)
        target, row, col = places[i]
        rows = pl.ds(pl.multiple_of(row + where[0].start, high), high)
        cols = pl.ds(pl.multiple_of(col + where[1].start, broad), broad)
        return pltpu.make_async_copy(
            wide.at[slot], targets[target].at[rows, cols], store_sem.at[slot]
        )

    zero = (pl.ds(0, high), pl.ds(0, broad))
    ahead = WIDEN_SLOTS - 1
    for k in range(ahead):
        pick(k, lambda i, where, k=k: load(k, i, where).start())

    def step(k, carry):
        @pl.when(k + ahead < total)
        def _():
            pick(k + ahead, lambda i, where: load(k + ahead, i, where).start())

        @pl.when(k >= WIDEN_SLOTS)
        def _():
            store(k - WIDEN_SLOTS, 0, zero).wait()

        load(k, 0, zero).wait()
        slot = lax.rem(k, WIDEN_SLOTS)
        wide[slot] = narrow[slot].astype(F32)
        pick(k, lambda i, where: store(k, i, where).start())
        return carry

    lax.fori_loop(0, total, step, 0)
    for k in range(total - WIDEN_SLOTS, total):
        store(k, 0, zero).wait()


def widen(groups, tile):
    arrays, places, targets = [], [], []
    for axis, *group in groups:
        shape = [0, 0]
        shape[1 - axis] = group[0].shape[1 - axis]
        for value in group:
            arrays.append(value)
            places.append((len(targets), *((shape[0], 0) if axis == 0 else (0, shape[1]))))
            shape[axis] += value.shape[axis]
        targets.append(tuple(shape))
    shapes = [value.shape for value in arrays]
    any_ = pl.BlockSpec(memory_space=pltpu.HBM)
    return pl.pallas_call(
        functools.partial(widen_kernel, shapes, places, len(targets), tile),
        in_specs=[any_] * len(arrays),
        out_specs=[any_] * len(targets),
        out_shape=[jax.ShapeDtypeStruct(shape, F32) for shape in targets],
        scratch_shapes=[
            pltpu.VMEM((WIDEN_SLOTS, *tile), BF16),
            pltpu.VMEM((WIDEN_SLOTS, *tile), F32),
            pltpu.SemaphoreType.DMA((WIDEN_SLOTS,)),
            pltpu.SemaphoreType.DMA((WIDEN_SLOTS,)),
        ],
        cost_estimate=pl.CostEstimate(
            flops=0, bytes_accessed=6 * sum(r * c for r, c in shapes), transcendentals=0
        ),
        compiler_params=pltpu.CompilerParams(vmem_limit_bytes=60 * 2**20),
    )(*arrays)


def attn_weights_kernel(
    rows_ref, d_out_ref, mixed_ref, d_query_ref, d_key_ref, d_value_ref,
    w_query_ref, w_key_ref, w_value_ref,
    d_rows_ref, grad_query_ref, grad_key_ref, grad_value_ref, grad_out_ref, gain_part_ref,
    flipped_mixed, flipped_rows,
):
    @pl.when(pl.program_id(0) == 0)
    def _():
        flipped_mixed[...] = mixed_ref[...].T

    flipped_rows[...] = rows_ref[...].T
    d_rows = (
        dot(d_query_ref[...], w_query_ref[...], NT)
        + dot(d_key_ref[...], w_key_ref[...], NT)
        + dot(d_value_ref[...], w_value_ref[...], NT)
    )
    d_rows_ref[...] = d_rows.astype(BF16)
    product = d_rows * rows_ref[...].astype(F32)
    gain_part_ref[...] = jnp.sum(product.reshape(-1, 8, product.shape[1]), axis=0)
    grad_query_ref[...] = dot(flipped_rows[...], d_query_ref[...], NN).astype(BF16)
    grad_key_ref[...] = dot(flipped_rows[...], d_key_ref[...], NN).astype(BF16)
    grad_value_ref[...] = dot(flipped_rows[...], d_value_ref[...], NN).astype(BF16)
    grad_out_ref[...] = dot(flipped_mixed[...], d_out_ref[...], NN).astype(BF16)


def attn_weights(rows, d_out, mixed, d_query, d_key, d_value, w_query, w_key, w_value):
    count, width = rows.shape
    cols = mixed.shape[1]
    block = 512
    once = pl.Buffered(1)
    slim = pl.BlockSpec((count, cols), lambda j: (0, 0), pipeline_mode=once)
    side = pl.BlockSpec((count, block), lambda j: (0, j))
    tall = pl.BlockSpec((block, cols), lambda j: (j, 0))
    wide = pl.BlockSpec((cols, block), lambda j: (0, j))
    tall_type = jax.ShapeDtypeStruct((width, cols), BF16)
    return pl.pallas_call(
        attn_weights_kernel,
        grid=(width // block,),
        in_specs=[side, side, slim, slim, slim, slim, tall, tall, tall],
        out_specs=[side, tall, tall, tall, wide, pl.BlockSpec((8, block), lambda j: (0, j))],
        out_shape=[
            jax.ShapeDtypeStruct((count, width), BF16),
            tall_type,
            tall_type,
            tall_type,
            jax.ShapeDtypeStruct((cols, width), BF16),
            jax.ShapeDtypeStruct((8, width), F32),
        ],
        scratch_shapes=[pltpu.VMEM((cols, count), BF16), pltpu.VMEM((block, count), BF16)],
        cost_estimate=pl.CostEstimate(
            flops=14 * count * width * cols,
            bytes_accessed=2 * (3 * count * width + 4 * count * cols + 7 * width * cols),
            transcendentals=0,
        ),
        compiler_params=pltpu.CompilerParams(vmem_limit_bytes=48 * 2**20),
    )(rows, d_out, mixed, d_query, d_key, d_value, w_query, w_key, w_value)


def from_behind(value, axis, steps):
    count = lax.axis_size(axis)
    initial, last = (max(0, -steps), min(count, count - steps))
    return lax.ppermute(value, axis, [(source, source + steps) for source in range(initial, last)])


def elu_plus(values):
    return jnp.where(values > 0, values + 1.0, jnp.exp(jnp.minimum(values, 0.0)))


def elu_slope(values):
    return jnp.where(values > 0, 1.0, jnp.exp(jnp.minimum(values, 0.0)))


def inverse_rms(values):
    return lax.rsqrt(jnp.mean(values * values, axis=-1, keepdims=True) + epsilon)


def norm_backward(values, inverse, gain_vec, grad_out):
    normal = values * inverse
    scaled = gain_vec * grad_out
    grad_in = inverse * (scaled - normal * jnp.mean(scaled * normal, axis=-1, keepdims=True))
    return grad_in


def dot(left, right, dims):
    return lax.dot_general(left, right, (dims, ((), ())), preferred_element_type=F32)


def in_two(values):
    if values.dtype == BF16:
        return (values,)
    top = values.astype(BF16)
    return top, (values - top.astype(F32)).astype(BF16)


def fine_dot(left, right, dims):
    lefts, rights = in_two(left), in_two(right)
    total = dot(lefts[0], rights[0], dims)
    for low in rights[1:]:
        total = total + dot(lefts[0], low, dims)
    for low in lefts[1:]:
        total = total + dot(low, rights[0], dims)
    return total


NN = ((1,), (0,))
NT = ((1,), (1,))
TN = ((0,), (0,))


def valid_column(valid_len):
    return (lax.broadcasted_iota(jnp.int32, (SEG_LEN, 1), 0) < valid_len).astype(F32)


def update_kernel(valid_ref, key_ref, value_ref, out_ref):
    key_feat = elu_plus(key_ref[...].astype(F32)) * valid_column(valid_ref[0])
    out_ref[0, :DH] = fine_dot(key_feat, value_ref[...], TN)
    out_ref[0, DH:] = jnp.broadcast_to(
        jnp.sum(key_feat, axis=0, keepdims=True), (MEM_ROWS - DH, DH)
    )


def block_probs(query_block, key_rows, start, valid_len):
    scores = dot(query_block, key_rows, NT) * (DH**-0.5)
    row_pos = start + lax.broadcasted_iota(jnp.int32, scores.shape, 0)
    col_pos = lax.broadcasted_iota(jnp.int32, scores.shape, 1)
    allowed = (row_pos >= col_pos) & (col_pos < valid_len)
    scores = jnp.where(allowed, scores, masked_score)
    weights = jnp.exp(scores - jnp.max(scores, axis=-1, keepdims=True))
    return weights / jnp.sum(weights, axis=-1, keepdims=True)


def local_kernel(valid_ref, query_ref, key_ref, value_ref, out_ref):
    for start in range(0, SEG_LEN, BLOCK):
        rows = slice(start, start + BLOCK)
        key_rows = key_ref[: start + BLOCK]
        probs = block_probs(query_ref[rows], key_rows, start, valid_ref[0])
        out_ref[rows] = dot(probs.astype(BF16), value_ref[: start + BLOCK], NN)


def retrieve(query_feat, memory, normal):
    numerator = fine_dot(query_feat, memory, NN)
    denominator = jnp.sum(query_feat * normal, axis=-1, keepdims=True) + 1.0
    return numerator / denominator, denominator


def mix_kernel(gate_ref, query_ref, local_ref, memory_ref, out_ref):
    gate = gate_ref[pl.program_id(0)]
    query_feat = elu_plus(query_ref[...].astype(F32))
    retrieved, _ = retrieve(query_feat, memory_ref[0, :DH], memory_ref[0, DH : DH + 1])
    out_ref[...] = (gate * retrieved + (1.0 - gate) * local_ref[...]).astype(BF16)


def greet_sequence():
    seg = lax.axis_index("seg")
    place = lax.rem(seg, SEGS)
    barrier = pltpu.get_barrier_semaphore()
    for distance in range(1, SEGS):
        other = seg - place + lax.rem(place + distance, SEGS)
        pl.semaphore_signal(barrier, inc=1, device_id={"seg": other}, device_id_type=MESH)
    pl.semaphore_wait(barrier, SEGS - 1)


def sequence_copies(source, land, send_sem, recv_sem, sign):
    seg = lax.axis_index("seg")
    count = lax.axis_size("seg")
    place = lax.rem(seg, SEGS)
    copies = []
    for distance in range(1, SEGS):
        copy = pltpu.make_async_remote_copy(
            src_ref=source,
            dst_ref=land.at[distance - 1],
            send_sem=send_sem.at[distance - 1],
            recv_sem=recv_sem.at[distance - 1],
            device_id={"seg": lax.rem(seg + count + sign * distance, count)},
            device_id_type=MESH,
        )
        after, before = place + distance < SEGS, place >= distance
        copies.append((copy, after, before) if sign > 0 else (copy, before, after))
    return copies


def head_cols(head):
    return pl.ds(pl.multiple_of(head * DH, DH), DH)


def attn_back_kernel(
    gate_ref, valid_ref, d_out_ref, weight_ref, query_ref, key_ref, value_ref, local_ref, memory_ref,
    d_query_ref, d_key_ref, d_value_ref, gate_grad_ref,
    d_mixed, feat, d_key_sum, d_value_sum, back, land, update, send_sem, recv_sem,
):
    heads = memory_ref.shape[0]
    valid_len = valid_ref[0]
    greet_sequence()
    copies = sequence_copies(back, land, send_sem, recv_sem, -1)
    d_mixed[...] = dot(d_out_ref[...], weight_ref[...], NT)

    def memory_back(head, carry):
        cols = head_cols(head)
        gate = gate_ref[head]
        query_vals = query_ref[:, cols].astype(F32)
        query_feat = elu_plus(query_vals)
        memory, normal = memory_ref[head, :DH], memory_ref[head, DH : DH + 1]
        retrieved, denominator = retrieve(query_feat, memory, normal)
        d_head = d_mixed[:, cols]
        gate_grad_ref[head] = jnp.broadcast_to(
            jnp.sum(d_head * (retrieved - local_ref[:, cols]), axis=0, keepdims=True), (8, DH)
        )
        d_retrieved = gate * d_head
        d_numerator = d_retrieved / denominator
        d_denominator = -jnp.sum(d_retrieved * retrieved, axis=-1, keepdims=True) / denominator
        d_feat = fine_dot(d_numerator, memory, NT) + d_denominator * normal
        feat[:, cols] = d_feat * elu_slope(query_vals)
        back[head, :DH] = fine_dot(query_feat, d_numerator, TN).astype(BF16)
        d_normal = jnp.sum(d_denominator * query_feat, axis=0, keepdims=True)
        back[head, DH:] = jnp.broadcast_to(d_normal, (MEM_ROWS - DH, DH)).astype(BF16)
        return carry

    lax.fori_loop(0, heads, memory_back, 0)
    for copy, sends, _ in copies:

        @pl.when(sends)
        def _(copy=copy):
            copy.start()

    d_key_sum[...] = jnp.zeros_like(d_key_sum)
    d_value_sum[...] = jnp.zeros_like(d_value_sum)

    def local_back(head, carry):
        cols = head_cols(head)
        keep = 1.0 - gate_ref[head]
        for start in range(0, SEG_LEN, BLOCK):
            rows, seen = slice(start, start + BLOCK), slice(0, start + BLOCK)
            query_block = query_ref[rows, cols]
            probs = block_probs(query_block, key_ref[seen, cols], start, valid_len)
            d_local = (keep * d_mixed[rows, cols]).astype(BF16)
            d_probs = dot(d_local, value_ref[seen, cols], NT)
            row_dot = jnp.sum(probs * d_probs, axis=-1, keepdims=True)
            d_scores = (probs * (d_probs - row_dot) * (DH**-0.5)).astype(BF16)
            d_query = dot(d_scores, key_ref[seen, cols], NN) + feat[rows, cols]
            d_query_ref[rows, cols] = d_query.astype(BF16)
            d_key_sum[seen, cols] += dot(d_scores, query_block, TN)
            d_value_sum[seen, cols] += dot(probs.astype(BF16), d_local, TN)
        return carry

    lax.fori_loop(0, heads, local_back, 0)
    update[...] = jnp.zeros_like(update)
    for distance, (copy, sends, gets) in enumerate(copies):

        @pl.when(sends)
        def _(copy=copy):
            copy.wait_send()

        @pl.when(gets)
        def _(copy=copy, distance=distance):
            copy.wait_recv()
            update[...] += land[distance].astype(F32)

    def finish_back(head, carry):
        cols = head_cols(head)
        valid = valid_column(valid_len)
        key_vals = key_ref[:, cols].astype(F32)
        memory, normal = update[head, :DH], update[head, DH : DH + 1]
        d_feat = (fine_dot(value_ref[:, cols], memory, NT) + normal) * valid
        d_key_ref[:, cols] = (d_key_sum[:, cols] + d_feat * elu_slope(key_vals)).astype(BF16)
        key_feat = elu_plus(key_vals) * valid
        d_value = d_value_sum[:, cols] + fine_dot(key_feat, memory, NN)
        d_value_ref[:, cols] = d_value.astype(BF16)
        return carry

    lax.fori_loop(0, heads, finish_back, 0)


def attn_back(gate, valid, d_out, weight, query, key, value, local, memory, cid):
    rows, cols = query.shape
    heads = cols // DH
    scalar, vmem = pl.BlockSpec(memory_space=pltpu.SMEM), pl.BlockSpec(memory_space=pltpu.VMEM)
    wide = pltpu.VMEM((rows, cols), F32)
    narrow = jax.ShapeDtypeStruct((rows, cols), BF16)
    return pl.pallas_call(
        attn_back_kernel,
        in_specs=[scalar] * 2 + [vmem] * 7,
        out_specs=[vmem] * 4,
        out_shape=[narrow, narrow, narrow, jax.ShapeDtypeStruct((heads, 8, DH), F32)],
        scratch_shapes=[
            wide,
            wide,
            wide,
            wide,
            pltpu.VMEM((heads, MEM_ROWS, DH), BF16),
            pltpu.VMEM((SEGS - 1, heads, MEM_ROWS, DH), BF16),
            pltpu.VMEM((heads, MEM_ROWS, DH), F32),
            pltpu.SemaphoreType.DMA((SEGS - 1,)),
            pltpu.SemaphoreType.DMA((SEGS - 1,)),
        ],
        cost_estimate=pl.CostEstimate(
            flops=10 * rows * rows * cols + 2 * rows * cols * d_out.shape[1],
            bytes_accessed=100 * 2**20,
            transcendentals=rows * rows * heads,
        ),
        compiler_params=pltpu.CompilerParams(
            collective_id=cid, has_side_effects=True, vmem_limit_bytes=48 * 2**20
        ),
    )(gate, valid, d_out, weight, query, key, value, local, memory)


SCALAR = pl.BlockSpec(memory_space=pltpu.SMEM)
COLUMN = pl.BlockSpec((SEG_LEN, DH), lambda head: (0, head))
MEMORY = pl.BlockSpec((1, MEM_ROWS, DH), lambda head: (head, 0, 0))


def per_head(kernel, heads, in_specs, out_specs, out_types, flops, transcendentals=0):
    moved = heads * SEG_LEN * DH * 4 * len(in_specs)
    return pl.pallas_call(
        kernel,
        grid=(heads,),
        in_specs=in_specs,
        out_specs=out_specs,
        out_shape=out_types,
        cost_estimate=pl.CostEstimate(
            flops=flops, bytes_accessed=moved, transcendentals=transcendentals
        ),
        compiler_params=pltpu.CompilerParams(vmem_limit_bytes=40 * 1024 * 1024),
    )


def per_device(
    tokens,
    cotangent,
    gain_attn,
    gain_mlp,
    w_query,
    w_key,
    w_value,
    w_out,
    w_gate,
    w_up,
    w_down,
    mem_gate,
    lengths,
):
    seg_index = lax.axis_index("seg")
    head_index = lax.axis_index("head")
    head_groups = lax.axis_size("head")
    seg_size = lax.axis_size("seg")
    position = seg_index % SEGS
    sequence = seg_index // SEGS
    seq_length = jnp.sum(jnp.where(lax.iota(jnp.int32, lengths.shape[0]) == sequence, lengths, 0))
    valid_len = jnp.where(position == SEGS - 1, seq_length, SEG_LEN).reshape(1)
    heads = mem_gate.shape[0]
    cols = heads * DH
    col_f32 = jax.ShapeDtypeStruct((SEG_LEN, cols), F32)
    col_bf16 = jax.ShapeDtypeStruct((SEG_LEN, cols), BF16)
    mem_f32 = jax.ShapeDtypeStruct((heads, MEM_ROWS, DH), F32)
    unit = 2 * heads * SEG_LEN * DH * DH
    pairs = heads * SEG_LEN * SEG_LEN

    token_vals = tokens.astype(F32)
    gathered_tokens, gathered_attn, query_rows, key_rows, value_rows = gather_project(
        tokens, gain_attn, w_query, w_key, w_value, head_groups, 4
    )
    cotangent, key_rows = lax.optimization_barrier((cotangent, key_rows))
    gathered_grad = lax.all_gather(cotangent, "head", axis=0, tiled=True)
    update = per_head(update_kernel, heads, [SCALAR, COLUMN, COLUMN], MEMORY, mem_f32, 6 * unit)(
        valid_len, key_rows, value_rows
    )
    memory_prev = jnp.zeros_like(update)
    for distance in range(1, SEGS):
        moved = from_behind(update, "seg", distance)
        memory_prev = memory_prev + jnp.where(position >= distance, moved, 0.0)
    local_attn = per_head(
        local_kernel, heads, [SCALAR, COLUMN, COLUMN, COLUMN], COLUMN, col_f32, 4 * pairs * DH, pairs
    )(valid_len, query_rows, key_rows, value_rows)
    after = memory_prev + update
    memory_after = (after[:, :DH] * SEG_LEN ** (-0.5))[None]
    normal_after = (after[:, DH] / SEG_LEN)[None]
    mix_sig = jax.nn.sigmoid(mem_gate)
    mixed_attn = per_head(
        mix_kernel, heads, [SCALAR, COLUMN, COLUMN, MEMORY], COLUMN, col_bf16, 6 * unit
    )(mix_sig, query_rows, local_attn, memory_prev)
    all_hidden, flip_mlp, silu, slope, act, mlp_part = attn_out_sum(
        mixed_attn, w_out, gathered_tokens, gain_mlp, w_gate, w_up, w_down, head_groups, 1
    )
    own_rows = tokens.shape[0]
    hidden_res = lax.dynamic_slice_in_dim(all_hidden, head_index * own_rows, own_rows, 0)
    d_gate_a, d_up_a, gate_a, up_a, down_a = mlp_half(
        flip_mlp, gathered_grad, silu, slope, act, w_down, 0
    )
    gate_a, up_a, down_a = lax.psum((gate_a, up_a, down_a), "seg")
    d_gate_b, d_up_b, gate_b, up_b, down_b = mlp_half(
        flip_mlp, gathered_grad, silu, slope, act, w_down, 1
    )
    gathered_hidden, d_hidden, gain_mlp_rows, down_b, gate_b = mlp_back_sum(
        (d_gate_a, d_gate_b),
        (d_up_a, d_up_b),
        w_gate,
        w_up,
        all_hidden,
        gathered_grad,
        gain_mlp,
        (down_b, gate_b),
        (BLOCK, cols),
        seg_size,
        head_groups,
        2,
    )
    mlp_part, gathered_hidden = lax.optimization_barrier((mlp_part, gathered_hidden))
    mlp_out = lax.psum_scatter(mlp_part, "head", scatter_dimension=0, tiled=True)
    output = (hidden_res + mlp_out.astype(F32)).astype(BF16)
    d_queries, d_keys, d_values, gate_cols = attn_back(
        mix_sig,
        valid_len,
        gathered_hidden,
        w_out,
        query_rows,
        key_rows,
        value_rows,
        local_attn,
        memory_prev,
        3,
    )
    d_part, grad_query, grad_key, grad_value, grad_out, gain_attn_rows = attn_weights(
        gathered_attn,
        gathered_hidden,
        mixed_attn,
        d_queries,
        d_keys,
        d_values,
        w_query,
        w_key,
        w_value,
    )
    d_normed_attn = lax.psum_scatter(d_part, "head", scatter_dimension=0, tiled=True).astype(F32)
    grad_in_attn = norm_backward(token_vals, inverse_rms(token_vals), gain_attn, d_normed_attn)
    grad_tokens = (d_hidden + grad_in_attn).astype(BF16)
    gate_part = mix_sig * (1.0 - mix_sig) * jnp.sum(gate_cols[:, 0], axis=-1)
    slots = jnp.where(
        (lax.iota(jnp.int32, head_groups) == head_index)[:, None], gate_part[None], 0.0
    )
    width = gain_attn.shape[0]
    gain_attn_part = jnp.sum(gain_attn_rows, axis=0) / gain_attn
    gain_mlp_part = jnp.sum(gain_mlp_rows, axis=0)
    parts = jnp.concatenate([gain_attn_part, gain_mlp_part, slots.reshape(-1)])
    lines = -(-parts.shape[0] // (8 * DH)) * 8
    parts = jnp.pad(parts, (0, lines * DH - parts.shape[0])).reshape(lines, DH)
    small, *late = grad_sum(
        parts,
        [up_b, grad_out, grad_query, grad_key, grad_value],
        (cols, cols),
        seg_size,
        head_groups,
        0,
    )
    small = small.reshape(-1)
    grad_mem_gate = lax.dynamic_slice(small, (2 * width + head_index * heads,), (heads,))
    grads = widen(
        [(1, gate_a, gate_b), (1, up_a, late[0]), (0, down_a, down_b)]
        + [(0, grad) for grad in late[1:]],
        (cols, cols),
    )
    return (
        output,
        grad_tokens,
        memory_after,
        normal_after,
        small[:width],
        small[width : 2 * width],
        grads[4],
        grads[5],
        grads[6],
        grads[3],
        grads[0],
        grads[1],
        grads[2],
        grad_mem_gate,
    )


def solution(mesh):
    return jax.shard_map(
        per_device,
        mesh=mesh,
        in_specs=(
            P(("seg", "head"), None),
            P(("seg", "head"), None),
            P(),
            P(),
            P(None, "head"),
            P(None, "head"),
            P(None, "head"),
            P("head", None),
            P(None, "head"),
            P(None, "head"),
            P("head", None),
            P("head"),
            P(),
        ),
        out_specs=(
            P(("seg", "head"), None),
            P(("seg", "head"), None),
            P("seg", "head", None, None),
            P("seg", "head", None),
            P(),
            P(),
            P(None, "head"),
            P(None, "head"),
            P(None, "head"),
            P("head", None),
            P(None, "head"),
            P(None, "head"),
            P("head", None),
            P("head"),
        ),
        check_vma=False,
    )
```

```python
import functools

import jax
import jax.numpy as jnp
from jax import lax
from jax.experimental import pallas as pl
from jax.experimental.pallas import tpu as pltpu
from jax.sharding import PartitionSpec as P

DH = 128
SEG_LEN = 1024
SEGS = 4
MEM_ROWS = DH + 16
BLOCK = 256

epsilon = 1e-05
masked_score = -1e30
F32 = jnp.float32
BF16 = jnp.bfloat16


MESH = pl.DeviceIdType.MESH
LAND_SLOTS = 12
RESULT_SLOTS = 16
SUM_SEMS = 8
SUM_HOP = 3


def bits_of(size):
    return size.bit_length() - 1


def flip(index, power):
    return index + power - 2 * power * lax.rem(index // power, 2)


def sum_engine(arrays, outs, tile, seg_bits, scratch):
    mine, result, send_sem, recv_sem, load_sem, store_sem, *lands = scratch
    seg = lax.axis_index("seg")
    planes = seg_bits - 1
    high, wide = tile
    shapes = [array.shape for array in arrays]
    counts = [(rows // high) * (cols // wide) for rows, cols in shapes]
    starts = [sum(counts[:i]) for i in range(len(counts))]
    total = sum(counts)

    def power(k, level):
        if level == 0:
            return 1
        which = lax.rem(k + level - 1, planes)
        value = 2
        for bit in range(1, planes):
            value = jnp.where(which == bit, 2 << bit, value)
        return value

    def my_bit(k, level):
        return lax.rem(seg // power(k, level), 2)

    def part(k, level, own):
        half = high >> (level + 1)
        bit = my_bit(k, level) if own else 1 - my_bit(k, level)
        return pl.ds(pl.multiple_of(bit * half, half), half)

    def kept(k, levels):
        first = 0
        for level in range(levels):
            first = first + my_bit(k, level) * (high >> (level + 1))
        return pl.ds(pl.multiple_of(first, high >> levels), high >> levels)

    def pick(k, act):
        for i in range(len(arrays)):

            @pl.when((k >= starts[i]) & (k < starts[i] + counts[i]))
            def _(i=i):
                across = shapes[i][1] // wide
                place = k - starts[i]
                row = pl.multiple_of((place // across) * high, high)
                col = pl.multiple_of(lax.rem(place, across) * wide, wide)
                act(i, row, col)

    def halving(k, level, source):
        return pltpu.make_async_remote_copy(
            src_ref=source,
            dst_ref=lands[level].at[lax.rem(k, LAND_SLOTS)],
            send_sem=send_sem.at[level, lax.rem(k, SUM_SEMS)],
            recv_sem=recv_sem.at[level, lax.rem(k, SUM_SEMS)],
            device_id={"seg": flip(seg, power(k, level))},
            device_id_type=MESH,
        )

    def first_source(k, i, row, col, own):
        half = high // 2
        bit = my_bit(k, 0) if own else 1 - my_bit(k, 0)
        return arrays[i].at[pl.ds(pl.multiple_of(row + bit * half, half), half), pl.ds(col, wide)]

    def keep(k, i, row, col):
        slot = lax.rem(k, 4)
        return pltpu.make_async_copy(
            first_source(k, i, row, col, True), mine.at[slot], load_sem.at[slot]
        )

    def level_source(k, level):
        return lands[level - 1].at[lax.rem(k, LAND_SLOTS), part(k, level, False)]

    def doubling(k, level):
        ref = result.at[lax.rem(k, RESULT_SLOTS), kept(k, level + 1)]
        return pltpu.make_async_remote_copy(
            src_ref=ref,
            dst_ref=ref,
            send_sem=send_sem.at[seg_bits + level, lax.rem(k, SUM_SEMS)],
            recv_sem=recv_sem.at[seg_bits + level, lax.rem(k, SUM_SEMS)],
            device_id={"seg": flip(seg, power(k, level))},
            device_id_type=MESH,
        )

    def store(k, i, row, col):
        slot = lax.rem(k, 4)
        return pltpu.make_async_copy(
            result.at[lax.rem(k, RESULT_SLOTS)],
            outs[i].at[pl.ds(row, high), pl.ds(col, wide)],
            store_sem.at[slot],
        )

    def do_first(k):
        def go(i, row, col):
            halving(k, 0, first_source(k, i, row, col, False)).start()
            keep(k, i, row, col).start()

        pick(k, go)

    def arrived(k, level):
        slot = lax.rem(k, LAND_SLOTS)
        if level == 0:
            halving(k, 0, first_source(k, 0, 0, 0, False)).wait()
            keep(k, 0, 0, 0).wait()
            other = mine[lax.rem(k, 4)]
        else:
            halving(k, level, level_source(k, level)).wait()
            other = lands[level - 1][slot, part(k, level, True)]
        return (lands[level][slot].astype(F32) + other.astype(F32)).astype(BF16)

    def do_level(k, level):
        lands[level - 1][lax.rem(k, LAND_SLOTS)] = arrived(k, level - 1)
        halving(k, level, level_source(k, level)).start()

    def do_total(k):
        result[lax.rem(k, RESULT_SLOTS), kept(k, seg_bits)] = arrived(k, seg_bits - 1)
        doubling(k, seg_bits - 1).start()

    def do_spread(k, level):
        doubling(k, level + 1).wait()
        doubling(k, level).start()

    def do_finish(k):
        doubling(k, 0).wait()
        pick(k, lambda i, row, col: store(k, i, row, col).start())

    def do_store(k):
        store(k, 0, 0, 0).wait()

    stages = [(0, do_first), (1, functools.partial(do_level, level=1))]
    when = 1
    for level in range(2, seg_bits):
        when += SUM_HOP
        stages.append((when, functools.partial(do_level, level=level)))
    when += SUM_HOP
    stages.append((when, do_total))
    for level in range(seg_bits - 2, -1, -1):
        when += SUM_HOP
        stages.append((when, functools.partial(do_spread, level=level)))
    stages.append((when + 1, do_finish))
    stages.append((when + 3, do_store))

    def step(t):
        for delay, act in reversed(stages):
            k = t - delay

            @pl.when((k >= 0) & (k < total))
            def _(act=act, k=k):
                act(k)

    return step, total + when + 3


def engine_scratch(tile, seg_bits):
    high, wide = tile
    return [
        pltpu.VMEM((4, high // 2, wide), BF16),
        pltpu.VMEM((RESULT_SLOTS, high, wide), BF16),
        pltpu.SemaphoreType.DMA((2 * seg_bits, SUM_SEMS)),
        pltpu.SemaphoreType.DMA((2 * seg_bits, SUM_SEMS)),
        pltpu.SemaphoreType.DMA((4,)),
        pltpu.SemaphoreType.DMA((4,)),
    ] + [pltpu.VMEM((LAND_SLOTS, high >> (l + 1), wide), BF16) for l in range(seg_bits)]


def greet_seg(seg_bits):
    barrier = pltpu.get_barrier_semaphore()
    seg = lax.axis_index("seg")
    for bit in range(seg_bits):
        pl.semaphore_signal(
            barrier, inc=1, device_id={"seg": flip(seg, 1 << bit)}, device_id_type=MESH
        )


def grad_sum_kernel(count, tile, seg_bits, head_bits, *refs):
    small_in, arrays = refs[0], refs[1 : 1 + count]
    small_out, outs = refs[1 + count], refs[2 + count : 2 + 2 * count]
    small_buf, small_land, small_send, small_recv, *scratch = refs[2 + 2 * count :]
    seg, head = lax.axis_index("seg"), lax.axis_index("head")
    greet_seg(seg_bits)
    barrier = pltpu.get_barrier_semaphore()
    for bit in range(head_bits):
        pl.semaphore_signal(
            barrier, inc=1, device_id={"head": flip(head, 1 << bit)}, device_id_type=MESH
        )
    pl.semaphore_wait(barrier, seg_bits + head_bits)
    rounds = seg_bits + head_bits

    def small_copy(j):
        if j < seg_bits:
            where = {"seg": flip(seg, 1 << j)}
        else:
            where = {"head": flip(head, 1 << (j - seg_bits))}
        return pltpu.make_async_remote_copy(
            src_ref=small_buf.at[j],
            dst_ref=small_land.at[j],
            send_sem=small_send.at[j],
            recv_sem=small_recv.at[j],
            device_id=where,
            device_id_type=MESH,
        )

    engine_step, steps = sum_engine(arrays, outs, tile, seg_bits, scratch)

    def step(t, carry):
        engine_step(t)
        for j in range(rounds + 1):

            @pl.when(t == 3 * j)
            def _(j=j):
                if j == 0:
                    small_buf[0] = small_in[...]
                else:
                    small_copy(j - 1).wait()
                    value = small_buf[j - 1] + small_land[j - 1]
                    if j < rounds:
                        small_buf[j] = value
                    else:
                        small_out[...] = value
                if j < rounds:
                    small_copy(j).start()

        return carry

    lax.fori_loop(0, max(steps, 3 * rounds + 1), step, 0)


def grad_sum(small, arrays, tile, seg_size, head_size, cid):
    seg_bits, head_bits = bits_of(seg_size), bits_of(head_size)
    rounds = seg_bits + head_bits
    count = len(arrays)
    moved = sum(rows * cols for rows, cols in (array.shape for array in arrays))
    any_, vmem = pl.BlockSpec(memory_space=pltpu.HBM), pl.BlockSpec(memory_space=pltpu.VMEM)
    return pl.pallas_call(
        functools.partial(grad_sum_kernel, count, tile, seg_bits, head_bits),
        in_specs=[vmem] + [any_] * count,
        out_specs=[vmem] + [any_] * count,
        out_shape=[jax.ShapeDtypeStruct(small.shape, F32)]
        + [jax.ShapeDtypeStruct(array.shape, BF16) for array in arrays],
        scratch_shapes=[
            pltpu.VMEM((rounds, *small.shape), F32),
            pltpu.VMEM((rounds, *small.shape), F32),
            pltpu.SemaphoreType.DMA((rounds,)),
            pltpu.SemaphoreType.DMA((rounds,)),
        ]
        + engine_scratch(tile, seg_bits),
        cost_estimate=pl.CostEstimate(flops=0, bytes_accessed=moved * 60, transcendentals=0),
        compiler_params=pltpu.CompilerParams(
            collective_id=cid, has_side_effects=True, vmem_limit_bytes=60 * 2**20
        ),
    )(small, *arrays)


ROWS = 32
FIRST_HOP = 2
SECOND_HOP = 3
SEND_SLOTS = 4
BLOCK_ROWS = 256
UNIT_GROUP = 512
LINE_REFS = 8


def line_exchange(own, finish, before, scratch, hop, extra, extra_steps):
    up_land, down_land, up_send, down_send, up_recv_sem, down_recv_sem, up_send_sem, down_send_sem = scratch
    size = lax.axis_size("head")
    place = lax.axis_index("head")
    slots = up_land.shape[0]
    chunks = own.shape[0] // ROWS
    last = size - 1

    def up_copy(k):
        return pltpu.make_async_remote_copy(
            src_ref=up_send.at[lax.rem(k, SEND_SLOTS)],
            dst_ref=up_land.at[lax.rem(k, slots)],
            send_sem=up_send_sem.at[lax.rem(k, SEND_SLOTS)],
            recv_sem=up_recv_sem.at[lax.rem(k, slots)],
            device_id={"head": lax.rem(place + 1, size)},
            device_id_type=MESH,
        )

    def down_copy(k):
        return pltpu.make_async_remote_copy(
            src_ref=down_send.at[lax.rem(k, SEND_SLOTS)],
            dst_ref=down_land.at[lax.rem(k, slots)],
            send_sem=down_send_sem.at[lax.rem(k, SEND_SLOTS)],
            recv_sem=down_recv_sem.at[lax.rem(k, slots)],
            device_id={"head": lax.rem(place + last, size)},
            device_id_type=MESH,
        )

    def rows_of(k):
        return pl.ds(pl.multiple_of(k * ROWS, ROWS), ROWS)

    def pass_on(k, copy, land, send, has_source, has_target):
        @pl.when(has_source)
        def _():
            copy(k).wait_recv()

        @pl.when(has_target)
        def _():
            slot = lax.rem(k, SEND_SLOTS)

            @pl.when(k >= SEND_SLOTS)
            def _():
                copy(k - SEND_SLOTS).wait_send()

            @pl.when(has_source)
            def _():
                send[slot] = (own[rows_of(k)] + land[lax.rem(k, slots)].astype(F32)).astype(BF16)

            @pl.when(jnp.logical_not(has_source))
            def _():
                send[slot] = own[rows_of(k)].astype(BF16)

            copy(k).start()

    far = jnp.maximum(place, last - place)

    def step(t, carry):
        before(t)
        down = t - (last - place) * hop

        @pl.when((down >= 0) & (down < chunks))
        def _():
            pass_on(down, down_copy, down_land, down_send, place < last, place > 0)

        up = t - place * hop

        @pl.when((up >= 0) & (up < chunks))
        def _():
            pass_on(up, up_copy, up_land, up_send, place > 0, place < last)

        k = t - far * hop

        @pl.when((k >= 0) & (k < chunks))
        def _():
            slot = lax.rem(k, slots)

            @pl.when(place == 0)
            def _():
                finish(k, own[rows_of(k)] + down_land[slot].astype(F32))

            @pl.when(place == last)
            def _():
                finish(k, own[rows_of(k)] + up_land[slot].astype(F32))

            @pl.when((place > 0) & (place < last))
            def _():
                finish(
                    k,
                    own[rows_of(k)] + up_land[slot].astype(F32) + down_land[slot].astype(F32),
                )

        extra(t)
        return carry

    lax.fori_loop(0, max(chunks + last * hop, extra_steps), step, 0)
    for k in range(chunks - SEND_SLOTS, chunks):

        @pl.when(place < last)
        def _(k=k):
            up_copy(k).wait_send()

        @pl.when(place > 0)
        def _(k=k):
            down_copy(k).wait_send()


def line_barrier(others=0):
    size = lax.axis_size("head")
    place = lax.axis_index("head")
    barrier = pltpu.get_barrier_semaphore()
    inner = (place > 0) & (place < size - 1)

    def greet(near):
        pl.semaphore_signal(
            barrier, inc=1, device_id={"head": lax.rem(near, size)}, device_id_type=MESH
        )

    @pl.when(place > 0)
    def _():
        greet(place + size - 1)

    @pl.when(place < size - 1)
    def _():
        greet(place + 1)

    @pl.when(inner)
    def _():
        pl.semaphore_wait(barrier, 2 + others)

    @pl.when(jnp.logical_not(inner))
    def _():
        pl.semaphore_wait(barrier, 1 + others)


def line_scratch(size, width, hop):
    slots = (size - 1) * hop + 2
    return [
        pltpu.VMEM((slots, ROWS, width), BF16),
        pltpu.VMEM((slots, ROWS, width), BF16),
        pltpu.VMEM((SEND_SLOTS, ROWS, width), BF16),
        pltpu.VMEM((SEND_SLOTS, ROWS, width), BF16),
        pltpu.SemaphoreType.DMA((slots,)),
        pltpu.SemaphoreType.DMA((slots,)),
        pltpu.SemaphoreType.DMA((SEND_SLOTS,)),
        pltpu.SemaphoreType.DMA((SEND_SLOTS,)),
    ]


GATHER_PARTS = 4


def gather_kernel(
    token_hbm, gain_ref, w_query_hbm, w_key_hbm, w_value_hbm,
    all_ref, normed_ref, query_ref, key_ref, value_ref,
    land, normed, w_query, w_key, w_value,
    own_sem, load_sem, all_sem, normed_sem, up_send, up_recv, down_send, down_recv,
):
    size = lax.axis_size("head")
    place = lax.axis_index("head")
    last = size - 1
    own_rows = token_hbm.shape[0]
    chunk = own_rows // GATHER_PARTS
    loads = [
        pltpu.make_async_copy(source, target, load_sem.at[i])
        for i, (source, target) in enumerate(
            ((w_key_hbm, w_key), (w_value_hbm, w_value), (w_query_hbm, w_query))
        )
    ]

    def shard_rows(shard):
        return pl.ds(pl.multiple_of(shard * own_rows, own_rows), own_rows)

    own = pltpu.make_async_copy(token_hbm, land.at[shard_rows(place)], own_sem)
    own.start()
    for load in loads:
        load.start()
    line_barrier()

    def chunk_copy(shard, i, send_sem, recv_sem, target):
        first = pl.multiple_of(shard * own_rows + lax.rem(i, GATHER_PARTS) * chunk, chunk)
        ref = land.at[pl.ds(first, chunk)]
        return pltpu.make_async_remote_copy(
            src_ref=ref,
            dst_ref=ref,
            send_sem=send_sem.at[i],
            recv_sem=recv_sem.at[i],
            device_id={"head": target},
            device_id_type=MESH,
        )

    above, below = lax.rem(place + 1, size), lax.rem(place + last, size)

    def up_copy(i, first_shard):
        return chunk_copy(first_shard - i // GATHER_PARTS, i, up_send, up_recv, above)

    def down_copy(i, first_shard):
        return chunk_copy(first_shard + i // GATHER_PARTS, i, down_send, down_recv, below)

    own.wait()
    for i in range(GATHER_PARTS):

        @pl.when(place < last)
        def _(i=i):
            up_copy(i, place).start()

        @pl.when(place > 0)
        def _(i=i):
            down_copy(i, place).start()

    def stores(shard):
        rows = shard_rows(shard)
        return (
            pltpu.make_async_copy(land.at[rows], all_ref.at[rows], all_sem.at[shard]),
            pltpu.make_async_copy(normed.at[rows], normed_ref.at[rows], normed_sem.at[shard]),
        )

    def project(shard):
        rows = shard_rows(shard)
        value = land[rows].astype(F32)
        normed[rows] = (value * inverse_rms(value) * gain_ref[...]).astype(BF16)
        for copy in stores(shard):
            copy.start()
        for weight, target in ((w_key, key_ref), (w_value, value_ref), (w_query, query_ref)):
            target[rows] = dot(normed[rows], weight[...], NN).astype(BF16)

    for load in loads:
        load.wait()
    project(place)

    def step(i, carry):
        @pl.when(i < place * GATHER_PARTS)
        def _():
            up_copy(i, place - 1).wait_recv()

            @pl.when(place < last)
            def _():
                up_copy(i + GATHER_PARTS, place).start()

        @pl.when(i < (last - place) * GATHER_PARTS)
        def _():
            down_copy(i, place + 1).wait_recv()

            @pl.when(place > 0)
            def _():
                down_copy(i + GATHER_PARTS, place).start()

        distance = (i + 1) // GATHER_PARTS
        whole = lax.rem(i + 1, GATHER_PARTS) == 0

        @pl.when(whole & (place >= distance))
        def _():
            project(place - distance)

        @pl.when(whole & (place + distance <= last))
        def _():
            project(place + distance)

        return carry

    lax.fori_loop(0, last * GATHER_PARTS, step, 0)

    def drain(i, carry):
        @pl.when((place < last) & (i < (place + 1) * GATHER_PARTS))
        def _():
            up_copy(i, place).wait_send()

        @pl.when((place > 0) & (i < (size - place) * GATHER_PARTS))
        def _():
            down_copy(i, place).wait_send()

        return carry

    lax.fori_loop(0, size * GATHER_PARTS, drain, 0)
    for shard in range(size):
        for copy in stores(shard):
            copy.wait()


def gather_project(tokens, gain, w_query, w_key, w_value, size, cid):
    own_rows, width = tokens.shape
    rows, cols = own_rows * size, w_query.shape[1]
    vmem, any_ = pl.BlockSpec(memory_space=pltpu.VMEM), pl.BlockSpec(memory_space=pltpu.HBM)
    weight = pltpu.VMEM((width, cols), BF16)
    hops = pltpu.SemaphoreType.DMA((size * GATHER_PARTS,))
    return pl.pallas_call(
        gather_kernel,
        in_specs=[any_, vmem] + [any_] * 3,
        out_specs=[any_, any_, vmem, vmem, vmem],
        out_shape=[jax.ShapeDtypeStruct((rows, width), BF16)] * 2
        + [jax.ShapeDtypeStruct((rows, cols), BF16)] * 3,
        scratch_shapes=[
            pltpu.VMEM((rows, width), BF16),
            pltpu.VMEM((rows, width), BF16),
            weight,
            weight,
            weight,
            pltpu.SemaphoreType.DMA(()),
            pltpu.SemaphoreType.DMA((3,)),
            pltpu.SemaphoreType.DMA((size,)),
            pltpu.SemaphoreType.DMA((size,)),
            hops,
            hops,
            hops,
            hops,
        ],
        cost_estimate=pl.CostEstimate(
            flops=6 * rows * width * cols, bytes_accessed=150 * 2**20, transcendentals=0
        ),
        compiler_params=pltpu.CompilerParams(
            collective_id=cid, has_side_effects=True, vmem_limit_bytes=48 * 2**20
        ),
    )(tokens, gain.reshape(1, width), w_query, w_key, w_value)


def attn_out_kernel(
    mixed_ref, weight_ref, token_ref, gain_ref, w_gate_hbm, w_up_hbm, w_down_hbm,
    hidden_ref, flip_ref, silu_ref, slope_ref, act_ref, part_ref,
    hidden, normed, w_gate, w_up, w_down, silu, slope, act, flip, part, part_out,
    hidden_sem, load_sem, out_sem, block_sem, *scratch
):
    loads = [
        pltpu.make_async_copy(source, target, load_sem.at[i])
        for i, (source, target) in enumerate(
            ((w_gate_hbm, w_gate), (w_up_hbm, w_up), (w_down_hbm, w_down))
        )
    ]
    for load in loads:
        load.start()
    line_barrier()
    per_block = BLOCK_ROWS // ROWS
    blocks = hidden.shape[0] // BLOCK_ROWS
    groups = w_gate.shape[1] // UNIT_GROUP
    slots = act.shape[0]
    lag = per_block + (lax.axis_size("head") - 1) * FIRST_HOP
    pace = per_block // groups

    def block_rows(b):
        return pl.ds(pl.multiple_of(b * BLOCK_ROWS, BLOCK_ROWS), BLOCK_ROWS)

    def unit_copies(u):
        slot = lax.rem(u, slots)
        where = (block_rows(u // groups), unit_cols(u))
        return [
            pltpu.make_async_copy(source.at[slot], target.at[where], out_sem.at[i, slot])
            for i, (source, target) in enumerate(
                ((silu, silu_ref), (slope, slope_ref), (act, act_ref))
            )
        ]

    def unit_cols(u):
        return pl.ds(pl.multiple_of(lax.rem(u, groups) * UNIT_GROUP, UNIT_GROUP), UNIT_GROUP)

    def flip_copy(b):
        return pltpu.make_async_copy(flip, flip_ref.at[:, block_rows(b)], block_sem.at[0])

    def part_copy(b):
        where = (block_rows(b), pl.ds(0, part_out.shape[1]))
        return pltpu.make_async_copy(part_out, part_ref.at[where], block_sem.at[1])

    def forward(u):
        slot = lax.rem(u, slots)
        b, group = u // groups, lax.rem(u, groups)

        @pl.when(group == 0)
        def _():
            @pl.when(b > 0)
            def _():
                flip_copy(b - 1).wait()

            flip[...] = normed[block_rows(b)].T
            flip_copy(b).start()

        @pl.when(u >= slots)
        def _():
            for copy in unit_copies(u - slots):
                copy.wait()

        rows, cols = normed[block_rows(u // groups)], unit_cols(u)
        gate_pre = dot(rows, w_gate[:, cols], NN)
        up_proj = dot(rows, w_up[:, cols], NN)
        gate_sig = jax.nn.sigmoid(gate_pre)
        silu_gate = gate_pre * gate_sig
        silu[slot] = silu_gate
        slope[slot] = up_proj * gate_sig * (1.0 + gate_pre * (1.0 - gate_sig))
        act[slot] = (silu_gate * up_proj).astype(BF16)
        for copy in unit_copies(u):
            copy.start()
        share = dot(act[slot], w_down[cols], NN)

        @pl.when(group == 0)
        def _():
            part[...] = share

        @pl.when(group > 0)
        def _():
            part[...] += share

        @pl.when(group == groups - 1)
        def _():
            @pl.when(b > 0)
            def _():
                part_copy(b - 1).wait()

            part_out[...] = part[...].astype(BF16)
            part_copy(b).start()

    def before(t):
        @pl.when((lax.rem(t, per_block) == 0) & (t < blocks * per_block))
        def _():
            rows = block_rows(t // per_block)
            hidden[rows] = dot(mixed_ref[rows], weight_ref[...], NN)

    def after(t):
        @pl.when(t == lag)
        def _():
            for load in loads:
                load.wait()

        late = t - lag

        @pl.when((late >= 0) & (lax.rem(late, pace) == 0) & (late // pace < blocks * groups))
        def _():
            forward(late // pace)

    def store(b):
        rows = block_rows(b)
        return pltpu.make_async_copy(hidden.at[rows], hidden_ref.at[rows], hidden_sem.at[b])

    def finish(k, total):
        rows = pl.ds(pl.multiple_of(k * ROWS, ROWS), ROWS)
        value = token_ref[rows].astype(F32) + total
        hidden[rows] = value
        normed[rows] = (value * inverse_rms(value) * gain_ref[...]).astype(BF16)

        @pl.when(lax.rem(k, per_block) == per_block - 1)
        def _():
            store(k // per_block).start()

    line_exchange(hidden, finish, before, scratch, FIRST_HOP, after, lag + blocks * per_block)
    for b in range(blocks):
        store(b).wait()
    flip_copy(blocks - 1).wait()
    part_copy(blocks - 1).wait()
    for u in range(blocks * groups - slots, blocks * groups):
        for copy in unit_copies(u):
            copy.wait()


def attn_out_sum(mixed, weight, tokens, gain, w_gate, w_up, w_down, size, cid):
    rows, width = tokens.shape
    units = w_gate.shape[1]
    vmem, any_ = pl.BlockSpec(memory_space=pltpu.VMEM), pl.BlockSpec(memory_space=pltpu.HBM)
    blocks, slots = rows // BLOCK_ROWS, 2
    return pl.pallas_call(
        attn_out_kernel,
        in_specs=[vmem] * 4 + [any_] * 3,
        out_specs=[any_] * 6,
        out_shape=[
            jax.ShapeDtypeStruct((rows, width), F32),
            jax.ShapeDtypeStruct((width, rows), BF16),
            jax.ShapeDtypeStruct((rows, units), F32),
            jax.ShapeDtypeStruct((rows, units), F32),
            jax.ShapeDtypeStruct((rows, units), BF16),
            jax.ShapeDtypeStruct((rows, 2 * width), BF16),
        ],
        scratch_shapes=[
            pltpu.VMEM((rows, width), F32),
            pltpu.VMEM((rows, width), BF16),
            pltpu.VMEM((width, units), BF16),
            pltpu.VMEM((width, units), BF16),
            pltpu.VMEM((units, width), BF16),
            pltpu.VMEM((slots, BLOCK_ROWS, UNIT_GROUP), F32),
            pltpu.VMEM((slots, BLOCK_ROWS, UNIT_GROUP), F32),
            pltpu.VMEM((slots, BLOCK_ROWS, UNIT_GROUP), BF16),
            pltpu.VMEM((width, BLOCK_ROWS), BF16),
            pltpu.VMEM((BLOCK_ROWS, width), F32),
            pltpu.VMEM((BLOCK_ROWS, width), BF16),
            pltpu.SemaphoreType.DMA((blocks,)),
            pltpu.SemaphoreType.DMA((3,)),
            pltpu.SemaphoreType.DMA((3, slots)),
            pltpu.SemaphoreType.DMA((2,)),
        ]
        + line_scratch(size, width, FIRST_HOP),
        cost_estimate=pl.CostEstimate(
            flops=2 * rows * width * (mixed.shape[1] + 3 * units),
            bytes_accessed=250 * 2**20,
            transcendentals=rows * units,
        ),
        compiler_params=pltpu.CompilerParams(
            collective_id=cid, has_side_effects=True, vmem_limit_bytes=60 * 2**20
        ),
    )(mixed, weight, tokens, gain.reshape(1, width), w_gate, w_up, w_down)


def mlp_back_kernel(
    tile, seg_bits,
    d_gate_a, d_gate_b, d_up_a, d_up_b, w_gate_hbm, w_up_hbm, hidden_hbm, grad_hbm, gain_ref,
    down_in, gate_in,
    d_out_ref, d_own_ref, gain_part_ref, down_out, gate_out,
    d_gate, d_up, w_gate, w_up, hidden, grad, own, load_sem, store_sem, *scratch
):
    per_block = BLOCK_ROWS // ROWS
    blocks = own.shape[0] // BLOCK_ROWS
    size = lax.axis_size("head")
    place = lax.axis_index("head")
    per_device = own.shape[0] // ROWS // size
    half = d_gate.shape[1] // 2
    low, high = pl.ds(0, half), pl.ds(half, half)
    loads = [
        pltpu.make_async_copy(source, target, load_sem.at[i])
        for i, (source, target) in enumerate(
            ((d_gate_a, d_gate.at[:, low]), (d_gate_b, d_gate.at[:, high]), (w_gate_hbm, w_gate),
             (d_up_a, d_up.at[:, low]), (d_up_b, d_up.at[:, high]), (w_up_hbm, w_up),
             (hidden_hbm, hidden), (grad_hbm, grad))
        )
    ]
    for load in loads:
        load.start()
    gain_part_ref[...] = jnp.zeros_like(gain_part_ref)
    greet_seg(seg_bits)
    line_barrier(seg_bits)
    engine_step, steps = sum_engine(
        [down_in, gate_in], [down_out, gate_out], tile, seg_bits, scratch[LINE_REFS:]
    )

    def block_rows(b):
        return pl.ds(pl.multiple_of(b * BLOCK_ROWS, BLOCK_ROWS), BLOCK_ROWS)

    for load in loads[:6]:
        load.wait()

    def before(t):
        @pl.when((lax.rem(t, per_block) == 0) & (t < blocks * per_block))
        def _():
            rows = block_rows(t // per_block)
            own[rows] = dot(d_gate[rows], w_gate[...], NT) + dot(d_up[rows], w_up[...], NT)

        @pl.when(t == 0)
        def _():
            for load in loads[6:]:
                load.wait()

    def store(b):
        rows = block_rows(b)
        return pltpu.make_async_copy(grad.at[rows], d_out_ref.at[rows], store_sem.at[b])

    def finish(k, total):
        rows = pl.ds(pl.multiple_of(k * ROWS, ROWS), ROWS)
        value = hidden[rows]
        inverse = inverse_rms(value)
        normal = value * inverse
        scaled = gain_ref[...] * total
        mean = jnp.mean(scaled * normal, axis=-1, keepdims=True)
        d_hidden = grad[rows].astype(F32) + inverse * (scaled - normal * mean)
        grad[rows] = d_hidden.astype(BF16)

        @pl.when(k // per_device == place)
        def _():
            mine = pl.ds(pl.multiple_of(lax.rem(k, per_device) * ROWS, ROWS), ROWS)
            d_own_ref[mine] = d_hidden
            gain_part_ref[...] += jnp.sum((total * normal).reshape(ROWS // 8, 8, -1), axis=0)

        @pl.when(lax.rem(k, per_block) == per_block - 1)
        def _():
            store(k // per_block).start()

    line_exchange(own, finish, before, scratch[:LINE_REFS], SECOND_HOP, engine_step, steps)
    for b in range(blocks):
        store(b).wait()


def mlp_back_sum(
    d_gate, d_up, w_gate, w_up, hidden, grad, gain, summed, tile, seg_size, size, cid
):
    rows, width = hidden.shape
    units = w_gate.shape[1]
    seg_bits = bits_of(seg_size)
    vmem, any_ = pl.BlockSpec(memory_space=pltpu.VMEM), pl.BlockSpec(memory_space=pltpu.HBM)
    blocks = rows // BLOCK_ROWS
    return pl.pallas_call(
        functools.partial(mlp_back_kernel, tile, seg_bits),
        in_specs=[any_] * 8 + [vmem, any_, any_],
        out_specs=[any_, vmem, vmem, any_, any_],
        out_shape=[
            jax.ShapeDtypeStruct((rows, width), BF16),
            jax.ShapeDtypeStruct((rows // size, width), F32),
            jax.ShapeDtypeStruct((8, width), F32),
        ]
        + [jax.ShapeDtypeStruct(array.shape, BF16) for array in summed],
        scratch_shapes=[
            pltpu.VMEM((rows, units), BF16),
            pltpu.VMEM((rows, units), BF16),
            pltpu.VMEM((width, units), BF16),
            pltpu.VMEM((width, units), BF16),
            pltpu.VMEM((rows, width), F32),
            pltpu.VMEM((rows, width), BF16),
            pltpu.VMEM((rows, width), F32),
            pltpu.SemaphoreType.DMA((8,)),
            pltpu.SemaphoreType.DMA((blocks,)),
        ]
        + line_scratch(size, width, SECOND_HOP)
        + engine_scratch(tile, seg_bits),
        cost_estimate=pl.CostEstimate(
            flops=4 * rows * width * units, bytes_accessed=250 * 2**20, transcendentals=0
        ),
        compiler_params=pltpu.CompilerParams(
            collective_id=cid, has_side_effects=True, vmem_limit_bytes=62 * 2**20
        ),
    )(*d_gate, *d_up, w_gate, w_up, hidden, grad, gain.reshape(1, width), *summed)


MLP_BLOCK = 512


def mlp_kernel(
    flip_ref, grad_ref, silu_ref, slope_ref, act_ref, w_down_ref,
    d_gate_ref, d_up_ref, grad_gate_ref, grad_up_ref, grad_down_ref,
):
    width = flip_ref.shape[0]
    d_act = dot(grad_ref[...], w_down_ref[...], NT)
    d_gate_ref[...] = (d_act * slope_ref[...]).astype(BF16)
    d_up_ref[...] = (d_act * silu_ref[...]).astype(BF16)
    half = width // 2
    for i in range(2):
        part = slice(i * half, (i + 1) * half)
        grad_gate_ref[part] = dot(flip_ref[part], d_gate_ref[...], NN).astype(BF16)
        grad_up_ref[part] = dot(flip_ref[part], d_up_ref[...], NN).astype(BF16)
        grad_down_ref[:, part] = dot(act_ref[...], grad_ref[:, part], TN).astype(BF16)


def mlp_half(flip, grad, silu, slope, act, w_down, which):
    width, count = flip.shape
    units = act.shape[1] // 2
    block = min(MLP_BLOCK, units)
    first = which * (units // block)
    once = pl.Buffered(1)
    side = pl.BlockSpec((count, block), lambda j: (0, first + j))
    side_out = pl.BlockSpec((count, block), lambda j: (0, j))
    tall = pl.BlockSpec((width, block), lambda j: (0, j))
    return pl.pallas_call(
        mlp_kernel,
        grid=(units // block,),
        in_specs=[
            pl.BlockSpec((width, count), lambda j: (0, 0), pipeline_mode=once),
            pl.BlockSpec((count, width), lambda j: (0, 0), pipeline_mode=once),
            side,
            side,
            side,
            pl.BlockSpec((block, width), lambda j: (first + j, 0)),
        ],
        out_specs=[side_out, side_out, tall, tall, pl.BlockSpec((block, width), lambda j: (j, 0))],
        out_shape=[
            jax.ShapeDtypeStruct((count, units), BF16),
            jax.ShapeDtypeStruct((count, units), BF16),
            jax.ShapeDtypeStruct((width, units), BF16),
            jax.ShapeDtypeStruct((width, units), BF16),
            jax.ShapeDtypeStruct((units, width), BF16),
        ],
        cost_estimate=pl.CostEstimate(
            flops=8 * count * width * units,
            bytes_accessed=2 * (2 * count * width + 4 * width * units + 7 * count * units),
            transcendentals=0,
        ),
        compiler_params=pltpu.CompilerParams(vmem_limit_bytes=56 * 2**20),
    )(flip, grad, silu, slope, act, w_down)


WIDEN_SLOTS = 4


def widen_kernel(shapes, places, wide_count, tile, *refs):
    count = len(shapes)
    sources, targets = refs[:count], refs[count : count + wide_count]
    narrow, wide, load_sem, store_sem = refs[count + wide_count :]
    high, broad = tile
    counts = [(rows // high) * (width // broad) for rows, width in shapes]
    total = sum(counts)

    def pick(k, act):
        first = 0
        for i in range(count):
            @pl.when((k >= first) & (k < first + counts[i]))
            def _(i=i, first=first):
                across = shapes[i][1] // broad
                place = k - first
                row = pl.multiple_of((place // across) * high, high)
                col = pl.multiple_of(lax.rem(place, across) * broad, broad)
                act(i, (pl.ds(row, high), pl.ds(col, broad)))
            first += counts[i]

    def load(k, i, where):
        slot = lax.rem(k, WIDEN_SLOTS)
        return pltpu.make_async_copy(sources[i].at[where], narrow.at[slot], load_sem.at[slot])

    def store(k, i, where):
        slot = lax.rem(k, WIDEN_SLOTS)
        target, row, col = places[i]
        rows = pl.ds(pl.multiple_of(row + where[0].start, high), high)
        cols = pl.ds(pl.multiple_of(col + where[1].start, broad), broad)
        return pltpu.make_async_copy(
            wide.at[slot], targets[target].at[rows, cols], store_sem.at[slot]
        )

    zero = (pl.ds(0, high), pl.ds(0, broad))
    ahead = WIDEN_SLOTS - 1
    for k in range(ahead):
        pick(k, lambda i, where, k=k: load(k, i, where).start())

    def step(k, carry):
        @pl.when(k + ahead < total)
        def _():
            pick(k + ahead, lambda i, where: load(k + ahead, i, where).start())

        @pl.when(k >= WIDEN_SLOTS)
        def _():
            store(k - WIDEN_SLOTS, 0, zero).wait()

        load(k, 0, zero).wait()
        slot = lax.rem(k, WIDEN_SLOTS)
        wide[slot] = narrow[slot].astype(F32)
        pick(k, lambda i, where: store(k, i, where).start())
        return carry

    lax.fori_loop(0, total, step, 0)
    for k in range(total - WIDEN_SLOTS, total):
        store(k, 0, zero).wait()


def widen(groups, tile):
    arrays, places, targets = [], [], []
    for axis, *group in groups:
        shape = [0, 0]
        shape[1 - axis] = group[0].shape[1 - axis]
        for value in group:
            arrays.append(value)
            places.append((len(targets), *((shape[0], 0) if axis == 0 else (0, shape[1]))))
            shape[axis] += value.shape[axis]
        targets.append(tuple(shape))
    shapes = [value.shape for value in arrays]
    any_ = pl.BlockSpec(memory_space=pltpu.HBM)
    return pl.pallas_call(
        functools.partial(widen_kernel, shapes, places, len(targets), tile),
        in_specs=[any_] * len(arrays),
        out_specs=[any_] * len(targets),
        out_shape=[jax.ShapeDtypeStruct(shape, F32) for shape in targets],
        scratch_shapes=[
            pltpu.VMEM((WIDEN_SLOTS, *tile), BF16),
            pltpu.VMEM((WIDEN_SLOTS, *tile), F32),
            pltpu.SemaphoreType.DMA((WIDEN_SLOTS,)),
            pltpu.SemaphoreType.DMA((WIDEN_SLOTS,)),
        ],
        cost_estimate=pl.CostEstimate(
            flops=0, bytes_accessed=6 * sum(r * c for r, c in shapes), transcendentals=0
        ),
        compiler_params=pltpu.CompilerParams(vmem_limit_bytes=60 * 2**20),
    )(*arrays)


def attn_weights_kernel(
    rows_ref, d_out_ref, mixed_ref, d_query_ref, d_key_ref, d_value_ref,
    w_query_ref, w_key_ref, w_value_ref, pair_ref,
    d_rows_ref, grad_query_ref, grad_key_ref, grad_value_ref, grad_out_ref, gain_part_ref,
    flipped_mixed, flipped_rows,
):
    @pl.when(pl.program_id(0) == 0)
    def _():
        flipped_mixed[...] = mixed_ref[...].T

    flipped_rows[...] = rows_ref[...].T
    d_rows = (
        dot(d_query_ref[...], w_query_ref[...], NT)
        + dot(d_key_ref[...], w_key_ref[...], NT)
        + dot(d_value_ref[...], w_value_ref[...], NT)
    )
    d_rows_ref[...] = d_rows.astype(BF16)
    product = d_rows * rows_ref[...].astype(F32)
    gain_part_ref[...] = jnp.sum(product.reshape(-1, 8, product.shape[1]), axis=0)
    grad_query_ref[...] = dot(flipped_rows[...], d_query_ref[...], NN).astype(BF16)
    grad_key_ref[...] = dot(flipped_rows[...], d_key_ref[...], NN).astype(BF16)
    grad_value_ref[...] = dot(flipped_rows[...], d_value_ref[...], NN).astype(BF16)
    grad_out_ref[...] = dot(flipped_mixed[...], d_out_ref[...], NN).astype(BF16)


def attn_weights(rows, d_out, mixed, d_query, d_key, d_value, w_query, w_key, w_value, pair):
    count, width = rows.shape
    cols = mixed.shape[1]
    block = 512
    once = pl.Buffered(1)
    slim = pl.BlockSpec((count, cols), lambda j: (0, 0), pipeline_mode=once)
    side = pl.BlockSpec((count, block), lambda j: (0, j))
    right = pl.BlockSpec((count, block), lambda j: (0, width // block + j))
    tall = pl.BlockSpec((block, cols), lambda j: (j, 0))
    wide = pl.BlockSpec((cols, block), lambda j: (0, j))
    tall_type = jax.ShapeDtypeStruct((width, cols), BF16)
    return pl.pallas_call(
        attn_weights_kernel,
        grid=(width // block,),
        in_specs=[side, side, slim, slim, slim, slim, tall, tall, tall]
        + [pl.BlockSpec(memory_space=pltpu.HBM)],
        out_specs=[right, tall, tall, tall, wide, pl.BlockSpec((8, block), lambda j: (0, j))],
        out_shape=[
            jax.ShapeDtypeStruct(pair.shape, BF16),
            tall_type,
            tall_type,
            tall_type,
            jax.ShapeDtypeStruct((cols, width), BF16),
            jax.ShapeDtypeStruct((8, width), F32),
        ],
        input_output_aliases={9: 0},
        scratch_shapes=[pltpu.VMEM((cols, count), BF16), pltpu.VMEM((block, count), BF16)],
        cost_estimate=pl.CostEstimate(
            flops=14 * count * width * cols,
            bytes_accessed=2 * (3 * count * width + 4 * count * cols + 7 * width * cols),
            transcendentals=0,
        ),
        compiler_params=pltpu.CompilerParams(vmem_limit_bytes=48 * 2**20),
    )(rows, d_out, mixed, d_query, d_key, d_value, w_query, w_key, w_value, pair)


def elu_plus(values):
    return jnp.where(values > 0, values + 1.0, jnp.exp(jnp.minimum(values, 0.0)))


def elu_slope(values):
    return jnp.where(values > 0, 1.0, jnp.exp(jnp.minimum(values, 0.0)))


def inverse_rms(values):
    return lax.rsqrt(jnp.mean(values * values, axis=-1, keepdims=True) + epsilon)


def norm_backward(values, inverse, gain_vec, grad_out):
    normal = values * inverse
    scaled = gain_vec * grad_out
    grad_in = inverse * (scaled - normal * jnp.mean(scaled * normal, axis=-1, keepdims=True))
    return grad_in


def dot(left, right, dims):
    return lax.dot_general(left, right, (dims, ((), ())), preferred_element_type=F32)


def in_two(values):
    if values.dtype == BF16:
        return (values,)
    top = values.astype(BF16)
    return top, (values - top.astype(F32)).astype(BF16)


def fine_dot(left, right, dims):
    lefts, rights = in_two(left), in_two(right)
    total = dot(lefts[0], rights[0], dims)
    for low in rights[1:]:
        total = total + dot(lefts[0], low, dims)
    for low in lefts[1:]:
        total = total + dot(low, rights[0], dims)
    return total


NN = ((1,), (0,))
NT = ((1,), (1,))
TN = ((0,), (0,))


def valid_column(valid_len):
    return (lax.broadcasted_iota(jnp.int32, (SEG_LEN, 1), 0) < valid_len).astype(F32)


def block_probs(query_block, key_rows, start, valid_len):
    scores = dot(query_block, key_rows, NT) * (DH**-0.5)
    row_pos = start + lax.broadcasted_iota(jnp.int32, scores.shape, 0)
    col_pos = lax.broadcasted_iota(jnp.int32, scores.shape, 1)
    allowed = (row_pos >= col_pos) & (col_pos < valid_len)
    scores = jnp.where(allowed, scores, masked_score)
    weights = jnp.exp(scores - jnp.max(scores, axis=-1, keepdims=True))
    return weights / jnp.sum(weights, axis=-1, keepdims=True)


def retrieve(query_feat, memory, normal):
    numerator = fine_dot(query_feat, memory, NN)
    denominator = jnp.sum(query_feat * normal, axis=-1, keepdims=True) + 1.0
    return numerator / denominator, denominator


def greet_sequence():
    seg = lax.axis_index("seg")
    place = lax.rem(seg, SEGS)
    barrier = pltpu.get_barrier_semaphore()
    for distance in range(1, SEGS):
        other = seg - place + lax.rem(place + distance, SEGS)
        pl.semaphore_signal(barrier, inc=1, device_id={"seg": other}, device_id_type=MESH)
    pl.semaphore_wait(barrier, SEGS - 1)


def sequence_copies(source, land, send_sem, recv_sem, sign):
    seg = lax.axis_index("seg")
    count = lax.axis_size("seg")
    place = lax.rem(seg, SEGS)
    copies = []
    for distance in range(1, SEGS):
        copy = pltpu.make_async_remote_copy(
            src_ref=source,
            dst_ref=land.at[distance - 1],
            send_sem=send_sem.at[distance - 1],
            recv_sem=recv_sem.at[distance - 1],
            device_id={"seg": lax.rem(seg + count + sign * distance, count)},
            device_id_type=MESH,
        )
        after, before = place + distance < SEGS, place >= distance
        copies.append((copy, after, before) if sign > 0 else (copy, before, after))
    return copies


def head_cols(head):
    return pl.ds(pl.multiple_of(head * DH, DH), DH)


def attn_front_kernel(
    gate_ref, valid_ref, query_ref, key_ref, value_ref,
    mixed_ref, local_ref, before_ref, update_ref,
    land, send_sem, recv_sem,
):
    heads = update_ref.shape[0]
    valid_len = valid_ref[0]
    greet_sequence()
    copies = sequence_copies(update_ref, land, send_sem, recv_sem, 1)

    def make_update(head, carry):
        cols = head_cols(head)
        key_feat = elu_plus(key_ref[:, cols].astype(F32)) * valid_column(valid_len)
        update_ref[head, :DH] = fine_dot(key_feat, value_ref[:, cols], TN)
        normal = jnp.sum(key_feat, axis=0, keepdims=True)
        update_ref[head, DH:] = jnp.broadcast_to(normal, (MEM_ROWS - DH, DH))
        return carry

    lax.fori_loop(0, heads, make_update, 0)
    for copy, sends, _ in copies:

        @pl.when(sends)
        def _(copy=copy):
            copy.start()

    def local(head, carry):
        cols = head_cols(head)
        for start in range(0, SEG_LEN, BLOCK):
            rows, seen = slice(start, start + BLOCK), slice(0, start + BLOCK)
            probs = block_probs(query_ref[rows, cols], key_ref[seen, cols], start, valid_len)
            local_ref[rows, cols] = dot(probs.astype(BF16), value_ref[seen, cols], NN)
        return carry

    lax.fori_loop(0, heads, local, 0)
    before_ref[...] = jnp.zeros_like(before_ref)
    for distance, (copy, sends, gets) in enumerate(copies):

        @pl.when(sends)
        def _(copy=copy):
            copy.wait_send()

        @pl.when(gets)
        def _(copy=copy, distance=distance):
            copy.wait_recv()
            before_ref[...] += land[distance]

    def mix(head, carry):
        cols = head_cols(head)
        gate = gate_ref[head]
        query_feat = elu_plus(query_ref[:, cols].astype(F32))
        memory, normal = before_ref[head, :DH], before_ref[head, DH : DH + 1]
        retrieved, _ = retrieve(query_feat, memory, normal)
        mixed_ref[:, cols] = (gate * retrieved + (1.0 - gate) * local_ref[:, cols]).astype(BF16)
        return carry

    lax.fori_loop(0, heads, mix, 0)


def attn_front(gate, valid, query, key, value, cid):
    rows, cols = query.shape
    heads = cols // DH
    scalar, vmem = pl.BlockSpec(memory_space=pltpu.SMEM), pl.BlockSpec(memory_space=pltpu.VMEM)
    memory = jax.ShapeDtypeStruct((heads, MEM_ROWS, DH), F32)
    return pl.pallas_call(
        attn_front_kernel,
        in_specs=[scalar] * 2 + [vmem] * 3,
        out_specs=[vmem] * 4,
        out_shape=[
            jax.ShapeDtypeStruct((rows, cols), BF16),
            jax.ShapeDtypeStruct((rows, cols), F32),
            memory,
            memory,
        ],
        scratch_shapes=[
            pltpu.VMEM((SEGS - 1, heads, MEM_ROWS, DH), F32),
            pltpu.SemaphoreType.DMA((SEGS - 1,)),
            pltpu.SemaphoreType.DMA((SEGS - 1,)),
        ],
        cost_estimate=pl.CostEstimate(
            flops=4 * rows * rows * cols, bytes_accessed=60 * 2**20, transcendentals=rows * rows * heads
        ),
        compiler_params=pltpu.CompilerParams(
            collective_id=cid, has_side_effects=True, vmem_limit_bytes=40 * 2**20
        ),
    )(gate, valid, query, key, value)


def attn_back_kernel(
    gate_ref, valid_ref, d_out_ref, weight_ref, query_ref, key_ref, value_ref, local_ref, memory_ref,
    d_query_ref, d_key_ref, d_value_ref, gate_grad_ref,
    d_mixed, feat, d_key_sum, d_value_sum, back, land, update, send_sem, recv_sem,
):
    heads = memory_ref.shape[0]
    valid_len = valid_ref[0]
    greet_sequence()
    copies = sequence_copies(back, land, send_sem, recv_sem, -1)
    d_mixed[...] = dot(d_out_ref[...], weight_ref[...], NT)

    def memory_back(head, carry):
        cols = head_cols(head)
        gate = gate_ref[head]
        query_vals = query_ref[:, cols].astype(F32)
        query_feat = elu_plus(query_vals)
        memory, normal = memory_ref[head, :DH], memory_ref[head, DH : DH + 1]
        retrieved, denominator = retrieve(query_feat, memory, normal)
        d_head = d_mixed[:, cols]
        gate_grad_ref[head] = jnp.broadcast_to(
            jnp.sum(d_head * (retrieved - local_ref[:, cols]), axis=0, keepdims=True), (8, DH)
        )
        d_retrieved = gate * d_head
        d_numerator = d_retrieved / denominator
        d_denominator = -jnp.sum(d_retrieved * retrieved, axis=-1, keepdims=True) / denominator
        d_feat = fine_dot(d_numerator, memory, NT) + d_denominator * normal
        feat[:, cols] = d_feat * elu_slope(query_vals)
        back[head, :DH] = fine_dot(query_feat, d_numerator, TN).astype(BF16)
        d_normal = jnp.sum(d_denominator * query_feat, axis=0, keepdims=True)
        back[head, DH:] = jnp.broadcast_to(d_normal, (MEM_ROWS - DH, DH)).astype(BF16)
        return carry

    lax.fori_loop(0, heads, memory_back, 0)
    for copy, sends, _ in copies:

        @pl.when(sends)
        def _(copy=copy):
            copy.start()

    d_key_sum[...] = jnp.zeros_like(d_key_sum)
    d_value_sum[...] = jnp.zeros_like(d_value_sum)

    def local_back(head, carry):
        cols = head_cols(head)
        keep = 1.0 - gate_ref[head]
        for start in range(0, SEG_LEN, BLOCK):
            rows, seen = slice(start, start + BLOCK), slice(0, start + BLOCK)
            query_block = query_ref[rows, cols]
            probs = block_probs(query_block, key_ref[seen, cols], start, valid_len)
            d_local = (keep * d_mixed[rows, cols]).astype(BF16)
            d_probs = dot(d_local, value_ref[seen, cols], NT)
            row_dot = jnp.sum(probs * d_probs, axis=-1, keepdims=True)
            d_scores = (probs * (d_probs - row_dot) * (DH**-0.5)).astype(BF16)
            d_query = dot(d_scores, key_ref[seen, cols], NN) + feat[rows, cols]
            d_query_ref[rows, cols] = d_query.astype(BF16)
            d_key_sum[seen, cols] += dot(d_scores, query_block, TN)
            d_value_sum[seen, cols] += dot(probs.astype(BF16), d_local, TN)
        return carry

    lax.fori_loop(0, heads, local_back, 0)
    update[...] = jnp.zeros_like(update)
    for distance, (copy, sends, gets) in enumerate(copies):

        @pl.when(sends)
        def _(copy=copy):
            copy.wait_send()

        @pl.when(gets)
        def _(copy=copy, distance=distance):
            copy.wait_recv()
            update[...] += land[distance].astype(F32)

    def finish_back(head, carry):
        cols = head_cols(head)
        valid = valid_column(valid_len)
        key_vals = key_ref[:, cols].astype(F32)
        memory, normal = update[head, :DH], update[head, DH : DH + 1]
        d_feat = (fine_dot(value_ref[:, cols], memory, NT) + normal) * valid
        d_key_ref[:, cols] = (d_key_sum[:, cols] + d_feat * elu_slope(key_vals)).astype(BF16)
        key_feat = elu_plus(key_vals) * valid
        d_value = d_value_sum[:, cols] + fine_dot(key_feat, memory, NN)
        d_value_ref[:, cols] = d_value.astype(BF16)
        return carry

    lax.fori_loop(0, heads, finish_back, 0)


def attn_back(gate, valid, d_out, weight, query, key, value, local, memory, cid):
    rows, cols = query.shape
    heads = cols // DH
    scalar, vmem = pl.BlockSpec(memory_space=pltpu.SMEM), pl.BlockSpec(memory_space=pltpu.VMEM)
    wide = pltpu.VMEM((rows, cols), F32)
    narrow = jax.ShapeDtypeStruct((rows, cols), BF16)
    return pl.pallas_call(
        attn_back_kernel,
        in_specs=[scalar] * 2 + [vmem] * 7,
        out_specs=[vmem] * 4,
        out_shape=[narrow, narrow, narrow, jax.ShapeDtypeStruct((heads, 8, DH), F32)],
        scratch_shapes=[
            wide,
            wide,
            wide,
            wide,
            pltpu.VMEM((heads, MEM_ROWS, DH), BF16),
            pltpu.VMEM((SEGS - 1, heads, MEM_ROWS, DH), BF16),
            pltpu.VMEM((heads, MEM_ROWS, DH), F32),
            pltpu.SemaphoreType.DMA((SEGS - 1,)),
            pltpu.SemaphoreType.DMA((SEGS - 1,)),
        ],
        cost_estimate=pl.CostEstimate(
            flops=10 * rows * rows * cols + 2 * rows * cols * d_out.shape[1],
            bytes_accessed=100 * 2**20,
            transcendentals=rows * rows * heads,
        ),
        compiler_params=pltpu.CompilerParams(
            collective_id=cid, has_side_effects=True, vmem_limit_bytes=48 * 2**20
        ),
    )(gate, valid, d_out, weight, query, key, value, local, memory)


def per_device(
    tokens,
    cotangent,
    gain_attn,
    gain_mlp,
    w_query,
    w_key,
    w_value,
    w_out,
    w_gate,
    w_up,
    w_down,
    mem_gate,
    lengths,
):
    seg_index = lax.axis_index("seg")
    head_index = lax.axis_index("head")
    head_groups = lax.axis_size("head")
    seg_size = lax.axis_size("seg")
    position = seg_index % SEGS
    sequence = seg_index // SEGS
    seq_length = jnp.sum(jnp.where(lax.iota(jnp.int32, lengths.shape[0]) == sequence, lengths, 0))
    valid_len = jnp.where(position == SEGS - 1, seq_length, SEG_LEN).reshape(1)
    heads = mem_gate.shape[0]
    cols = heads * DH

    token_vals = tokens.astype(F32)
    gathered_tokens, gathered_attn, query_rows, key_rows, value_rows = gather_project(
        tokens, gain_attn, w_query, w_key, w_value, head_groups, 4
    )
    cotangent, key_rows = lax.optimization_barrier((cotangent, key_rows))
    gathered_grad = lax.all_gather(cotangent, "head", axis=0, tiled=True)
    mix_sig = jax.nn.sigmoid(mem_gate)
    mixed_attn, local_attn, memory_prev, update = attn_front(
        mix_sig, valid_len, query_rows, key_rows, value_rows, 5
    )
    after = memory_prev + update
    memory_after = (after[:, :DH] * SEG_LEN ** (-0.5))[None]
    normal_after = (after[:, DH] / SEG_LEN)[None]
    all_hidden, flip_mlp, silu, slope, act, pair = attn_out_sum(
        mixed_attn, w_out, gathered_tokens, gain_mlp, w_gate, w_up, w_down, head_groups, 1
    )
    own_rows = tokens.shape[0]
    hidden_res = lax.dynamic_slice_in_dim(all_hidden, head_index * own_rows, own_rows, 0)
    d_gate_a, d_up_a, gate_a, up_a, down_a = mlp_half(
        flip_mlp, gathered_grad, silu, slope, act, w_down, 0
    )
    gate_a, up_a, down_a = lax.psum((gate_a, up_a, down_a), "seg")
    d_gate_b, d_up_b, gate_b, up_b, down_b = mlp_half(
        flip_mlp, gathered_grad, silu, slope, act, w_down, 1
    )
    gathered_hidden, d_hidden, gain_mlp_rows, down_b, gate_b = mlp_back_sum(
        (d_gate_a, d_gate_b),
        (d_up_a, d_up_b),
        w_gate,
        w_up,
        all_hidden,
        gathered_grad,
        gain_mlp,
        (down_b, gate_b),
        (BLOCK, cols),
        seg_size,
        head_groups,
        2,
    )
    d_queries, d_keys, d_values, gate_cols = attn_back(
        mix_sig,
        valid_len,
        gathered_hidden,
        w_out,
        query_rows,
        key_rows,
        value_rows,
        local_attn,
        memory_prev,
        3,
    )
    pair, grad_query, grad_key, grad_value, grad_out, gain_attn_rows = attn_weights(
        gathered_attn,
        gathered_hidden,
        mixed_attn,
        d_queries,
        d_keys,
        d_values,
        w_query,
        w_key,
        w_value,
        pair,
    )
    width = gain_attn.shape[0]
    pair = lax.psum_scatter(pair, "head", scatter_dimension=0, tiled=True).astype(F32)
    output = (hidden_res + pair[:, :width]).astype(BF16)
    d_normed_attn = pair[:, width:]
    grad_in_attn = norm_backward(token_vals, inverse_rms(token_vals), gain_attn, d_normed_attn)
    grad_tokens = (d_hidden + grad_in_attn).astype(BF16)
    gate_part = mix_sig * (1.0 - mix_sig) * jnp.sum(gate_cols[:, 0], axis=-1)
    slots = jnp.where(
        (lax.iota(jnp.int32, head_groups) == head_index)[:, None], gate_part[None], 0.0
    )
    gain_attn_part = jnp.sum(gain_attn_rows, axis=0) / gain_attn
    gain_mlp_part = jnp.sum(gain_mlp_rows, axis=0)
    parts = jnp.concatenate([gain_attn_part, gain_mlp_part, slots.reshape(-1)])
    lines = -(-parts.shape[0] // (8 * DH)) * 8
    parts = jnp.pad(parts, (0, lines * DH - parts.shape[0])).reshape(lines, DH)
    small, *late = grad_sum(
        parts,
        [up_b, grad_out, grad_query, grad_key, grad_value],
        (cols, cols),
        seg_size,
        head_groups,
        0,
    )
    small = small.reshape(-1)
    grad_mem_gate = lax.dynamic_slice(small, (2 * width + head_index * heads,), (heads,))
    grads = widen(
        [(1, gate_a, gate_b), (1, up_a, late[0]), (0, down_a, down_b)]
        + [(0, grad) for grad in late[1:]],
        (cols, cols),
    )
    return (
        output,
        grad_tokens,
        memory_after,
        normal_after,
        small[:width],
        small[width : 2 * width],
        grads[4],
        grads[5],
        grads[6],
        grads[3],
        grads[0],
        grads[1],
        grads[2],
        grad_mem_gate,
    )


def solution(mesh):
    return jax.shard_map(
        per_device,
        mesh=mesh,
        in_specs=(
            P(("seg", "head"), None),
            P(("seg", "head"), None),
            P(),
            P(),
            P(None, "head"),
            P(None, "head"),
            P(None, "head"),
            P("head", None),
            P(None, "head"),
            P(None, "head"),
            P("head", None),
            P("head"),
            P(),
        ),
        out_specs=(
            P(("seg", "head"), None),
            P(("seg", "head"), None),
            P("seg", "head", None, None),
            P("seg", "head", None),
            P(),
            P(),
            P(None, "head"),
            P(None, "head"),
            P(None, "head"),
            P("head", None),
            P(None, "head"),
            P(None, "head"),
            P("head", None),
            P("head"),
        ),
        check_vma=False,
    )
```

```python
import functools

import jax
import jax.numpy as jnp
from jax import lax
from jax.experimental import pallas as pl
from jax.experimental.pallas import tpu as pltpu
from jax.sharding import PartitionSpec as P

DH = 128
SEG_LEN = 1024
SEGS = 4
MEM_ROWS = DH + 16
BLOCK = 256

epsilon = 1e-05
masked_score = -1e30
F32 = jnp.float32
BF16 = jnp.bfloat16


MESH = pl.DeviceIdType.MESH
LAND_SLOTS = 12
RESULT_SLOTS = 16
SUM_SEMS = 8
SUM_HOP = 3


def bits_of(size):
    return size.bit_length() - 1


def flip(index, power):
    return index + power - 2 * power * lax.rem(index // power, 2)


def sum_engine(arrays, outs, tile, seg_bits, scratch):
    mine, result, send_sem, recv_sem, load_sem, store_sem, *lands = scratch
    seg = lax.axis_index("seg")
    planes = seg_bits - 1
    high, wide = tile
    shapes = [array.shape for array in arrays]
    counts = [(rows // high) * (cols // wide) for rows, cols in shapes]
    starts = [sum(counts[:i]) for i in range(len(counts))]
    total = sum(counts)

    def power(k, level):
        if level == 0:
            return 1
        which = lax.rem(k + level - 1, planes)
        value = 2
        for bit in range(1, planes):
            value = jnp.where(which == bit, 2 << bit, value)
        return value

    def my_bit(k, level):
        return lax.rem(seg // power(k, level), 2)

    def part(k, level, own):
        half = high >> (level + 1)
        bit = my_bit(k, level) if own else 1 - my_bit(k, level)
        return pl.ds(pl.multiple_of(bit * half, half), half)

    def kept(k, levels):
        first = 0
        for level in range(levels):
            first = first + my_bit(k, level) * (high >> (level + 1))
        return pl.ds(pl.multiple_of(first, high >> levels), high >> levels)

    def pick(k, act):
        for i in range(len(arrays)):

            @pl.when((k >= starts[i]) & (k < starts[i] + counts[i]))
            def _(i=i):
                across = shapes[i][1] // wide
                place = k - starts[i]
                row = pl.multiple_of((place // across) * high, high)
                col = pl.multiple_of(lax.rem(place, across) * wide, wide)
                act(i, row, col)

    def halving(k, level, source):
        return pltpu.make_async_remote_copy(
            src_ref=source,
            dst_ref=lands[level].at[lax.rem(k, LAND_SLOTS)],
            send_sem=send_sem.at[level, lax.rem(k, SUM_SEMS)],
            recv_sem=recv_sem.at[level, lax.rem(k, SUM_SEMS)],
            device_id={"seg": flip(seg, power(k, level))},
            device_id_type=MESH,
        )

    def first_source(k, i, row, col, own):
        half = high // 2
        bit = my_bit(k, 0) if own else 1 - my_bit(k, 0)
        return arrays[i].at[pl.ds(pl.multiple_of(row + bit * half, half), half), pl.ds(col, wide)]

    def keep(k, i, row, col):
        slot = lax.rem(k, 4)
        return pltpu.make_async_copy(
            first_source(k, i, row, col, True), mine.at[slot], load_sem.at[slot]
        )

    def level_source(k, level):
        return lands[level - 1].at[lax.rem(k, LAND_SLOTS), part(k, level, False)]

    def doubling(k, level):
        ref = result.at[lax.rem(k, RESULT_SLOTS), kept(k, level + 1)]
        return pltpu.make_async_remote_copy(
            src_ref=ref,
            dst_ref=ref,
            send_sem=send_sem.at[seg_bits + level, lax.rem(k, SUM_SEMS)],
            recv_sem=recv_sem.at[seg_bits + level, lax.rem(k, SUM_SEMS)],
            device_id={"seg": flip(seg, power(k, level))},
            device_id_type=MESH,
        )

    def store(k, i, row, col):
        slot = lax.rem(k, 4)
        return pltpu.make_async_copy(
            result.at[lax.rem(k, RESULT_SLOTS)],
            outs[i].at[pl.ds(row, high), pl.ds(col, wide)],
            store_sem.at[slot],
        )

    def do_first(k):
        def go(i, row, col):
            halving(k, 0, first_source(k, i, row, col, False)).start()
            keep(k, i, row, col).start()

        pick(k, go)

    def arrived(k, level):
        slot = lax.rem(k, LAND_SLOTS)
        if level == 0:
            halving(k, 0, first_source(k, 0, 0, 0, False)).wait()
            keep(k, 0, 0, 0).wait()
            other = mine[lax.rem(k, 4)]
        else:
            halving(k, level, level_source(k, level)).wait()
            other = lands[level - 1][slot, part(k, level, True)]
        return (lands[level][slot].astype(F32) + other.astype(F32)).astype(BF16)

    def do_level(k, level):
        lands[level - 1][lax.rem(k, LAND_SLOTS)] = arrived(k, level - 1)
        halving(k, level, level_source(k, level)).start()

    def do_total(k):
        result[lax.rem(k, RESULT_SLOTS), kept(k, seg_bits)] = arrived(k, seg_bits - 1)
        doubling(k, seg_bits - 1).start()

    def do_spread(k, level):
        doubling(k, level + 1).wait()
        doubling(k, level).start()

    def do_finish(k):
        doubling(k, 0).wait()
        pick(k, lambda i, row, col: store(k, i, row, col).start())

    def do_store(k):
        store(k, 0, 0, 0).wait()

    stages = [(0, do_first), (1, functools.partial(do_level, level=1))]
    when = 1
    for level in range(2, seg_bits):
        when += SUM_HOP
        stages.append((when, functools.partial(do_level, level=level)))
    when += SUM_HOP
    stages.append((when, do_total))
    for level in range(seg_bits - 2, -1, -1):
        when += SUM_HOP
        stages.append((when, functools.partial(do_spread, level=level)))
    stages.append((when + 1, do_finish))
    stages.append((when + 3, do_store))

    def step(t):
        for delay, act in reversed(stages):
            k = t - delay

            @pl.when((k >= 0) & (k < total))
            def _(act=act, k=k):
                act(k)

    return step, total + when + 3


def engine_scratch(tile, seg_bits):
    high, wide = tile
    return [
        pltpu.VMEM((4, high // 2, wide), BF16),
        pltpu.VMEM((RESULT_SLOTS, high, wide), BF16),
        pltpu.SemaphoreType.DMA((2 * seg_bits, SUM_SEMS)),
        pltpu.SemaphoreType.DMA((2 * seg_bits, SUM_SEMS)),
        pltpu.SemaphoreType.DMA((4,)),
        pltpu.SemaphoreType.DMA((4,)),
    ] + [pltpu.VMEM((LAND_SLOTS, high >> (l + 1), wide), BF16) for l in range(seg_bits)]


def greet_seg(seg_bits):
    barrier = pltpu.get_barrier_semaphore()
    seg = lax.axis_index("seg")
    for bit in range(seg_bits):
        pl.semaphore_signal(
            barrier, inc=1, device_id={"seg": flip(seg, 1 << bit)}, device_id_type=MESH
        )


def grad_sum_kernel(count, tile, seg_bits, head_bits, *refs):
    small_in, arrays = refs[0], refs[1 : 1 + count]
    small_out, outs = refs[1 + count], refs[2 + count : 2 + 2 * count]
    small_buf, small_land, small_send, small_recv, *scratch = refs[2 + 2 * count :]
    seg, head = lax.axis_index("seg"), lax.axis_index("head")
    greet_seg(seg_bits)
    barrier = pltpu.get_barrier_semaphore()
    for bit in range(head_bits):
        pl.semaphore_signal(
            barrier, inc=1, device_id={"head": flip(head, 1 << bit)}, device_id_type=MESH
        )
    pl.semaphore_wait(barrier, seg_bits + head_bits)
    rounds = seg_bits + head_bits

    def small_copy(j):
        if j < seg_bits:
            where = {"seg": flip(seg, 1 << j)}
        else:
            where = {"head": flip(head, 1 << (j - seg_bits))}
        return pltpu.make_async_remote_copy(
            src_ref=small_buf.at[j],
            dst_ref=small_land.at[j],
            send_sem=small_send.at[j],
            recv_sem=small_recv.at[j],
            device_id=where,
            device_id_type=MESH,
        )

    engine_step, steps = sum_engine(arrays, outs, tile, seg_bits, scratch)

    def step(t, carry):
        engine_step(t)
        for j in range(rounds + 1):

            @pl.when(t == 3 * j)
            def _(j=j):
                if j == 0:
                    small_buf[0] = small_in[...]
                else:
                    small_copy(j - 1).wait()
                    value = small_buf[j - 1] + small_land[j - 1]
                    if j < rounds:
                        small_buf[j] = value
                    else:
                        small_out[...] = value
                if j < rounds:
                    small_copy(j).start()

        return carry

    lax.fori_loop(0, max(steps, 3 * rounds + 1), step, 0)


def grad_sum(small, arrays, tile, seg_size, head_size, cid):
    seg_bits, head_bits = bits_of(seg_size), bits_of(head_size)
    rounds = seg_bits + head_bits
    count = len(arrays)
    moved = sum(rows * cols for rows, cols in (array.shape for array in arrays))
    any_, vmem = pl.BlockSpec(memory_space=pltpu.HBM), pl.BlockSpec(memory_space=pltpu.VMEM)
    return pl.pallas_call(
        functools.partial(grad_sum_kernel, count, tile, seg_bits, head_bits),
        in_specs=[vmem] + [any_] * count,
        out_specs=[vmem] + [any_] * count,
        out_shape=[jax.ShapeDtypeStruct(small.shape, F32)]
        + [jax.ShapeDtypeStruct(array.shape, BF16) for array in arrays],
        scratch_shapes=[
            pltpu.VMEM((rounds, *small.shape), F32),
            pltpu.VMEM((rounds, *small.shape), F32),
            pltpu.SemaphoreType.DMA((rounds,)),
            pltpu.SemaphoreType.DMA((rounds,)),
        ]
        + engine_scratch(tile, seg_bits),
        cost_estimate=pl.CostEstimate(flops=0, bytes_accessed=moved * 60, transcendentals=0),
        compiler_params=pltpu.CompilerParams(
            collective_id=cid, has_side_effects=True, vmem_limit_bytes=60 * 2**20
        ),
    )(small, *arrays)


ROWS = 32
FIRST_HOP = 2
SECOND_HOP = 3
SEND_SLOTS = 4
BLOCK_ROWS = 256
FORWARD_ROWS = 128
UNIT_GROUP = 512
LINE_REFS = 8


def line_exchange(own, finish, before, scratch, hop, extra, extra_steps):
    up_land, down_land, up_send, down_send, up_recv_sem, down_recv_sem, up_send_sem, down_send_sem = scratch
    size = lax.axis_size("head")
    place = lax.axis_index("head")
    slots = up_land.shape[0]
    chunks = own.shape[0] // ROWS
    last = size - 1

    def up_copy(k):
        return pltpu.make_async_remote_copy(
            src_ref=up_send.at[lax.rem(k, SEND_SLOTS)],
            dst_ref=up_land.at[lax.rem(k, slots)],
            send_sem=up_send_sem.at[lax.rem(k, SEND_SLOTS)],
            recv_sem=up_recv_sem.at[lax.rem(k, slots)],
            device_id={"head": lax.rem(place + 1, size)},
            device_id_type=MESH,
        )

    def down_copy(k):
        return pltpu.make_async_remote_copy(
            src_ref=down_send.at[lax.rem(k, SEND_SLOTS)],
            dst_ref=down_land.at[lax.rem(k, slots)],
            send_sem=down_send_sem.at[lax.rem(k, SEND_SLOTS)],
            recv_sem=down_recv_sem.at[lax.rem(k, slots)],
            device_id={"head": lax.rem(place + last, size)},
            device_id_type=MESH,
        )

    def rows_of(k):
        return pl.ds(pl.multiple_of(k * ROWS, ROWS), ROWS)

    def pass_on(k, copy, land, send, has_source, has_target):
        @pl.when(has_source)
        def _():
            copy(k).wait_recv()

        @pl.when(has_target)
        def _():
            slot = lax.rem(k, SEND_SLOTS)

            @pl.when(k >= SEND_SLOTS)
            def _():
                copy(k - SEND_SLOTS).wait_send()

            @pl.when(has_source)
            def _():
                send[slot] = (own[rows_of(k)] + land[lax.rem(k, slots)].astype(F32)).astype(BF16)

            @pl.when(jnp.logical_not(has_source))
            def _():
                send[slot] = own[rows_of(k)].astype(BF16)

            copy(k).start()

    far = jnp.maximum(place, last - place)

    def step(t, carry):
        before(t)
        down = t - (last - place) * hop

        @pl.when((down >= 0) & (down < chunks))
        def _():
            pass_on(down, down_copy, down_land, down_send, place < last, place > 0)

        up = t - place * hop

        @pl.when((up >= 0) & (up < chunks))
        def _():
            pass_on(up, up_copy, up_land, up_send, place > 0, place < last)

        k = t - far * hop

        @pl.when((k >= 0) & (k < chunks))
        def _():
            slot = lax.rem(k, slots)

            @pl.when(place == 0)
            def _():
                finish(k, own[rows_of(k)] + down_land[slot].astype(F32))

            @pl.when(place == last)
            def _():
                finish(k, own[rows_of(k)] + up_land[slot].astype(F32))

            @pl.when((place > 0) & (place < last))
            def _():
                finish(
                    k,
                    own[rows_of(k)] + up_land[slot].astype(F32) + down_land[slot].astype(F32),
                )

        extra(t)
        return carry

    lax.fori_loop(0, max(chunks + last * hop, extra_steps), step, 0)
    for k in range(chunks - SEND_SLOTS, chunks):

        @pl.when(place < last)
        def _(k=k):
            up_copy(k).wait_send()

        @pl.when(place > 0)
        def _(k=k):
            down_copy(k).wait_send()


def line_barrier(others=0):
    size = lax.axis_size("head")
    place = lax.axis_index("head")
    barrier = pltpu.get_barrier_semaphore()
    inner = (place > 0) & (place < size - 1)

    def greet(near):
        pl.semaphore_signal(
            barrier, inc=1, device_id={"head": lax.rem(near, size)}, device_id_type=MESH
        )

    @pl.when(place > 0)
    def _():
        greet(place + size - 1)

    @pl.when(place < size - 1)
    def _():
        greet(place + 1)

    @pl.when(inner)
    def _():
        pl.semaphore_wait(barrier, 2 + others)

    @pl.when(jnp.logical_not(inner))
    def _():
        pl.semaphore_wait(barrier, 1 + others)


def line_scratch(size, width, hop):
    slots = (size - 1) * hop + 2
    return [
        pltpu.VMEM((slots, ROWS, width), BF16),
        pltpu.VMEM((slots, ROWS, width), BF16),
        pltpu.VMEM((SEND_SLOTS, ROWS, width), BF16),
        pltpu.VMEM((SEND_SLOTS, ROWS, width), BF16),
        pltpu.SemaphoreType.DMA((slots,)),
        pltpu.SemaphoreType.DMA((slots,)),
        pltpu.SemaphoreType.DMA((SEND_SLOTS,)),
        pltpu.SemaphoreType.DMA((SEND_SLOTS,)),
    ]


GATHER_PARTS = 4


def gather_kernel(
    token_hbm, gain_ref, w_query_hbm, w_key_hbm, w_value_hbm,
    all_ref, normed_ref, query_ref, key_ref, value_ref,
    land, normed, w_query, w_key, w_value,
    own_sem, load_sem, all_sem, normed_sem, up_send, up_recv, down_send, down_recv,
):
    size = lax.axis_size("head")
    place = lax.axis_index("head")
    last = size - 1
    own_rows = token_hbm.shape[0]
    chunk = own_rows // GATHER_PARTS
    loads = [
        pltpu.make_async_copy(source, target, load_sem.at[i])
        for i, (source, target) in enumerate(
            ((w_key_hbm, w_key), (w_value_hbm, w_value), (w_query_hbm, w_query))
        )
    ]

    def shard_rows(shard):
        return pl.ds(pl.multiple_of(shard * own_rows, own_rows), own_rows)

    own = pltpu.make_async_copy(token_hbm, land.at[shard_rows(place)], own_sem)
    own.start()
    for load in loads:
        load.start()
    line_barrier()

    def chunk_copy(shard, i, send_sem, recv_sem, target):
        first = pl.multiple_of(shard * own_rows + lax.rem(i, GATHER_PARTS) * chunk, chunk)
        ref = land.at[pl.ds(first, chunk)]
        return pltpu.make_async_remote_copy(
            src_ref=ref,
            dst_ref=ref,
            send_sem=send_sem.at[i],
            recv_sem=recv_sem.at[i],
            device_id={"head": target},
            device_id_type=MESH,
        )

    above, below = lax.rem(place + 1, size), lax.rem(place + last, size)

    def up_copy(i, first_shard):
        return chunk_copy(first_shard - i // GATHER_PARTS, i, up_send, up_recv, above)

    def down_copy(i, first_shard):
        return chunk_copy(first_shard + i // GATHER_PARTS, i, down_send, down_recv, below)

    own.wait()
    for i in range(GATHER_PARTS):

        @pl.when(place < last)
        def _(i=i):
            up_copy(i, place).start()

        @pl.when(place > 0)
        def _(i=i):
            down_copy(i, place).start()

    def stores(shard):
        rows = shard_rows(shard)
        return (
            pltpu.make_async_copy(land.at[rows], all_ref.at[rows], all_sem.at[shard]),
            pltpu.make_async_copy(normed.at[rows], normed_ref.at[rows], normed_sem.at[shard]),
        )

    def project(shard):
        rows = shard_rows(shard)
        value = land[rows].astype(F32)
        normed[rows] = (value * inverse_rms(value) * gain_ref[...]).astype(BF16)
        for copy in stores(shard):
            copy.start()
        for weight, target in ((w_key, key_ref), (w_value, value_ref), (w_query, query_ref)):
            target[rows] = dot(normed[rows], weight[...], NN).astype(BF16)

    for load in loads:
        load.wait()
    project(place)

    def step(i, carry):
        @pl.when(i < place * GATHER_PARTS)
        def _():
            up_copy(i, place - 1).wait_recv()

            @pl.when(place < last)
            def _():
                up_copy(i + GATHER_PARTS, place).start()

        @pl.when(i < (last - place) * GATHER_PARTS)
        def _():
            down_copy(i, place + 1).wait_recv()

            @pl.when(place > 0)
            def _():
                down_copy(i + GATHER_PARTS, place).start()

        distance = (i + 1) // GATHER_PARTS
        whole = lax.rem(i + 1, GATHER_PARTS) == 0

        @pl.when(whole & (place >= distance))
        def _():
            project(place - distance)

        @pl.when(whole & (place + distance <= last))
        def _():
            project(place + distance)

        return carry

    lax.fori_loop(0, last * GATHER_PARTS, step, 0)

    def drain(i, carry):
        @pl.when((place < last) & (i < (place + 1) * GATHER_PARTS))
        def _():
            up_copy(i, place).wait_send()

        @pl.when((place > 0) & (i < (size - place) * GATHER_PARTS))
        def _():
            down_copy(i, place).wait_send()

        return carry

    lax.fori_loop(0, size * GATHER_PARTS, drain, 0)
    for shard in range(size):
        for copy in stores(shard):
            copy.wait()


def gather_project(tokens, gain, w_query, w_key, w_value, size, cid):
    own_rows, width = tokens.shape
    rows, cols = own_rows * size, w_query.shape[1]
    vmem, any_ = pl.BlockSpec(memory_space=pltpu.VMEM), pl.BlockSpec(memory_space=pltpu.HBM)
    weight = pltpu.VMEM((width, cols), BF16)
    hops = pltpu.SemaphoreType.DMA((size * GATHER_PARTS,))
    return pl.pallas_call(
        gather_kernel,
        in_specs=[any_, vmem] + [any_] * 3,
        out_specs=[any_, any_, vmem, vmem, vmem],
        out_shape=[jax.ShapeDtypeStruct((rows, width), BF16)] * 2
        + [jax.ShapeDtypeStruct((rows, cols), BF16)] * 3,
        scratch_shapes=[
            pltpu.VMEM((rows, width), BF16),
            pltpu.VMEM((rows, width), BF16),
            weight,
            weight,
            weight,
            pltpu.SemaphoreType.DMA(()),
            pltpu.SemaphoreType.DMA((3,)),
            pltpu.SemaphoreType.DMA((size,)),
            pltpu.SemaphoreType.DMA((size,)),
            hops,
            hops,
            hops,
            hops,
        ],
        cost_estimate=pl.CostEstimate(
            flops=6 * rows * width * cols, bytes_accessed=150 * 2**20, transcendentals=0
        ),
        compiler_params=pltpu.CompilerParams(
            collective_id=cid, has_side_effects=True, vmem_limit_bytes=48 * 2**20
        ),
    )(tokens, gain.reshape(1, width), w_query, w_key, w_value)


def attn_out_kernel(
    mixed_ref, weight_ref, token_ref, gain_ref, w_gate_hbm, w_up_hbm, w_down_hbm,
    hidden_ref, flip_ref, silu_ref, slope_ref, act_ref, part_ref,
    hidden, normed, w_gate, w_up, w_down, silu, slope, act, flip, part, part_out,
    hidden_sem, load_sem, out_sem, block_sem, *scratch
):
    loads = [
        pltpu.make_async_copy(source, target, load_sem.at[i])
        for i, (source, target) in enumerate(
            ((w_gate_hbm, w_gate), (w_up_hbm, w_up), (w_down_hbm, w_down))
        )
    ]
    for load in loads:
        load.start()
    line_barrier()
    per_block = FORWARD_ROWS // ROWS
    blocks = hidden.shape[0] // FORWARD_ROWS
    groups = w_gate.shape[1] // UNIT_GROUP
    slots = act.shape[0]
    lag = per_block + (lax.axis_size("head") - 1) * FIRST_HOP
    pace = per_block // groups

    def block_rows(b):
        return pl.ds(pl.multiple_of(b * FORWARD_ROWS, FORWARD_ROWS), FORWARD_ROWS)

    def unit_copies(u):
        slot = lax.rem(u, slots)
        where = (block_rows(u // groups), unit_cols(u))
        return [
            pltpu.make_async_copy(source.at[slot], target.at[where], out_sem.at[i, slot])
            for i, (source, target) in enumerate(
                ((silu, silu_ref), (slope, slope_ref), (act, act_ref))
            )
        ]

    def unit_cols(u):
        return pl.ds(pl.multiple_of(lax.rem(u, groups) * UNIT_GROUP, UNIT_GROUP), UNIT_GROUP)

    def flip_copy(b):
        return pltpu.make_async_copy(flip, flip_ref.at[:, block_rows(b)], block_sem.at[0])

    def part_copy(b):
        where = (block_rows(b), pl.ds(0, part_out.shape[1]))
        return pltpu.make_async_copy(part_out, part_ref.at[where], block_sem.at[1])

    def forward(u):
        slot = lax.rem(u, slots)
        b, group = u // groups, lax.rem(u, groups)

        @pl.when(group == 0)
        def _():
            @pl.when(b > 0)
            def _():
                flip_copy(b - 1).wait()

            flip[...] = normed[block_rows(b)].T
            flip_copy(b).start()

        @pl.when(u >= slots)
        def _():
            for copy in unit_copies(u - slots):
                copy.wait()

        rows, cols = normed[block_rows(u // groups)], unit_cols(u)
        gate_pre = dot(rows, w_gate[:, cols], NN)
        up_proj = dot(rows, w_up[:, cols], NN)
        gate_sig = jax.nn.sigmoid(gate_pre)
        silu_gate = gate_pre * gate_sig
        silu[slot] = silu_gate
        slope[slot] = up_proj * gate_sig * (1.0 + gate_pre * (1.0 - gate_sig))
        act[slot] = (silu_gate * up_proj).astype(BF16)
        for copy in unit_copies(u):
            copy.start()
        share = dot(act[slot], w_down[cols], NN)

        @pl.when(group == 0)
        def _():
            part[...] = share

        @pl.when(group > 0)
        def _():
            part[...] += share

        @pl.when(group == groups - 1)
        def _():
            @pl.when(b > 0)
            def _():
                part_copy(b - 1).wait()

            part_out[...] = part[...].astype(BF16)
            part_copy(b).start()

    def before(t):
        @pl.when((lax.rem(t, per_block) == 0) & (t < blocks * per_block))
        def _():
            rows = block_rows(t // per_block)
            hidden[rows] = dot(mixed_ref[rows], weight_ref[...], NN)

    def after(t):
        @pl.when(t == lag)
        def _():
            for load in loads:
                load.wait()

        late = t - lag

        @pl.when((late >= 0) & (lax.rem(late, pace) == 0) & (late // pace < blocks * groups))
        def _():
            forward(late // pace)

    def store(b):
        rows = block_rows(b)
        return pltpu.make_async_copy(hidden.at[rows], hidden_ref.at[rows], hidden_sem.at[b])

    def finish(k, total):
        rows = pl.ds(pl.multiple_of(k * ROWS, ROWS), ROWS)
        value = token_ref[rows].astype(F32) + total
        hidden[rows] = value
        normed[rows] = (value * inverse_rms(value) * gain_ref[...]).astype(BF16)

        @pl.when(lax.rem(k, per_block) == per_block - 1)
        def _():
            store(k // per_block).start()

    line_exchange(hidden, finish, before, scratch, FIRST_HOP, after, lag + blocks * per_block)
    for b in range(blocks):
        store(b).wait()
    flip_copy(blocks - 1).wait()
    part_copy(blocks - 1).wait()
    for u in range(blocks * groups - slots, blocks * groups):
        for copy in unit_copies(u):
            copy.wait()


def attn_out_sum(mixed, weight, tokens, gain, w_gate, w_up, w_down, size, cid):
    rows, width = tokens.shape
    units = w_gate.shape[1]
    vmem, any_ = pl.BlockSpec(memory_space=pltpu.VMEM), pl.BlockSpec(memory_space=pltpu.HBM)
    blocks, slots = rows // FORWARD_ROWS, 2
    return pl.pallas_call(
        attn_out_kernel,
        in_specs=[vmem] * 4 + [any_] * 3,
        out_specs=[any_] * 6,
        out_shape=[
            jax.ShapeDtypeStruct((rows, width), F32),
            jax.ShapeDtypeStruct((width, rows), BF16),
            jax.ShapeDtypeStruct((rows, units), F32),
            jax.ShapeDtypeStruct((rows, units), F32),
            jax.ShapeDtypeStruct((rows, units), BF16),
            jax.ShapeDtypeStruct((rows, 2 * width), BF16),
        ],
        scratch_shapes=[
            pltpu.VMEM((rows, width), F32),
            pltpu.VMEM((rows, width), BF16),
            pltpu.VMEM((width, units), BF16),
            pltpu.VMEM((width, units), BF16),
            pltpu.VMEM((units, width), BF16),
            pltpu.VMEM((slots, FORWARD_ROWS, UNIT_GROUP), F32),
            pltpu.VMEM((slots, FORWARD_ROWS, UNIT_GROUP), F32),
            pltpu.VMEM((slots, FORWARD_ROWS, UNIT_GROUP), BF16),
            pltpu.VMEM((width, FORWARD_ROWS), BF16),
            pltpu.VMEM((FORWARD_ROWS, width), F32),
            pltpu.VMEM((FORWARD_ROWS, width), BF16),
            pltpu.SemaphoreType.DMA((blocks,)),
            pltpu.SemaphoreType.DMA((3,)),
            pltpu.SemaphoreType.DMA((3, slots)),
            pltpu.SemaphoreType.DMA((2,)),
        ]
        + line_scratch(size, width, FIRST_HOP),
        cost_estimate=pl.CostEstimate(
            flops=2 * rows * width * (mixed.shape[1] + 3 * units),
            bytes_accessed=250 * 2**20,
            transcendentals=rows * units,
        ),
        compiler_params=pltpu.CompilerParams(
            collective_id=cid, has_side_effects=True, vmem_limit_bytes=60 * 2**20
        ),
    )(mixed, weight, tokens, gain.reshape(1, width), w_gate, w_up, w_down)


def mlp_back_kernel(
    tile, seg_bits,
    d_gate_a, d_gate_b, d_up_a, d_up_b, w_gate_hbm, w_up_hbm, hidden_hbm, grad_hbm, gain_ref,
    down_in, gate_in,
    d_out_ref, d_own_ref, gain_part_ref, down_out, gate_out,
    d_gate, d_up, w_gate, w_up, hidden, grad, own, load_sem, store_sem, *scratch
):
    per_block = BLOCK_ROWS // ROWS
    blocks = own.shape[0] // BLOCK_ROWS
    size = lax.axis_size("head")
    place = lax.axis_index("head")
    per_device = own.shape[0] // ROWS // size
    half = d_gate.shape[1] // 2
    low, high = pl.ds(0, half), pl.ds(half, half)
    loads = [
        pltpu.make_async_copy(source, target, load_sem.at[i])
        for i, (source, target) in enumerate(
            ((d_gate_a, d_gate.at[:, low]), (d_gate_b, d_gate.at[:, high]), (w_gate_hbm, w_gate),
             (d_up_a, d_up.at[:, low]), (d_up_b, d_up.at[:, high]), (w_up_hbm, w_up),
             (hidden_hbm, hidden), (grad_hbm, grad))
        )
    ]
    for load in loads:
        load.start()
    gain_part_ref[...] = jnp.zeros_like(gain_part_ref)
    greet_seg(seg_bits)
    line_barrier(seg_bits)
    engine_step, steps = sum_engine(
        [down_in, gate_in], [down_out, gate_out], tile, seg_bits, scratch[LINE_REFS:]
    )

    def block_rows(b):
        return pl.ds(pl.multiple_of(b * BLOCK_ROWS, BLOCK_ROWS), BLOCK_ROWS)

    for load in loads[:3]:
        load.wait()

    def before(t):
        @pl.when((lax.rem(t, per_block) == 0) & (t < blocks * per_block))
        def _():
            rows = block_rows(t // per_block)
            own[rows] = dot(d_gate[rows], w_gate[...], NT)

            @pl.when(t == 0)
            def _():
                for load in loads[3:6]:
                    load.wait()

            own[rows] += dot(d_up[rows], w_up[...], NT)

        @pl.when(t == 1)
        def _():
            for load in loads[6:]:
                load.wait()

    def store(b):
        rows = block_rows(b)
        return pltpu.make_async_copy(grad.at[rows], d_out_ref.at[rows], store_sem.at[b])

    def finish(k, total):
        rows = pl.ds(pl.multiple_of(k * ROWS, ROWS), ROWS)
        value = hidden[rows]
        inverse = inverse_rms(value)
        normal = value * inverse
        scaled = gain_ref[...] * total
        mean = jnp.mean(scaled * normal, axis=-1, keepdims=True)
        d_hidden = grad[rows].astype(F32) + inverse * (scaled - normal * mean)
        grad[rows] = d_hidden.astype(BF16)

        @pl.when(k // per_device == place)
        def _():
            mine = pl.ds(pl.multiple_of(lax.rem(k, per_device) * ROWS, ROWS), ROWS)
            d_own_ref[mine] = d_hidden
            gain_part_ref[...] += jnp.sum((total * normal).reshape(ROWS // 8, 8, -1), axis=0)

        @pl.when(lax.rem(k, per_block) == per_block - 1)
        def _():
            store(k // per_block).start()

    line_exchange(own, finish, before, scratch[:LINE_REFS], SECOND_HOP, engine_step, steps)
    for b in range(blocks):
        store(b).wait()


def mlp_back_sum(
    d_gate, d_up, w_gate, w_up, hidden, grad, gain, summed, tile, seg_size, size, cid
):
    rows, width = hidden.shape
    units = w_gate.shape[1]
    seg_bits = bits_of(seg_size)
    vmem, any_ = pl.BlockSpec(memory_space=pltpu.VMEM), pl.BlockSpec(memory_space=pltpu.HBM)
    blocks = rows // BLOCK_ROWS
    return pl.pallas_call(
        functools.partial(mlp_back_kernel, tile, seg_bits),
        in_specs=[any_] * 8 + [vmem, any_, any_],
        out_specs=[any_, vmem, vmem, any_, any_],
        out_shape=[
            jax.ShapeDtypeStruct((rows, width), BF16),
            jax.ShapeDtypeStruct((rows // size, width), F32),
            jax.ShapeDtypeStruct((8, width), F32),
        ]
        + [jax.ShapeDtypeStruct(array.shape, BF16) for array in summed],
        scratch_shapes=[
            pltpu.VMEM((rows, units), BF16),
            pltpu.VMEM((rows, units), BF16),
            pltpu.VMEM((width, units), BF16),
            pltpu.VMEM((width, units), BF16),
            pltpu.VMEM((rows, width), F32),
            pltpu.VMEM((rows, width), BF16),
            pltpu.VMEM((rows, width), F32),
            pltpu.SemaphoreType.DMA((8,)),
            pltpu.SemaphoreType.DMA((blocks,)),
        ]
        + line_scratch(size, width, SECOND_HOP)
        + engine_scratch(tile, seg_bits),
        cost_estimate=pl.CostEstimate(
            flops=4 * rows * width * units, bytes_accessed=250 * 2**20, transcendentals=0
        ),
        compiler_params=pltpu.CompilerParams(
            collective_id=cid, has_side_effects=True, vmem_limit_bytes=62 * 2**20
        ),
    )(*d_gate, *d_up, w_gate, w_up, hidden, grad, gain.reshape(1, width), *summed)


MLP_BLOCK = 512


def mlp_kernel(
    flip_ref, grad_ref, silu_ref, slope_ref, act_ref, w_down_ref,
    d_gate_ref, d_up_ref, grad_gate_ref, grad_up_ref, grad_down_ref,
):
    width = flip_ref.shape[0]
    d_act = dot(grad_ref[...], w_down_ref[...], NT)
    d_gate_ref[...] = (d_act * slope_ref[...]).astype(BF16)
    d_up_ref[...] = (d_act * silu_ref[...]).astype(BF16)
    half = width // 2
    for i in range(2):
        part = slice(i * half, (i + 1) * half)
        grad_gate_ref[part] = dot(flip_ref[part], d_gate_ref[...], NN).astype(BF16)
        grad_up_ref[part] = dot(flip_ref[part], d_up_ref[...], NN).astype(BF16)
        grad_down_ref[:, part] = dot(act_ref[...], grad_ref[:, part], TN).astype(BF16)


def mlp_half(flip, grad, silu, slope, act, w_down, which):
    width, count = flip.shape
    units = act.shape[1] // 2
    block = min(MLP_BLOCK, units)
    first = which * (units // block)
    once = pl.Buffered(1)
    side = pl.BlockSpec((count, block), lambda j: (0, first + j))
    side_out = pl.BlockSpec((count, block), lambda j: (0, j))
    tall = pl.BlockSpec((width, block), lambda j: (0, j))
    return pl.pallas_call(
        mlp_kernel,
        grid=(units // block,),
        in_specs=[
            pl.BlockSpec((width, count), lambda j: (0, 0), pipeline_mode=once),
            pl.BlockSpec((count, width), lambda j: (0, 0), pipeline_mode=once),
            side,
            side,
            side,
            pl.BlockSpec((block, width), lambda j: (first + j, 0)),
        ],
        out_specs=[side_out, side_out, tall, tall, pl.BlockSpec((block, width), lambda j: (j, 0))],
        out_shape=[
            jax.ShapeDtypeStruct((count, units), BF16),
            jax.ShapeDtypeStruct((count, units), BF16),
            jax.ShapeDtypeStruct((width, units), BF16),
            jax.ShapeDtypeStruct((width, units), BF16),
            jax.ShapeDtypeStruct((units, width), BF16),
        ],
        cost_estimate=pl.CostEstimate(
            flops=8 * count * width * units,
            bytes_accessed=2 * (2 * count * width + 4 * width * units + 7 * count * units),
            transcendentals=0,
        ),
        compiler_params=pltpu.CompilerParams(vmem_limit_bytes=56 * 2**20),
    )(flip, grad, silu, slope, act, w_down)


WIDEN_SLOTS = 4


def widen_kernel(shapes, places, wide_count, tile, *refs):
    count = len(shapes)
    sources, targets = refs[:count], refs[count : count + wide_count]
    narrow, wide, load_sem, store_sem = refs[count + wide_count :]
    high, broad = tile
    counts = [(rows // high) * (width // broad) for rows, width in shapes]
    total = sum(counts)

    def pick(k, act):
        first = 0
        for i in range(count):
            @pl.when((k >= first) & (k < first + counts[i]))
            def _(i=i, first=first):
                across = shapes[i][1] // broad
                place = k - first
                row = pl.multiple_of((place // across) * high, high)
                col = pl.multiple_of(lax.rem(place, across) * broad, broad)
                act(i, (pl.ds(row, high), pl.ds(col, broad)))
            first += counts[i]

    def load(k, i, where):
        slot = lax.rem(k, WIDEN_SLOTS)
        return pltpu.make_async_copy(sources[i].at[where], narrow.at[slot], load_sem.at[slot])

    def store(k, i, where):
        slot = lax.rem(k, WIDEN_SLOTS)
        target, row, col = places[i]
        rows = pl.ds(pl.multiple_of(row + where[0].start, high), high)
        cols = pl.ds(pl.multiple_of(col + where[1].start, broad), broad)
        return pltpu.make_async_copy(
            wide.at[slot], targets[target].at[rows, cols], store_sem.at[slot]
        )

    zero = (pl.ds(0, high), pl.ds(0, broad))
    ahead = WIDEN_SLOTS - 1
    for k in range(ahead):
        pick(k, lambda i, where, k=k: load(k, i, where).start())

    def step(k, carry):
        @pl.when(k + ahead < total)
        def _():
            pick(k + ahead, lambda i, where: load(k + ahead, i, where).start())

        @pl.when(k >= WIDEN_SLOTS)
        def _():
            store(k - WIDEN_SLOTS, 0, zero).wait()

        load(k, 0, zero).wait()
        slot = lax.rem(k, WIDEN_SLOTS)
        wide[slot] = narrow[slot].astype(F32)
        pick(k, lambda i, where: store(k, i, where).start())
        return carry

    lax.fori_loop(0, total, step, 0)
    for k in range(total - WIDEN_SLOTS, total):
        store(k, 0, zero).wait()


def widen(groups, tile):
    arrays, places, targets = [], [], []
    for axis, *group in groups:
        shape = [0, 0]
        shape[1 - axis] = group[0].shape[1 - axis]
        for value in group:
            arrays.append(value)
            places.append((len(targets), *((shape[0], 0) if axis == 0 else (0, shape[1]))))
            shape[axis] += value.shape[axis]
        targets.append(tuple(shape))
    shapes = [value.shape for value in arrays]
    any_ = pl.BlockSpec(memory_space=pltpu.HBM)
    return pl.pallas_call(
        functools.partial(widen_kernel, shapes, places, len(targets), tile),
        in_specs=[any_] * len(arrays),
        out_specs=[any_] * len(targets),
        out_shape=[jax.ShapeDtypeStruct(shape, F32) for shape in targets],
        scratch_shapes=[
            pltpu.VMEM((WIDEN_SLOTS, *tile), BF16),
            pltpu.VMEM((WIDEN_SLOTS, *tile), F32),
            pltpu.SemaphoreType.DMA((WIDEN_SLOTS,)),
            pltpu.SemaphoreType.DMA((WIDEN_SLOTS,)),
        ],
        cost_estimate=pl.CostEstimate(
            flops=0, bytes_accessed=6 * sum(r * c for r, c in shapes), transcendentals=0
        ),
        compiler_params=pltpu.CompilerParams(vmem_limit_bytes=60 * 2**20),
    )(*arrays)


def attn_weights_kernel(
    rows_ref, d_out_ref, mixed_ref, d_query_ref, d_key_ref, d_value_ref,
    w_query_ref, w_key_ref, w_value_ref, pair_ref,
    d_rows_ref, grad_query_ref, grad_key_ref, grad_value_ref, grad_out_ref, gain_part_ref,
    flipped_mixed, flipped_rows,
):
    @pl.when(pl.program_id(0) == 0)
    def _():
        flipped_mixed[...] = mixed_ref[...].T

    flipped_rows[...] = rows_ref[...].T
    d_rows = (
        dot(d_query_ref[...], w_query_ref[...], NT)
        + dot(d_key_ref[...], w_key_ref[...], NT)
        + dot(d_value_ref[...], w_value_ref[...], NT)
    )
    d_rows_ref[...] = d_rows.astype(BF16)
    product = d_rows * rows_ref[...].astype(F32)
    gain_part_ref[...] = jnp.sum(product.reshape(-1, 8, product.shape[1]), axis=0)
    grad_query_ref[...] = dot(flipped_rows[...], d_query_ref[...], NN).astype(BF16)
    grad_key_ref[...] = dot(flipped_rows[...], d_key_ref[...], NN).astype(BF16)
    grad_value_ref[...] = dot(flipped_rows[...], d_value_ref[...], NN).astype(BF16)
    grad_out_ref[...] = dot(flipped_mixed[...], d_out_ref[...], NN).astype(BF16)


def attn_weights(rows, d_out, mixed, d_query, d_key, d_value, w_query, w_key, w_value, pair):
    count, width = rows.shape
    cols = mixed.shape[1]
    block = 512
    once = pl.Buffered(1)
    slim = pl.BlockSpec((count, cols), lambda j: (0, 0), pipeline_mode=once)
    side = pl.BlockSpec((count, block), lambda j: (0, j))
    right = pl.BlockSpec((count, block), lambda j: (0, width // block + j))
    tall = pl.BlockSpec((block, cols), lambda j: (j, 0))
    wide = pl.BlockSpec((cols, block), lambda j: (0, j))
    tall_type = jax.ShapeDtypeStruct((width, cols), BF16)
    return pl.pallas_call(
        attn_weights_kernel,
        grid=(width // block,),
        in_specs=[side, side, slim, slim, slim, slim, tall, tall, tall]
        + [pl.BlockSpec(memory_space=pltpu.HBM)],
        out_specs=[right, tall, tall, tall, wide, pl.BlockSpec((8, block), lambda j: (0, j))],
        out_shape=[
            jax.ShapeDtypeStruct(pair.shape, BF16),
            tall_type,
            tall_type,
            tall_type,
            jax.ShapeDtypeStruct((cols, width), BF16),
            jax.ShapeDtypeStruct((8, width), F32),
        ],
        input_output_aliases={9: 0},
        scratch_shapes=[pltpu.VMEM((cols, count), BF16), pltpu.VMEM((block, count), BF16)],
        cost_estimate=pl.CostEstimate(
            flops=14 * count * width * cols,
            bytes_accessed=2 * (3 * count * width + 4 * count * cols + 7 * width * cols),
            transcendentals=0,
        ),
        compiler_params=pltpu.CompilerParams(vmem_limit_bytes=48 * 2**20),
    )(rows, d_out, mixed, d_query, d_key, d_value, w_query, w_key, w_value, pair)


def elu_plus(values):
    return jnp.where(values > 0, values + 1.0, jnp.exp(jnp.minimum(values, 0.0)))


def elu_slope(values):
    return jnp.where(values > 0, 1.0, jnp.exp(jnp.minimum(values, 0.0)))


def inverse_rms(values):
    return lax.rsqrt(jnp.mean(values * values, axis=-1, keepdims=True) + epsilon)


def norm_backward(values, inverse, gain_vec, grad_out):
    normal = values * inverse
    scaled = gain_vec * grad_out
    grad_in = inverse * (scaled - normal * jnp.mean(scaled * normal, axis=-1, keepdims=True))
    return grad_in


def dot(left, right, dims):
    return lax.dot_general(left, right, (dims, ((), ())), preferred_element_type=F32)


def in_two(values):
    if values.dtype == BF16:
        return (values,)
    top = values.astype(BF16)
    return top, (values - top.astype(F32)).astype(BF16)


def fine_dot(left, right, dims):
    lefts, rights = in_two(left), in_two(right)
    total = dot(lefts[0], rights[0], dims)
    for low in rights[1:]:
        total = total + dot(lefts[0], low, dims)
    for low in lefts[1:]:
        total = total + dot(low, rights[0], dims)
    return total


NN = ((1,), (0,))
NT = ((1,), (1,))
TN = ((0,), (0,))


def valid_column(valid_len):
    return (lax.broadcasted_iota(jnp.int32, (SEG_LEN, 1), 0) < valid_len).astype(F32)


def block_probs(query_block, key_rows, start, valid_len):
    scores = dot(query_block, key_rows, NT) * (DH**-0.5)
    row_pos = start + lax.broadcasted_iota(jnp.int32, scores.shape, 0)
    col_pos = lax.broadcasted_iota(jnp.int32, scores.shape, 1)
    allowed = (row_pos >= col_pos) & (col_pos < valid_len)
    scores = jnp.where(allowed, scores, masked_score)
    weights = jnp.exp(scores - jnp.max(scores, axis=-1, keepdims=True))
    return weights / jnp.sum(weights, axis=-1, keepdims=True)


def retrieve(query_feat, memory, normal):
    numerator = fine_dot(query_feat, memory, NN)
    denominator = jnp.sum(query_feat * normal, axis=-1, keepdims=True) + 1.0
    return numerator / denominator, denominator


def greet_sequence():
    seg = lax.axis_index("seg")
    place = lax.rem(seg, SEGS)
    barrier = pltpu.get_barrier_semaphore()
    for distance in range(1, SEGS):
        other = seg - place + lax.rem(place + distance, SEGS)
        pl.semaphore_signal(barrier, inc=1, device_id={"seg": other}, device_id_type=MESH)
    pl.semaphore_wait(barrier, SEGS - 1)


def sequence_copies(source, land, send_sem, recv_sem, sign):
    seg = lax.axis_index("seg")
    count = lax.axis_size("seg")
    place = lax.rem(seg, SEGS)
    copies = []
    for distance in range(1, SEGS):
        copy = pltpu.make_async_remote_copy(
            src_ref=source,
            dst_ref=land.at[distance - 1],
            send_sem=send_sem.at[distance - 1],
            recv_sem=recv_sem.at[distance - 1],
            device_id={"seg": lax.rem(seg + count + sign * distance, count)},
            device_id_type=MESH,
        )
        after, before = place + distance < SEGS, place >= distance
        copies.append((copy, after, before) if sign > 0 else (copy, before, after))
    return copies


def head_cols(head):
    return pl.ds(pl.multiple_of(head * DH, DH), DH)


def attn_front_kernel(
    gate_ref, valid_ref, query_ref, key_ref, value_ref,
    mixed_ref, local_ref, before_ref, update_ref,
    land, send_sem, recv_sem,
):
    heads = update_ref.shape[0]
    valid_len = valid_ref[0]
    greet_sequence()
    copies = sequence_copies(update_ref, land, send_sem, recv_sem, 1)

    def make_update(head, carry):
        cols = head_cols(head)
        key_feat = elu_plus(key_ref[:, cols].astype(F32)) * valid_column(valid_len)
        update_ref[head, :DH] = fine_dot(key_feat, value_ref[:, cols], TN)
        normal = jnp.sum(key_feat, axis=0, keepdims=True)
        update_ref[head, DH:] = jnp.broadcast_to(normal, (MEM_ROWS - DH, DH))
        return carry

    lax.fori_loop(0, heads, make_update, 0)
    for copy, sends, _ in copies:

        @pl.when(sends)
        def _(copy=copy):
            copy.start()

    def local(head, carry):
        cols = head_cols(head)
        for start in range(0, SEG_LEN, BLOCK):
            rows, seen = slice(start, start + BLOCK), slice(0, start + BLOCK)
            probs = block_probs(query_ref[rows, cols], key_ref[seen, cols], start, valid_len)
            local_ref[rows, cols] = dot(probs.astype(BF16), value_ref[seen, cols], NN)
        return carry

    lax.fori_loop(0, heads, local, 0)
    before_ref[...] = jnp.zeros_like(before_ref)
    for distance, (copy, sends, gets) in enumerate(copies):

        @pl.when(sends)
        def _(copy=copy):
            copy.wait_send()

        @pl.when(gets)
        def _(copy=copy, distance=distance):
            copy.wait_recv()
            before_ref[...] += land[distance]

    def mix(head, carry):
        cols = head_cols(head)
        gate = gate_ref[head]
        query_feat = elu_plus(query_ref[:, cols].astype(F32))
        memory, normal = before_ref[head, :DH], before_ref[head, DH : DH + 1]
        retrieved, _ = retrieve(query_feat, memory, normal)
        mixed_ref[:, cols] = (gate * retrieved + (1.0 - gate) * local_ref[:, cols]).astype(BF16)
        return carry

    lax.fori_loop(0, heads, mix, 0)


def attn_front(gate, valid, query, key, value, cid):
    rows, cols = query.shape
    heads = cols // DH
    scalar, vmem = pl.BlockSpec(memory_space=pltpu.SMEM), pl.BlockSpec(memory_space=pltpu.VMEM)
    memory = jax.ShapeDtypeStruct((heads, MEM_ROWS, DH), F32)
    return pl.pallas_call(
        attn_front_kernel,
        in_specs=[scalar] * 2 + [vmem] * 3,
        out_specs=[vmem] * 4,
        out_shape=[
            jax.ShapeDtypeStruct((rows, cols), BF16),
            jax.ShapeDtypeStruct((rows, cols), F32),
            memory,
            memory,
        ],
        scratch_shapes=[
            pltpu.VMEM((SEGS - 1, heads, MEM_ROWS, DH), F32),
            pltpu.SemaphoreType.DMA((SEGS - 1,)),
            pltpu.SemaphoreType.DMA((SEGS - 1,)),
        ],
        cost_estimate=pl.CostEstimate(
            flops=4 * rows * rows * cols, bytes_accessed=60 * 2**20, transcendentals=rows * rows * heads
        ),
        compiler_params=pltpu.CompilerParams(
            collective_id=cid, has_side_effects=True, vmem_limit_bytes=40 * 2**20
        ),
    )(gate, valid, query, key, value)


def attn_back_kernel(
    gate_ref, valid_ref, d_out_ref, weight_ref, query_ref, key_ref, value_ref, local_ref, memory_ref,
    d_query_ref, d_key_ref, d_value_ref, gate_grad_ref,
    d_mixed, feat, d_key_sum, d_value_sum, back, land, update, send_sem, recv_sem,
):
    heads = memory_ref.shape[0]
    valid_len = valid_ref[0]
    greet_sequence()
    copies = sequence_copies(back, land, send_sem, recv_sem, -1)
    d_mixed[...] = dot(d_out_ref[...], weight_ref[...], NT)

    def memory_back(head, carry):
        cols = head_cols(head)
        gate = gate_ref[head]
        query_vals = query_ref[:, cols].astype(F32)
        query_feat = elu_plus(query_vals)
        memory, normal = memory_ref[head, :DH], memory_ref[head, DH : DH + 1]
        retrieved, denominator = retrieve(query_feat, memory, normal)
        d_head = d_mixed[:, cols]
        gate_grad_ref[head] = jnp.broadcast_to(
            jnp.sum(d_head * (retrieved - local_ref[:, cols]), axis=0, keepdims=True), (8, DH)
        )
        d_retrieved = gate * d_head
        d_numerator = d_retrieved / denominator
        d_denominator = -jnp.sum(d_retrieved * retrieved, axis=-1, keepdims=True) / denominator
        d_feat = fine_dot(d_numerator, memory, NT) + d_denominator * normal
        feat[:, cols] = d_feat * elu_slope(query_vals)
        back[head, :DH] = fine_dot(query_feat, d_numerator, TN).astype(BF16)
        d_normal = jnp.sum(d_denominator * query_feat, axis=0, keepdims=True)
        back[head, DH:] = jnp.broadcast_to(d_normal, (MEM_ROWS - DH, DH)).astype(BF16)
        return carry

    lax.fori_loop(0, heads, memory_back, 0)
    for copy, sends, _ in copies:

        @pl.when(sends)
        def _(copy=copy):
            copy.start()

    d_key_sum[...] = jnp.zeros_like(d_key_sum)
    d_value_sum[...] = jnp.zeros_like(d_value_sum)

    def local_back(head, carry):
        cols = head_cols(head)
        keep = 1.0 - gate_ref[head]
        for start in range(0, SEG_LEN, BLOCK):
            rows, seen = slice(start, start + BLOCK), slice(0, start + BLOCK)
            query_block = query_ref[rows, cols]
            probs = block_probs(query_block, key_ref[seen, cols], start, valid_len)
            d_local = (keep * d_mixed[rows, cols]).astype(BF16)
            d_probs = dot(d_local, value_ref[seen, cols], NT)
            row_dot = jnp.sum(probs * d_probs, axis=-1, keepdims=True)
            d_scores = (probs * (d_probs - row_dot) * (DH**-0.5)).astype(BF16)
            d_query = dot(d_scores, key_ref[seen, cols], NN) + feat[rows, cols]
            d_query_ref[rows, cols] = d_query.astype(BF16)
            d_key_sum[seen, cols] += dot(d_scores, query_block, TN)
            d_value_sum[seen, cols] += dot(probs.astype(BF16), d_local, TN)
        return carry

    lax.fori_loop(0, heads, local_back, 0)
    update[...] = jnp.zeros_like(update)
    for distance, (copy, sends, gets) in enumerate(copies):

        @pl.when(sends)
        def _(copy=copy):
            copy.wait_send()

        @pl.when(gets)
        def _(copy=copy, distance=distance):
            copy.wait_recv()
            update[...] += land[distance].astype(F32)

    def finish_back(head, carry):
        cols = head_cols(head)
        valid = valid_column(valid_len)
        key_vals = key_ref[:, cols].astype(F32)
        memory, normal = update[head, :DH], update[head, DH : DH + 1]
        d_feat = (fine_dot(value_ref[:, cols], memory, NT) + normal) * valid
        d_key_ref[:, cols] = (d_key_sum[:, cols] + d_feat * elu_slope(key_vals)).astype(BF16)
        key_feat = elu_plus(key_vals) * valid
        d_value = d_value_sum[:, cols] + fine_dot(key_feat, memory, NN)
        d_value_ref[:, cols] = d_value.astype(BF16)
        return carry

    lax.fori_loop(0, heads, finish_back, 0)


def attn_back(gate, valid, d_out, weight, query, key, value, local, memory, cid):
    rows, cols = query.shape
    heads = cols // DH
    scalar, vmem = pl.BlockSpec(memory_space=pltpu.SMEM), pl.BlockSpec(memory_space=pltpu.VMEM)
    wide = pltpu.VMEM((rows, cols), F32)
    narrow = jax.ShapeDtypeStruct((rows, cols), BF16)
    return pl.pallas_call(
        attn_back_kernel,
        in_specs=[scalar] * 2 + [vmem] * 7,
        out_specs=[vmem] * 4,
        out_shape=[narrow, narrow, narrow, jax.ShapeDtypeStruct((heads, 8, DH), F32)],
        scratch_shapes=[
            wide,
            wide,
            wide,
            wide,
            pltpu.VMEM((heads, MEM_ROWS, DH), BF16),
            pltpu.VMEM((SEGS - 1, heads, MEM_ROWS, DH), BF16),
            pltpu.VMEM((heads, MEM_ROWS, DH), F32),
            pltpu.SemaphoreType.DMA((SEGS - 1,)),
            pltpu.SemaphoreType.DMA((SEGS - 1,)),
        ],
        cost_estimate=pl.CostEstimate(
            flops=10 * rows * rows * cols + 2 * rows * cols * d_out.shape[1],
            bytes_accessed=100 * 2**20,
            transcendentals=rows * rows * heads,
        ),
        compiler_params=pltpu.CompilerParams(
            collective_id=cid, has_side_effects=True, vmem_limit_bytes=48 * 2**20
        ),
    )(gate, valid, d_out, weight, query, key, value, local, memory)


def per_device(
    tokens,
    cotangent,
    gain_attn,
    gain_mlp,
    w_query,
    w_key,
    w_value,
    w_out,
    w_gate,
    w_up,
    w_down,
    mem_gate,
    lengths,
):
    seg_index = lax.axis_index("seg")
    head_index = lax.axis_index("head")
    head_groups = lax.axis_size("head")
    seg_size = lax.axis_size("seg")
    position = seg_index % SEGS
    sequence = seg_index // SEGS
    seq_length = jnp.sum(jnp.where(lax.iota(jnp.int32, lengths.shape[0]) == sequence, lengths, 0))
    valid_len = jnp.where(position == SEGS - 1, seq_length, SEG_LEN).reshape(1)
    heads = mem_gate.shape[0]
    cols = heads * DH

    token_vals = tokens.astype(F32)
    gathered_tokens, gathered_attn, query_rows, key_rows, value_rows = gather_project(
        tokens, gain_attn, w_query, w_key, w_value, head_groups, 4
    )
    cotangent, key_rows = lax.optimization_barrier((cotangent, key_rows))
    gathered_grad = lax.all_gather(cotangent, "head", axis=0, tiled=True)
    mix_sig = jax.nn.sigmoid(mem_gate)
    mixed_attn, local_attn, memory_prev, update = attn_front(
        mix_sig, valid_len, query_rows, key_rows, value_rows, 5
    )
    after = memory_prev + update
    memory_after = (after[:, :DH] * SEG_LEN ** (-0.5))[None]
    normal_after = (after[:, DH] / SEG_LEN)[None]
    all_hidden, flip_mlp, silu, slope, act, pair = attn_out_sum(
        mixed_attn, w_out, gathered_tokens, gain_mlp, w_gate, w_up, w_down, head_groups, 1
    )
    own_rows = tokens.shape[0]
    hidden_res = lax.dynamic_slice_in_dim(all_hidden, head_index * own_rows, own_rows, 0)
    d_gate_a, d_up_a, gate_a, up_a, down_a = mlp_half(
        flip_mlp, gathered_grad, silu, slope, act, w_down, 0
    )
    gate_a, up_a, down_a = lax.psum((gate_a, up_a, down_a), "seg")
    d_gate_b, d_up_b, gate_b, up_b, down_b = mlp_half(
        flip_mlp, gathered_grad, silu, slope, act, w_down, 1
    )
    gathered_hidden, d_hidden, gain_mlp_rows, down_b, gate_b = mlp_back_sum(
        (d_gate_a, d_gate_b),
        (d_up_a, d_up_b),
        w_gate,
        w_up,
        all_hidden,
        gathered_grad,
        gain_mlp,
        (down_b, gate_b),
        (BLOCK, cols),
        seg_size,
        head_groups,
        2,
    )
    d_queries, d_keys, d_values, gate_cols = attn_back(
        mix_sig,
        valid_len,
        gathered_hidden,
        w_out,
        query_rows,
        key_rows,
        value_rows,
        local_attn,
        memory_prev,
        3,
    )
    pair, grad_query, grad_key, grad_value, grad_out, gain_attn_rows = attn_weights(
        gathered_attn,
        gathered_hidden,
        mixed_attn,
        d_queries,
        d_keys,
        d_values,
        w_query,
        w_key,
        w_value,
        pair,
    )
    width = gain_attn.shape[0]
    pair = lax.psum_scatter(pair, "head", scatter_dimension=0, tiled=True)
    output = (hidden_res + pair[:, :width].astype(F32)).astype(BF16)
    d_normed_attn = pair[:, width:].astype(F32)
    grad_in_attn = norm_backward(token_vals, inverse_rms(token_vals), gain_attn, d_normed_attn)
    grad_tokens = (d_hidden + grad_in_attn).astype(BF16)
    gate_part = mix_sig * (1.0 - mix_sig) * jnp.sum(gate_cols[:, 0], axis=-1)
    slots = jnp.where(
        (lax.iota(jnp.int32, head_groups) == head_index)[:, None], gate_part[None], 0.0
    )
    gain_attn_part = jnp.sum(gain_attn_rows, axis=0) / gain_attn
    gain_mlp_part = jnp.sum(gain_mlp_rows, axis=0)
    parts = jnp.concatenate([gain_attn_part, gain_mlp_part, slots.reshape(-1)])
    lines = -(-parts.shape[0] // (8 * DH)) * 8
    parts = jnp.pad(parts, (0, lines * DH - parts.shape[0])).reshape(lines, DH)
    small, *late = grad_sum(
        parts,
        [up_b, grad_out, grad_query, grad_key, grad_value],
        (cols, cols),
        seg_size,
        head_groups,
        0,
    )
    small = small.reshape(-1)
    grad_mem_gate = lax.dynamic_slice(small, (2 * width + head_index * heads,), (heads,))
    grads = widen(
        [(1, gate_a, gate_b), (1, up_a, late[0]), (0, down_a, down_b)]
        + [(0, grad) for grad in late[1:]],
        (cols, cols),
    )
    return (
        output,
        grad_tokens,
        memory_after,
        normal_after,
        small[:width],
        small[width : 2 * width],
        grads[4],
        grads[5],
        grads[6],
        grads[3],
        grads[0],
        grads[1],
        grads[2],
        grad_mem_gate,
    )


def solution(mesh):
    return jax.shard_map(
        per_device,
        mesh=mesh,
        in_specs=(
            P(("seg", "head"), None),
            P(("seg", "head"), None),
            P(),
            P(),
            P(None, "head"),
            P(None, "head"),
            P(None, "head"),
            P("head", None),
            P(None, "head"),
            P(None, "head"),
            P("head", None),
            P("head"),
            P(),
        ),
        out_specs=(
            P(("seg", "head"), None),
            P(("seg", "head"), None),
            P("seg", "head", None, None),
            P("seg", "head", None),
            P(),
            P(),
            P(None, "head"),
            P(None, "head"),
            P(None, "head"),
            P("head", None),
            P(None, "head"),
            P(None, "head"),
            P("head", None),
            P("head"),
        ),
        check_vma=False,
    )
```

```python
import functools

import jax
import jax.numpy as jnp
from jax import lax
from jax.experimental import pallas as pl
from jax.experimental.pallas import tpu as pltpu
from jax.sharding import PartitionSpec as P

DH = 128
SEG_LEN = 1024
SEGS = 4
MEM_ROWS = DH + 16
BLOCK = 256

epsilon = 1e-05
masked_score = -1e30
F32 = jnp.float32
BF16 = jnp.bfloat16


MESH = pl.DeviceIdType.MESH
LAND_SLOTS = 12
RESULT_SLOTS = 16
SUM_SEMS = 8
SUM_HOP = 3


def bits_of(size):
    return size.bit_length() - 1


def flip(index, power):
    return index + power - 2 * power * lax.rem(index // power, 2)


def sum_engine(arrays, outs, tile, seg_bits, scratch):
    mine, result, send_sem, recv_sem, load_sem, store_sem, *lands = scratch
    seg = lax.axis_index("seg")
    planes = seg_bits - 1
    high, wide = tile
    shapes = [array.shape for array in arrays]
    counts = [(rows // high) * (cols // wide) for rows, cols in shapes]
    starts = [sum(counts[:i]) for i in range(len(counts))]
    total = sum(counts)

    def power(k, level):
        if level == 0:
            return 1
        which = lax.rem(k + level - 1, planes)
        value = 2
        for bit in range(1, planes):
            value = jnp.where(which == bit, 2 << bit, value)
        return value

    def my_bit(k, level):
        return lax.rem(seg // power(k, level), 2)

    def part(k, level, own):
        half = high >> (level + 1)
        bit = my_bit(k, level) if own else 1 - my_bit(k, level)
        return pl.ds(pl.multiple_of(bit * half, half), half)

    def kept(k, levels):
        first = 0
        for level in range(levels):
            first = first + my_bit(k, level) * (high >> (level + 1))
        return pl.ds(pl.multiple_of(first, high >> levels), high >> levels)

    def pick(k, act):
        for i in range(len(arrays)):

            @pl.when((k >= starts[i]) & (k < starts[i] + counts[i]))
            def _(i=i):
                across = shapes[i][1] // wide
                place = k - starts[i]
                row = pl.multiple_of((place // across) * high, high)
                col = pl.multiple_of(lax.rem(place, across) * wide, wide)
                act(i, row, col)

    def halving(k, level, source):
        return pltpu.make_async_remote_copy(
            src_ref=source,
            dst_ref=lands[level].at[lax.rem(k, LAND_SLOTS)],
            send_sem=send_sem.at[level, lax.rem(k, SUM_SEMS)],
            recv_sem=recv_sem.at[level, lax.rem(k, SUM_SEMS)],
            device_id={"seg": flip(seg, power(k, level))},
            device_id_type=MESH,
        )

    def first_source(k, i, row, col, own):
        half = high // 2
        bit = my_bit(k, 0) if own else 1 - my_bit(k, 0)
        return arrays[i].at[pl.ds(pl.multiple_of(row + bit * half, half), half), pl.ds(col, wide)]

    def keep(k, i, row, col):
        slot = lax.rem(k, 4)
        return pltpu.make_async_copy(
            first_source(k, i, row, col, True), mine.at[slot], load_sem.at[slot]
        )

    def level_source(k, level):
        return lands[level - 1].at[lax.rem(k, LAND_SLOTS), part(k, level, False)]

    def doubling(k, level):
        ref = result.at[lax.rem(k, RESULT_SLOTS), kept(k, level + 1)]
        return pltpu.make_async_remote_copy(
            src_ref=ref,
            dst_ref=ref,
            send_sem=send_sem.at[seg_bits + level, lax.rem(k, SUM_SEMS)],
            recv_sem=recv_sem.at[seg_bits + level, lax.rem(k, SUM_SEMS)],
            device_id={"seg": flip(seg, power(k, level))},
            device_id_type=MESH,
        )

    def store(k, i, row, col):
        slot = lax.rem(k, 4)
        return pltpu.make_async_copy(
            result.at[lax.rem(k, RESULT_SLOTS)],
            outs[i].at[pl.ds(row, high), pl.ds(col, wide)],
            store_sem.at[slot],
        )

    def do_first(k):
        def go(i, row, col):
            halving(k, 0, first_source(k, i, row, col, False)).start()
            keep(k, i, row, col).start()

        pick(k, go)

    def arrived(k, level):
        slot = lax.rem(k, LAND_SLOTS)
        if level == 0:
            halving(k, 0, first_source(k, 0, 0, 0, False)).wait()
            keep(k, 0, 0, 0).wait()
            other = mine[lax.rem(k, 4)]
        else:
            halving(k, level, level_source(k, level)).wait()
            other = lands[level - 1][slot, part(k, level, True)]
        return (lands[level][slot].astype(F32) + other.astype(F32)).astype(BF16)

    def do_level(k, level):
        lands[level - 1][lax.rem(k, LAND_SLOTS)] = arrived(k, level - 1)
        halving(k, level, level_source(k, level)).start()

    def do_total(k):
        result[lax.rem(k, RESULT_SLOTS), kept(k, seg_bits)] = arrived(k, seg_bits - 1)
        doubling(k, seg_bits - 1).start()

    def do_spread(k, level):
        doubling(k, level + 1).wait()
        doubling(k, level).start()

    def do_finish(k):
        doubling(k, 0).wait()
        pick(k, lambda i, row, col: store(k, i, row, col).start())

    def do_store(k):
        store(k, 0, 0, 0).wait()

    stages = [(0, do_first), (1, functools.partial(do_level, level=1))]
    when = 1
    for level in range(2, seg_bits):
        when += SUM_HOP
        stages.append((when, functools.partial(do_level, level=level)))
    when += SUM_HOP
    stages.append((when, do_total))
    for level in range(seg_bits - 2, -1, -1):
        when += SUM_HOP
        stages.append((when, functools.partial(do_spread, level=level)))
    stages.append((when + 1, do_finish))
    stages.append((when + 3, do_store))

    def step(t):
        for delay, act in reversed(stages):
            k = t - delay

            @pl.when((k >= 0) & (k < total))
            def _(act=act, k=k):
                act(k)

    return step, total + when + 3


def engine_scratch(tile, seg_bits):
    high, wide = tile
    return [
        pltpu.VMEM((4, high // 2, wide), BF16),
        pltpu.VMEM((RESULT_SLOTS, high, wide), BF16),
        pltpu.SemaphoreType.DMA((2 * seg_bits, SUM_SEMS)),
        pltpu.SemaphoreType.DMA((2 * seg_bits, SUM_SEMS)),
        pltpu.SemaphoreType.DMA((4,)),
        pltpu.SemaphoreType.DMA((4,)),
    ] + [pltpu.VMEM((LAND_SLOTS, high >> (l + 1), wide), BF16) for l in range(seg_bits)]


def greet_seg(seg_bits):
    barrier = pltpu.get_barrier_semaphore()
    seg = lax.axis_index("seg")
    for bit in range(seg_bits):
        pl.semaphore_signal(
            barrier, inc=1, device_id={"seg": flip(seg, 1 << bit)}, device_id_type=MESH
        )


def grad_sum_kernel(count, tile, seg_bits, head_bits, *refs):
    small_in, arrays = refs[0], refs[1 : 1 + count]
    small_out, outs = refs[1 + count], refs[2 + count : 2 + 2 * count]
    small_buf, small_land, small_send, small_recv, *scratch = refs[2 + 2 * count :]
    seg, head = lax.axis_index("seg"), lax.axis_index("head")
    greet_seg(seg_bits)
    barrier = pltpu.get_barrier_semaphore()
    for bit in range(head_bits):
        pl.semaphore_signal(
            barrier, inc=1, device_id={"head": flip(head, 1 << bit)}, device_id_type=MESH
        )
    pl.semaphore_wait(barrier, seg_bits + head_bits)
    rounds = seg_bits + head_bits

    def small_copy(j):
        if j < seg_bits:
            where = {"seg": flip(seg, 1 << j)}
        else:
            where = {"head": flip(head, 1 << (j - seg_bits))}
        return pltpu.make_async_remote_copy(
            src_ref=small_buf.at[j],
            dst_ref=small_land.at[j],
            send_sem=small_send.at[j],
            recv_sem=small_recv.at[j],
            device_id=where,
            device_id_type=MESH,
        )

    engine_step, steps = sum_engine(arrays, outs, tile, seg_bits, scratch)

    def step(t, carry):
        engine_step(t)
        for j in range(rounds + 1):

            @pl.when(t == 3 * j)
            def _(j=j):
                if j == 0:
                    small_buf[0] = small_in[...]
                else:
                    small_copy(j - 1).wait()
                    value = small_buf[j - 1] + small_land[j - 1]
                    if j < rounds:
                        small_buf[j] = value
                    else:
                        small_out[...] = value
                if j < rounds:
                    small_copy(j).start()

        return carry

    lax.fori_loop(0, max(steps, 3 * rounds + 1), step, 0)


def grad_sum(small, arrays, tile, seg_size, head_size, cid):
    seg_bits, head_bits = bits_of(seg_size), bits_of(head_size)
    rounds = seg_bits + head_bits
    count = len(arrays)
    moved = sum(rows * cols for rows, cols in (array.shape for array in arrays))
    any_, vmem = pl.BlockSpec(memory_space=pltpu.HBM), pl.BlockSpec(memory_space=pltpu.VMEM)
    return pl.pallas_call(
        functools.partial(grad_sum_kernel, count, tile, seg_bits, head_bits),
        in_specs=[vmem] + [any_] * count,
        out_specs=[vmem] + [any_] * count,
        out_shape=[jax.ShapeDtypeStruct(small.shape, F32)]
        + [jax.ShapeDtypeStruct(array.shape, BF16) for array in arrays],
        scratch_shapes=[
            pltpu.VMEM((rounds, *small.shape), F32),
            pltpu.VMEM((rounds, *small.shape), F32),
            pltpu.SemaphoreType.DMA((rounds,)),
            pltpu.SemaphoreType.DMA((rounds,)),
        ]
        + engine_scratch(tile, seg_bits),
        cost_estimate=pl.CostEstimate(flops=0, bytes_accessed=moved * 60, transcendentals=0),
        compiler_params=pltpu.CompilerParams(
            collective_id=cid, has_side_effects=True, vmem_limit_bytes=60 * 2**20
        ),
    )(small, *arrays)


ROWS = 32
FIRST_HOP = 2
SECOND_HOP = 4
SEND_SLOTS = 6
BLOCK_ROWS = 256
FORWARD_ROWS = 128
UNIT_GROUP = 1024
LINE_REFS = 8


def line_exchange(own, finish, before, scratch, hop, extra, extra_steps):
    up_land, down_land, up_send, down_send, up_recv_sem, down_recv_sem, up_send_sem, down_send_sem = scratch
    size = lax.axis_size("head")
    place = lax.axis_index("head")
    slots = up_land.shape[0]
    chunks = own.shape[0] // ROWS
    last = size - 1

    def up_copy(k):
        return pltpu.make_async_remote_copy(
            src_ref=up_send.at[lax.rem(k, SEND_SLOTS)],
            dst_ref=up_land.at[lax.rem(k, slots)],
            send_sem=up_send_sem.at[lax.rem(k, SEND_SLOTS)],
            recv_sem=up_recv_sem.at[lax.rem(k, slots)],
            device_id={"head": lax.rem(place + 1, size)},
            device_id_type=MESH,
        )

    def down_copy(k):
        return pltpu.make_async_remote_copy(
            src_ref=down_send.at[lax.rem(k, SEND_SLOTS)],
            dst_ref=down_land.at[lax.rem(k, slots)],
            send_sem=down_send_sem.at[lax.rem(k, SEND_SLOTS)],
            recv_sem=down_recv_sem.at[lax.rem(k, slots)],
            device_id={"head": lax.rem(place + last, size)},
            device_id_type=MESH,
        )

    def rows_of(k):
        return pl.ds(pl.multiple_of(k * ROWS, ROWS), ROWS)

    def pass_on(k, copy, land, send, has_source, has_target):
        @pl.when(has_source)
        def _():
            copy(k).wait_recv()

        @pl.when(has_target)
        def _():
            slot = lax.rem(k, SEND_SLOTS)

            @pl.when(k >= SEND_SLOTS)
            def _():
                copy(k - SEND_SLOTS).wait_send()

            @pl.when(has_source)
            def _():
                send[slot] = (own[rows_of(k)] + land[lax.rem(k, slots)].astype(F32)).astype(BF16)

            @pl.when(jnp.logical_not(has_source))
            def _():
                send[slot] = own[rows_of(k)].astype(BF16)

            copy(k).start()

    far = jnp.maximum(place, last - place)

    def step(t, carry):
        before(t)
        down = t - (last - place) * hop

        @pl.when((down >= 0) & (down < chunks))
        def _():
            pass_on(down, down_copy, down_land, down_send, place < last, place > 0)

        up = t - place * hop

        @pl.when((up >= 0) & (up < chunks))
        def _():
            pass_on(up, up_copy, up_land, up_send, place > 0, place < last)

        k = t - far * hop

        @pl.when((k >= 0) & (k < chunks))
        def _():
            slot = lax.rem(k, slots)

            @pl.when(place == 0)
            def _():
                finish(k, own[rows_of(k)] + down_land[slot].astype(F32))

            @pl.when(place == last)
            def _():
                finish(k, own[rows_of(k)] + up_land[slot].astype(F32))

            @pl.when((place > 0) & (place < last))
            def _():
                finish(
                    k,
                    own[rows_of(k)] + up_land[slot].astype(F32) + down_land[slot].astype(F32),
                )

        extra(t)
        return carry

    lax.fori_loop(0, max(chunks + last * hop, extra_steps), step, 0)
    for k in range(chunks - SEND_SLOTS, chunks):

        @pl.when(place < last)
        def _(k=k):
            up_copy(k).wait_send()

        @pl.when(place > 0)
        def _(k=k):
            down_copy(k).wait_send()


def line_barrier(others=0):
    size = lax.axis_size("head")
    place = lax.axis_index("head")
    barrier = pltpu.get_barrier_semaphore()
    inner = (place > 0) & (place < size - 1)

    def greet(near):
        pl.semaphore_signal(
            barrier, inc=1, device_id={"head": lax.rem(near, size)}, device_id_type=MESH
        )

    @pl.when(place > 0)
    def _():
        greet(place + size - 1)

    @pl.when(place < size - 1)
    def _():
        greet(place + 1)

    @pl.when(inner)
    def _():
        pl.semaphore_wait(barrier, 2 + others)

    @pl.when(jnp.logical_not(inner))
    def _():
        pl.semaphore_wait(barrier, 1 + others)


def line_scratch(size, width, hop):
    slots = (size - 1) * hop + 2
    return [
        pltpu.VMEM((slots, ROWS, width), BF16),
        pltpu.VMEM((slots, ROWS, width), BF16),
        pltpu.VMEM((SEND_SLOTS, ROWS, width), BF16),
        pltpu.VMEM((SEND_SLOTS, ROWS, width), BF16),
        pltpu.SemaphoreType.DMA((slots,)),
        pltpu.SemaphoreType.DMA((slots,)),
        pltpu.SemaphoreType.DMA((SEND_SLOTS,)),
        pltpu.SemaphoreType.DMA((SEND_SLOTS,)),
    ]


GATHER_PARTS = 4


def gather_kernel(
    token_hbm, gain_ref, w_query_hbm, w_key_hbm, w_value_hbm,
    all_ref, normed_ref, query_ref, key_ref, value_ref,
    land, normed, w_query, w_key, w_value,
    own_sem, load_sem, all_sem, normed_sem, up_send, up_recv, down_send, down_recv,
):
    size = lax.axis_size("head")
    place = lax.axis_index("head")
    last = size - 1
    own_rows = token_hbm.shape[0]
    chunk = own_rows // GATHER_PARTS
    loads = [
        pltpu.make_async_copy(source, target, load_sem.at[i])
        for i, (source, target) in enumerate(
            ((w_key_hbm, w_key), (w_value_hbm, w_value), (w_query_hbm, w_query))
        )
    ]

    def shard_rows(shard):
        return pl.ds(pl.multiple_of(shard * own_rows, own_rows), own_rows)

    own = pltpu.make_async_copy(token_hbm, land.at[shard_rows(place)], own_sem)
    own.start()
    for load in loads:
        load.start()
    line_barrier()

    def chunk_copy(shard, i, send_sem, recv_sem, target):
        first = pl.multiple_of(shard * own_rows + lax.rem(i, GATHER_PARTS) * chunk, chunk)
        ref = land.at[pl.ds(first, chunk)]
        return pltpu.make_async_remote_copy(
            src_ref=ref,
            dst_ref=ref,
            send_sem=send_sem.at[i],
            recv_sem=recv_sem.at[i],
            device_id={"head": target},
            device_id_type=MESH,
        )

    above, below = lax.rem(place + 1, size), lax.rem(place + last, size)

    def up_copy(i, first_shard):
        return chunk_copy(first_shard - i // GATHER_PARTS, i, up_send, up_recv, above)

    def down_copy(i, first_shard):
        return chunk_copy(first_shard + i // GATHER_PARTS, i, down_send, down_recv, below)

    own.wait()
    for i in range(GATHER_PARTS):

        @pl.when(place < last)
        def _(i=i):
            up_copy(i, place).start()

        @pl.when(place > 0)
        def _(i=i):
            down_copy(i, place).start()

    def stores(shard):
        rows = shard_rows(shard)
        return (
            pltpu.make_async_copy(land.at[rows], all_ref.at[rows], all_sem.at[shard]),
            pltpu.make_async_copy(normed.at[rows], normed_ref.at[rows], normed_sem.at[shard]),
        )

    def project(shard):
        rows = shard_rows(shard)
        value = land[rows].astype(F32)
        normed[rows] = (value * inverse_rms(value) * gain_ref[...]).astype(BF16)
        for copy in stores(shard):
            copy.start()
        for weight, target in ((w_key, key_ref), (w_value, value_ref), (w_query, query_ref)):
            target[rows] = dot(normed[rows], weight[...], NN).astype(BF16)

    for load in loads:
        load.wait()
    project(place)

    def step(i, carry):
        @pl.when(i < place * GATHER_PARTS)
        def _():
            up_copy(i, place - 1).wait_recv()

            @pl.when(place < last)
            def _():
                up_copy(i + GATHER_PARTS, place).start()

        @pl.when(i < (last - place) * GATHER_PARTS)
        def _():
            down_copy(i, place + 1).wait_recv()

            @pl.when(place > 0)
            def _():
                down_copy(i + GATHER_PARTS, place).start()

        distance = (i + 1) // GATHER_PARTS
        whole = lax.rem(i + 1, GATHER_PARTS) == 0

        @pl.when(whole & (place >= distance))
        def _():
            project(place - distance)

        @pl.when(whole & (place + distance <= last))
        def _():
            project(place + distance)

        return carry

    lax.fori_loop(0, last * GATHER_PARTS, step, 0)

    def drain(i, carry):
        @pl.when((place < last) & (i < (place + 1) * GATHER_PARTS))
        def _():
            up_copy(i, place).wait_send()

        @pl.when((place > 0) & (i < (size - place) * GATHER_PARTS))
        def _():
            down_copy(i, place).wait_send()

        return carry

    lax.fori_loop(0, size * GATHER_PARTS, drain, 0)
    for shard in range(size):
        for copy in stores(shard):
            copy.wait()


def gather_project(tokens, gain, w_query, w_key, w_value, size, cid):
    own_rows, width = tokens.shape
    rows, cols = own_rows * size, w_query.shape[1]
    vmem, any_ = pl.BlockSpec(memory_space=pltpu.VMEM), pl.BlockSpec(memory_space=pltpu.HBM)
    weight = pltpu.VMEM((width, cols), BF16)
    hops = pltpu.SemaphoreType.DMA((size * GATHER_PARTS,))
    return pl.pallas_call(
        gather_kernel,
        in_specs=[any_, vmem] + [any_] * 3,
        out_specs=[any_, any_, vmem, vmem, vmem],
        out_shape=[jax.ShapeDtypeStruct((rows, width), BF16)] * 2
        + [jax.ShapeDtypeStruct((rows, cols), BF16)] * 3,
        scratch_shapes=[
            pltpu.VMEM((rows, width), BF16),
            pltpu.VMEM((rows, width), BF16),
            weight,
            weight,
            weight,
            pltpu.SemaphoreType.DMA(()),
            pltpu.SemaphoreType.DMA((3,)),
            pltpu.SemaphoreType.DMA((size,)),
            pltpu.SemaphoreType.DMA((size,)),
            hops,
            hops,
            hops,
            hops,
        ],
        cost_estimate=pl.CostEstimate(
            flops=6 * rows * width * cols, bytes_accessed=150 * 2**20, transcendentals=0
        ),
        compiler_params=pltpu.CompilerParams(
            collective_id=cid, has_side_effects=True, vmem_limit_bytes=48 * 2**20
        ),
    )(tokens, gain.reshape(1, width), w_query, w_key, w_value)


def attn_out_kernel(
    mixed_ref, weight_ref, token_ref, gain_ref, w_gate_hbm, w_up_hbm, w_down_hbm,
    hidden_ref, flip_ref, silu_ref, slope_ref, act_ref, part_ref,
    hidden, normed, w_gate, w_up, w_down, silu, slope, act, flip, part, part_out,
    hidden_sem, load_sem, out_sem, block_sem, *scratch
):
    loads = [
        pltpu.make_async_copy(source, target, load_sem.at[i])
        for i, (source, target) in enumerate(
            ((w_gate_hbm, w_gate), (w_up_hbm, w_up), (w_down_hbm, w_down))
        )
    ]
    for load in loads:
        load.start()
    line_barrier()
    per_block = FORWARD_ROWS // ROWS
    blocks = hidden.shape[0] // FORWARD_ROWS
    groups = w_gate.shape[1] // UNIT_GROUP
    slots = act.shape[0]
    lag = per_block + (lax.axis_size("head") - 1) * FIRST_HOP
    pace = per_block // groups

    def block_rows(b):
        return pl.ds(pl.multiple_of(b * FORWARD_ROWS, FORWARD_ROWS), FORWARD_ROWS)

    def unit_copies(u):
        slot = lax.rem(u, slots)
        where = (block_rows(u // groups), unit_cols(u))
        return [
            pltpu.make_async_copy(source.at[slot], target.at[where], out_sem.at[i, slot])
            for i, (source, target) in enumerate(
                ((silu, silu_ref), (slope, slope_ref), (act, act_ref))
            )
        ]

    def unit_cols(u):
        return pl.ds(pl.multiple_of(lax.rem(u, groups) * UNIT_GROUP, UNIT_GROUP), UNIT_GROUP)

    def flip_copy(b):
        return pltpu.make_async_copy(flip, flip_ref.at[:, block_rows(b)], block_sem.at[0])

    def part_copy(b):
        where = (block_rows(b), pl.ds(0, part_out.shape[1]))
        return pltpu.make_async_copy(part_out, part_ref.at[where], block_sem.at[1])

    def forward(u):
        slot = lax.rem(u, slots)
        b, group = u // groups, lax.rem(u, groups)

        @pl.when(group == 0)
        def _():
            @pl.when(b > 0)
            def _():
                flip_copy(b - 1).wait()

            flip[...] = normed[block_rows(b)].T
            flip_copy(b).start()

        @pl.when(u >= slots)
        def _():
            for copy in unit_copies(u - slots):
                copy.wait()

        rows, cols = normed[block_rows(u // groups)], unit_cols(u)
        gate_pre = dot(rows, w_gate[:, cols], NN)
        up_proj = dot(rows, w_up[:, cols], NN)
        gate_sig = jax.nn.sigmoid(gate_pre)
        silu_gate = gate_pre * gate_sig
        silu[slot] = silu_gate
        slope[slot] = up_proj * gate_sig * (1.0 + gate_pre * (1.0 - gate_sig))
        act[slot] = (silu_gate * up_proj).astype(BF16)
        for copy in unit_copies(u):
            copy.start()
        share = dot(act[slot], w_down[cols], NN)

        @pl.when(group == 0)
        def _():
            part[...] = share

        @pl.when(group > 0)
        def _():
            part[...] += share

        @pl.when(group == groups - 1)
        def _():
            @pl.when(b > 0)
            def _():
                part_copy(b - 1).wait()

            part_out[...] = part[...].astype(BF16)
            part_copy(b).start()

    def before(t):
        @pl.when((lax.rem(t, per_block) == 0) & (t < blocks * per_block))
        def _():
            rows = block_rows(t // per_block)
            hidden[rows] = dot(mixed_ref[rows], weight_ref[...], NN)

    def after(t):
        @pl.when(t == lag)
        def _():
            for load in loads:
                load.wait()

        late = t - lag

        @pl.when((late >= 0) & (lax.rem(late, pace) == 0) & (late // pace < blocks * groups))
        def _():
            forward(late // pace)

    def store(b):
        rows = block_rows(b)
        return pltpu.make_async_copy(hidden.at[rows], hidden_ref.at[rows], hidden_sem.at[b])

    def finish(k, total):
        rows = pl.ds(pl.multiple_of(k * ROWS, ROWS), ROWS)
        value = token_ref[rows].astype(F32) + total
        hidden[rows] = value
        normed[rows] = (value * inverse_rms(value) * gain_ref[...]).astype(BF16)

        @pl.when(lax.rem(k, per_block) == per_block - 1)
        def _():
            store(k // per_block).start()

    line_exchange(hidden, finish, before, scratch, FIRST_HOP, after, lag + blocks * per_block)
    for b in range(blocks):
        store(b).wait()
    flip_copy(blocks - 1).wait()
    part_copy(blocks - 1).wait()
    for u in range(blocks * groups - slots, blocks * groups):
        for copy in unit_copies(u):
            copy.wait()


def attn_out_sum(mixed, weight, tokens, gain, w_gate, w_up, w_down, size, cid):
    rows, width = tokens.shape
    units = w_gate.shape[1]
    vmem, any_ = pl.BlockSpec(memory_space=pltpu.VMEM), pl.BlockSpec(memory_space=pltpu.HBM)
    blocks, slots = rows // FORWARD_ROWS, 2
    return pl.pallas_call(
        attn_out_kernel,
        in_specs=[vmem] * 4 + [any_] * 3,
        out_specs=[any_] * 6,
        out_shape=[
            jax.ShapeDtypeStruct((rows, width), F32),
            jax.ShapeDtypeStruct((width, rows), BF16),
            jax.ShapeDtypeStruct((rows, units), F32),
            jax.ShapeDtypeStruct((rows, units), F32),
            jax.ShapeDtypeStruct((rows, units), BF16),
            jax.ShapeDtypeStruct((rows, 2 * width), BF16),
        ],
        scratch_shapes=[
            pltpu.VMEM((rows, width), F32),
            pltpu.VMEM((rows, width), BF16),
            pltpu.VMEM((width, units), BF16),
            pltpu.VMEM((width, units), BF16),
            pltpu.VMEM((units, width), BF16),
            pltpu.VMEM((slots, FORWARD_ROWS, UNIT_GROUP), F32),
            pltpu.VMEM((slots, FORWARD_ROWS, UNIT_GROUP), F32),
            pltpu.VMEM((slots, FORWARD_ROWS, UNIT_GROUP), BF16),
            pltpu.VMEM((width, FORWARD_ROWS), BF16),
            pltpu.VMEM((FORWARD_ROWS, width), F32),
            pltpu.VMEM((FORWARD_ROWS, width), BF16),
            pltpu.SemaphoreType.DMA((blocks,)),
            pltpu.SemaphoreType.DMA((3,)),
            pltpu.SemaphoreType.DMA((3, slots)),
            pltpu.SemaphoreType.DMA((2,)),
        ]
        + line_scratch(size, width, FIRST_HOP),
        cost_estimate=pl.CostEstimate(
            flops=2 * rows * width * (mixed.shape[1] + 3 * units),
            bytes_accessed=250 * 2**20,
            transcendentals=rows * units,
        ),
        compiler_params=pltpu.CompilerParams(
            collective_id=cid, has_side_effects=True, vmem_limit_bytes=60 * 2**20
        ),
    )(mixed, weight, tokens, gain.reshape(1, width), w_gate, w_up, w_down)


def mlp_back_kernel(
    tile, seg_bits,
    d_gate_a, d_gate_b, d_up_a, d_up_b, w_gate_hbm, w_up_hbm, hidden_hbm, grad_hbm, gain_ref,
    down_in, gate_in,
    d_out_ref, d_own_ref, gain_part_ref, down_out, gate_out,
    d_gate, d_up, w_gate, w_up, hidden, grad, own, load_sem, store_sem, *scratch
):
    per_block = BLOCK_ROWS // ROWS
    blocks = own.shape[0] // BLOCK_ROWS
    size = lax.axis_size("head")
    place = lax.axis_index("head")
    per_device = own.shape[0] // ROWS // size
    half = d_gate.shape[1] // 2
    low, high = pl.ds(0, half), pl.ds(half, half)
    loads = [
        pltpu.make_async_copy(source, target, load_sem.at[i])
        for i, (source, target) in enumerate(
            ((d_gate_a, d_gate.at[:, low]), (d_gate_b, d_gate.at[:, high]), (w_gate_hbm, w_gate),
             (d_up_a, d_up.at[:, low]), (d_up_b, d_up.at[:, high]), (w_up_hbm, w_up),
             (hidden_hbm, hidden), (grad_hbm, grad))
        )
    ]
    for load in loads:
        load.start()
    gain_part_ref[...] = jnp.zeros_like(gain_part_ref)
    greet_seg(seg_bits)
    line_barrier(seg_bits)
    engine_step, steps = sum_engine(
        [down_in, gate_in], [down_out, gate_out], tile, seg_bits, scratch[LINE_REFS:]
    )

    def block_rows(b):
        return pl.ds(pl.multiple_of(b * BLOCK_ROWS, BLOCK_ROWS), BLOCK_ROWS)

    for load in loads[:3]:
        load.wait()

    def before(t):
        @pl.when((lax.rem(t, per_block) == 0) & (t < blocks * per_block))
        def _():
            rows = block_rows(t // per_block)
            own[rows] = dot(d_gate[rows], w_gate[...], NT)

            @pl.when(t == 0)
            def _():
                for load in loads[3:6]:
                    load.wait()

            own[rows] += dot(d_up[rows], w_up[...], NT)

        @pl.when(t == 1)
        def _():
            for load in loads[6:]:
                load.wait()

    def store(b):
        rows = block_rows(b)
        return pltpu.make_async_copy(grad.at[rows], d_out_ref.at[rows], store_sem.at[b])

    def finish(k, total):
        rows = pl.ds(pl.multiple_of(k * ROWS, ROWS), ROWS)
        value = hidden[rows]
        inverse = inverse_rms(value)
        normal = value * inverse
        scaled = gain_ref[...] * total
        mean = jnp.mean(scaled * normal, axis=-1, keepdims=True)
        d_hidden = grad[rows].astype(F32) + inverse * (scaled - normal * mean)
        grad[rows] = d_hidden.astype(BF16)

        @pl.when(k // per_device == place)
        def _():
            mine = pl.ds(pl.multiple_of(lax.rem(k, per_device) * ROWS, ROWS), ROWS)
            d_own_ref[mine] = d_hidden
            gain_part_ref[...] += jnp.sum((total * normal).reshape(ROWS // 8, 8, -1), axis=0)

        @pl.when(lax.rem(k, per_block) == per_block - 1)
        def _():
            store(k // per_block).start()

    line_exchange(own, finish, before, scratch[:LINE_REFS], SECOND_HOP, engine_step, steps)
    for b in range(blocks):
        store(b).wait()


def mlp_back_sum(
    d_gate, d_up, w_gate, w_up, hidden, grad, gain, summed, tile, seg_size, size, cid
):
    rows, width = hidden.shape
    units = w_gate.shape[1]
    seg_bits = bits_of(seg_size)
    vmem, any_ = pl.BlockSpec(memory_space=pltpu.VMEM), pl.BlockSpec(memory_space=pltpu.HBM)
    blocks = rows // BLOCK_ROWS
    return pl.pallas_call(
        functools.partial(mlp_back_kernel, tile, seg_bits),
        in_specs=[any_] * 8 + [vmem, any_, any_],
        out_specs=[any_, vmem, vmem, any_, any_],
        out_shape=[
            jax.ShapeDtypeStruct((rows, width), BF16),
            jax.ShapeDtypeStruct((rows // size, width), F32),
            jax.ShapeDtypeStruct((8, width), F32),
        ]
        + [jax.ShapeDtypeStruct(array.shape, BF16) for array in summed],
        scratch_shapes=[
            pltpu.VMEM((rows, units), BF16),
            pltpu.VMEM((rows, units), BF16),
            pltpu.VMEM((width, units), BF16),
            pltpu.VMEM((width, units), BF16),
            pltpu.VMEM((rows, width), F32),
            pltpu.VMEM((rows, width), BF16),
            pltpu.VMEM((rows, width), F32),
            pltpu.SemaphoreType.DMA((8,)),
            pltpu.SemaphoreType.DMA((blocks,)),
        ]
        + line_scratch(size, width, SECOND_HOP)
        + engine_scratch(tile, seg_bits),
        cost_estimate=pl.CostEstimate(
            flops=4 * rows * width * units, bytes_accessed=250 * 2**20, transcendentals=0
        ),
        compiler_params=pltpu.CompilerParams(
            collective_id=cid, has_side_effects=True, vmem_limit_bytes=62 * 2**20
        ),
    )(*d_gate, *d_up, w_gate, w_up, hidden, grad, gain.reshape(1, width), *summed)


MLP_BLOCK = 512


def mlp_kernel(
    flip_ref, grad_ref, silu_ref, slope_ref, act_ref, w_down_ref,
    d_gate_ref, d_up_ref, grad_gate_ref, grad_up_ref, grad_down_ref,
):
    width = flip_ref.shape[0]
    d_act = dot(grad_ref[...], w_down_ref[...], NT)
    d_gate_ref[...] = (d_act * slope_ref[...]).astype(BF16)
    d_up_ref[...] = (d_act * silu_ref[...]).astype(BF16)
    half = width // 2
    for i in range(2):
        part = slice(i * half, (i + 1) * half)
        grad_gate_ref[part] = dot(flip_ref[part], d_gate_ref[...], NN).astype(BF16)
        grad_up_ref[part] = dot(flip_ref[part], d_up_ref[...], NN).astype(BF16)
        grad_down_ref[:, part] = dot(act_ref[...], grad_ref[:, part], TN).astype(BF16)


def mlp_half(flip, grad, silu, slope, act, w_down, which):
    width, count = flip.shape
    units = act.shape[1] // 2
    block = min(MLP_BLOCK, units)
    first = which * (units // block)
    once = pl.Buffered(1)
    side = pl.BlockSpec((count, block), lambda j: (0, first + j))
    side_out = pl.BlockSpec((count, block), lambda j: (0, j))
    tall = pl.BlockSpec((width, block), lambda j: (0, j))
    return pl.pallas_call(
        mlp_kernel,
        grid=(units // block,),
        in_specs=[
            pl.BlockSpec((width, count), lambda j: (0, 0), pipeline_mode=once),
            pl.BlockSpec((count, width), lambda j: (0, 0), pipeline_mode=once),
            side,
            side,
            side,
            pl.BlockSpec((block, width), lambda j: (first + j, 0)),
        ],
        out_specs=[side_out, side_out, tall, tall, pl.BlockSpec((block, width), lambda j: (j, 0))],
        out_shape=[
            jax.ShapeDtypeStruct((count, units), BF16),
            jax.ShapeDtypeStruct((count, units), BF16),
            jax.ShapeDtypeStruct((width, units), BF16),
            jax.ShapeDtypeStruct((width, units), BF16),
            jax.ShapeDtypeStruct((units, width), BF16),
        ],
        cost_estimate=pl.CostEstimate(
            flops=8 * count * width * units,
            bytes_accessed=2 * (2 * count * width + 4 * width * units + 7 * count * units),
            transcendentals=0,
        ),
        compiler_params=pltpu.CompilerParams(vmem_limit_bytes=56 * 2**20),
    )(flip, grad, silu, slope, act, w_down)


WIDEN_SLOTS = 4


def widen_kernel(shapes, places, wide_count, tile, *refs):
    count = len(shapes)
    sources, targets = refs[:count], refs[count : count + wide_count]
    narrow, wide, load_sem, store_sem = refs[count + wide_count :]
    high, broad = tile
    counts = [(rows // high) * (width // broad) for rows, width in shapes]
    total = sum(counts)

    def pick(k, act):
        first = 0
        for i in range(count):
            @pl.when((k >= first) & (k < first + counts[i]))
            def _(i=i, first=first):
                across = shapes[i][1] // broad
                place = k - first
                row = pl.multiple_of((place // across) * high, high)
                col = pl.multiple_of(lax.rem(place, across) * broad, broad)
                act(i, (pl.ds(row, high), pl.ds(col, broad)))
            first += counts[i]

    def load(k, i, where):
        slot = lax.rem(k, WIDEN_SLOTS)
        return pltpu.make_async_copy(sources[i].at[where], narrow.at[slot], load_sem.at[slot])

    def store(k, i, where):
        slot = lax.rem(k, WIDEN_SLOTS)
        target, row, col = places[i]
        rows = pl.ds(pl.multiple_of(row + where[0].start, high), high)
        cols = pl.ds(pl.multiple_of(col + where[1].start, broad), broad)
        return pltpu.make_async_copy(
            wide.at[slot], targets[target].at[rows, cols], store_sem.at[slot]
        )

    zero = (pl.ds(0, high), pl.ds(0, broad))
    ahead = WIDEN_SLOTS - 1
    for k in range(ahead):
        pick(k, lambda i, where, k=k: load(k, i, where).start())

    def step(k, carry):
        @pl.when(k + ahead < total)
        def _():
            pick(k + ahead, lambda i, where: load(k + ahead, i, where).start())

        @pl.when(k >= WIDEN_SLOTS)
        def _():
            store(k - WIDEN_SLOTS, 0, zero).wait()

        load(k, 0, zero).wait()
        slot = lax.rem(k, WIDEN_SLOTS)
        wide[slot] = narrow[slot].astype(F32)
        pick(k, lambda i, where: store(k, i, where).start())
        return carry

    lax.fori_loop(0, total, step, 0)
    for k in range(total - WIDEN_SLOTS, total):
        store(k, 0, zero).wait()


def widen(groups, tile):
    arrays, places, targets = [], [], []
    for axis, *group in groups:
        shape = [0, 0]
        shape[1 - axis] = group[0].shape[1 - axis]
        for value in group:
            arrays.append(value)
            places.append((len(targets), *((shape[0], 0) if axis == 0 else (0, shape[1]))))
            shape[axis] += value.shape[axis]
        targets.append(tuple(shape))
    shapes = [value.shape for value in arrays]
    any_ = pl.BlockSpec(memory_space=pltpu.HBM)
    return pl.pallas_call(
        functools.partial(widen_kernel, shapes, places, len(targets), tile),
        in_specs=[any_] * len(arrays),
        out_specs=[any_] * len(targets),
        out_shape=[jax.ShapeDtypeStruct(shape, F32) for shape in targets],
        scratch_shapes=[
            pltpu.VMEM((WIDEN_SLOTS, *tile), BF16),
            pltpu.VMEM((WIDEN_SLOTS, *tile), F32),
            pltpu.SemaphoreType.DMA((WIDEN_SLOTS,)),
            pltpu.SemaphoreType.DMA((WIDEN_SLOTS,)),
        ],
        cost_estimate=pl.CostEstimate(
            flops=0, bytes_accessed=6 * sum(r * c for r, c in shapes), transcendentals=0
        ),
        compiler_params=pltpu.CompilerParams(vmem_limit_bytes=60 * 2**20),
    )(*arrays)


def attn_weights_kernel(
    rows_ref, d_out_ref, mixed_ref, d_query_ref, d_key_ref, d_value_ref,
    w_query_ref, w_key_ref, w_value_ref, pair_ref,
    d_rows_ref, grad_query_ref, grad_key_ref, grad_value_ref, grad_out_ref, gain_part_ref,
    flipped_mixed, flipped_rows,
):
    @pl.when(pl.program_id(0) == 0)
    def _():
        flipped_mixed[...] = mixed_ref[...].T

    flipped_rows[...] = rows_ref[...].T
    d_rows = (
        dot(d_query_ref[...], w_query_ref[...], NT)
        + dot(d_key_ref[...], w_key_ref[...], NT)
        + dot(d_value_ref[...], w_value_ref[...], NT)
    )
    d_rows_ref[...] = d_rows.astype(BF16)
    product = d_rows * rows_ref[...].astype(F32)
    gain_part_ref[...] = jnp.sum(product.reshape(-1, 8, product.shape[1]), axis=0)
    grad_query_ref[...] = dot(flipped_rows[...], d_query_ref[...], NN).astype(BF16)
    grad_key_ref[...] = dot(flipped_rows[...], d_key_ref[...], NN).astype(BF16)
    grad_value_ref[...] = dot(flipped_rows[...], d_value_ref[...], NN).astype(BF16)
    grad_out_ref[...] = dot(flipped_mixed[...], d_out_ref[...], NN).astype(BF16)


def attn_weights(rows, d_out, mixed, d_query, d_key, d_value, w_query, w_key, w_value, pair):
    count, width = rows.shape
    cols = mixed.shape[1]
    block = 512
    once = pl.Buffered(1)
    slim = pl.BlockSpec((count, cols), lambda j: (0, 0), pipeline_mode=once)
    side = pl.BlockSpec((count, block), lambda j: (0, j))
    right = pl.BlockSpec((count, block), lambda j: (0, width // block + j))
    tall = pl.BlockSpec((block, cols), lambda j: (j, 0))
    wide = pl.BlockSpec((cols, block), lambda j: (0, j))
    tall_type = jax.ShapeDtypeStruct((width, cols), BF16)
    return pl.pallas_call(
        attn_weights_kernel,
        grid=(width // block,),
        in_specs=[side, side, slim, slim, slim, slim, tall, tall, tall]
        + [pl.BlockSpec(memory_space=pltpu.HBM)],
        out_specs=[right, tall, tall, tall, wide, pl.BlockSpec((8, block), lambda j: (0, j))],
        out_shape=[
            jax.ShapeDtypeStruct(pair.shape, BF16),
            tall_type,
            tall_type,
            tall_type,
            jax.ShapeDtypeStruct((cols, width), BF16),
            jax.ShapeDtypeStruct((8, width), F32),
        ],
        input_output_aliases={9: 0},
        scratch_shapes=[pltpu.VMEM((cols, count), BF16), pltpu.VMEM((block, count), BF16)],
        cost_estimate=pl.CostEstimate(
            flops=14 * count * width * cols,
            bytes_accessed=2 * (3 * count * width + 4 * count * cols + 7 * width * cols),
            transcendentals=0,
        ),
        compiler_params=pltpu.CompilerParams(vmem_limit_bytes=48 * 2**20),
    )(rows, d_out, mixed, d_query, d_key, d_value, w_query, w_key, w_value, pair)


def elu_plus(values):
    return jnp.where(values > 0, values + 1.0, jnp.exp(jnp.minimum(values, 0.0)))


def elu_slope(values):
    return jnp.where(values > 0, 1.0, jnp.exp(jnp.minimum(values, 0.0)))


def inverse_rms(values):
    return lax.rsqrt(jnp.mean(values * values, axis=-1, keepdims=True) + epsilon)


def norm_backward(values, inverse, gain_vec, grad_out):
    normal = values * inverse
    scaled = gain_vec * grad_out
    grad_in = inverse * (scaled - normal * jnp.mean(scaled * normal, axis=-1, keepdims=True))
    return grad_in


def dot(left, right, dims):
    return lax.dot_general(left, right, (dims, ((), ())), preferred_element_type=F32)


def in_two(values):
    if values.dtype == BF16:
        return (values,)
    top = values.astype(BF16)
    return top, (values - top.astype(F32)).astype(BF16)


def fine_dot(left, right, dims):
    lefts, rights = in_two(left), in_two(right)
    total = dot(lefts[0], rights[0], dims)
    for low in rights[1:]:
        total = total + dot(lefts[0], low, dims)
    for low in lefts[1:]:
        total = total + dot(low, rights[0], dims)
    return total


NN = ((1,), (0,))
NT = ((1,), (1,))
TN = ((0,), (0,))


def valid_column(valid_len):
    return (lax.broadcasted_iota(jnp.int32, (SEG_LEN, 1), 0) < valid_len).astype(F32)


def block_probs(query_block, key_rows, start, valid_len):
    scores = dot(query_block, key_rows, NT) * (DH**-0.5)
    row_pos = start + lax.broadcasted_iota(jnp.int32, scores.shape, 0)
    col_pos = lax.broadcasted_iota(jnp.int32, scores.shape, 1)
    allowed = (row_pos >= col_pos) & (col_pos < valid_len)
    scores = jnp.where(allowed, scores, masked_score)
    weights = jnp.exp(scores - jnp.max(scores, axis=-1, keepdims=True))
    return weights / jnp.sum(weights, axis=-1, keepdims=True)


def retrieve(query_feat, memory, normal):
    numerator = fine_dot(query_feat, memory, NN)
    denominator = jnp.sum(query_feat * normal, axis=-1, keepdims=True) + 1.0
    return numerator / denominator, denominator


def greet_sequence():
    seg = lax.axis_index("seg")
    place = lax.rem(seg, SEGS)
    barrier = pltpu.get_barrier_semaphore()
    for distance in range(1, SEGS):
        other = seg - place + lax.rem(place + distance, SEGS)
        pl.semaphore_signal(barrier, inc=1, device_id={"seg": other}, device_id_type=MESH)
    pl.semaphore_wait(barrier, SEGS - 1)


def sequence_copies(source, land, send_sem, recv_sem, sign):
    seg = lax.axis_index("seg")
    count = lax.axis_size("seg")
    place = lax.rem(seg, SEGS)
    copies = []
    for distance in range(1, SEGS):
        copy = pltpu.make_async_remote_copy(
            src_ref=source,
            dst_ref=land.at[distance - 1],
            send_sem=send_sem.at[distance - 1],
            recv_sem=recv_sem.at[distance - 1],
            device_id={"seg": lax.rem(seg + count + sign * distance, count)},
            device_id_type=MESH,
        )
        after, before = place + distance < SEGS, place >= distance
        copies.append((copy, after, before) if sign > 0 else (copy, before, after))
    return copies


def head_cols(head):
    return pl.ds(pl.multiple_of(head * DH, DH), DH)


def attn_front_kernel(
    gate_ref, valid_ref, query_ref, key_ref, value_ref,
    mixed_ref, local_ref, before_ref, update_ref,
    land, send_sem, recv_sem,
):
    heads = update_ref.shape[0]
    valid_len = valid_ref[0]
    greet_sequence()
    copies = sequence_copies(update_ref, land, send_sem, recv_sem, 1)

    def make_update(head, carry):
        cols = head_cols(head)
        key_feat = elu_plus(key_ref[:, cols].astype(F32)) * valid_column(valid_len)
        update_ref[head, :DH] = fine_dot(key_feat, value_ref[:, cols], TN)
        normal = jnp.sum(key_feat, axis=0, keepdims=True)
        update_ref[head, DH:] = jnp.broadcast_to(normal, (MEM_ROWS - DH, DH))
        return carry

    lax.fori_loop(0, heads, make_update, 0)
    for copy, sends, _ in copies:

        @pl.when(sends)
        def _(copy=copy):
            copy.start()

    def local(head, carry):
        cols = head_cols(head)
        for start in range(0, SEG_LEN, BLOCK):
            rows, seen = slice(start, start + BLOCK), slice(0, start + BLOCK)
            probs = block_probs(query_ref[rows, cols], key_ref[seen, cols], start, valid_len)
            local_ref[rows, cols] = dot(probs.astype(BF16), value_ref[seen, cols], NN)
        return carry

    lax.fori_loop(0, heads, local, 0)
    before_ref[...] = jnp.zeros_like(before_ref)
    for distance, (copy, sends, gets) in enumerate(copies):

        @pl.when(sends)
        def _(copy=copy):
            copy.wait_send()

        @pl.when(gets)
        def _(copy=copy, distance=distance):
            copy.wait_recv()
            before_ref[...] += land[distance]

    def mix(head, carry):
        cols = head_cols(head)
        gate = gate_ref[head]
        query_feat = elu_plus(query_ref[:, cols].astype(F32))
        memory, normal = before_ref[head, :DH], before_ref[head, DH : DH + 1]
        retrieved, _ = retrieve(query_feat, memory, normal)
        mixed_ref[:, cols] = (gate * retrieved + (1.0 - gate) * local_ref[:, cols]).astype(BF16)
        return carry

    lax.fori_loop(0, heads, mix, 0)


def attn_front(gate, valid, query, key, value, cid):
    rows, cols = query.shape
    heads = cols // DH
    scalar, vmem = pl.BlockSpec(memory_space=pltpu.SMEM), pl.BlockSpec(memory_space=pltpu.VMEM)
    memory = jax.ShapeDtypeStruct((heads, MEM_ROWS, DH), F32)
    return pl.pallas_call(
        attn_front_kernel,
        in_specs=[scalar] * 2 + [vmem] * 3,
        out_specs=[vmem] * 4,
        out_shape=[
            jax.ShapeDtypeStruct((rows, cols), BF16),
            jax.ShapeDtypeStruct((rows, cols), F32),
            memory,
            memory,
        ],
        scratch_shapes=[
            pltpu.VMEM((SEGS - 1, heads, MEM_ROWS, DH), F32),
            pltpu.SemaphoreType.DMA((SEGS - 1,)),
            pltpu.SemaphoreType.DMA((SEGS - 1,)),
        ],
        cost_estimate=pl.CostEstimate(
            flops=4 * rows * rows * cols, bytes_accessed=60 * 2**20, transcendentals=rows * rows * heads
        ),
        compiler_params=pltpu.CompilerParams(
            collective_id=cid, has_side_effects=True, vmem_limit_bytes=40 * 2**20
        ),
    )(gate, valid, query, key, value)


def attn_back_kernel(
    gate_ref, valid_ref, d_out_ref, weight_ref, query_ref, key_ref, value_ref, local_ref, memory_ref,
    d_query_ref, d_key_ref, d_value_ref, gate_grad_ref,
    d_mixed, feat, d_key_sum, d_value_sum, back, land, update, send_sem, recv_sem,
):
    heads = memory_ref.shape[0]
    valid_len = valid_ref[0]
    greet_sequence()
    copies = sequence_copies(back, land, send_sem, recv_sem, -1)
    d_mixed[...] = dot(d_out_ref[...], weight_ref[...], NT)

    def memory_back(head, carry):
        cols = head_cols(head)
        gate = gate_ref[head]
        query_vals = query_ref[:, cols].astype(F32)
        query_feat = elu_plus(query_vals)
        memory, normal = memory_ref[head, :DH], memory_ref[head, DH : DH + 1]
        retrieved, denominator = retrieve(query_feat, memory, normal)
        d_head = d_mixed[:, cols]
        gate_grad_ref[head] = jnp.broadcast_to(
            jnp.sum(d_head * (retrieved - local_ref[:, cols]), axis=0, keepdims=True), (8, DH)
        )
        d_retrieved = gate * d_head
        d_numerator = d_retrieved / denominator
        d_denominator = -jnp.sum(d_retrieved * retrieved, axis=-1, keepdims=True) / denominator
        d_feat = fine_dot(d_numerator, memory, NT) + d_denominator * normal
        feat[:, cols] = d_feat * elu_slope(query_vals)
        back[head, :DH] = fine_dot(query_feat, d_numerator, TN).astype(BF16)
        d_normal = jnp.sum(d_denominator * query_feat, axis=0, keepdims=True)
        back[head, DH:] = jnp.broadcast_to(d_normal, (MEM_ROWS - DH, DH)).astype(BF16)
        return carry

    lax.fori_loop(0, heads, memory_back, 0)
    for copy, sends, _ in copies:

        @pl.when(sends)
        def _(copy=copy):
            copy.start()

    d_key_sum[...] = jnp.zeros_like(d_key_sum)
    d_value_sum[...] = jnp.zeros_like(d_value_sum)

    def local_back(head, carry):
        cols = head_cols(head)
        keep = 1.0 - gate_ref[head]
        for start in range(0, SEG_LEN, BLOCK):
            rows, seen = slice(start, start + BLOCK), slice(0, start + BLOCK)
            query_block = query_ref[rows, cols]
            probs = block_probs(query_block, key_ref[seen, cols], start, valid_len)
            d_local = (keep * d_mixed[rows, cols]).astype(BF16)
            d_probs = dot(d_local, value_ref[seen, cols], NT)
            row_dot = jnp.sum(probs * d_probs, axis=-1, keepdims=True)
            d_scores = (probs * (d_probs - row_dot) * (DH**-0.5)).astype(BF16)
            d_query = dot(d_scores, key_ref[seen, cols], NN) + feat[rows, cols]
            d_query_ref[rows, cols] = d_query.astype(BF16)
            d_key_sum[seen, cols] += dot(d_scores, query_block, TN)
            d_value_sum[seen, cols] += dot(probs.astype(BF16), d_local, TN)
        return carry

    lax.fori_loop(0, heads, local_back, 0)
    update[...] = jnp.zeros_like(update)
    for distance, (copy, sends, gets) in enumerate(copies):

        @pl.when(sends)
        def _(copy=copy):
            copy.wait_send()

        @pl.when(gets)
        def _(copy=copy, distance=distance):
            copy.wait_recv()
            update[...] += land[distance].astype(F32)

    def finish_back(head, carry):
        cols = head_cols(head)
        valid = valid_column(valid_len)
        key_vals = key_ref[:, cols].astype(F32)
        memory, normal = update[head, :DH], update[head, DH : DH + 1]
        d_feat = (fine_dot(value_ref[:, cols], memory, NT) + normal) * valid
        d_key_ref[:, cols] = (d_key_sum[:, cols] + d_feat * elu_slope(key_vals)).astype(BF16)
        key_feat = elu_plus(key_vals) * valid
        d_value = d_value_sum[:, cols] + fine_dot(key_feat, memory, NN)
        d_value_ref[:, cols] = d_value.astype(BF16)
        return carry

    lax.fori_loop(0, heads, finish_back, 0)


def attn_back(gate, valid, d_out, weight, query, key, value, local, memory, cid):
    rows, cols = query.shape
    heads = cols // DH
    scalar, vmem = pl.BlockSpec(memory_space=pltpu.SMEM), pl.BlockSpec(memory_space=pltpu.VMEM)
    wide = pltpu.VMEM((rows, cols), F32)
    narrow = jax.ShapeDtypeStruct((rows, cols), BF16)
    return pl.pallas_call(
        attn_back_kernel,
        in_specs=[scalar] * 2 + [vmem] * 7,
        out_specs=[vmem] * 4,
        out_shape=[narrow, narrow, narrow, jax.ShapeDtypeStruct((heads, 8, DH), F32)],
        scratch_shapes=[
            wide,
            wide,
            wide,
            wide,
            pltpu.VMEM((heads, MEM_ROWS, DH), BF16),
            pltpu.VMEM((SEGS - 1, heads, MEM_ROWS, DH), BF16),
            pltpu.VMEM((heads, MEM_ROWS, DH), F32),
            pltpu.SemaphoreType.DMA((SEGS - 1,)),
            pltpu.SemaphoreType.DMA((SEGS - 1,)),
        ],
        cost_estimate=pl.CostEstimate(
            flops=10 * rows * rows * cols + 2 * rows * cols * d_out.shape[1],
            bytes_accessed=100 * 2**20,
            transcendentals=rows * rows * heads,
        ),
        compiler_params=pltpu.CompilerParams(
            collective_id=cid, has_side_effects=True, vmem_limit_bytes=48 * 2**20
        ),
    )(gate, valid, d_out, weight, query, key, value, local, memory)


def per_device(
    tokens,
    cotangent,
    gain_attn,
    gain_mlp,
    w_query,
    w_key,
    w_value,
    w_out,
    w_gate,
    w_up,
    w_down,
    mem_gate,
    lengths,
):
    seg_index = lax.axis_index("seg")
    head_index = lax.axis_index("head")
    head_groups = lax.axis_size("head")
    seg_size = lax.axis_size("seg")
    position = seg_index % SEGS
    sequence = seg_index // SEGS
    seq_length = jnp.sum(jnp.where(lax.iota(jnp.int32, lengths.shape[0]) == sequence, lengths, 0))
    valid_len = jnp.where(position == SEGS - 1, seq_length, SEG_LEN).reshape(1)
    heads = mem_gate.shape[0]
    cols = heads * DH

    token_vals = tokens.astype(F32)
    gathered_tokens, gathered_attn, query_rows, key_rows, value_rows = gather_project(
        tokens, gain_attn, w_query, w_key, w_value, head_groups, 4
    )
    cotangent, key_rows = lax.optimization_barrier((cotangent, key_rows))
    gathered_grad = lax.all_gather(cotangent, "head", axis=0, tiled=True)
    mix_sig = jax.nn.sigmoid(mem_gate)
    mixed_attn, local_attn, memory_prev, update = attn_front(
        mix_sig, valid_len, query_rows, key_rows, value_rows, 5
    )
    after = memory_prev + update
    memory_after = (after[:, :DH] * SEG_LEN ** (-0.5))[None]
    normal_after = (after[:, DH] / SEG_LEN)[None]
    all_hidden, flip_mlp, silu, slope, act, pair = attn_out_sum(
        mixed_attn, w_out, gathered_tokens, gain_mlp, w_gate, w_up, w_down, head_groups, 1
    )
    own_rows = tokens.shape[0]
    hidden_res = lax.dynamic_slice_in_dim(all_hidden, head_index * own_rows, own_rows, 0)
    d_gate_a, d_up_a, gate_a, up_a, down_a = mlp_half(
        flip_mlp, gathered_grad, silu, slope, act, w_down, 0
    )
    gate_a, up_a, down_a = lax.psum((gate_a, up_a, down_a), "seg")
    d_gate_b, d_up_b, gate_b, up_b, down_b = mlp_half(
        flip_mlp, gathered_grad, silu, slope, act, w_down, 1
    )
    gathered_hidden, d_hidden, gain_mlp_rows, down_b, gate_b = mlp_back_sum(
        (d_gate_a, d_gate_b),
        (d_up_a, d_up_b),
        w_gate,
        w_up,
        all_hidden,
        gathered_grad,
        gain_mlp,
        (down_b, gate_b),
        (BLOCK, cols),
        seg_size,
        head_groups,
        2,
    )
    d_queries, d_keys, d_values, gate_cols = attn_back(
        mix_sig,
        valid_len,
        gathered_hidden,
        w_out,
        query_rows,
        key_rows,
        value_rows,
        local_attn,
        memory_prev,
        3,
    )
    pair, grad_query, grad_key, grad_value, grad_out, gain_attn_rows = attn_weights(
        gathered_attn,
        gathered_hidden,
        mixed_attn,
        d_queries,
        d_keys,
        d_values,
        w_query,
        w_key,
        w_value,
        pair,
    )
    width = gain_attn.shape[0]
    pair = lax.psum_scatter(pair, "head", scatter_dimension=0, tiled=True)
    output = (hidden_res + pair[:, :width].astype(F32)).astype(BF16)
    d_normed_attn = pair[:, width:].astype(F32)
    grad_in_attn = norm_backward(token_vals, inverse_rms(token_vals), gain_attn, d_normed_attn)
    grad_tokens = (d_hidden + grad_in_attn).astype(BF16)
    gate_part = mix_sig * (1.0 - mix_sig) * jnp.sum(gate_cols[:, 0], axis=-1)
    slots = jnp.where(
        (lax.iota(jnp.int32, head_groups) == head_index)[:, None], gate_part[None], 0.0
    )
    gain_attn_part = jnp.sum(gain_attn_rows, axis=0) / gain_attn
    gain_mlp_part = jnp.sum(gain_mlp_rows, axis=0)
    parts = jnp.concatenate([gain_attn_part, gain_mlp_part, slots.reshape(-1)])
    lines = -(-parts.shape[0] // (8 * DH)) * 8
    parts = jnp.pad(parts, (0, lines * DH - parts.shape[0])).reshape(lines, DH)
    small, *late = grad_sum(
        parts,
        [up_b, grad_out, grad_query, grad_key, grad_value],
        (cols, cols),
        seg_size,
        head_groups,
        0,
    )
    small = small.reshape(-1)
    grad_mem_gate = lax.dynamic_slice(small, (2 * width + head_index * heads,), (heads,))
    grads = widen(
        [(1, gate_a, gate_b), (1, up_a, late[0]), (0, down_a, down_b)]
        + [(0, grad) for grad in late[1:]],
        (cols, cols),
    )
    return (
        output,
        grad_tokens,
        memory_after,
        normal_after,
        small[:width],
        small[width : 2 * width],
        grads[4],
        grads[5],
        grads[6],
        grads[3],
        grads[0],
        grads[1],
        grads[2],
        grad_mem_gate,
    )


def solution(mesh):
    return jax.shard_map(
        per_device,
        mesh=mesh,
        in_specs=(
            P(("seg", "head"), None),
            P(("seg", "head"), None),
            P(),
            P(),
            P(None, "head"),
            P(None, "head"),
            P(None, "head"),
            P("head", None),
            P(None, "head"),
            P(None, "head"),
            P("head", None),
            P("head"),
            P(),
        ),
        out_specs=(
            P(("seg", "head"), None),
            P(("seg", "head"), None),
            P("seg", "head", None, None),
            P("seg", "head", None),
            P(),
            P(),
            P(None, "head"),
            P(None, "head"),
            P(None, "head"),
            P("head", None),
            P(None, "head"),
            P(None, "head"),
            P("head", None),
            P("head"),
        ),
        check_vma=False,
    )
```

```python
import functools

import jax
import jax.numpy as jnp
from jax import lax
from jax.experimental import pallas as pl
from jax.experimental.pallas import tpu as pltpu
from jax.sharding import PartitionSpec as P

DH = 128
SEG_LEN = 1024
SEGS = 4
MEM_ROWS = DH + 16
BLOCK = 256

epsilon = 1e-05
masked_score = -1e30
F32 = jnp.float32
BF16 = jnp.bfloat16


MESH = pl.DeviceIdType.MESH
LAND_SLOTS = 12
RESULT_SLOTS = 16
SUM_SEMS = 8
SUM_HOP = 3


def bits_of(size):
    return size.bit_length() - 1


def flip(index, power):
    return index + power - 2 * power * lax.rem(index // power, 2)


def sum_engine(arrays, outs, tile, seg_bits, scratch):
    mine, result, send_sem, recv_sem, load_sem, store_sem, *lands = scratch
    seg = lax.axis_index("seg")
    planes = seg_bits - 1
    high, wide = tile
    shapes = [array.shape for array in arrays]
    counts = [(rows // high) * (cols // wide) for rows, cols in shapes]
    starts = [sum(counts[:i]) for i in range(len(counts))]
    total = sum(counts)

    def power(k, level):
        if level == 0:
            return 1
        which = lax.rem(k + level - 1, planes)
        value = 2
        for bit in range(1, planes):
            value = jnp.where(which == bit, 2 << bit, value)
        return value

    def my_bit(k, level):
        return lax.rem(seg // power(k, level), 2)

    def part(k, level, own):
        half = high >> (level + 1)
        bit = my_bit(k, level) if own else 1 - my_bit(k, level)
        return pl.ds(pl.multiple_of(bit * half, half), half)

    def kept(k, levels):
        first = 0
        for level in range(levels):
            first = first + my_bit(k, level) * (high >> (level + 1))
        return pl.ds(pl.multiple_of(first, high >> levels), high >> levels)

    def pick(k, act):
        for i in range(len(arrays)):

            @pl.when((k >= starts[i]) & (k < starts[i] + counts[i]))
            def _(i=i):
                across = shapes[i][1] // wide
                place = k - starts[i]
                row = pl.multiple_of((place // across) * high, high)
                col = pl.multiple_of(lax.rem(place, across) * wide, wide)
                act(i, row, col)

    def halving(k, level, source):
        return pltpu.make_async_remote_copy(
            src_ref=source,
            dst_ref=lands[level].at[lax.rem(k, LAND_SLOTS)],
            send_sem=send_sem.at[level, lax.rem(k, SUM_SEMS)],
            recv_sem=recv_sem.at[level, lax.rem(k, SUM_SEMS)],
            device_id={"seg": flip(seg, power(k, level))},
            device_id_type=MESH,
        )

    def first_source(k, i, row, col, own):
        half = high // 2
        bit = my_bit(k, 0) if own else 1 - my_bit(k, 0)
        return arrays[i].at[pl.ds(pl.multiple_of(row + bit * half, half), half), pl.ds(col, wide)]

    def keep(k, i, row, col):
        slot = lax.rem(k, 4)
        return pltpu.make_async_copy(
            first_source(k, i, row, col, True), mine.at[slot], load_sem.at[slot]
        )

    def level_source(k, level):
        return lands[level - 1].at[lax.rem(k, LAND_SLOTS), part(k, level, False)]

    def doubling(k, level):
        ref = result.at[lax.rem(k, RESULT_SLOTS), kept(k, level + 1)]
        return pltpu.make_async_remote_copy(
            src_ref=ref,
            dst_ref=ref,
            send_sem=send_sem.at[seg_bits + level, lax.rem(k, SUM_SEMS)],
            recv_sem=recv_sem.at[seg_bits + level, lax.rem(k, SUM_SEMS)],
            device_id={"seg": flip(seg, power(k, level))},
            device_id_type=MESH,
        )

    def store(k, i, row, col):
        slot = lax.rem(k, 4)
        return pltpu.make_async_copy(
            result.at[lax.rem(k, RESULT_SLOTS)],
            outs[i].at[pl.ds(row, high), pl.ds(col, wide)],
            store_sem.at[slot],
        )

    def do_first(k):
        def go(i, row, col):
            halving(k, 0, first_source(k, i, row, col, False)).start()
            keep(k, i, row, col).start()

        pick(k, go)

    def arrived(k, level):
        slot = lax.rem(k, LAND_SLOTS)
        if level == 0:
            halving(k, 0, first_source(k, 0, 0, 0, False)).wait()
            keep(k, 0, 0, 0).wait()
            other = mine[lax.rem(k, 4)]
        else:
            halving(k, level, level_source(k, level)).wait()
            other = lands[level - 1][slot, part(k, level, True)]
        return (lands[level][slot].astype(F32) + other.astype(F32)).astype(BF16)

    def do_level(k, level):
        lands[level - 1][lax.rem(k, LAND_SLOTS)] = arrived(k, level - 1)
        halving(k, level, level_source(k, level)).start()

    def do_total(k):
        result[lax.rem(k, RESULT_SLOTS), kept(k, seg_bits)] = arrived(k, seg_bits - 1)
        doubling(k, seg_bits - 1).start()

    def do_spread(k, level):
        doubling(k, level + 1).wait()
        doubling(k, level).start()

    def do_finish(k):
        doubling(k, 0).wait()
        pick(k, lambda i, row, col: store(k, i, row, col).start())

    def do_store(k):
        store(k, 0, 0, 0).wait()

    stages = [(0, do_first), (1, functools.partial(do_level, level=1))]
    when = 1
    for level in range(2, seg_bits):
        when += SUM_HOP
        stages.append((when, functools.partial(do_level, level=level)))
    when += SUM_HOP
    stages.append((when, do_total))
    for level in range(seg_bits - 2, -1, -1):
        when += SUM_HOP
        stages.append((when, functools.partial(do_spread, level=level)))
    stages.append((when + 1, do_finish))
    stages.append((when + 3, do_store))

    def step(t):
        for delay, act in reversed(stages):
            k = t - delay

            @pl.when((k >= 0) & (k < total))
            def _(act=act, k=k):
                act(k)

    return step, total + when + 3


def engine_scratch(tile, seg_bits):
    high, wide = tile
    return [
        pltpu.VMEM((4, high // 2, wide), BF16),
        pltpu.VMEM((RESULT_SLOTS, high, wide), BF16),
        pltpu.SemaphoreType.DMA((2 * seg_bits, SUM_SEMS)),
        pltpu.SemaphoreType.DMA((2 * seg_bits, SUM_SEMS)),
        pltpu.SemaphoreType.DMA((4,)),
        pltpu.SemaphoreType.DMA((4,)),
    ] + [pltpu.VMEM((LAND_SLOTS, high >> (l + 1), wide), BF16) for l in range(seg_bits)]


def greet_seg(seg_bits):
    barrier = pltpu.get_barrier_semaphore()
    seg = lax.axis_index("seg")
    for bit in range(seg_bits):
        pl.semaphore_signal(
            barrier, inc=1, device_id={"seg": flip(seg, 1 << bit)}, device_id_type=MESH
        )


def grad_sum_kernel(count, tile, seg_bits, head_bits, *refs):
    small_in, arrays = refs[0], refs[1 : 1 + count]
    small_out, outs = refs[1 + count], refs[2 + count : 2 + 2 * count]
    small_buf, small_land, small_send, small_recv, *scratch = refs[2 + 2 * count :]
    seg, head = lax.axis_index("seg"), lax.axis_index("head")
    greet_seg(seg_bits)
    barrier = pltpu.get_barrier_semaphore()
    for bit in range(head_bits):
        pl.semaphore_signal(
            barrier, inc=1, device_id={"head": flip(head, 1 << bit)}, device_id_type=MESH
        )
    pl.semaphore_wait(barrier, seg_bits + head_bits)
    rounds = seg_bits + head_bits

    def small_copy(j):
        if j < seg_bits:
            where = {"seg": flip(seg, 1 << j)}
        else:
            where = {"head": flip(head, 1 << (j - seg_bits))}
        return pltpu.make_async_remote_copy(
            src_ref=small_buf.at[j],
            dst_ref=small_land.at[j],
            send_sem=small_send.at[j],
            recv_sem=small_recv.at[j],
            device_id=where,
            device_id_type=MESH,
        )

    engine_step, steps = sum_engine(arrays, outs, tile, seg_bits, scratch)

    def step(t, carry):
        engine_step(t)
        for j in range(rounds + 1):

            @pl.when(t == 3 * j)
            def _(j=j):
                if j == 0:
                    small_buf[0] = small_in[...]
                else:
                    small_copy(j - 1).wait()
                    value = small_buf[j - 1] + small_land[j - 1]
                    if j < rounds:
                        small_buf[j] = value
                    else:
                        small_out[...] = value
                if j < rounds:
                    small_copy(j).start()

        return carry

    lax.fori_loop(0, max(steps, 3 * rounds + 1), step, 0)


def grad_sum(small, arrays, tile, seg_size, head_size, cid):
    seg_bits, head_bits = bits_of(seg_size), bits_of(head_size)
    rounds = seg_bits + head_bits
    count = len(arrays)
    moved = sum(rows * cols for rows, cols in (array.shape for array in arrays))
    any_, vmem = pl.BlockSpec(memory_space=pltpu.HBM), pl.BlockSpec(memory_space=pltpu.VMEM)
    return pl.pallas_call(
        functools.partial(grad_sum_kernel, count, tile, seg_bits, head_bits),
        in_specs=[vmem] + [any_] * count,
        out_specs=[vmem] + [any_] * count,
        out_shape=[jax.ShapeDtypeStruct(small.shape, F32)]
        + [jax.ShapeDtypeStruct(array.shape, BF16) for array in arrays],
        scratch_shapes=[
            pltpu.VMEM((rounds, *small.shape), F32),
            pltpu.VMEM((rounds, *small.shape), F32),
            pltpu.SemaphoreType.DMA((rounds,)),
            pltpu.SemaphoreType.DMA((rounds,)),
        ]
        + engine_scratch(tile, seg_bits),
        cost_estimate=pl.CostEstimate(flops=0, bytes_accessed=moved * 60, transcendentals=0),
        compiler_params=pltpu.CompilerParams(
            collective_id=cid, has_side_effects=True, vmem_limit_bytes=60 * 2**20
        ),
    )(small, *arrays)


ROWS = 32
FIRST_HOP = 2
SECOND_HOP = 4
SEND_SLOTS = 6
BLOCK_ROWS = 256
FORWARD_ROWS = 128
UNIT_GROUP = 1024
LINE_REFS = 8


def line_exchange(own, finish, before, scratch, hop, extra, extra_steps):
    up_land, down_land, up_send, down_send, up_recv_sem, down_recv_sem, up_send_sem, down_send_sem = scratch
    size = lax.axis_size("head")
    place = lax.axis_index("head")
    slots = up_land.shape[0]
    chunks = own.shape[0] // ROWS
    last = size - 1

    def up_copy(k):
        return pltpu.make_async_remote_copy(
            src_ref=up_send.at[lax.rem(k, SEND_SLOTS)],
            dst_ref=up_land.at[lax.rem(k, slots)],
            send_sem=up_send_sem.at[lax.rem(k, SEND_SLOTS)],
            recv_sem=up_recv_sem.at[lax.rem(k, slots)],
            device_id={"head": lax.rem(place + 1, size)},
            device_id_type=MESH,
        )

    def down_copy(k):
        return pltpu.make_async_remote_copy(
            src_ref=down_send.at[lax.rem(k, SEND_SLOTS)],
            dst_ref=down_land.at[lax.rem(k, slots)],
            send_sem=down_send_sem.at[lax.rem(k, SEND_SLOTS)],
            recv_sem=down_recv_sem.at[lax.rem(k, slots)],
            device_id={"head": lax.rem(place + last, size)},
            device_id_type=MESH,
        )

    def rows_of(k):
        return pl.ds(pl.multiple_of(k * ROWS, ROWS), ROWS)

    def pass_on(k, copy, land, send, has_source, has_target):
        @pl.when(has_source)
        def _():
            copy(k).wait_recv()

        @pl.when(has_target)
        def _():
            slot = lax.rem(k, SEND_SLOTS)

            @pl.when(k >= SEND_SLOTS)
            def _():
                copy(k - SEND_SLOTS).wait_send()

            @pl.when(has_source)
            def _():
                send[slot] = (own[rows_of(k)] + land[lax.rem(k, slots)].astype(F32)).astype(BF16)

            @pl.when(jnp.logical_not(has_source))
            def _():
                send[slot] = own[rows_of(k)].astype(BF16)

            copy(k).start()

    far = jnp.maximum(place, last - place)

    def step(t, carry):
        before(t)
        down = t - (last - place) * hop

        @pl.when((down >= 0) & (down < chunks))
        def _():
            pass_on(down, down_copy, down_land, down_send, place < last, place > 0)

        up = t - place * hop

        @pl.when((up >= 0) & (up < chunks))
        def _():
            pass_on(up, up_copy, up_land, up_send, place > 0, place < last)

        k = t - far * hop

        @pl.when((k >= 0) & (k < chunks))
        def _():
            slot = lax.rem(k, slots)

            @pl.when(place == 0)
            def _():
                finish(k, own[rows_of(k)] + down_land[slot].astype(F32))

            @pl.when(place == last)
            def _():
                finish(k, own[rows_of(k)] + up_land[slot].astype(F32))

            @pl.when((place > 0) & (place < last))
            def _():
                finish(
                    k,
                    own[rows_of(k)] + up_land[slot].astype(F32) + down_land[slot].astype(F32),
                )

        extra(t)
        return carry

    lax.fori_loop(0, max(chunks + last * hop, extra_steps), step, 0)
    for k in range(chunks - SEND_SLOTS, chunks):

        @pl.when(place < last)
        def _(k=k):
            up_copy(k).wait_send()

        @pl.when(place > 0)
        def _(k=k):
            down_copy(k).wait_send()


def line_barrier(others=0):
    size = lax.axis_size("head")
    place = lax.axis_index("head")
    barrier = pltpu.get_barrier_semaphore()
    inner = (place > 0) & (place < size - 1)

    def greet(near):
        pl.semaphore_signal(
            barrier, inc=1, device_id={"head": lax.rem(near, size)}, device_id_type=MESH
        )

    @pl.when(place > 0)
    def _():
        greet(place + size - 1)

    @pl.when(place < size - 1)
    def _():
        greet(place + 1)

    @pl.when(inner)
    def _():
        pl.semaphore_wait(barrier, 2 + others)

    @pl.when(jnp.logical_not(inner))
    def _():
        pl.semaphore_wait(barrier, 1 + others)


def line_scratch(size, width, hop):
    slots = (size - 1) * hop + 2
    return [
        pltpu.VMEM((slots, ROWS, width), BF16),
        pltpu.VMEM((slots, ROWS, width), BF16),
        pltpu.VMEM((SEND_SLOTS, ROWS, width), BF16),
        pltpu.VMEM((SEND_SLOTS, ROWS, width), BF16),
        pltpu.SemaphoreType.DMA((slots,)),
        pltpu.SemaphoreType.DMA((slots,)),
        pltpu.SemaphoreType.DMA((SEND_SLOTS,)),
        pltpu.SemaphoreType.DMA((SEND_SLOTS,)),
    ]


GATHER_PARTS = 4


def gather_kernel(
    token_hbm, gain_ref, w_query_hbm, w_key_hbm, w_value_hbm,
    all_ref, normed_ref, query_ref, key_ref, value_ref,
    land, normed, w_query, w_key, w_value,
    own_sem, load_sem, all_sem, normed_sem, up_send, up_recv, down_send, down_recv,
):
    size = lax.axis_size("head")
    place = lax.axis_index("head")
    last = size - 1
    own_rows = token_hbm.shape[0]
    chunk = own_rows // GATHER_PARTS
    loads = [
        pltpu.make_async_copy(source, target, load_sem.at[i])
        for i, (source, target) in enumerate(
            ((w_key_hbm, w_key), (w_value_hbm, w_value), (w_query_hbm, w_query))
        )
    ]

    def shard_rows(shard):
        return pl.ds(pl.multiple_of(shard * own_rows, own_rows), own_rows)

    own = pltpu.make_async_copy(token_hbm, land.at[shard_rows(place)], own_sem)
    own.start()
    for load in loads:
        load.start()
    line_barrier()

    def chunk_copy(shard, i, send_sem, recv_sem, target):
        first = pl.multiple_of(shard * own_rows + lax.rem(i, GATHER_PARTS) * chunk, chunk)
        ref = land.at[pl.ds(first, chunk)]
        return pltpu.make_async_remote_copy(
            src_ref=ref,
            dst_ref=ref,
            send_sem=send_sem.at[i],
            recv_sem=recv_sem.at[i],
            device_id={"head": target},
            device_id_type=MESH,
        )

    above, below = lax.rem(place + 1, size), lax.rem(place + last, size)

    def up_copy(i, first_shard):
        return chunk_copy(first_shard - i // GATHER_PARTS, i, up_send, up_recv, above)

    def down_copy(i, first_shard):
        return chunk_copy(first_shard + i // GATHER_PARTS, i, down_send, down_recv, below)

    own.wait()
    for i in range(GATHER_PARTS):

        @pl.when(place < last)
        def _(i=i):
            up_copy(i, place).start()

        @pl.when(place > 0)
        def _(i=i):
            down_copy(i, place).start()

    def stores(shard):
        rows = shard_rows(shard)
        return (
            pltpu.make_async_copy(land.at[rows], all_ref.at[rows], all_sem.at[shard]),
            pltpu.make_async_copy(normed.at[rows], normed_ref.at[rows], normed_sem.at[shard]),
        )

    def project(shard):
        rows = shard_rows(shard)
        value = land[rows].astype(F32)
        normed[rows] = (value * inverse_rms(value) * gain_ref[...]).astype(BF16)
        for copy in stores(shard):
            copy.start()
        for weight, target in ((w_key, key_ref), (w_value, value_ref), (w_query, query_ref)):
            target[rows] = dot(normed[rows], weight[...], NN).astype(BF16)

    for load in loads:
        load.wait()
    project(place)

    def step(i, carry):
        @pl.when(i < place * GATHER_PARTS)
        def _():
            up_copy(i, place - 1).wait_recv()

            @pl.when(place < last)
            def _():
                up_copy(i + GATHER_PARTS, place).start()

        @pl.when(i < (last - place) * GATHER_PARTS)
        def _():
            down_copy(i, place + 1).wait_recv()

            @pl.when(place > 0)
            def _():
                down_copy(i + GATHER_PARTS, place).start()

        distance = (i + 1) // GATHER_PARTS
        whole = lax.rem(i + 1, GATHER_PARTS) == 0

        @pl.when(whole & (place >= distance))
        def _():
            project(place - distance)

        @pl.when(whole & (place + distance <= last))
        def _():
            project(place + distance)

        return carry

    lax.fori_loop(0, last * GATHER_PARTS, step, 0)

    def drain(i, carry):
        @pl.when((place < last) & (i < (place + 1) * GATHER_PARTS))
        def _():
            up_copy(i, place).wait_send()

        @pl.when((place > 0) & (i < (size - place) * GATHER_PARTS))
        def _():
            down_copy(i, place).wait_send()

        return carry

    lax.fori_loop(0, size * GATHER_PARTS, drain, 0)
    for shard in range(size):
        for copy in stores(shard):
            copy.wait()


def gather_project(tokens, gain, w_query, w_key, w_value, size, cid):
    own_rows, width = tokens.shape
    rows, cols = own_rows * size, w_query.shape[1]
    vmem, any_ = pl.BlockSpec(memory_space=pltpu.VMEM), pl.BlockSpec(memory_space=pltpu.HBM)
    weight = pltpu.VMEM((width, cols), BF16)
    hops = pltpu.SemaphoreType.DMA((size * GATHER_PARTS,))
    return pl.pallas_call(
        gather_kernel,
        in_specs=[any_, vmem] + [any_] * 3,
        out_specs=[any_, any_, vmem, vmem, vmem],
        out_shape=[jax.ShapeDtypeStruct((rows, width), BF16)] * 2
        + [jax.ShapeDtypeStruct((rows, cols), BF16)] * 3,
        scratch_shapes=[
            pltpu.VMEM((rows, width), BF16),
            pltpu.VMEM((rows, width), BF16),
            weight,
            weight,
            weight,
            pltpu.SemaphoreType.DMA(()),
            pltpu.SemaphoreType.DMA((3,)),
            pltpu.SemaphoreType.DMA((size,)),
            pltpu.SemaphoreType.DMA((size,)),
            hops,
            hops,
            hops,
            hops,
        ],
        cost_estimate=pl.CostEstimate(
            flops=6 * rows * width * cols, bytes_accessed=150 * 2**20, transcendentals=0
        ),
        compiler_params=pltpu.CompilerParams(
            collective_id=cid, has_side_effects=True, vmem_limit_bytes=48 * 2**20
        ),
    )(tokens, gain.reshape(1, width), w_query, w_key, w_value)


def attn_out_kernel(
    mixed_ref, weight_ref, token_ref, gain_ref, w_gate_hbm, w_up_hbm, w_down_hbm,
    hidden_ref, flip_ref, silu_ref, slope_ref, act_ref, part_ref,
    hidden, normed, w_gate, w_up, w_down, silu, slope, act, flip, part, part_out,
    hidden_sem, load_sem, out_sem, block_sem, *scratch
):
    loads = [
        pltpu.make_async_copy(source, target, load_sem.at[i])
        for i, (source, target) in enumerate(
            ((w_gate_hbm, w_gate), (w_up_hbm, w_up), (w_down_hbm, w_down))
        )
    ]
    for load in loads:
        load.start()
    line_barrier()
    per_block = FORWARD_ROWS // ROWS
    blocks = hidden.shape[0] // FORWARD_ROWS
    groups = w_gate.shape[1] // UNIT_GROUP
    slots = act.shape[0]
    lag = per_block + (lax.axis_size("head") - 1) * FIRST_HOP
    pace = per_block // groups

    def block_rows(b):
        return pl.ds(pl.multiple_of(b * FORWARD_ROWS, FORWARD_ROWS), FORWARD_ROWS)

    def unit_copies(u):
        slot = lax.rem(u, slots)
        where = (block_rows(u // groups), unit_cols(u))
        return [
            pltpu.make_async_copy(source.at[slot], target.at[where], out_sem.at[i, slot])
            for i, (source, target) in enumerate(
                ((silu, silu_ref), (slope, slope_ref), (act, act_ref))
            )
        ]

    def unit_cols(u):
        return pl.ds(pl.multiple_of(lax.rem(u, groups) * UNIT_GROUP, UNIT_GROUP), UNIT_GROUP)

    def flip_copy(b):
        return pltpu.make_async_copy(flip, flip_ref.at[:, block_rows(b)], block_sem.at[0])

    def part_copy(b):
        where = (block_rows(b), pl.ds(0, part_out.shape[1]))
        return pltpu.make_async_copy(part_out, part_ref.at[where], block_sem.at[1])

    def forward(u):
        slot = lax.rem(u, slots)
        b, group = u // groups, lax.rem(u, groups)

        @pl.when(group == 0)
        def _():
            @pl.when(b > 0)
            def _():
                flip_copy(b - 1).wait()

            flip[...] = normed[block_rows(b)].T
            flip_copy(b).start()

        @pl.when(u >= slots)
        def _():
            for copy in unit_copies(u - slots):
                copy.wait()

        rows, cols = normed[block_rows(u // groups)], unit_cols(u)
        gate_pre = dot(rows, w_gate[:, cols], NN)
        up_proj = dot(rows, w_up[:, cols], NN)
        gate_sig = jax.nn.sigmoid(gate_pre)
        silu_gate = gate_pre * gate_sig
        silu[slot] = silu_gate.astype(BF16)
        factor = up_proj * gate_sig * (1.0 + gate_pre * (1.0 - gate_sig))
        slope[slot] = factor.astype(BF16)
        act[slot] = (silu_gate * up_proj).astype(BF16)
        for copy in unit_copies(u):
            copy.start()
        share = dot(act[slot], w_down[cols], NN)

        @pl.when(group == 0)
        def _():
            part[...] = share

        @pl.when(group > 0)
        def _():
            part[...] += share

        @pl.when(group == groups - 1)
        def _():
            @pl.when(b > 0)
            def _():
                part_copy(b - 1).wait()

            part_out[...] = part[...].astype(BF16)
            part_copy(b).start()

    def before(t):
        @pl.when((lax.rem(t, per_block) == 0) & (t < blocks * per_block))
        def _():
            rows = block_rows(t // per_block)
            hidden[rows] = dot(mixed_ref[rows], weight_ref[...], NN)

    def after(t):
        @pl.when(t == lag)
        def _():
            for load in loads:
                load.wait()

        late = t - lag

        @pl.when((late >= 0) & (lax.rem(late, pace) == 0) & (late // pace < blocks * groups))
        def _():
            forward(late // pace)

    def store(b):
        rows = block_rows(b)
        return pltpu.make_async_copy(hidden.at[rows], hidden_ref.at[rows], hidden_sem.at[b])

    def finish(k, total):
        rows = pl.ds(pl.multiple_of(k * ROWS, ROWS), ROWS)
        value = token_ref[rows].astype(F32) + total
        hidden[rows] = value
        normed[rows] = (value * inverse_rms(value) * gain_ref[...]).astype(BF16)

        @pl.when(lax.rem(k, per_block) == per_block - 1)
        def _():
            store(k // per_block).start()

    line_exchange(hidden, finish, before, scratch, FIRST_HOP, after, lag + blocks * per_block)
    for b in range(blocks):
        store(b).wait()
    flip_copy(blocks - 1).wait()
    part_copy(blocks - 1).wait()
    for u in range(blocks * groups - slots, blocks * groups):
        for copy in unit_copies(u):
            copy.wait()


def attn_out_sum(mixed, weight, tokens, gain, w_gate, w_up, w_down, size, cid):
    rows, width = tokens.shape
    units = w_gate.shape[1]
    vmem, any_ = pl.BlockSpec(memory_space=pltpu.VMEM), pl.BlockSpec(memory_space=pltpu.HBM)
    blocks, slots = rows // FORWARD_ROWS, 2
    return pl.pallas_call(
        attn_out_kernel,
        in_specs=[vmem] * 4 + [any_] * 3,
        out_specs=[any_] * 6,
        out_shape=[
            jax.ShapeDtypeStruct((rows, width), F32),
            jax.ShapeDtypeStruct((width, rows), BF16),
            jax.ShapeDtypeStruct((rows, units), BF16),
            jax.ShapeDtypeStruct((rows, units), BF16),
            jax.ShapeDtypeStruct((rows, units), BF16),
            jax.ShapeDtypeStruct((rows, 2 * width), BF16),
        ],
        scratch_shapes=[
            pltpu.VMEM((rows, width), F32),
            pltpu.VMEM((rows, width), BF16),
            pltpu.VMEM((width, units), BF16),
            pltpu.VMEM((width, units), BF16),
            pltpu.VMEM((units, width), BF16),
            pltpu.VMEM((slots, FORWARD_ROWS, UNIT_GROUP), BF16),
            pltpu.VMEM((slots, FORWARD_ROWS, UNIT_GROUP), BF16),
            pltpu.VMEM((slots, FORWARD_ROWS, UNIT_GROUP), BF16),
            pltpu.VMEM((width, FORWARD_ROWS), BF16),
            pltpu.VMEM((FORWARD_ROWS, width), F32),
            pltpu.VMEM((FORWARD_ROWS, width), BF16),
            pltpu.SemaphoreType.DMA((blocks,)),
            pltpu.SemaphoreType.DMA((3,)),
            pltpu.SemaphoreType.DMA((3, slots)),
            pltpu.SemaphoreType.DMA((2,)),
        ]
        + line_scratch(size, width, FIRST_HOP),
        cost_estimate=pl.CostEstimate(
            flops=2 * rows * width * (mixed.shape[1] + 3 * units),
            bytes_accessed=250 * 2**20,
            transcendentals=rows * units,
        ),
        compiler_params=pltpu.CompilerParams(
            collective_id=cid, has_side_effects=True, vmem_limit_bytes=60 * 2**20
        ),
    )(mixed, weight, tokens, gain.reshape(1, width), w_gate, w_up, w_down)


def mlp_back_kernel(
    tile, seg_bits,
    d_gate_a, d_gate_b, d_up_a, d_up_b, w_gate_hbm, w_up_hbm, hidden_hbm, grad_hbm, gain_ref,
    down_in, gate_in,
    d_out_ref, d_own_ref, gain_part_ref, down_out, gate_out,
    d_gate, d_up, w_gate, w_up, hidden, grad, own, load_sem, store_sem, *scratch
):
    per_block = BLOCK_ROWS // ROWS
    blocks = own.shape[0] // BLOCK_ROWS
    size = lax.axis_size("head")
    place = lax.axis_index("head")
    per_device = own.shape[0] // ROWS // size
    half = d_gate.shape[1] // 2
    low, high = pl.ds(0, half), pl.ds(half, half)
    loads = [
        pltpu.make_async_copy(source, target, load_sem.at[i])
        for i, (source, target) in enumerate(
            ((d_gate_a, d_gate.at[:, low]), (d_gate_b, d_gate.at[:, high]), (w_gate_hbm, w_gate),
             (d_up_a, d_up.at[:, low]), (d_up_b, d_up.at[:, high]), (w_up_hbm, w_up),
             (hidden_hbm, hidden), (grad_hbm, grad))
        )
    ]
    for load in loads:
        load.start()
    gain_part_ref[...] = jnp.zeros_like(gain_part_ref)
    greet_seg(seg_bits)
    line_barrier(seg_bits)
    engine_step, steps = sum_engine(
        [down_in, gate_in], [down_out, gate_out], tile, seg_bits, scratch[LINE_REFS:]
    )

    def block_rows(b):
        return pl.ds(pl.multiple_of(b * BLOCK_ROWS, BLOCK_ROWS), BLOCK_ROWS)

    for load in loads[:3]:
        load.wait()

    def before(t):
        @pl.when((lax.rem(t, per_block) == 0) & (t < blocks * per_block))
        def _():
            rows = block_rows(t // per_block)
            own[rows] = dot(d_gate[rows], w_gate[...], NT)

            @pl.when(t == 0)
            def _():
                for load in loads[3:6]:
                    load.wait()

            own[rows] += dot(d_up[rows], w_up[...], NT)

        @pl.when(t == 1)
        def _():
            for load in loads[6:]:
                load.wait()

    def store(b):
        rows = block_rows(b)
        return pltpu.make_async_copy(grad.at[rows], d_out_ref.at[rows], store_sem.at[b])

    def finish(k, total):
        rows = pl.ds(pl.multiple_of(k * ROWS, ROWS), ROWS)
        value = hidden[rows]
        inverse = inverse_rms(value)
        normal = value * inverse
        scaled = gain_ref[...] * total
        mean = jnp.mean(scaled * normal, axis=-1, keepdims=True)
        d_hidden = grad[rows].astype(F32) + inverse * (scaled - normal * mean)
        grad[rows] = d_hidden.astype(BF16)

        @pl.when(k // per_device == place)
        def _():
            mine = pl.ds(pl.multiple_of(lax.rem(k, per_device) * ROWS, ROWS), ROWS)
            d_own_ref[mine] = d_hidden
            gain_part_ref[...] += jnp.sum((total * normal).reshape(ROWS // 8, 8, -1), axis=0)

        @pl.when(lax.rem(k, per_block) == per_block - 1)
        def _():
            store(k // per_block).start()

    line_exchange(own, finish, before, scratch[:LINE_REFS], SECOND_HOP, engine_step, steps)
    for b in range(blocks):
        store(b).wait()


def mlp_back_sum(
    d_gate, d_up, w_gate, w_up, hidden, grad, gain, summed, tile, seg_size, size, cid
):
    rows, width = hidden.shape
    units = w_gate.shape[1]
    seg_bits = bits_of(seg_size)
    vmem, any_ = pl.BlockSpec(memory_space=pltpu.VMEM), pl.BlockSpec(memory_space=pltpu.HBM)
    blocks = rows // BLOCK_ROWS
    return pl.pallas_call(
        functools.partial(mlp_back_kernel, tile, seg_bits),
        in_specs=[any_] * 8 + [vmem, any_, any_],
        out_specs=[any_, vmem, vmem, any_, any_],
        out_shape=[
            jax.ShapeDtypeStruct((rows, width), BF16),
            jax.ShapeDtypeStruct((rows // size, width), F32),
            jax.ShapeDtypeStruct((8, width), F32),
        ]
        + [jax.ShapeDtypeStruct(array.shape, BF16) for array in summed],
        scratch_shapes=[
            pltpu.VMEM((rows, units), BF16),
            pltpu.VMEM((rows, units), BF16),
            pltpu.VMEM((width, units), BF16),
            pltpu.VMEM((width, units), BF16),
            pltpu.VMEM((rows, width), F32),
            pltpu.VMEM((rows, width), BF16),
            pltpu.VMEM((rows, width), F32),
            pltpu.SemaphoreType.DMA((8,)),
            pltpu.SemaphoreType.DMA((blocks,)),
        ]
        + line_scratch(size, width, SECOND_HOP)
        + engine_scratch(tile, seg_bits),
        cost_estimate=pl.CostEstimate(
            flops=4 * rows * width * units, bytes_accessed=250 * 2**20, transcendentals=0
        ),
        compiler_params=pltpu.CompilerParams(
            collective_id=cid, has_side_effects=True, vmem_limit_bytes=62 * 2**20
        ),
    )(*d_gate, *d_up, w_gate, w_up, hidden, grad, gain.reshape(1, width), *summed)


MLP_BLOCK = 512


def mlp_kernel(
    flip_ref, grad_ref, silu_ref, slope_ref, act_ref, w_down_ref,
    d_gate_ref, d_up_ref, grad_gate_ref, grad_up_ref, grad_down_ref,
):
    width = flip_ref.shape[0]
    d_act = dot(grad_ref[...], w_down_ref[...], NT)
    d_gate_ref[...] = (d_act * slope_ref[...].astype(F32)).astype(BF16)
    d_up_ref[...] = (d_act * silu_ref[...].astype(F32)).astype(BF16)
    half = width // 2
    for i in range(2):
        part = slice(i * half, (i + 1) * half)
        grad_gate_ref[part] = dot(flip_ref[part], d_gate_ref[...], NN).astype(BF16)
        grad_up_ref[part] = dot(flip_ref[part], d_up_ref[...], NN).astype(BF16)
        grad_down_ref[:, part] = dot(act_ref[...], grad_ref[:, part], TN).astype(BF16)


def mlp_half(flip, grad, silu, slope, act, w_down, which):
    width, count = flip.shape
    units = act.shape[1] // 2
    block = min(MLP_BLOCK, units)
    first = which * (units // block)
    once = pl.Buffered(1)
    side = pl.BlockSpec((count, block), lambda j: (0, first + j))
    side_out = pl.BlockSpec((count, block), lambda j: (0, j))
    tall = pl.BlockSpec((width, block), lambda j: (0, j))
    return pl.pallas_call(
        mlp_kernel,
        grid=(units // block,),
        in_specs=[
            pl.BlockSpec((width, count), lambda j: (0, 0), pipeline_mode=once),
            pl.BlockSpec((count, width), lambda j: (0, 0), pipeline_mode=once),
            side,
            side,
            side,
            pl.BlockSpec((block, width), lambda j: (first + j, 0)),
        ],
        out_specs=[side_out, side_out, tall, tall, pl.BlockSpec((block, width), lambda j: (j, 0))],
        out_shape=[
            jax.ShapeDtypeStruct((count, units), BF16),
            jax.ShapeDtypeStruct((count, units), BF16),
            jax.ShapeDtypeStruct((width, units), BF16),
            jax.ShapeDtypeStruct((width, units), BF16),
            jax.ShapeDtypeStruct((units, width), BF16),
        ],
        cost_estimate=pl.CostEstimate(
            flops=8 * count * width * units,
            bytes_accessed=2 * (2 * count * width + 4 * width * units + 7 * count * units),
            transcendentals=0,
        ),
        compiler_params=pltpu.CompilerParams(vmem_limit_bytes=56 * 2**20),
    )(flip, grad, silu, slope, act, w_down)


WIDEN_SLOTS = 4


def widen_kernel(shapes, places, wide_count, tile, *refs):
    count = len(shapes)
    sources, targets = refs[:count], refs[count : count + wide_count]
    narrow, wide, load_sem, store_sem = refs[count + wide_count :]
    high, broad = tile
    counts = [(rows // high) * (width // broad) for rows, width in shapes]
    total = sum(counts)

    def pick(k, act):
        first = 0
        for i in range(count):
            @pl.when((k >= first) & (k < first + counts[i]))
            def _(i=i, first=first):
                across = shapes[i][1] // broad
                place = k - first
                row = pl.multiple_of((place // across) * high, high)
                col = pl.multiple_of(lax.rem(place, across) * broad, broad)
                act(i, (pl.ds(row, high), pl.ds(col, broad)))
            first += counts[i]

    def load(k, i, where):
        slot = lax.rem(k, WIDEN_SLOTS)
        return pltpu.make_async_copy(sources[i].at[where], narrow.at[slot], load_sem.at[slot])

    def store(k, i, where):
        slot = lax.rem(k, WIDEN_SLOTS)
        target, row, col = places[i]
        rows = pl.ds(pl.multiple_of(row + where[0].start, high), high)
        cols = pl.ds(pl.multiple_of(col + where[1].start, broad), broad)
        return pltpu.make_async_copy(
            wide.at[slot], targets[target].at[rows, cols], store_sem.at[slot]
        )

    zero = (pl.ds(0, high), pl.ds(0, broad))
    ahead = WIDEN_SLOTS - 1
    for k in range(ahead):
        pick(k, lambda i, where, k=k: load(k, i, where).start())

    def step(k, carry):
        @pl.when(k + ahead < total)
        def _():
            pick(k + ahead, lambda i, where: load(k + ahead, i, where).start())

        @pl.when(k >= WIDEN_SLOTS)
        def _():
            store(k - WIDEN_SLOTS, 0, zero).wait()

        load(k, 0, zero).wait()
        slot = lax.rem(k, WIDEN_SLOTS)
        wide[slot] = narrow[slot].astype(F32)
        pick(k, lambda i, where: store(k, i, where).start())
        return carry

    lax.fori_loop(0, total, step, 0)
    for k in range(total - WIDEN_SLOTS, total):
        store(k, 0, zero).wait()


def widen(groups, tile):
    arrays, places, targets = [], [], []
    for axis, *group in groups:
        shape = [0, 0]
        shape[1 - axis] = group[0].shape[1 - axis]
        for value in group:
            arrays.append(value)
            places.append((len(targets), *((shape[0], 0) if axis == 0 else (0, shape[1]))))
            shape[axis] += value.shape[axis]
        targets.append(tuple(shape))
    shapes = [value.shape for value in arrays]
    any_ = pl.BlockSpec(memory_space=pltpu.HBM)
    return pl.pallas_call(
        functools.partial(widen_kernel, shapes, places, len(targets), tile),
        in_specs=[any_] * len(arrays),
        out_specs=[any_] * len(targets),
        out_shape=[jax.ShapeDtypeStruct(shape, F32) for shape in targets],
        scratch_shapes=[
            pltpu.VMEM((WIDEN_SLOTS, *tile), BF16),
            pltpu.VMEM((WIDEN_SLOTS, *tile), F32),
            pltpu.SemaphoreType.DMA((WIDEN_SLOTS,)),
            pltpu.SemaphoreType.DMA((WIDEN_SLOTS,)),
        ],
        cost_estimate=pl.CostEstimate(
            flops=0, bytes_accessed=6 * sum(r * c for r, c in shapes), transcendentals=0
        ),
        compiler_params=pltpu.CompilerParams(vmem_limit_bytes=60 * 2**20),
    )(*arrays)


def attn_weights_kernel(
    rows_ref, d_out_ref, mixed_ref, d_query_ref, d_key_ref, d_value_ref,
    w_query_ref, w_key_ref, w_value_ref, pair_ref,
    d_rows_ref, grad_query_ref, grad_key_ref, grad_value_ref, grad_out_ref, gain_part_ref,
    flipped_mixed, flipped_rows,
):
    @pl.when(pl.program_id(0) == 0)
    def _():
        flipped_mixed[...] = mixed_ref[...].T

    flipped_rows[...] = rows_ref[...].T
    d_rows = (
        dot(d_query_ref[...], w_query_ref[...], NT)
        + dot(d_key_ref[...], w_key_ref[...], NT)
        + dot(d_value_ref[...], w_value_ref[...], NT)
    )
    d_rows_ref[...] = d_rows.astype(BF16)
    product = d_rows * rows_ref[...].astype(F32)
    gain_part_ref[...] = jnp.sum(product.reshape(-1, 8, product.shape[1]), axis=0)
    grad_query_ref[...] = dot(flipped_rows[...], d_query_ref[...], NN).astype(BF16)
    grad_key_ref[...] = dot(flipped_rows[...], d_key_ref[...], NN).astype(BF16)
    grad_value_ref[...] = dot(flipped_rows[...], d_value_ref[...], NN).astype(BF16)
    grad_out_ref[...] = dot(flipped_mixed[...], d_out_ref[...], NN).astype(BF16)


def attn_weights(rows, d_out, mixed, d_query, d_key, d_value, w_query, w_key, w_value, pair):
    count, width = rows.shape
    cols = mixed.shape[1]
    block = 512
    once = pl.Buffered(1)
    slim = pl.BlockSpec((count, cols), lambda j: (0, 0), pipeline_mode=once)
    side = pl.BlockSpec((count, block), lambda j: (0, j))
    right = pl.BlockSpec((count, block), lambda j: (0, width // block + j))
    tall = pl.BlockSpec((block, cols), lambda j: (j, 0))
    wide = pl.BlockSpec((cols, block), lambda j: (0, j))
    tall_type = jax.ShapeDtypeStruct((width, cols), BF16)
    return pl.pallas_call(
        attn_weights_kernel,
        grid=(width // block,),
        in_specs=[side, side, slim, slim, slim, slim, tall, tall, tall]
        + [pl.BlockSpec(memory_space=pltpu.HBM)],
        out_specs=[right, tall, tall, tall, wide, pl.BlockSpec((8, block), lambda j: (0, j))],
        out_shape=[
            jax.ShapeDtypeStruct(pair.shape, BF16),
            tall_type,
            tall_type,
            tall_type,
            jax.ShapeDtypeStruct((cols, width), BF16),
            jax.ShapeDtypeStruct((8, width), F32),
        ],
        input_output_aliases={9: 0},
        scratch_shapes=[pltpu.VMEM((cols, count), BF16), pltpu.VMEM((block, count), BF16)],
        cost_estimate=pl.CostEstimate(
            flops=14 * count * width * cols,
            bytes_accessed=2 * (3 * count * width + 4 * count * cols + 7 * width * cols),
            transcendentals=0,
        ),
        compiler_params=pltpu.CompilerParams(vmem_limit_bytes=48 * 2**20),
    )(rows, d_out, mixed, d_query, d_key, d_value, w_query, w_key, w_value, pair)


def elu_plus(values):
    return jnp.where(values > 0, values + 1.0, jnp.exp(jnp.minimum(values, 0.0)))


def elu_slope(values):
    return jnp.where(values > 0, 1.0, jnp.exp(jnp.minimum(values, 0.0)))


def inverse_rms(values):
    return lax.rsqrt(jnp.mean(values * values, axis=-1, keepdims=True) + epsilon)


def norm_backward(values, inverse, gain_vec, grad_out):
    normal = values * inverse
    scaled = gain_vec * grad_out
    grad_in = inverse * (scaled - normal * jnp.mean(scaled * normal, axis=-1, keepdims=True))
    return grad_in


def dot(left, right, dims):
    return lax.dot_general(left, right, (dims, ((), ())), preferred_element_type=F32)


def in_two(values):
    if values.dtype == BF16:
        return (values,)
    top = values.astype(BF16)
    return top, (values - top.astype(F32)).astype(BF16)


def fine_dot(left, right, dims):
    lefts, rights = in_two(left), in_two(right)
    total = dot(lefts[0], rights[0], dims)
    for low in rights[1:]:
        total = total + dot(lefts[0], low, dims)
    for low in lefts[1:]:
        total = total + dot(low, rights[0], dims)
    return total


NN = ((1,), (0,))
NT = ((1,), (1,))
TN = ((0,), (0,))


def valid_column(valid_len):
    return (lax.broadcasted_iota(jnp.int32, (SEG_LEN, 1), 0) < valid_len).astype(F32)


def block_probs(query_block, key_rows, start, valid_len):
    scores = dot(query_block, key_rows, NT) * (DH**-0.5)
    row_pos = start + lax.broadcasted_iota(jnp.int32, scores.shape, 0)
    col_pos = lax.broadcasted_iota(jnp.int32, scores.shape, 1)
    allowed = (row_pos >= col_pos) & (col_pos < valid_len)
    scores = jnp.where(allowed, scores, masked_score)
    weights = jnp.exp(scores - jnp.max(scores, axis=-1, keepdims=True))
    return weights / jnp.sum(weights, axis=-1, keepdims=True)


def retrieve(query_feat, memory, normal):
    numerator = fine_dot(query_feat, memory, NN)
    denominator = jnp.sum(query_feat * normal, axis=-1, keepdims=True) + 1.0
    return numerator / denominator, denominator


def greet_sequence():
    seg = lax.axis_index("seg")
    place = lax.rem(seg, SEGS)
    barrier = pltpu.get_barrier_semaphore()
    for distance in range(1, SEGS):
        other = seg - place + lax.rem(place + distance, SEGS)
        pl.semaphore_signal(barrier, inc=1, device_id={"seg": other}, device_id_type=MESH)
    pl.semaphore_wait(barrier, SEGS - 1)


def sequence_copies(source, land, send_sem, recv_sem, sign):
    seg = lax.axis_index("seg")
    count = lax.axis_size("seg")
    place = lax.rem(seg, SEGS)
    copies = []
    for distance in range(1, SEGS):
        copy = pltpu.make_async_remote_copy(
            src_ref=source,
            dst_ref=land.at[distance - 1],
            send_sem=send_sem.at[distance - 1],
            recv_sem=recv_sem.at[distance - 1],
            device_id={"seg": lax.rem(seg + count + sign * distance, count)},
            device_id_type=MESH,
        )
        after, before = place + distance < SEGS, place >= distance
        copies.append((copy, after, before) if sign > 0 else (copy, before, after))
    return copies


def head_cols(head):
    return pl.ds(pl.multiple_of(head * DH, DH), DH)


def attn_front_kernel(
    gate_ref, valid_ref, query_ref, key_ref, value_ref,
    mixed_ref, local_ref, before_ref, update_ref,
    land, send_sem, recv_sem,
):
    heads = update_ref.shape[0]
    valid_len = valid_ref[0]
    greet_sequence()
    copies = sequence_copies(update_ref, land, send_sem, recv_sem, 1)

    def make_update(head, carry):
        cols = head_cols(head)
        key_feat = elu_plus(key_ref[:, cols].astype(F32)) * valid_column(valid_len)
        update_ref[head, :DH] = fine_dot(key_feat, value_ref[:, cols], TN)
        normal = jnp.sum(key_feat, axis=0, keepdims=True)
        update_ref[head, DH:] = jnp.broadcast_to(normal, (MEM_ROWS - DH, DH))
        return carry

    lax.fori_loop(0, heads, make_update, 0)
    for copy, sends, _ in copies:

        @pl.when(sends)
        def _(copy=copy):
            copy.start()

    def local(head, carry):
        cols = head_cols(head)
        for start in range(0, SEG_LEN, BLOCK):
            rows, seen = slice(start, start + BLOCK), slice(0, start + BLOCK)
            probs = block_probs(query_ref[rows, cols], key_ref[seen, cols], start, valid_len)
            local_ref[rows, cols] = dot(probs.astype(BF16), value_ref[seen, cols], NN)
        return carry

    lax.fori_loop(0, heads, local, 0)
    before_ref[...] = jnp.zeros_like(before_ref)
    for distance, (copy, sends, gets) in enumerate(copies):

        @pl.when(sends)
        def _(copy=copy):
            copy.wait_send()

        @pl.when(gets)
        def _(copy=copy, distance=distance):
            copy.wait_recv()
            before_ref[...] += land[distance]

    def mix(head, carry):
        cols = head_cols(head)
        gate = gate_ref[head]
        query_feat = elu_plus(query_ref[:, cols].astype(F32))
        memory, normal = before_ref[head, :DH], before_ref[head, DH : DH + 1]
        retrieved, _ = retrieve(query_feat, memory, normal)
        mixed_ref[:, cols] = (gate * retrieved + (1.0 - gate) * local_ref[:, cols]).astype(BF16)
        return carry

    lax.fori_loop(0, heads, mix, 0)


def attn_front(gate, valid, query, key, value, cid):
    rows, cols = query.shape
    heads = cols // DH
    scalar, vmem = pl.BlockSpec(memory_space=pltpu.SMEM), pl.BlockSpec(memory_space=pltpu.VMEM)
    memory = jax.ShapeDtypeStruct((heads, MEM_ROWS, DH), F32)
    return pl.pallas_call(
        attn_front_kernel,
        in_specs=[scalar] * 2 + [vmem] * 3,
        out_specs=[vmem] * 4,
        out_shape=[
            jax.ShapeDtypeStruct((rows, cols), BF16),
            jax.ShapeDtypeStruct((rows, cols), F32),
            memory,
            memory,
        ],
        scratch_shapes=[
            pltpu.VMEM((SEGS - 1, heads, MEM_ROWS, DH), F32),
            pltpu.SemaphoreType.DMA((SEGS - 1,)),
            pltpu.SemaphoreType.DMA((SEGS - 1,)),
        ],
        cost_estimate=pl.CostEstimate(
            flops=4 * rows * rows * cols, bytes_accessed=60 * 2**20, transcendentals=rows * rows * heads
        ),
        compiler_params=pltpu.CompilerParams(
            collective_id=cid, has_side_effects=True, vmem_limit_bytes=40 * 2**20
        ),
    )(gate, valid, query, key, value)


def attn_back_kernel(
    gate_ref, valid_ref, d_out_ref, weight_ref, query_ref, key_ref, value_ref, local_ref, memory_ref,
    d_query_ref, d_key_ref, d_value_ref, gate_grad_ref,
    d_mixed, feat, d_key_sum, d_value_sum, back, land, update, send_sem, recv_sem,
):
    heads = memory_ref.shape[0]
    valid_len = valid_ref[0]
    greet_sequence()
    copies = sequence_copies(back, land, send_sem, recv_sem, -1)
    d_mixed[...] = dot(d_out_ref[...], weight_ref[...], NT)

    def memory_back(head, carry):
        cols = head_cols(head)
        gate = gate_ref[head]
        query_vals = query_ref[:, cols].astype(F32)
        query_feat = elu_plus(query_vals)
        memory, normal = memory_ref[head, :DH], memory_ref[head, DH : DH + 1]
        retrieved, denominator = retrieve(query_feat, memory, normal)
        d_head = d_mixed[:, cols]
        gate_grad_ref[head] = jnp.broadcast_to(
            jnp.sum(d_head * (retrieved - local_ref[:, cols]), axis=0, keepdims=True), (8, DH)
        )
        d_retrieved = gate * d_head
        d_numerator = d_retrieved / denominator
        d_denominator = -jnp.sum(d_retrieved * retrieved, axis=-1, keepdims=True) / denominator
        d_feat = fine_dot(d_numerator, memory, NT) + d_denominator * normal
        feat[:, cols] = d_feat * elu_slope(query_vals)
        back[head, :DH] = fine_dot(query_feat, d_numerator, TN).astype(BF16)
        d_normal = jnp.sum(d_denominator * query_feat, axis=0, keepdims=True)
        back[head, DH:] = jnp.broadcast_to(d_normal, (MEM_ROWS - DH, DH)).astype(BF16)
        return carry

    lax.fori_loop(0, heads, memory_back, 0)
    for copy, sends, _ in copies:

        @pl.when(sends)
        def _(copy=copy):
            copy.start()

    d_key_sum[...] = jnp.zeros_like(d_key_sum)
    d_value_sum[...] = jnp.zeros_like(d_value_sum)

    def local_back(head, carry):
        cols = head_cols(head)
        keep = 1.0 - gate_ref[head]
        for start in range(0, SEG_LEN, BLOCK):
            rows, seen = slice(start, start + BLOCK), slice(0, start + BLOCK)
            query_block = query_ref[rows, cols]
            probs = block_probs(query_block, key_ref[seen, cols], start, valid_len)
            d_local = (keep * d_mixed[rows, cols]).astype(BF16)
            d_probs = dot(d_local, value_ref[seen, cols], NT)
            row_dot = jnp.sum(probs * d_probs, axis=-1, keepdims=True)
            d_scores = (probs * (d_probs - row_dot) * (DH**-0.5)).astype(BF16)
            d_query = dot(d_scores, key_ref[seen, cols], NN) + feat[rows, cols]
            d_query_ref[rows, cols] = d_query.astype(BF16)
            d_key_sum[seen, cols] += dot(d_scores, query_block, TN)
            d_value_sum[seen, cols] += dot(probs.astype(BF16), d_local, TN)
        return carry

    lax.fori_loop(0, heads, local_back, 0)
    update[...] = jnp.zeros_like(update)
    for distance, (copy, sends, gets) in enumerate(copies):

        @pl.when(sends)
        def _(copy=copy):
            copy.wait_send()

        @pl.when(gets)
        def _(copy=copy, distance=distance):
            copy.wait_recv()
            update[...] += land[distance].astype(F32)

    def finish_back(head, carry):
        cols = head_cols(head)
        valid = valid_column(valid_len)
        key_vals = key_ref[:, cols].astype(F32)
        memory, normal = update[head, :DH], update[head, DH : DH + 1]
        d_feat = (fine_dot(value_ref[:, cols], memory, NT) + normal) * valid
        d_key_ref[:, cols] = (d_key_sum[:, cols] + d_feat * elu_slope(key_vals)).astype(BF16)
        key_feat = elu_plus(key_vals) * valid
        d_value = d_value_sum[:, cols] + fine_dot(key_feat, memory, NN)
        d_value_ref[:, cols] = d_value.astype(BF16)
        return carry

    lax.fori_loop(0, heads, finish_back, 0)


def attn_back(gate, valid, d_out, weight, query, key, value, local, memory, cid):
    rows, cols = query.shape
    heads = cols // DH
    scalar, vmem = pl.BlockSpec(memory_space=pltpu.SMEM), pl.BlockSpec(memory_space=pltpu.VMEM)
    wide = pltpu.VMEM((rows, cols), F32)
    narrow = jax.ShapeDtypeStruct((rows, cols), BF16)
    return pl.pallas_call(
        attn_back_kernel,
        in_specs=[scalar] * 2 + [vmem] * 7,
        out_specs=[vmem] * 4,
        out_shape=[narrow, narrow, narrow, jax.ShapeDtypeStruct((heads, 8, DH), F32)],
        scratch_shapes=[
            wide,
            wide,
            wide,
            wide,
            pltpu.VMEM((heads, MEM_ROWS, DH), BF16),
            pltpu.VMEM((SEGS - 1, heads, MEM_ROWS, DH), BF16),
            pltpu.VMEM((heads, MEM_ROWS, DH), F32),
            pltpu.SemaphoreType.DMA((SEGS - 1,)),
            pltpu.SemaphoreType.DMA((SEGS - 1,)),
        ],
        cost_estimate=pl.CostEstimate(
            flops=10 * rows * rows * cols + 2 * rows * cols * d_out.shape[1],
            bytes_accessed=100 * 2**20,
            transcendentals=rows * rows * heads,
        ),
        compiler_params=pltpu.CompilerParams(
            collective_id=cid, has_side_effects=True, vmem_limit_bytes=48 * 2**20
        ),
    )(gate, valid, d_out, weight, query, key, value, local, memory)


def per_device(
    tokens,
    cotangent,
    gain_attn,
    gain_mlp,
    w_query,
    w_key,
    w_value,
    w_out,
    w_gate,
    w_up,
    w_down,
    mem_gate,
    lengths,
):
    seg_index = lax.axis_index("seg")
    head_index = lax.axis_index("head")
    head_groups = lax.axis_size("head")
    seg_size = lax.axis_size("seg")
    position = seg_index % SEGS
    sequence = seg_index // SEGS
    seq_length = jnp.sum(jnp.where(lax.iota(jnp.int32, lengths.shape[0]) == sequence, lengths, 0))
    valid_len = jnp.where(position == SEGS - 1, seq_length, SEG_LEN).reshape(1)
    heads = mem_gate.shape[0]
    cols = heads * DH

    token_vals = tokens.astype(F32)
    gathered_tokens, gathered_attn, query_rows, key_rows, value_rows = gather_project(
        tokens, gain_attn, w_query, w_key, w_value, head_groups, 4
    )
    cotangent, key_rows = lax.optimization_barrier((cotangent, key_rows))
    gathered_grad = lax.all_gather(cotangent, "head", axis=0, tiled=True)
    mix_sig = jax.nn.sigmoid(mem_gate)
    mixed_attn, local_attn, memory_prev, update = attn_front(
        mix_sig, valid_len, query_rows, key_rows, value_rows, 5
    )
    after = memory_prev + update
    memory_after = (after[:, :DH] * SEG_LEN ** (-0.5))[None]
    normal_after = (after[:, DH] / SEG_LEN)[None]
    all_hidden, flip_mlp, silu, slope, act, pair = attn_out_sum(
        mixed_attn, w_out, gathered_tokens, gain_mlp, w_gate, w_up, w_down, head_groups, 1
    )
    own_rows = tokens.shape[0]
    hidden_res = lax.dynamic_slice_in_dim(all_hidden, head_index * own_rows, own_rows, 0)
    d_gate_a, d_up_a, gate_a, up_a, down_a = mlp_half(
        flip_mlp, gathered_grad, silu, slope, act, w_down, 0
    )
    gate_a, up_a, down_a = lax.psum((gate_a, up_a, down_a), "seg")
    d_gate_b, d_up_b, gate_b, up_b, down_b = mlp_half(
        flip_mlp, gathered_grad, silu, slope, act, w_down, 1
    )
    gathered_hidden, d_hidden, gain_mlp_rows, down_b, gate_b = mlp_back_sum(
        (d_gate_a, d_gate_b),
        (d_up_a, d_up_b),
        w_gate,
        w_up,
        all_hidden,
        gathered_grad,
        gain_mlp,
        (down_b, gate_b),
        (BLOCK, cols),
        seg_size,
        head_groups,
        2,
    )
    d_queries, d_keys, d_values, gate_cols = attn_back(
        mix_sig,
        valid_len,
        gathered_hidden,
        w_out,
        query_rows,
        key_rows,
        value_rows,
        local_attn,
        memory_prev,
        3,
    )
    pair, grad_query, grad_key, grad_value, grad_out, gain_attn_rows = attn_weights(
        gathered_attn,
        gathered_hidden,
        mixed_attn,
        d_queries,
        d_keys,
        d_values,
        w_query,
        w_key,
        w_value,
        pair,
    )
    width = gain_attn.shape[0]
    pair = lax.psum_scatter(pair, "head", scatter_dimension=0, tiled=True)
    output = (hidden_res + pair[:, :width].astype(F32)).astype(BF16)
    d_normed_attn = pair[:, width:].astype(F32)
    grad_in_attn = norm_backward(token_vals, inverse_rms(token_vals), gain_attn, d_normed_attn)
    grad_tokens = (d_hidden + grad_in_attn).astype(BF16)
    gate_part = mix_sig * (1.0 - mix_sig) * jnp.sum(gate_cols[:, 0], axis=-1)
    slots = jnp.where(
        (lax.iota(jnp.int32, head_groups) == head_index)[:, None], gate_part[None], 0.0
    )
    gain_attn_part = jnp.sum(gain_attn_rows, axis=0) / gain_attn
    gain_mlp_part = jnp.sum(gain_mlp_rows, axis=0)
    parts = jnp.concatenate([gain_attn_part, gain_mlp_part, slots.reshape(-1)])
    lines = -(-parts.shape[0] // (8 * DH)) * 8
    parts = jnp.pad(parts, (0, lines * DH - parts.shape[0])).reshape(lines, DH)
    small, *late = grad_sum(
        parts,
        [up_b, grad_out, grad_query, grad_key, grad_value],
        (cols, cols),
        seg_size,
        head_groups,
        0,
    )
    small = small.reshape(-1)
    grad_mem_gate = lax.dynamic_slice(small, (2 * width + head_index * heads,), (heads,))
    grads = widen(
        [(1, gate_a, gate_b), (1, up_a, late[0]), (0, down_a, down_b)]
        + [(0, grad) for grad in late[1:]],
        (cols, cols),
    )
    return (
        output,
        grad_tokens,
        memory_after,
        normal_after,
        small[:width],
        small[width : 2 * width],
        grads[4],
        grads[5],
        grads[6],
        grads[3],
        grads[0],
        grads[1],
        grads[2],
        grad_mem_gate,
    )


def solution(mesh):
    return jax.shard_map(
        per_device,
        mesh=mesh,
        in_specs=(
            P(("seg", "head"), None),
            P(("seg", "head"), None),
            P(),
            P(),
            P(None, "head"),
            P(None, "head"),
            P(None, "head"),
            P("head", None),
            P(None, "head"),
            P(None, "head"),
            P("head", None),
            P("head"),
            P(),
        ),
        out_specs=(
            P(("seg", "head"), None),
            P(("seg", "head"), None),
            P("seg", "head", None, None),
            P("seg", "head", None),
            P(),
            P(),
            P(None, "head"),
            P(None, "head"),
            P(None, "head"),
            P("head", None),
            P(None, "head"),
            P(None, "head"),
            P("head", None),
            P("head"),
        ),
        check_vma=False,
    )
```
